32 devices in a mesh: groups: 2 (over y), tx: 4 (over z), ty: 2 (over x), pb: 2 (over core).
Axes of the slice: x: 2, y: 2, z: 4, core: 2. Of those that a mesh axis runs over, the one named last changes fastest.
Arguments:
- displacement: float32 [6, 256, 256], P(None, ('tx', 'pb'), 'ty'), may hold values from -3 to 3
- direction: float32 [6, 256, 256], P(None, ('tx', 'pb'), 'ty'), may hold values from -3 to 3
- load: float32 [6, 256, 256], P(None, ('tx', 'pb'), 'ty'), may hold values from -6 to 6
- w_in: bfloat16 [256, 12], replicated, may hold values from -1.75 to 1.75
- b_in: float32 [256], replicated, may hold values from -3 to 3
- w_mid: bfloat16 [256, 256], replicated, may hold values from -0.375 to 0.375
- b_mid: float32 [256], replicated, may hold values from -3 to 3
- w_out: bfloat16 [12, 256], replicated, may hold values from -0.375 to 0.375
- fitting_disp: float32 [6, 4096], P(None, ('groups', 'tx', 'ty', 'pb')), parts along dimension 1, may hold values from -3 to 3
- fitting_dir: float32 [6, 4096], P(None, ('groups', 'tx', 'ty', 'pb')), parts along dimension 1, may hold values from -3 to 3
- tie_node: int32 [24576], P(('groups', 'tx', 'ty', 'pb')), parts along dimension 0, may hold values from 0 to 4095
- tie_owner: int32 [24576, 1], P(('groups', 'tx', 'ty', 'pb')), parts along dimension 0, may hold values from 0 to 7; in each aligned block of 768 rows (0 to 767, 768 to 1535, ...) at most 288 rows name the same one
- tie_slot: int32 [24576], P(('groups', 'tx', 'ty', 'pb')), parts along dimension 0, may hold values from 0 to 127
Outputs:
- node_residual: float32 [6, 512, 256], P(None, ('groups', 'tx', 'pb'), 'ty'), parts along dimension 1
- node_tangent: float32 [6, 512, 256], P(None, ('groups', 'tx', 'pb'), 'ty'), parts along dimension 1
- fitting_residual: float32 [6, 4096], P(None, ('groups', 'tx', 'ty', 'pb')), parts along dimension 1
- fitting_tangent: float32 [6, 4096], P(None, ('groups', 'tx', 'ty', 'pb')), parts along dimension 1
The draws below stay inside these ranges and needn't reach their ends.
There are 2 independent parts, one for each index of `groups`. The reference program is written for one: setup_inputs(seed, part) draws one part's arguments, and reference() takes and returns one part's arrays. A program takes and returns all parts, laid end to end along the dimension named above; an argument that names none is the same for every part. Nothing has to cross between parts.
Inputs may be any that keep to these rules, and one draw needn't show every extreme that they name: `tie_owner`: in each aligned block of 768 ties (the ties of one device) no owner is named more than 288 times, a bound that some block reaches.
All inputs are finite; a program needn't handle non-finite values.
Results may differ from the reference program's by a relative error of at most 0.0003.
Values sent between devices are 32-bit elements; how exact they have to be, the bound alone decides.
No kernel may reach another device: no remote copies, remote signals or barrier semaphores. Data moves between devices by JAX's collectives and lax.ppermute only.
A program may use at most 64 MiB of HBM per device.

```python
import math
import jax
import jax.numpy as jnp
import numpy as np
from jax import lax

CX = 32
CY = 128
HID = 256
TIE_DEV = 768
FIT_DEV = 128
NX = 256
NY = 256
CAP = 288
TIES = 12288
FITS = 2048
N_TX = 4
N_TY = 2
N_PB = 2


def touch_ends(entries, rng, least, high):
    shape = entries.shape
    index_at = [jax.random.randint(jax.random.fold_in(rng, axis), (), 0, shape[axis]) for axis in range(len(shape))]
    entries = entries.at[tuple(index_at)].set(least)
    longest = shape.index(max(shape))
    index_at[longest] = (index_at[longest] + 1) % shape[longest]
    return entries.at[tuple(index_at)].set(high)


def levels(stream_key, extent, shards, smallest, largest):
    def one(dim, parts):
        heights = jax.random.uniform(jax.random.fold_in(jax.random.fold_in(stream_key, 6), dim), (parts,), jnp.float32, smallest / len(shards), largest / len(shards))
        return jnp.repeat(jnp.exp(heights), extent[dim] // parts).reshape((-1,) + (1,) * (len(extent) - dim - 1))

    loudness = one(*shards[0])
    for cut in shards[1:]:
        loudness = loudness * one(*cut)
    return loudness


def assign_block(own_key, own, number, rows, count, top, reach, skew):
    order = jax.random.permutation(own_key, count)
    crowded, common = portions_of(count, rows * top, reach, skew, True), portions_of(count, rows * top, reach, skew, False)
    places = jnp.arange(count)

    def named(tallies, rotation):
        used = int((tallies > 0).sum())
        fixed = max(1, used // 4)
        shifted = fixed + (places - fixed + rotation * (used - fixed)) % max(1, count - fixed)
        return jnp.zeros((count,), jnp.int32).at[order[jnp.where(places < fixed, places, shifted)]].set(jnp.asarray(tallies, jnp.int32))

    tallies = jnp.where(number % 4 == 0, named(crowded, number // 4), named(common, number - number // 4 - 1))
    mixed = jax.random.permutation(jax.random.fold_in(own, 3), count)
    source_of, receiver = mixed[0:count // 2 * 2:2], mixed[1:count // 2 * 2:2]
    room = jnp.minimum(tallies[source_of] - 1, reach - tallies[receiver]) // 2
    room = jnp.where((source_of == order[0]) | (receiver == order[0]) | (tallies[receiver] == 0), 0, jnp.maximum(room, 0))
    shifted = jax.random.randint(jax.random.fold_in(own, 4), (count // 2,), 0, 1 << 20) % (room + 1)
    tallies = tallies.at[source_of].add(-shifted).at[receiver].add(shifted)
    members = jnp.searchsorted(jnp.cumsum(tallies), jnp.arange(rows * top), side="right").astype(jnp.int32)
    table = members.reshape(top, rows).T
    table = table[jax.random.permutation(jax.random.fold_in(own, 1), rows)]
    rotation = jax.random.randint(jax.random.fold_in(own, 2), (rows, 1), 0, top)
    return jnp.take_along_axis(table, (jnp.arange(top)[None, :] + rotation) % top, axis=1)


def portions_of(count, total, bound, slope, full):
    portions = [(1 << 20) // math.isqrt(standing ** slope) + 1 for standing in range(1, count + 1)]
    largest = bound if full else min(bound, max(-(-total // count), total * portions[0] // sum(portions)))
    least = 1 if total - largest >= count - 1 else 0
    holding, rest = [largest] + [least] * (count - 1), total - largest - least * (count - 1)
    while rest > 0:
        free = [i for i in range(1, count) if holding[i] < largest] or [i for i in range(1, count) if holding[i] < bound]
        mass, left = sum([portions[i] for i in free]), rest
        for i in free:
            addition = min(bound - holding[i], max(1, left * portions[i] // mass), rest)
            holding[i] = holding[i] + addition
            rest = rest - addition
    return np.array(holding)


def bell_draw(key, dims, deviation, limit, cuts=(), held_as=jnp.bfloat16):
    factor_of = levels(key, dims, cuts, -0.22, 0.18) if cuts else 1.0
    entries = jax.random.normal(key, dims, jnp.float32) * deviation * factor_of
    return jnp.minimum(jnp.maximum(entries, -limit), limit).astype(held_as)


def setup_inputs(seed: int = 0, part: int = 0) -> dict:
    key_list = jax.random.split(jax.random.key(seed), 14)
    own_keys = jax.random.split(jax.random.fold_in(key_list[13], part), 14)
    displacement = bell_draw(key_list[0], (6, NX, NY), 0.5, 3.0, ((1, 8), (2, 2)), jnp.float32)
    direction = bell_draw(key_list[1], (6, NX, NY), 0.5, 3.0, ((1, 8), (2, 2)), jnp.float32)
    load = bell_draw(key_list[2], (6, NX, NY), 1.0, 6.0, ((1, 8), (2, 2)), jnp.float32)
    w_in = bell_draw(key_list[3], (HID, 12), 12 ** -0.5, 1.75)
    b_in = bell_draw(key_list[4], (HID,), 0.5, 3.0, (), jnp.float32)
    w_mid = bell_draw(key_list[5], (HID, HID), HID ** -0.5, 0.375)
    b_mid = bell_draw(key_list[6], (HID,), 0.5, 3.0, (), jnp.float32)
    w_out = bell_draw(key_list[7], (12, HID), HID ** -0.5, 0.375)
    fitting_disp = bell_draw(own_keys[8], (6, FITS), 0.5, 3.0, ((1, 16),), jnp.float32)
    fitting_dir = bell_draw(own_keys[9], (6, FITS), 0.5, 3.0, ((1, 16),), jnp.float32)
    tie_node = touch_ends(jax.random.randint(own_keys[10], (TIES,), 0, CX * CY), jax.random.fold_in(own_keys[10], 1), 0, (CX * CY) - 1).astype(jnp.int32)
    tie_owner_keys = jax.random.split(jax.random.fold_in(own_keys[11], 1), TIES // TIE_DEV)
    tie_owner_turns = jax.random.permutation(jax.random.fold_in(own_keys[11], 3), TIES // TIE_DEV)
    tie_owner = jax.vmap(lambda own, number: assign_block(jax.random.fold_in(own_keys[11], 2), own, number, TIE_DEV, N_TX * N_TY, 1, CAP, 2))(tie_owner_keys, tie_owner_turns).reshape((TIES, 1))
    tie_slot = touch_ends(jax.random.randint(own_keys[12], (TIES,), 0, FIT_DEV), jax.random.fold_in(own_keys[12], 1), 0, FIT_DEV - 1).astype(jnp.int32)
    return dict(displacement=displacement, direction=direction, load=load, w_in=w_in, b_in=b_in, w_mid=w_mid, b_mid=b_mid, w_out=w_out, fitting_disp=fitting_disp, fitting_dir=fitting_dir, tie_node=tie_node, tie_owner=tie_owner, tie_slot=tie_slot)


tie_stiffness = 2.0
gauss_low = 0.5 - 0.5 / math.sqrt(3.0)
gauss_high = 0.5 + 0.5 / math.sqrt(3.0)

def stress_pair(strain, strain_dir, w_in, b_in, w_mid, b_mid, w_out):
    col_width = strain.shape[1]
    joined = jnp.concatenate([strain, strain_dir], axis=1).astype(jnp.bfloat16)
    layer_one = jnp.dot(w_in, joined, preferred_element_type=jnp.float32)
    act_one = jnp.tanh(layer_one[:, :col_width] + b_in[:, None])
    hid_one = act_one.astype(jnp.bfloat16)
    lin_one = ((1.0 - act_one * act_one) * layer_one[:, col_width:]).astype(jnp.bfloat16)
    layer_two = jnp.dot(w_mid, jnp.concatenate([hid_one, lin_one], axis=1), preferred_element_type=jnp.float32)
    act_two = jnp.tanh(layer_two[:, :col_width] + b_mid[:, None])
    hid_two = act_two.astype(jnp.bfloat16)
    lin_two = ((1.0 - act_two * act_two) * layer_two[:, col_width:]).astype(jnp.bfloat16)
    layer_three = jnp.dot(w_out, jnp.concatenate([hid_two, lin_two], axis=1), preferred_element_type=jnp.float32)
    return (layer_three[:, :col_width], layer_three[:, col_width:])

def strain_points(extended, points):
    node_base = extended[:, :-1, :-1]
    node_right = extended[:, 1:, :-1]
    node_upper = extended[:, :-1, 1:]
    node_corner = extended[:, 1:, 1:]
    along_low = node_right - node_base
    along_high = node_corner - node_upper
    across_low = node_upper - node_base
    across_high = node_corner - node_right
    strains = []
    tangents = []
    for right_frac, right_rest, upper_frac, upper_rest in points:
        grad_x = upper_rest * along_low + upper_frac * along_high
        grad_y = right_rest * across_low + right_frac * across_high
        strains.append(jnp.concatenate([grad_x[:6], grad_y[:6]], axis=0))
        tangents.append(jnp.concatenate([grad_x[6:], grad_y[6:]], axis=0))
    return (jnp.stack(strains, 1), jnp.stack(tangents, 1))

def assemble(stress, stress_dir, points):
    total = None
    for position, (right_frac, right_rest, upper_frac, upper_rest) in enumerate(points):
        along = jnp.concatenate([stress[:6, position], stress_dir[:6, position]], 0) * 0.25
        across = jnp.concatenate([stress[6:, position], stress_dir[6:, position]], 0) * 0.25
        at_base = -upper_rest * along - right_rest * across
        at_right = upper_rest * along - right_frac * across
        at_upper = -upper_frac * along + right_rest * across
        at_corner = upper_frac * along + right_frac * across
        term = jnp.pad(at_base, ((0, 0), (0, 1), (0, 1))) + jnp.pad(at_right, ((0, 0), (1, 0), (0, 1))) + jnp.pad(at_upper, ((0, 0), (0, 1), (1, 0))) + jnp.pad(at_corner, ((0, 0), (1, 0), (1, 0)))
        total = term if total is None else total + term
    return total

def reference(displacement, direction, load, w_in, b_in, w_mid, b_mid, w_out, fitting_disp, fitting_dir, tie_node, tie_owner, tie_slot):
    fields = jnp.concatenate([displacement, direction], 0)
    extended = jnp.pad(fields, ((0, 0), (0, 1), (0, 1)))
    points = []
    for upper_frac in (gauss_low, gauss_high):
        for right_frac in (gauss_low, gauss_high):
            points.append((right_frac, 1.0 - right_frac, upper_frac, 1.0 - upper_frac))
    strain, strain_dir = strain_points(extended, points)
    block_x = math.gcd(NX, 8)
    block_count = NX // block_x

    def to_blocks(values):
        return values.reshape(12, 4, block_count, block_x, NY).transpose(2, 0, 1, 3, 4).reshape(block_count, 12, 4 * block_x * NY)

    def from_blocks(values):
        return values.reshape(block_count, 12, 4, block_x, NY).transpose(1, 2, 0, 3, 4).reshape(12, 4, NX, NY)

    def apply_block(pair):
        return stress_pair(pair[0], pair[1], w_in, b_in, w_mid, b_mid, w_out)
    stress_blocks, dir_blocks = lax.map(apply_block, (to_blocks(strain), to_blocks(strain_dir)))
    stress = from_blocks(stress_blocks)
    stress_dir = from_blocks(dir_blocks)
    forces = assemble(stress, stress_dir, points)[:, :NX, :NY]
    tie_total = tie_node.shape[0]
    device_ids = jnp.arange(tie_total, dtype=jnp.int32) // TIE_DEV
    core_ids = device_ids % N_PB
    tile_ids = device_ids // N_PB
    node_row = (tile_ids // N_TY * N_PB + core_ids) * CX + tie_node // CY
    node_col = tile_ids % N_TY * CY + tie_node % CY
    fit_index = (tie_owner[:, 0] * N_PB + core_ids) * FIT_DEV + tie_slot
    fitting = jnp.concatenate([fitting_disp, fitting_dir], 0)
    pulled = tie_stiffness * (fields[:, node_row, node_col] - fitting[:, fit_index])
    forces = forces.at[:, node_row, node_col].add(pulled)
    reaction = jnp.zeros_like(fitting).at[:, fit_index].add(-pulled)
    return (forces[:6] - load, forces[6:], reaction[:6], reaction[6:])
```

```python
import math

import jax
import jax.numpy as jnp
from jax import lax
from jax.experimental import pallas as pl
from jax.experimental.pallas import tpu as pltpu
from jax.sharding import PartitionSpec as P

F32 = jnp.float32
BF16 = jnp.bfloat16
GAUSS = (0.5 - 0.5 / math.sqrt(3.0), 0.5 + 0.5 / math.sqrt(3.0))
COMPS = 16
COUNT_ROW = 6
DIRECT_PEERS = 8


def dot(a, b, dims=((1,), (0,))):
    return lax.dot_general(a, b, (dims, ((), ())), preferred_element_type=F32)


def split(value, terms):
    parts = []
    for _ in range(terms):
        part = value.astype(BF16)
        parts.append(part)
        value = value - part.astype(F32)
    return parts


def rows_of(value):
    return lax.broadcasted_iota(jnp.int32, value, 0)


def lanes_of(value):
    return lax.broadcasted_iota(jnp.int32, value, 1)


def one_hot(index, size):
    shape = (size, index.shape[1])
    return (rows_of(shape) == index).astype(F32).astype(BF16)


def as_line(ref):
    return jnp.concatenate([ref[row : row + 1, :] for row in range(ref.shape[0])], axis=1)


def paired(top, bottom):
    spare = jnp.zeros((2, top.shape[1]), F32)
    return jnp.concatenate([top, spare, bottom, spare], axis=0)


def strain_tile(f00, f10, f01, f11):
    along_low = f10 - f00
    along_high = f11 - f01
    across_low = f01 - f00
    across_high = f11 - f10
    shape = f00.shape
    row = rows_of(shape)
    ones = ((row == 6) | (row == 7) | (row == 14)).astype(F32)
    groups = []
    for frac in GAUSS:
        groups.append((((1.0 - frac) * along_low + frac * along_high) + ones).astype(BF16))
    for frac in GAUSS:
        groups.append(((1.0 - frac) * across_low + frac * across_high).astype(BF16))
    return jnp.concatenate(groups, axis=0)


def stress_sums(strain, w_first, w_mid, b_mid, w_last):
    hid = w_mid.shape[0]
    total = [None, None]
    for point in range(4):
        first = dot(w_first[point * 2 * hid : (point + 1) * 2 * hid, :], strain)
        act = jnp.tanh(first[:hid])
        lin = ((1.0 - act * act) * first[hid:]).astype(BF16)
        second = dot(w_mid[...], act.astype(BF16))
        second_dir = dot(w_mid[...], lin)
        bias = b_mid[...]
        bias = jnp.concatenate([bias] * (second.shape[1] // bias.shape[1]), axis=1)
        act = jnp.tanh(second + bias)
        lin = ((1.0 - act * act) * second_dir).astype(BF16)
        last = w_last[point * 32 : (point + 1) * 32, :]
        for side, hidden in enumerate((act.astype(BF16), lin)):
            part = dot(last, hidden)
            total[side] = part if total[side] is None else total[side] + part
    return total


def corner_forces(primal, tangent):
    def both(group):
        return jnp.concatenate([primal[group * 8 : group * 8 + 8], tangent[group * 8 : group * 8 + 8]], axis=0)

    along = (both(0), both(1))
    across = (both(2), both(3))

    def mix(pair, weights):
        return (0.25 * weights[0]) * pair[0] + (0.25 * weights[1]) * pair[1]

    rest = (1.0 - GAUSS[0], 1.0 - GAUSS[1])
    along_rest = mix(along, rest)
    along_frac = mix(along, GAUSS)
    across_rest = mix(across, rest)
    across_frac = mix(across, GAUSS)
    return (
        -along_rest - across_rest,
        along_rest - across_frac,
        across_rest - along_frac,
        along_frac + across_frac,
    )


def prepare(name_count, separate, axes, *refs):
    (disp, dirn, fit_disp, fit_dir, node_ref, owner_ref, slot_ref, w_in, b_in, b_mid, w_out) = refs[:11]
    outs = list(refs[11:])
    fields, ties, w_first, w_last, b_cols, row_out, col_out = outs[:7]
    pay = outs[7:]
    peers, ty_count = axes
    row_total = fields.shape[0] // COMPS
    cols = fields.shape[1]
    slots = fit_disp.shape[1]
    tie_total = ties.shape[1]
    hid = w_in.shape[1]

    fields[...] = jnp.zeros(fields.shape, F32)
    for comp in range(6):
        fields[pl.ds(comp, row_total, stride=COMPS), :] = disp[comp * row_total : (comp + 1) * row_total, :]
        fields[pl.ds(8 + comp, row_total, stride=COMPS), :] = dirn[comp * row_total : (comp + 1) * row_total, :]

    row_out[0:COMPS, :] = fields[0:COMPS, :]
    row_out[COMPS : 2 * COMPS, :] = fields[(row_total - 1) * COMPS :, :]
    lane = lanes_of((COMPS, cols))
    for side, column in enumerate((0, cols - 1)):
        gathered = jnp.zeros((COMPS, cols), F32)
        for row in range(row_total):
            value = fields[row * COMPS : (row + 1) * COMPS, column : column + 1]
            gathered = jnp.where(lane == row, value, gathered)
        col_out[side * COMPS : (side + 1) * COMPS, :] = gathered

    bias_rows = split(b_in[...], 3)
    row = rows_of((8, hid))
    stacked = jnp.zeros((8, hid), F32)
    mid_stacked = jnp.zeros((8, hid), F32)
    for at, (one, two) in enumerate(zip(bias_rows, split(b_mid[...], 3))):
        stacked = jnp.where(row == at, one.astype(F32), stacked)
        mid_stacked = jnp.where(row == at, two.astype(F32), mid_stacked)
    lhs = jnp.concatenate([w_in[...].astype(F32), jnp.zeros((4, hid), F32), stacked], axis=0).astype(BF16)
    sel_shape = (24, 4 * COMPS)
    source = rows_of(sel_shape)
    target = lanes_of(sel_shape)
    for point in range(4):
        a_base = (point // 2) * COMPS
        c_base = (2 + point % 2) * COMPS
        for side in range(2):
            hit = (source < 6) & (target == a_base + 8 * side + source)
            hit = hit | ((source >= 6) & (source < 12) & (target == c_base + 8 * side + source - 6))
            if side == 0:
                for at, spot in enumerate((6, 7, 14)):
                    hit = hit | ((source == 16 + at) & (target == a_base + spot))
            block = dot(lhs, hit.astype(F32).astype(BF16), ((0,), (0,)))
            start = (2 * point + side) * hid
            w_first[start : start + hid, :] = block.astype(BF16)
    ones = (rows_of((8, 128)) < 3).astype(F32).astype(BF16)
    b_cols[...] = dot(mid_stacked.astype(BF16), ones, ((0,), (0,)))
    last_shape = (128, 12)
    target = rows_of(last_shape)
    source = lanes_of(last_shape)
    hit = target < 0
    for point in range(4):
        a_base = point * 32 + (point // 2) * 8
        c_base = point * 32 + 16 + (point % 2) * 8
        hit = hit | ((source < 6) & (target == a_base + source))
        hit = hit | ((source >= 6) & (target == c_base + source - 6))
    w_last[...] = dot(hit.astype(F32).astype(BF16), w_out[...]).astype(BF16)

    here = lax.axis_index("tx") * ty_count + lax.axis_index("ty")
    node = as_line(node_ref)
    slot = as_line(slot_ref)
    owner = owner_ref[...]
    if separate:
        owner = jnp.bitwise_xor(owner, here)
    node_row = lax.shift_right_logical(node, cols.bit_length() - 1)
    node_col = jnp.bitwise_and(node, cols - 1)
    hot_col = one_hot(node_col, cols)
    wide = dot(
        jnp.concatenate(split(fields[...], 3), axis=1), jnp.concatenate([hot_col] * 3, axis=0)
    )
    value = jnp.zeros((COMPS, tie_total), F32)
    for row in range(row_total):
        value = jnp.where(node_row == row, wide[row * COMPS : (row + 1) * COMPS], value)
    value = jnp.where(rows_of(value.shape) == COUNT_ROW, 1.0, value)
    ties[...] = value
    stack = jnp.concatenate(split(value, 3), axis=0)
    hot_slot = one_hot(slot, slots)
    fitting = paired(fit_disp[...], fit_dir[...])

    def bins(first, count):
        lhs = [
            stack * (owner == first + at).astype(F32).astype(BF16) for at in range(count)
        ]
        return dot(jnp.concatenate(lhs, axis=0), hot_slot, ((1,), (1,)))

    def folded(wide_bins, at):
        part = wide_bins[at * 48 : at * 48 + 48]
        return part[0:16] + part[16:32] + part[32:48]

    if separate:
        wide_bins = bins(0, peers)
        for peer in range(peers):
            pay[peer][0:COMPS, :] = fitting
            pay[peer][COMPS : 2 * COMPS, :] = folded(wide_bins, peer)
    else:
        block = math.gcd(peers, 8)

        def step(at, carry):
            wide_bins = bins(at * block, block)
            for peer in range(block):
                pay[0][at * block + peer, 0:COMPS, :] = fitting
                pay[0][at * block + peer, COMPS : 2 * COMPS, :] = folded(wide_bins, peer)
            return carry

        lax.fori_loop(0, peers // block, step, 0)


def interior(fields, w_first, w_mid, b_mid, w_last, forces, strain):
    row_total, cols = fields.shape[0] // COMPS, fields.shape[1]
    pairs = (row_total - 1) // 2
    keep = lanes_of((COMPS, cols)) < cols - 1

    def row_strain(row):
        base = fields[pl.ds(row * COMPS, COMPS), :]
        right = fields[pl.ds(row * COMPS + COMPS, COMPS), :]
        return strain_tile(base, right, pltpu.roll(base, cols - 1, 1), pltpu.roll(right, cols - 1, 1))

    def build(pair, carry):
        strain[pair] = jnp.concatenate([row_strain(2 * pair), row_strain(2 * pair + 1)], axis=1)
        return carry

    lax.fori_loop(0, pairs, build, 0)
    forces[...] = jnp.zeros(forces.shape, F32)

    def step(pair, carry):
        primal, tangent = stress_sums(strain[pair], w_first, w_mid, b_mid, w_last)
        for half in range(2):
            lanes = slice(half * cols, (half + 1) * cols)
            base, right, upper, corner = corner_forces(primal[:, lanes], tangent[:, lanes])
            base, right, upper, corner = (jnp.where(keep, part, 0.0) for part in (base, right, upper, corner))
            at = (2 * pair + half) * COMPS
            forces[pl.ds(at, COMPS), :] += base + pltpu.roll(upper, 1, 1)
            forces[pl.ds(at + COMPS, COMPS), :] += right + pltpu.roll(corner, 1, 1)
        return carry

    lax.fori_loop(0, pairs, step, 0)


def finish(names, axes, separate, *refs):
    ref = dict(zip(names, refs))
    peers, ty_count, tx_count, pb_count, col_phases = axes
    fields, ties, forces_in, load = ref["fields"], ref["ties"], ref["forces"], ref["load"]
    scratch = ref["scratch"]
    row_total, cols = fields.shape[0] // COMPS, fields.shape[1]
    slots = ref["pay0"].shape[-1]
    tie_total = ties.shape[1]
    lane = lanes_of((COMPS, cols))

    place = lax.axis_index("tx") * pb_count + lax.axis_index("pb")
    across = lax.axis_index("ty")
    row_even = place % 2 == 0
    col_even = across % 2 == 0

    def pick(cond, one, two):
        return jnp.where(cond, one, two)

    prev_row = pick(row_even, ref["row_b"][...], ref["row_a"][...])
    next_row = pick(row_even, ref["row_a"][...], ref["row_b"][...])

    zero = jnp.zeros((COMPS, cols), F32)
    col = [ref["col_" + phase][...] for phase in col_phases]
    diag = [(ref["diag_a" + phase][...], ref["diag_b" + phase][...]) for phase in col_phases]
    if len(col_phases) == 1:
        col.append(zero)
        diag.append((zero, zero))
    next_col = pick(col_even, col[0], col[1])
    prev_col = pick(col_even, col[1], col[0])
    next_diag = [pick(col_even, diag[0][at], diag[1][at]) for at in range(2)]
    prev_diag = [pick(col_even, diag[1][at], diag[0][at]) for at in range(2)]
    next_corner = (pick(row_even, next_diag[1], next_diag[0])[:, 0:1], pick(row_even, next_diag[0], next_diag[1])[:, 0:1])
    prev_corner = (
        pick(row_even, prev_diag[1], prev_diag[0])[:, cols - 1 : cols],
        pick(row_even, prev_diag[0], prev_diag[1])[:, cols - 1 : cols],
    )

    def column(inner, before, after):
        line = pltpu.roll(inner, 1, 1)
        line = jnp.where(lane == 0, before, line)
        return jnp.where(lane == row_total + 1, after, line)

    own_cols = ref["cols"]
    line_prev = column(prev_col, prev_corner[0], prev_corner[1])
    line_next = column(next_col, next_corner[0], next_corner[1])
    line_first = column(own_cols[0:COMPS, :], prev_row[:, 0:1], next_row[:, 0:1])
    line_final = column(
        own_cols[COMPS : 2 * COMPS, :], prev_row[:, cols - 1 : cols], next_row[:, cols - 1 : cols]
    )

    def shifted(row_value, beyond):
        return jnp.where(lane == cols - 1, beyond, pltpu.roll(row_value, cols - 1, 1))

    first_row = fields[0:COMPS, :]
    last_row = fields[(row_total - 1) * COMPS :, :]
    inner_row = fields[(row_total - 2) * COMPS : (row_total - 1) * COMPS, :]

    tile_inner = strain_tile(
        inner_row, last_row, pltpu.roll(inner_row, cols - 1, 1), pltpu.roll(last_row, cols - 1, 1)
    )
    tile_before = strain_tile(
        prev_row,
        first_row,
        shifted(prev_row, next_corner[0]),
        shifted(first_row, next_col[:, 0:1]),
    )
    tile_after = strain_tile(
        last_row,
        next_row,
        shifted(last_row, next_col[:, row_total - 1 : row_total]),
        shifted(next_row, next_corner[1]),
    )
    half = cols // 2
    low = lane < half
    back = cols - 1

    def two(left, right_line):
        return jnp.where(low, left, pltpu.roll(right_line, half + back, 1))

    left_base = two(line_prev, line_final)
    left_upper = two(line_first, line_next)
    right_base = two(pltpu.roll(line_prev, back, 1), pltpu.roll(line_final, back, 1))
    right_upper = two(pltpu.roll(line_first, back, 1), pltpu.roll(line_next, back, 1))
    tile_side = strain_tile(left_base, right_base, left_upper, right_upper)

    parts = []
    for pair in ((tile_inner, tile_before), (tile_after, tile_side)):
        primal, tangent = stress_sums(
            jnp.concatenate(pair, axis=1), ref["w_first"], ref["w_mid"], ref["b_mid"], ref["w_last"]
        )
        for at in range(2):
            lanes = slice(at * cols, (at + 1) * cols)
            parts.append(corner_forces(primal[:, lanes], tangent[:, lanes]))
    part_inner, part_before, part_after, part_side = parts

    def mask(value, keep):
        return jnp.where(keep, value, 0.0)

    def moved(value, keep):
        return pltpu.roll(mask(value, keep), 1, 1)

    inside = lane < cols - 1
    i_base, i_right, i_upper, i_corner = part_inner
    _, b_right, _, b_corner = part_before
    a_base, _, a_upper, _ = part_after
    s_base, s_right, s_upper, s_corner = part_side
    has_row = place > 0
    has_col = across > 0
    row_first = mask(mask(b_right, lane < cols) + moved(b_corner, inside), has_row)
    row_inner = mask(i_base, inside) + moved(i_upper, inside)
    row_last = mask(i_right, inside) + moved(i_corner, inside) + a_base + moved(a_upper, inside)
    first_lane = jnp.where(has_row, 0, 1)
    s_corner = mask(s_corner, (lane >= first_lane) & (lane < row_total))
    s_upper = mask(s_upper, (lane >= 1) & (lane <= row_total))
    col_first = mask(pltpu.roll(s_upper, back, 1) + s_corner, has_col)
    s_base = mask(s_base, (lane >= half) & (lane < half + row_total - 1))
    s_right = mask(s_right, (lane >= half) & (lane < half + row_total - 1))
    col_last = pltpu.roll(s_base + pltpu.roll(s_right, 1, 1), cols - half, 1)

    node = as_line(ref["node"])
    slot = as_line(ref["slot"])
    owner = ref["owner"][...]
    here = lax.axis_index("tx") * ty_count + across
    if separate:
        owner = jnp.bitwise_xor(owner, here)
    hot_slot = one_hot(slot, slots)
    hot_three = jnp.concatenate([hot_slot] * 3, axis=0)
    fit_value = jnp.zeros((COMPS, tie_total), F32)
    bins = jnp.zeros((COMPS, slots), F32)
    if separate:
        got = [ref["pay" + str(peer)][...] for peer in range(peers)]
        fit_all = jnp.concatenate([block[0:COMPS] for block in got], axis=0)
        wide = dot(jnp.concatenate(split(fit_all, 3), axis=1), hot_three)
        for peer in range(peers):
            fit_value = jnp.where(owner == peer, wide[peer * COMPS : (peer + 1) * COMPS], fit_value)
            bins = bins + got[peer][COMPS : 2 * COMPS]
    else:

        def step(peer, carry):
            fit_value, bins = carry
            block = ref["pay0"][peer]
            wide = dot(jnp.concatenate(split(block[0:COMPS], 3), axis=1), hot_three)
            return jnp.where(owner == peer, wide, fit_value), bins + block[COMPS : 2 * COMPS]

        fit_value, bins = lax.fori_loop(0, peers, step, (fit_value, bins))
    count = bins[COUNT_ROW : COUNT_ROW + 1]
    for out, fit, base in (("fit_res", "fit_disp", 0), ("fit_tan", "fit_dir", 8)):
        ref[out][...] = 2.0 * (count * ref[fit][...] - bins[base : base + 6])

    pulled = 2.0 * (ties[...] - fit_value)
    node_row = lax.shift_right_logical(node, cols.bit_length() - 1)
    node_col = jnp.bitwise_and(node, cols - 1)
    hot_col = one_hot(node_col, cols)
    sides = split(pulled, 2)
    lhs = []
    for row in range(row_total):
        hit = (node_row == row).astype(F32).astype(BF16)
        lhs.append(jnp.concatenate([side * hit for side in sides], axis=1))
    tie_forces = dot(
        jnp.concatenate(lhs, axis=0), jnp.concatenate([hot_col] * 2, axis=1), ((1,), (1,))
    )

    for row in range(row_total):
        total = forces_in[row * COMPS : (row + 1) * COMPS, :] + tie_forces[row * COMPS : (row + 1) * COMPS]
        total = total + jnp.where(lane == 0, col_first[:, row : row + 1], 0.0)
        total = total + jnp.where(lane == cols - 1, col_last[:, row : row + 1], 0.0)
        if row == 0:
            total = total + row_first
        if row == row_total - 2:
            total = total + row_inner
        if row == row_total - 1:
            total = total + row_last
        scratch[row * COMPS : (row + 1) * COMPS, :] = total
    for comp in range(6):
        rows = slice(comp * row_total, (comp + 1) * row_total)
        ref["res"][rows, :] = scratch[pl.ds(comp, row_total, stride=COMPS), :] - load[rows, :]
        ref["tan"][rows, :] = scratch[pl.ds(8 + comp, row_total, stride=COMPS), :]


def swaps(count, offset):
    pairs = []
    for low in range(offset, count - 1, 2):
        pairs += [(low, low + 1), (low + 1, low)]
    return pairs


def per_device(
    displacement,
    direction,
    load,
    w_in,
    b_in,
    w_mid,
    b_mid,
    w_out,
    fitting_disp,
    fitting_dir,
    tie_node,
    tie_owner,
    tie_slot,
):
    tx_count = lax.axis_size("tx")
    ty_count = lax.axis_size("ty")
    pb_count = lax.axis_size("pb")
    peers = tx_count * ty_count
    separate = peers <= DIRECT_PEERS and peers & (peers - 1) == 0
    _, row_total, cols = displacement.shape
    slots = fitting_disp.shape[1]
    tie_total = tie_node.shape[0]
    hid = w_mid.shape[0]
    flat = (6 * row_total, cols)
    disp2 = displacement.reshape(flat)
    dir2 = direction.reshape(flat)
    load2 = load.reshape(flat)
    node2 = tie_node.reshape(tie_total // 128, 128)
    slot2 = tie_slot.reshape(tie_total // 128, 128)
    owner2 = tie_owner.reshape(1, tie_total)

    def shape(*dims, dtype=F32):
        return jax.ShapeDtypeStruct(dims, dtype)

    if separate:
        pay_shapes = [shape(2 * COMPS, slots)] * peers
    else:
        pay_shapes = [shape(peers, 2 * COMPS, slots)]
    outs = pl.pallas_call(
        lambda *refs: prepare(0, separate, (peers, ty_count), *refs),
        out_shape=[
            shape(row_total * COMPS, cols),
            shape(COMPS, tie_total),
            shape(8 * hid, 4 * COMPS, dtype=BF16),
            shape(128, hid, dtype=BF16),
            shape(hid, 128),
            shape(2 * COMPS, cols),
            shape(2 * COMPS, cols),
        ]
        + pay_shapes,
        name="prepare",
    )(
        disp2,
        dir2,
        fitting_disp,
        fitting_dir,
        node2,
        owner2,
        slot2,
        w_in.T,
        b_in.reshape(1, hid),
        b_mid.reshape(1, hid),
        w_out,
    )
    fields, ties, w_first, w_last, b_cols, rows_out, cols_out = outs[:7]
    pay = outs[7:]

    place = lax.axis_index("tx") * pb_count + lax.axis_index("pb")
    across = lax.axis_index("ty")
    row_count = tx_count * pb_count
    low_row, high_row = rows_out[:COMPS], rows_out[COMPS:]
    low_col, high_col = cols_out[:COMPS], cols_out[COMPS:]
    row_even = place % 2 == 0
    col_even = across % 2 == 0
    send_a = jnp.where(row_even, high_row, low_row)
    send_b = jnp.where(row_even, low_row, high_row)
    row_pairs = {"a": swaps(row_count, 0), "b": swaps(row_count, 1)}
    col_pairs = {"a": swaps(ty_count, 0)}
    if ty_count > 2:
        col_pairs["b"] = swaps(ty_count, 1)
    named = {
        "row_a": lax.ppermute(send_a, ("tx", "pb"), row_pairs["a"]),
        "row_b": lax.ppermute(send_b, ("tx", "pb"), row_pairs["b"]),
    }
    for phase, pairs in col_pairs.items():
        send = jnp.where(col_even == (phase == "a"), high_col, low_col)
        named["col_" + phase] = lax.ppermute(send, "ty", pairs)
        for row_phase, row_send in (("a", send_a), ("b", send_b)):
            both = []
            for row_from, row_to in row_pairs[row_phase]:
                for col_from, col_to in pairs:
                    both.append(
                        (
                            ((row_from // pb_count) * ty_count + col_from) * pb_count + row_from % pb_count,
                            ((row_to // pb_count) * ty_count + col_to) * pb_count + row_to % pb_count,
                        )
                    )
            named["diag_" + row_phase + phase] = lax.ppermute(row_send, ("tx", "ty", "pb"), both)

    if separate:
        named["pay0"] = pay[0]
        for peer in range(1, peers):
            pairs = [(source, source ^ peer) for source in range(peers)]
            named["pay" + str(peer)] = lax.ppermute(pay[peer], ("tx", "ty"), pairs)
    else:
        named["pay0"] = lax.all_to_all(pay[0], ("tx", "ty"), split_axis=0, concat_axis=0, tiled=True)

    forces = pl.pallas_call(
        interior,
        out_shape=shape(row_total * COMPS, cols),
        scratch_shapes=[pltpu.VMEM(((row_total - 1) // 2, 4 * COMPS, 2 * cols), BF16)],
        name="interior",
    )(fields, w_first, w_mid, b_cols, w_last)

    named.update(
        fields=fields,
        ties=ties,
        forces=forces,
        load=load2,
        cols=cols_out,
        w_first=w_first,
        w_mid=w_mid,
        b_mid=b_cols,
        w_last=w_last,
        node=node2,
        slot=slot2,
        owner=owner2,
        fit_disp=fitting_disp,
        fit_dir=fitting_dir,
    )
    names = list(named)
    axes = (peers, ty_count, tx_count, pb_count, tuple(col_pairs))
    res, tan, fit_res, fit_tan = pl.pallas_call(
        lambda *refs: finish(names + ["res", "tan", "fit_res", "fit_tan", "scratch"], axes, separate, *refs),
        out_shape=[shape(*flat), shape(*flat), shape(6, slots), shape(6, slots)],
        scratch_shapes=[pltpu.VMEM((row_total * COMPS, cols), F32)],
        name="finish",
    )(*named.values())
    cube = displacement.shape
    return (res.reshape(cube), tan.reshape(cube), fit_res, fit_tan)


def solution(mesh):
    in_specs = (
        P(None, ("tx", "pb"), "ty"),
        P(None, ("tx", "pb"), "ty"),
        P(None, ("tx", "pb"), "ty"),
        P(),
        P(),
        P(),
        P(),
        P(),
        P(None, ("groups", "tx", "ty", "pb")),
        P(None, ("groups", "tx", "ty", "pb")),
        P(("groups", "tx", "ty", "pb")),
        P(("groups", "tx", "ty", "pb"), None),
        P(("groups", "tx", "ty", "pb")),
    )
    out_specs = (
        P(None, ("groups", "tx", "pb"), "ty"),
        P(None, ("groups", "tx", "pb"), "ty"),
        P(None, ("groups", "tx", "ty", "pb")),
        P(None, ("groups", "tx", "ty", "pb")),
    )
    return jax.shard_map(
        per_device, mesh=mesh, in_specs=in_specs, out_specs=out_specs, check_vma=False
    )
```

```python
import math

import jax
import jax.numpy as jnp
from jax import lax
from jax.experimental import pallas as pl
from jax.experimental.pallas import tpu as pltpu
from jax.sharding import PartitionSpec as P

F32 = jnp.float32
BF16 = jnp.bfloat16
GAUSS = (0.5 - 0.5 / math.sqrt(3.0), 0.5 + 0.5 / math.sqrt(3.0))
COMPS = 16
COUNT_ROW = 6
SPARE_ROWS = (6, 7, 14)
GROUP = 3


def dot(a, b, dims=((1,), (0,))):
    return lax.dot_general(a, b, (dims, ((), ())), preferred_element_type=F32)


def split(value, terms):
    parts = []
    for _ in range(terms):
        part = value.astype(BF16)
        parts.append(part)
        value = value - part.astype(F32)
    return parts


def rows_of(value):
    return lax.broadcasted_iota(jnp.int32, value, 0)


def lanes_of(value):
    return lax.broadcasted_iota(jnp.int32, value, 1)


def one_hot(index, size):
    shape = (size, index.shape[1])
    return (rows_of(shape) == index).astype(F32).astype(BF16)


def as_line(ref):
    return jnp.concatenate([ref[row : row + 1, :] for row in range(ref.shape[0])], axis=1)


def paired(top, bottom):
    spare = jnp.zeros((2, top.shape[1]), F32)
    return jnp.concatenate([top, spare, bottom, spare], axis=0)


def strain_tile(f00, f10, f01, f11):
    along_low = f10 - f00
    along_high = f11 - f01
    across_low = f01 - f00
    across_high = f11 - f10
    shape = f00.shape
    row = rows_of(shape)
    ones = ((row == 6) | (row == 7) | (row == 14)).astype(F32)
    groups = []
    for frac in GAUSS:
        groups.append((((1.0 - frac) * along_low + frac * along_high) + ones).astype(BF16))
    for frac in GAUSS:
        groups.append(((1.0 - frac) * across_low + frac * across_high).astype(BF16))
    return jnp.concatenate(groups, axis=0)


def stress_sums(strains, w_first, w_mid, b_mid, w_last):
    hid = w_mid.shape[0]
    tasks = [(tile, point) for tile in range(len(strains)) for point in range(4)]
    totals = [[None, None] for _ in strains]

    def layer_one(task):
        tile, point = task
        start = point * 2 * hid
        return (
            dot(w_first[start : start + hid, :], strains[tile]),
            dot(w_first[start + hid : start + 2 * hid, :], strains[tile]),
        )

    def activate(value, slope):
        act = jnp.tanh(value)
        return (act.astype(BF16), ((1.0 - act * act) * slope).astype(BF16))

    def layer_two(hidden):
        bias = b_mid[...]
        value = dot(w_mid[...], hidden[0])
        slope = dot(w_mid[...], hidden[1])
        bias = jnp.concatenate([bias] * (value.shape[1] // bias.shape[1]), axis=1)
        return (value + bias, slope)

    def layer_three(task, hidden):
        tile, point = task
        last = w_last[point * 32 : (point + 1) * 32, :]
        for side in range(2):
            part = dot(last, hidden[side])
            old = totals[tile][side]
            totals[tile][side] = part if old is None else old + part

    ones = {0: layer_one(tasks[0])}
    twos = {}
    for at in range(len(tasks) + 1):
        if at + 1 < len(tasks):
            ones[at + 1] = layer_one(tasks[at + 1])
        if at < len(tasks):
            hidden = activate(*ones.pop(at))
            twos[at] = layer_two(hidden)
        if at >= 1:
            layer_three(tasks[at - 1], activate(*twos.pop(at - 1)))
    return totals


def corner_forces(primal, tangent):
    def both(group):
        return jnp.concatenate([primal[group * 8 : group * 8 + 8], tangent[group * 8 : group * 8 + 8]], axis=0)

    along = (both(0), both(1))
    across = (both(2), both(3))

    def mix(pair, weights):
        return (0.25 * weights[0]) * pair[0] + (0.25 * weights[1]) * pair[1]

    rest = (1.0 - GAUSS[0], 1.0 - GAUSS[1])
    along_rest = mix(along, rest)
    along_frac = mix(along, GAUSS)
    across_rest = mix(across, rest)
    across_frac = mix(across, GAUSS)
    return (
        -along_rest - across_rest,
        along_rest - across_frac,
        across_rest - along_frac,
        along_frac + across_frac,
    )


def block_of(row_place, across, ty_count, pb_count):
    return (row_place // pb_count * ty_count + across) * pb_count + row_place % pb_count


def prepare(axes, *refs):
    (disp, dirn, fit_disp, fit_dir, node_ref, owner_ref, slot_ref, w_in, b_in, b_mid, w_out) = refs[:11]
    (fields, ties, w_first, w_last, b_cols, col_out, pay) = refs[11:]
    tx_count, ty_count, pb_count = axes
    row_total = fields.shape[0] // COMPS
    cols = fields.shape[1]
    slots = fit_disp.shape[1]
    tie_total = ties.shape[1]
    hid = w_in.shape[1]
    core = lax.axis_index("pb")
    across = lax.axis_index("ty")
    place = lax.axis_index("tx") * pb_count + core

    fields[...] = jnp.zeros(fields.shape, F32)
    for comp in range(6):
        fields[pl.ds(comp, row_total, stride=COMPS), :] = disp[comp * row_total : (comp + 1) * row_total, :]
        fields[pl.ds(8 + comp, row_total, stride=COMPS), :] = dirn[comp * row_total : (comp + 1) * row_total, :]

    lane = lanes_of((COMPS, cols))
    for side, column in enumerate((0, cols - 1)):
        gathered = jnp.zeros((COMPS, cols), F32)
        for row in range(row_total):
            value = fields[row * COMPS : (row + 1) * COMPS, column : column + 1]
            gathered = jnp.where(lane == row, value, gathered)
        col_out[side * COMPS : (side + 1) * COMPS, :] = gathered

    bias_rows = split(b_in[...], 3)
    row = rows_of((8, hid))
    stacked = jnp.zeros((8, hid), F32)
    mid_stacked = jnp.zeros((8, hid), F32)
    for at, (one, two) in enumerate(zip(bias_rows, split(b_mid[...], 3))):
        stacked = jnp.where(row == at, one.astype(F32), stacked)
        mid_stacked = jnp.where(row == at, two.astype(F32), mid_stacked)
    lhs = jnp.concatenate([w_in[...].astype(F32), jnp.zeros((4, hid), F32), stacked], axis=0).astype(BF16)
    sel_shape = (24, 4 * COMPS)
    source = rows_of(sel_shape)
    target = lanes_of(sel_shape)
    for point in range(4):
        a_base = (point // 2) * COMPS
        c_base = (2 + point % 2) * COMPS
        for side in range(2):
            hit = (source < 6) & (target == a_base + 8 * side + source)
            hit = hit | ((source >= 6) & (source < 12) & (target == c_base + 8 * side + source - 6))
            if side == 0:
                for at, spot in enumerate((6, 7, 14)):
                    hit = hit | ((source == 16 + at) & (target == a_base + spot))
            block = dot(lhs, hit.astype(F32).astype(BF16), ((0,), (0,)))
            start = (2 * point + side) * hid
            w_first[start : start + hid, :] = block.astype(BF16)
    ones = (rows_of((8, 128)) < 3).astype(F32).astype(BF16)
    b_cols[...] = dot(mid_stacked.astype(BF16), ones, ((0,), (0,)))
    last_shape = (128, 12)
    target = rows_of(last_shape)
    source = lanes_of(last_shape)
    hit = target < 0
    for point in range(4):
        a_base = point * 32 + (point // 2) * 8
        c_base = point * 32 + 16 + (point % 2) * 8
        hit = hit | ((source < 6) & (target == a_base + source))
        hit = hit | ((source >= 6) & (target == c_base + source - 6))
    w_last[...] = dot(hit.astype(F32).astype(BF16), w_out[...]).astype(BF16)

    node = as_line(node_ref)
    slot = as_line(slot_ref)
    owner = owner_ref[...]
    node_row = lax.shift_right_logical(node, cols.bit_length() - 1)
    node_col = jnp.bitwise_and(node, cols - 1)
    hot_col = one_hot(node_col, cols)
    wide = dot(
        jnp.concatenate(split(fields[...], 3), axis=1), jnp.concatenate([hot_col] * 3, axis=0)
    )
    value = jnp.zeros((COMPS, tie_total), F32)
    for row in range(row_total):
        value = jnp.where(node_row == row, wide[row * COMPS : (row + 1) * COMPS], value)
    value = jnp.where(rows_of(value.shape) == COUNT_ROW, 1.0, value)
    ties[...] = value
    stack = jnp.concatenate(split(value, 3), axis=0)
    hot_slot = one_hot(slot, slots)
    fitting = paired(fit_disp[...], fit_dir[...])

    def bins(first, count):
        lhs = [
            stack * (owner == first + at).astype(F32).astype(BF16) for at in range(count)
        ]
        return dot(jnp.concatenate(lhs, axis=0), hot_slot, ((1,), (1,)))

    def folded(wide_bins, at):
        part = wide_bins[at * 48 : at * 48 + 48]
        return part[0:16] + part[16:32] + part[32:48]

    peers = tx_count * ty_count
    block = math.gcd(peers, 8)

    def fill(first):
        wide_bins = bins(first, block)
        for peer in range(block):
            at = (first + peer) * pb_count + core
            pay[at, 0:COMPS, :] = fitting
            pay[at, COMPS : 2 * COMPS, :] = folded(wide_bins, peer)

    if block == peers:
        fill(0)
    else:
        lax.fori_loop(0, peers // block, lambda at, carry: (fill(at * block), carry)[1], 0)

    for step, edge in ((-1, fields[0:COMPS, :]), (1, fields[(row_total - 1) * COMPS :, :])):
        for side in (-1, 0, 1):
            there, over = place + step, across + side
            valid = (there >= 0) & (there < tx_count * pb_count) & (over >= 0) & (over < ty_count)

            @pl.when(valid)
            def _():
                pay[block_of(there, over, ty_count, pb_count), 0:COMPS, :] = edge

    for side, edge in ((-1, 0), (1, 1)):
        over = across + side
        packed = pack_column(col_out[edge * COMPS : (edge + 1) * COMPS, :], row_total)

        @pl.when((over >= 0) & (over < ty_count))
        def _():
            at = block_of(place, over, ty_count, pb_count)
            for line, row in zip(packed, SPARE_ROWS):
                pay[at, row : row + 1, :] = line


def pack_column(column, width):
    each = column.shape[1] // width
    lines = []
    for first in range(0, 12, each):
        line = None
        for at in range(first, min(first + each, 12)):
            row = at % 6 + at // 6 * 8
            part = column[row : row + 1]
            if at > first:
                part = pltpu.roll(part, (at - first) * width, 1)
            line = part if line is None else line + part
        lines.append(line)
    assert len(lines) <= len(SPARE_ROWS)
    return lines


def unpack_column(block, width):
    shape = (COMPS, block.shape[1])
    each = shape[1] // width
    row = rows_of(shape)
    column = jnp.zeros(shape, F32)
    for at in range(12):
        spare = SPARE_ROWS[at // each]
        line = block[spare : spare + 1]
        if at % each:
            line = pltpu.roll(line, shape[1] - at % each * width, 1)
        column = jnp.where(row == at % 6 + at // 6 * 8, line, column)
    return jnp.where(lanes_of(shape) < width, column, 0.0)


def interior(fields, w_first, w_mid, b_mid, w_last, forces, strain):
    row_total, cols = fields.shape[0] // COMPS, fields.shape[1]
    pairs = (row_total - 1) // 2
    group = next(size for size in (GROUP, 3, 2, 1) if pairs % size == 0)
    keep = lanes_of((COMPS, cols)) < cols - 1

    def row_strain(row):
        base = fields[pl.ds(row * COMPS, COMPS), :]
        right = fields[pl.ds(row * COMPS + COMPS, COMPS), :]
        return strain_tile(base, right, pltpu.roll(base, cols - 1, 1), pltpu.roll(right, cols - 1, 1))

    def build(pair, carry):
        strain[pair] = jnp.concatenate([row_strain(2 * pair), row_strain(2 * pair + 1)], axis=1)
        return carry

    lax.fori_loop(0, pairs, build, 0)
    forces[...] = jnp.zeros(forces.shape, F32)

    def step(pair, carry):
        start = pair * group
        sums = stress_sums([strain[start + at] for at in range(group)], w_first, w_mid, b_mid, w_last)
        for tile, (primal, tangent) in enumerate(sums):
            for half in range(2):
                lanes = slice(half * cols, (half + 1) * cols)
                parts = corner_forces(primal[:, lanes], tangent[:, lanes])
                base, right, upper, corner = (jnp.where(keep, part, 0.0) for part in parts)
                at = (2 * (start + tile) + half) * COMPS
                forces[pl.ds(at, COMPS), :] += base + pltpu.roll(upper, 1, 1)
                forces[pl.ds(at + COMPS, COMPS), :] += right + pltpu.roll(corner, 1, 1)
        return carry

    lax.fori_loop(0, pairs // group, step, 0)


def finish(names, axes, *refs):
    ref = dict(zip(names, refs))
    tx_count, ty_count, pb_count = axes
    fields, ties, forces_in, load = ref["fields"], ref["ties"], ref["forces"], ref["load"]
    scratch, got = ref["scratch"], ref["got"]
    row_total, cols = fields.shape[0] // COMPS, fields.shape[1]
    slots = got.shape[2]
    tie_total = ties.shape[1]
    lane = lanes_of((COMPS, cols))
    core = lax.axis_index("pb")
    across = lax.axis_index("ty")
    place = lax.axis_index("tx") * pb_count + core

    def around(step, side):
        there, over = place + step, across + side
        valid = (there >= 0) & (there < tx_count * pb_count) & (over >= 0) & (over < ty_count)
        at = jnp.where(valid, block_of(there, over, ty_count, pb_count), 0)
        value = got[at, 0:COMPS, :]
        if step == 0:
            value = unpack_column(value, row_total)
        return jnp.where(valid, value, 0.0)

    prev_row = around(-1, 0)
    next_row = around(1, 0)
    next_col = around(0, 1)
    prev_col = around(0, -1)
    next_corner = (around(-1, 1)[:, 0:1], around(1, 1)[:, 0:1])
    prev_corner = (around(-1, -1)[:, cols - 1 : cols], around(1, -1)[:, cols - 1 : cols])

    def column(inner, before, after):
        line = pltpu.roll(inner, 1, 1)
        line = jnp.where(lane == 0, before, line)
        return jnp.where(lane == row_total + 1, after, line)

    own_cols = ref["cols"]
    line_prev = column(prev_col, prev_corner[0], prev_corner[1])
    line_next = column(next_col, next_corner[0], next_corner[1])
    line_first = column(own_cols[0:COMPS, :], prev_row[:, 0:1], next_row[:, 0:1])
    line_final = column(
        own_cols[COMPS : 2 * COMPS, :], prev_row[:, cols - 1 : cols], next_row[:, cols - 1 : cols]
    )

    def shifted(row_value, beyond):
        return jnp.where(lane == cols - 1, beyond, pltpu.roll(row_value, cols - 1, 1))

    first_row = fields[0:COMPS, :]
    last_row = fields[(row_total - 1) * COMPS :, :]
    inner_row = fields[(row_total - 2) * COMPS : (row_total - 1) * COMPS, :]

    tile_inner = strain_tile(
        inner_row, last_row, pltpu.roll(inner_row, cols - 1, 1), pltpu.roll(last_row, cols - 1, 1)
    )
    tile_before = strain_tile(
        prev_row,
        first_row,
        shifted(prev_row, next_corner[0]),
        shifted(first_row, next_col[:, 0:1]),
    )
    tile_after = strain_tile(
        last_row,
        next_row,
        shifted(last_row, next_col[:, row_total - 1 : row_total]),
        shifted(next_row, next_corner[1]),
    )
    half = cols // 2
    low = lane < half
    back = cols - 1

    def two(left, right_line):
        return jnp.where(low, left, pltpu.roll(right_line, half + back, 1))

    left_base = two(line_prev, line_final)
    left_upper = two(line_first, line_next)
    right_base = two(pltpu.roll(line_prev, back, 1), pltpu.roll(line_final, back, 1))
    right_upper = two(pltpu.roll(line_first, back, 1), pltpu.roll(line_next, back, 1))
    tile_side = strain_tile(left_base, right_base, left_upper, right_upper)

    parts = []
    edge_tiles = [jnp.concatenate(pair, axis=1) for pair in ((tile_inner, tile_before), (tile_after, tile_side))]
    edge_sums = stress_sums(edge_tiles, ref["w_first"], ref["w_mid"], ref["b_mid"], ref["w_last"])
    for primal, tangent in edge_sums:
        for at in range(2):
            lanes = slice(at * cols, (at + 1) * cols)
            parts.append(corner_forces(primal[:, lanes], tangent[:, lanes]))
    part_inner, part_before, part_after, part_side = parts

    def mask(value, keep):
        return jnp.where(keep, value, 0.0)

    def moved(value, keep):
        return pltpu.roll(mask(value, keep), 1, 1)

    inside = lane < cols - 1
    i_base, i_right, i_upper, i_corner = part_inner
    _, b_right, _, b_corner = part_before
    a_base, _, a_upper, _ = part_after
    s_base, s_right, s_upper, s_corner = part_side
    has_row = place > 0
    has_col = across > 0
    row_first = mask(mask(b_right, lane < cols) + moved(b_corner, inside), has_row)
    row_inner = mask(i_base, inside) + moved(i_upper, inside)
    row_last = mask(i_right, inside) + moved(i_corner, inside) + a_base + moved(a_upper, inside)
    first_lane = jnp.where(has_row, 0, 1)
    s_corner = mask(s_corner, (lane >= first_lane) & (lane < row_total))
    s_upper = mask(s_upper, (lane >= 1) & (lane <= row_total))
    col_first = mask(pltpu.roll(s_upper, back, 1) + s_corner, has_col)
    s_base = mask(s_base, (lane >= half) & (lane < half + row_total - 1))
    s_right = mask(s_right, (lane >= half) & (lane < half + row_total - 1))
    col_last = pltpu.roll(s_base + pltpu.roll(s_right, 1, 1), cols - half, 1)

    node = as_line(ref["node"])
    slot = as_line(ref["slot"])
    owner = ref["owner"][...]
    hot_slot = one_hot(slot, slots)
    hot_three = jnp.concatenate([hot_slot] * 3, axis=0)
    fit_value = jnp.zeros((COMPS, tie_total), F32)
    bins = jnp.zeros((COMPS, slots), F32)
    peers = tx_count * ty_count
    block = math.gcd(peers, 8)

    def collect(first, carry):
        fit_value, bins = carry
        parts = [got[(first + peer) * pb_count + core] for peer in range(block)]
        fit_all = jnp.concatenate([part[0:COMPS] for part in parts], axis=0)
        wide = dot(jnp.concatenate(split(fit_all, 3), axis=1), hot_three)
        for peer, part in enumerate(parts):
            fit_value = jnp.where(owner == first + peer, wide[peer * COMPS : (peer + 1) * COMPS], fit_value)
            bins = bins + part[COMPS : 2 * COMPS]
        return fit_value, bins

    if block == peers:
        fit_value, bins = collect(0, (fit_value, bins))
    else:
        fit_value, bins = lax.fori_loop(
            0, peers // block, lambda at, carry: collect(at * block, carry), (fit_value, bins)
        )
    count = bins[COUNT_ROW : COUNT_ROW + 1]
    for out, fit, base in (("fit_res", "fit_disp", 0), ("fit_tan", "fit_dir", 8)):
        ref[out][...] = 2.0 * (count * ref[fit][...] - bins[base : base + 6])

    pulled = 2.0 * (ties[...] - fit_value)
    node_row = lax.shift_right_logical(node, cols.bit_length() - 1)
    node_col = jnp.bitwise_and(node, cols - 1)
    hot_col = one_hot(node_col, cols)
    sides = split(pulled, 2)
    lhs = []
    for row in range(row_total):
        hit = (node_row == row).astype(F32).astype(BF16)
        lhs.append(jnp.concatenate([side * hit for side in sides], axis=1))
    tie_forces = dot(
        jnp.concatenate(lhs, axis=0), jnp.concatenate([hot_col] * 2, axis=1), ((1,), (1,))
    )

    for row in range(row_total):
        total = forces_in[row * COMPS : (row + 1) * COMPS, :] + tie_forces[row * COMPS : (row + 1) * COMPS]
        total = total + jnp.where(lane == 0, col_first[:, row : row + 1], 0.0)
        total = total + jnp.where(lane == cols - 1, col_last[:, row : row + 1], 0.0)
        if row == 0:
            total = total + row_first
        if row == row_total - 2:
            total = total + row_inner
        if row == row_total - 1:
            total = total + row_last
        scratch[row * COMPS : (row + 1) * COMPS, :] = total
    for comp in range(6):
        rows = slice(comp * row_total, (comp + 1) * row_total)
        ref["res"][rows, :] = scratch[pl.ds(comp, row_total, stride=COMPS), :] - load[rows, :]
        ref["tan"][rows, :] = scratch[pl.ds(8 + comp, row_total, stride=COMPS), :]


def per_device(
    displacement,
    direction,
    load,
    w_in,
    b_in,
    w_mid,
    b_mid,
    w_out,
    fitting_disp,
    fitting_dir,
    tie_node,
    tie_owner,
    tie_slot,
):
    tx_count = lax.axis_size("tx")
    ty_count = lax.axis_size("ty")
    pb_count = lax.axis_size("pb")
    peers = tx_count * ty_count
    axes = (tx_count, ty_count, pb_count)
    _, row_total, cols = displacement.shape
    slots = fitting_disp.shape[1]
    tie_total = tie_node.shape[0]
    hid = w_mid.shape[0]
    flat = (6 * row_total, cols)
    disp2 = displacement.reshape(flat)
    dir2 = direction.reshape(flat)
    load2 = load.reshape(flat)
    node2 = tie_node.reshape(tie_total // 128, 128)
    slot2 = tie_slot.reshape(tie_total // 128, 128)
    owner2 = tie_owner.reshape(1, tie_total)

    def shape(*dims, dtype=F32):
        return jax.ShapeDtypeStruct(dims, dtype)

    outs = pl.pallas_call(
        lambda *refs: prepare(axes, *refs),
        out_shape=[
            shape(row_total * COMPS, cols),
            shape(COMPS, tie_total),
            shape(8 * hid, 4 * COMPS, dtype=BF16),
            shape(128, hid, dtype=BF16),
            shape(hid, 128),
            shape(2 * COMPS, cols),
            shape(peers * pb_count, 2 * COMPS, slots),
        ],
        name="prepare",
    )(
        disp2,
        dir2,
        fitting_disp,
        fitting_dir,
        node2,
        owner2,
        slot2,
        w_in.T,
        b_in.reshape(1, hid),
        b_mid.reshape(1, hid),
        w_out,
    )
    fields, ties, w_first, w_last, b_cols, cols_out, pay = outs
    got = lax.all_to_all(pay, ("tx", "ty", "pb"), split_axis=0, concat_axis=0, tiled=True)

    forces = pl.pallas_call(
        interior,
        out_shape=shape(row_total * COMPS, cols),
        scratch_shapes=[pltpu.VMEM(((row_total - 1) // 2, 4 * COMPS, 2 * cols), BF16)],
        name="interior",
    )(fields, w_first, w_mid, b_cols, w_last)

    named = dict(
        got=got,
        fields=fields,
        ties=ties,
        forces=forces,
        load=load2,
        cols=cols_out,
        w_first=w_first,
        w_mid=w_mid,
        b_mid=b_cols,
        w_last=w_last,
        node=node2,
        slot=slot2,
        owner=owner2,
        fit_disp=fitting_disp,
        fit_dir=fitting_dir,
    )
    names = list(named)
    res, tan, fit_res, fit_tan = pl.pallas_call(
        lambda *refs: finish(names + ["res", "tan", "fit_res", "fit_tan", "scratch"], axes, *refs),
        out_shape=[shape(*flat), shape(*flat), shape(6, slots), shape(6, slots)],
        scratch_shapes=[pltpu.VMEM((row_total * COMPS, cols), F32)],
        name="finish",
    )(*named.values())
    cube = displacement.shape
    return (res.reshape(cube), tan.reshape(cube), fit_res, fit_tan)


def solution(mesh):
    in_specs = (
        P(None, ("tx", "pb"), "ty"),
        P(None, ("tx", "pb"), "ty"),
        P(None, ("tx", "pb"), "ty"),
        P(),
        P(),
        P(),
        P(),
        P(),
        P(None, ("groups", "tx", "ty", "pb")),
        P(None, ("groups", "tx", "ty", "pb")),
        P(("groups", "tx", "ty", "pb")),
        P(("groups", "tx", "ty", "pb"), None),
        P(("groups", "tx", "ty", "pb")),
    )
    out_specs = (
        P(None, ("groups", "tx", "pb"), "ty"),
        P(None, ("groups", "tx", "pb"), "ty"),
        P(None, ("groups", "tx", "ty", "pb")),
        P(None, ("groups", "tx", "ty", "pb")),
    )
    return jax.shard_map(
        per_device, mesh=mesh, in_specs=in_specs, out_specs=out_specs, check_vma=False
    )
```

```python
import math

import jax
import jax.numpy as jnp
from jax import lax
from jax.experimental import pallas as pl
from jax.experimental.pallas import tpu as pltpu
from jax.sharding import PartitionSpec as P

F32 = jnp.float32
BF16 = jnp.bfloat16
GAUSS = (0.5 - 0.5 / math.sqrt(3.0), 0.5 + 0.5 / math.sqrt(3.0))
COMPS = 16
COUNT_ROW = 6
SPARE_ROWS = (6, 7, 14)
GROUP = 5


def local(count):
    return [pl.BlockSpec(memory_space=pltpu.VMEM)] * count


def dot(a, b, dims=((1,), (0,))):
    return lax.dot_general(a, b, (dims, ((), ())), preferred_element_type=F32)


def split(value, terms):
    parts = []
    for _ in range(terms):
        part = value.astype(BF16)
        parts.append(part)
        value = value - part.astype(F32)
    return parts


def rows_of(value):
    return lax.broadcasted_iota(jnp.int32, value, 0)


def lanes_of(value):
    return lax.broadcasted_iota(jnp.int32, value, 1)


def one_hot(index, size):
    shape = (size, index.shape[1])
    return (rows_of(shape) == index).astype(F32).astype(BF16)


def as_line(ref):
    return jnp.concatenate([ref[row : row + 1, :] for row in range(ref.shape[0])], axis=1)


def paired(top, bottom):
    spare = jnp.zeros((2, top.shape[1]), F32)
    return jnp.concatenate([top, spare, bottom, spare], axis=0)


def strain_tile(f00, f10, f01, f11):
    along_low = f10 - f00
    along_high = f11 - f01
    across_low = f01 - f00
    across_high = f11 - f10
    shape = f00.shape
    row = rows_of(shape)
    ones = ((row == 6) | (row == 7) | (row == 14)).astype(F32)
    groups = []
    for frac in GAUSS:
        groups.append((((1.0 - frac) * along_low + frac * along_high) + ones).astype(BF16))
    for frac in GAUSS:
        groups.append(((1.0 - frac) * across_low + frac * across_high).astype(BF16))
    return jnp.concatenate(groups, axis=0)


def stress_sums(strains, w_first, w_mid, b_mid, w_last):
    hid = w_mid.shape[0]
    tasks = [(tile, point) for tile in range(len(strains)) for point in range(4)]
    totals = [[None, None] for _ in strains]

    def layer_one(task):
        tile, point = task
        start = point * 2 * hid
        return (
            dot(w_first[start : start + hid, :], strains[tile]),
            dot(w_first[start + hid : start + 2 * hid, :], strains[tile]),
        )

    def activate(value, slope):
        act = jnp.tanh(value)
        return (act.astype(BF16), ((1.0 - act * act) * slope).astype(BF16))

    def layer_two(hidden):
        bias = b_mid[...]
        value = dot(w_mid[...], hidden[0])
        slope = dot(w_mid[...], hidden[1])
        bias = jnp.concatenate([bias] * (value.shape[1] // bias.shape[1]), axis=1)
        return (value + bias, slope)

    def layer_three(task, hidden):
        tile, point = task
        last = w_last[point * 32 : (point + 1) * 32, :]
        for side in range(2):
            part = dot(last, hidden[side])
            old = totals[tile][side]
            totals[tile][side] = part if old is None else old + part

    ones = {0: layer_one(tasks[0])}
    twos = {}
    for at in range(len(tasks) + 1):
        if at + 1 < len(tasks):
            ones[at + 1] = layer_one(tasks[at + 1])
        if at < len(tasks):
            hidden = activate(*ones.pop(at))
            twos[at] = layer_two(hidden)
        if at >= 1:
            layer_three(tasks[at - 1], activate(*twos.pop(at - 1)))
    return totals


def corner_forces(primal, tangent):
    def both(group):
        return jnp.concatenate([primal[group * 8 : group * 8 + 8], tangent[group * 8 : group * 8 + 8]], axis=0)

    along = (both(0), both(1))
    across = (both(2), both(3))

    def mix(pair, weights):
        return (0.25 * weights[0]) * pair[0] + (0.25 * weights[1]) * pair[1]

    rest = (1.0 - GAUSS[0], 1.0 - GAUSS[1])
    along_rest = mix(along, rest)
    along_frac = mix(along, GAUSS)
    across_rest = mix(across, rest)
    across_frac = mix(across, GAUSS)
    return (
        -along_rest - across_rest,
        along_rest - across_frac,
        across_rest - along_frac,
        along_frac + across_frac,
    )


def block_of(row_place, across, ty_count, pb_count):
    return (row_place // pb_count * ty_count + across) * pb_count + row_place % pb_count


def prepare(axes, *refs):
    (disp, dirn, fit_disp, fit_dir, node_ref, owner_ref, slot_ref) = refs[:7]
    (fields, ties, col_out, pay) = refs[7:]
    tx_count, ty_count, pb_count = axes
    row_total = fields.shape[0] // COMPS
    cols = fields.shape[1]
    slots = fit_disp.shape[1]
    tie_total = ties.shape[1]
    core = lax.axis_index("pb")
    across = lax.axis_index("ty")
    place = lax.axis_index("tx") * pb_count + core

    fields[...] = jnp.zeros(fields.shape, F32)
    for comp in range(6):
        fields[pl.ds(comp, row_total, stride=COMPS), :] = disp[comp * row_total : (comp + 1) * row_total, :]
        fields[pl.ds(8 + comp, row_total, stride=COMPS), :] = dirn[comp * row_total : (comp + 1) * row_total, :]

    lane = lanes_of((COMPS, cols))
    for side, column in enumerate((0, cols - 1)):
        gathered = jnp.zeros((COMPS, cols), F32)
        for row in range(row_total):
            value = fields[row * COMPS : (row + 1) * COMPS, column : column + 1]
            gathered = jnp.where(lane == row, value, gathered)
        col_out[side * COMPS : (side + 1) * COMPS, :] = gathered

    node = as_line(node_ref)
    slot = as_line(slot_ref)
    owner = owner_ref[...]
    node_row = lax.shift_right_logical(node, cols.bit_length() - 1)
    node_col = jnp.bitwise_and(node, cols - 1)
    hot_col = one_hot(node_col, cols)
    wide = dot(
        jnp.concatenate(split(fields[...], 2), axis=1), jnp.concatenate([hot_col] * 2, axis=0)
    )
    value = jnp.zeros((COMPS, tie_total), F32)
    for row in range(row_total):
        value = jnp.where(node_row == row, wide[row * COMPS : (row + 1) * COMPS], value)
    value = jnp.where(rows_of(value.shape) == COUNT_ROW, 1.0, value)
    ties[...] = value
    stack = jnp.concatenate(split(value, 2), axis=0)
    hot_slot = one_hot(slot, slots)
    fitting = paired(fit_disp[...], fit_dir[...])

    def bins(first, count):
        lhs = [
            stack * (owner == first + at).astype(F32).astype(BF16) for at in range(count)
        ]
        return dot(jnp.concatenate(lhs, axis=0), hot_slot, ((1,), (1,)))

    def folded(wide_bins, at):
        part = wide_bins[at * 2 * COMPS : (at + 1) * 2 * COMPS]
        return part[0:COMPS] + part[COMPS : 2 * COMPS]

    peers = tx_count * ty_count
    block = math.gcd(peers, 8)

    def fill(first):
        wide_bins = bins(first, block)
        for peer in range(block):
            at = (first + peer) * pb_count + core
            pay[at, 0:COMPS, :] = fitting
            pay[at, COMPS : 2 * COMPS, :] = folded(wide_bins, peer)

    if block == peers:
        fill(0)
    else:
        lax.fori_loop(0, peers // block, lambda at, carry: (fill(at * block), carry)[1], 0)

    for step, edge in ((-1, fields[0:COMPS, :]), (1, fields[(row_total - 1) * COMPS :, :])):
        for side in (-1, 0, 1):
            there, over = place + step, across + side
            valid = (there >= 0) & (there < tx_count * pb_count) & (over >= 0) & (over < ty_count)

            @pl.when(valid)
            def _():
                pay[block_of(there, over, ty_count, pb_count), 0:COMPS, :] = edge

    for side, edge in ((-1, 0), (1, 1)):
        over = across + side
        packed = pack_column(col_out[edge * COMPS : (edge + 1) * COMPS, :], row_total)

        @pl.when((over >= 0) & (over < ty_count))
        def _():
            at = block_of(place, over, ty_count, pb_count)
            for line, row in zip(packed, SPARE_ROWS):
                pay[at, row : row + 1, :] = line


def pack_column(column, width):
    each = column.shape[1] // width
    lines = []
    for first in range(0, 12, each):
        line = None
        for at in range(first, min(first + each, 12)):
            row = at % 6 + at // 6 * 8
            part = column[row : row + 1]
            if at > first:
                part = pltpu.roll(part, (at - first) * width, 1)
            line = part if line is None else line + part
        lines.append(line)
    assert len(lines) <= len(SPARE_ROWS)
    return lines


def unpack_column(block, width):
    shape = (COMPS, block.shape[1])
    each = shape[1] // width
    row = rows_of(shape)
    column = jnp.zeros(shape, F32)
    for at in range(12):
        spare = SPARE_ROWS[at // each]
        line = block[spare : spare + 1]
        if at % each:
            line = pltpu.roll(line, shape[1] - at % each * width, 1)
        column = jnp.where(row == at % 6 + at // 6 * 8, line, column)
    return jnp.where(lanes_of(shape) < width, column, 0.0)


def build_weights(w_in, b_in, b_mid, w_out, w_first, w_last, b_cols):
    hid = w_in.shape[1]
    bias_rows = split(b_in[...], 3)
    row = rows_of((8, hid))
    stacked = jnp.zeros((8, hid), F32)
    mid_stacked = jnp.zeros((8, hid), F32)
    for at, (one, two) in enumerate(zip(bias_rows, split(b_mid[...], 3))):
        stacked = jnp.where(row == at, one.astype(F32), stacked)
        mid_stacked = jnp.where(row == at, two.astype(F32), mid_stacked)
    lhs = jnp.concatenate([w_in[...].astype(F32), jnp.zeros((4, hid), F32), stacked], axis=0).astype(BF16)
    sel_shape = (24, 4 * COMPS)
    source = rows_of(sel_shape)
    target = lanes_of(sel_shape)
    for point in range(4):
        a_base = (point // 2) * COMPS
        c_base = (2 + point % 2) * COMPS
        for side in range(2):
            hit = (source < 6) & (target == a_base + 8 * side + source)
            hit = hit | ((source >= 6) & (source < 12) & (target == c_base + 8 * side + source - 6))
            if side == 0:
                for at, spot in enumerate((6, 7, 14)):
                    hit = hit | ((source == 16 + at) & (target == a_base + spot))
            block = dot(lhs, hit.astype(F32).astype(BF16), ((0,), (0,)))
            start = (2 * point + side) * hid
            w_first[start : start + hid, :] = block.astype(BF16)
    ones = (rows_of((8, 128)) < 3).astype(F32).astype(BF16)
    b_cols[...] = dot(mid_stacked.astype(BF16), ones, ((0,), (0,)))
    last_shape = (128, 12)
    target = rows_of(last_shape)
    source = lanes_of(last_shape)
    hit = target < 0
    for point in range(4):
        a_base = point * 32 + (point // 2) * 8
        c_base = point * 32 + 16 + (point % 2) * 8
        hit = hit | ((source < 6) & (target == a_base + source))
        hit = hit | ((source >= 6) & (target == c_base + source - 6))
    w_last[...] = dot(hit.astype(F32).astype(BF16), w_out[...]).astype(BF16)


def interior(fields, w_in, b_in, w_mid, b_mid, w_out, forces, w_first, w_last, b_cols):
    row_total, cols = fields.shape[0] // COMPS, fields.shape[1]
    pairs = (row_total - 1) // 2
    group = next(size for size in (GROUP, 3, 2, 1) if pairs % size == 0)
    keep = lanes_of((COMPS, cols)) < cols - 1
    build_weights(w_in, b_in, b_mid, w_out, w_first, w_last, b_cols)
    forces[...] = jnp.zeros(forces.shape, F32)

    def row_of(row):
        base = fields[pl.ds(pl.multiple_of(row * COMPS, COMPS), COMPS), :]
        return base, pltpu.roll(base, cols - 1, 1)

    def step(pair, carry):
        start = pair * group
        lines = [row_of(2 * start + at) for at in range(2 * group + 1)]
        tiles = [
            strain_tile(lines[at][0], lines[at + 1][0], lines[at][1], lines[at + 1][1])
            for at in range(2 * group)
        ]
        tiles = [jnp.concatenate(tiles[at : at + 2], axis=1) for at in range(0, 2 * group, 2)]
        sums = stress_sums(tiles, w_first, w_mid, b_cols, w_last)
        for tile, (primal, tangent) in enumerate(sums):
            for half in range(2):
                lanes = slice(half * cols, (half + 1) * cols)
                parts = corner_forces(primal[:, lanes], tangent[:, lanes])
                base, right, upper, corner = (jnp.where(keep, part, 0.0) for part in parts)
                at = pl.multiple_of((2 * (start + tile) + half) * COMPS, COMPS)
                forces[pl.ds(at, COMPS), :] += base + pltpu.roll(upper, 1, 1)
                forces[pl.ds(at + COMPS, COMPS), :] += right + pltpu.roll(corner, 1, 1)
        return carry

    lax.fori_loop(0, pairs // group, step, 0)


def finish(names, axes, *refs):
    ref = dict(zip(names, refs))
    tx_count, ty_count, pb_count = axes
    fields, ties, forces_in, load = ref["fields"], ref["ties"], ref["forces"], ref["load"]
    scratch, got = ref["scratch"], ref["got"]
    row_total, cols = fields.shape[0] // COMPS, fields.shape[1]
    slots = got.shape[2]
    tie_total = ties.shape[1]
    lane = lanes_of((COMPS, cols))
    core = lax.axis_index("pb")
    across = lax.axis_index("ty")
    place = lax.axis_index("tx") * pb_count + core

    def around(step, side):
        there, over = place + step, across + side
        valid = (there >= 0) & (there < tx_count * pb_count) & (over >= 0) & (over < ty_count)
        at = jnp.where(valid, block_of(there, over, ty_count, pb_count), 0)
        value = got[at, 0:COMPS, :]
        if step == 0:
            value = unpack_column(value, row_total)
        return jnp.where(valid, value, 0.0)

    prev_row = around(-1, 0)
    next_row = around(1, 0)
    next_col = around(0, 1)
    prev_col = around(0, -1)
    next_corner = (around(-1, 1)[:, 0:1], around(1, 1)[:, 0:1])
    prev_corner = (around(-1, -1)[:, cols - 1 : cols], around(1, -1)[:, cols - 1 : cols])

    def column(inner, before, after):
        line = pltpu.roll(inner, 1, 1)
        line = jnp.where(lane == 0, before, line)
        return jnp.where(lane == row_total + 1, after, line)

    own_cols = ref["cols"]
    line_prev = column(prev_col, prev_corner[0], prev_corner[1])
    line_next = column(next_col, next_corner[0], next_corner[1])
    line_first = column(own_cols[0:COMPS, :], prev_row[:, 0:1], next_row[:, 0:1])
    line_final = column(
        own_cols[COMPS : 2 * COMPS, :], prev_row[:, cols - 1 : cols], next_row[:, cols - 1 : cols]
    )

    def shifted(row_value, beyond):
        return jnp.where(lane == cols - 1, beyond, pltpu.roll(row_value, cols - 1, 1))

    first_row = fields[0:COMPS, :]
    last_row = fields[(row_total - 1) * COMPS :, :]
    inner_row = fields[(row_total - 2) * COMPS : (row_total - 1) * COMPS, :]

    tile_inner = strain_tile(
        inner_row, last_row, pltpu.roll(inner_row, cols - 1, 1), pltpu.roll(last_row, cols - 1, 1)
    )
    tile_before = strain_tile(
        prev_row,
        first_row,
        shifted(prev_row, next_corner[0]),
        shifted(first_row, next_col[:, 0:1]),
    )
    tile_after = strain_tile(
        last_row,
        next_row,
        shifted(last_row, next_col[:, row_total - 1 : row_total]),
        shifted(next_row, next_corner[1]),
    )
    half = cols // 2
    low = lane < half
    back = cols - 1

    def two(left, right_line):
        return jnp.where(low, left, pltpu.roll(right_line, half + back, 1))

    left_base = two(line_prev, line_final)
    left_upper = two(line_first, line_next)
    right_base = two(pltpu.roll(line_prev, back, 1), pltpu.roll(line_final, back, 1))
    right_upper = two(pltpu.roll(line_first, back, 1), pltpu.roll(line_next, back, 1))
    tile_side = strain_tile(left_base, right_base, left_upper, right_upper)

    parts = []
    edge_tiles = [jnp.concatenate(pair, axis=1) for pair in ((tile_inner, tile_before), (tile_after, tile_side))]
    edge_sums = stress_sums(edge_tiles, ref["w_first"], ref["w_mid"], ref["b_mid"], ref["w_last"])
    for primal, tangent in edge_sums:
        for at in range(2):
            lanes = slice(at * cols, (at + 1) * cols)
            parts.append(corner_forces(primal[:, lanes], tangent[:, lanes]))
    part_inner, part_before, part_after, part_side = parts

    def mask(value, keep):
        return jnp.where(keep, value, 0.0)

    def moved(value, keep):
        return pltpu.roll(mask(value, keep), 1, 1)

    inside = lane < cols - 1
    i_base, i_right, i_upper, i_corner = part_inner
    _, b_right, _, b_corner = part_before
    a_base, _, a_upper, _ = part_after
    s_base, s_right, s_upper, s_corner = part_side
    has_row = place > 0
    has_col = across > 0
    row_first = mask(mask(b_right, lane < cols) + moved(b_corner, inside), has_row)
    row_inner = mask(i_base, inside) + moved(i_upper, inside)
    row_last = mask(i_right, inside) + moved(i_corner, inside) + a_base + moved(a_upper, inside)
    first_lane = jnp.where(has_row, 0, 1)
    s_corner = mask(s_corner, (lane >= first_lane) & (lane < row_total))
    s_upper = mask(s_upper, (lane >= 1) & (lane <= row_total))
    col_first = mask(pltpu.roll(s_upper, back, 1) + s_corner, has_col)
    s_base = mask(s_base, (lane >= half) & (lane < half + row_total - 1))
    s_right = mask(s_right, (lane >= half) & (lane < half + row_total - 1))
    col_last = pltpu.roll(s_base + pltpu.roll(s_right, 1, 1), cols - half, 1)

    node = as_line(ref["node"])
    slot = as_line(ref["slot"])
    owner = ref["owner"][...]
    hot_slot = one_hot(slot, slots)
    hot_two = jnp.concatenate([hot_slot] * 2, axis=0)
    fit_value = jnp.zeros((COMPS, tie_total), F32)
    bins = jnp.zeros((COMPS, slots), F32)
    peers = tx_count * ty_count
    block = math.gcd(peers, 8)

    def collect(first, carry):
        fit_value, bins = carry
        parts = [got[(first + peer) * pb_count + core] for peer in range(block)]
        fit_all = jnp.concatenate([part[0:COMPS] for part in parts], axis=0)
        wide = dot(jnp.concatenate(split(fit_all, 2), axis=1), hot_two)
        for peer, part in enumerate(parts):
            fit_value = jnp.where(owner == first + peer, wide[peer * COMPS : (peer + 1) * COMPS], fit_value)
            bins = bins + part[COMPS : 2 * COMPS]
        return fit_value, bins

    if block == peers:
        fit_value, bins = collect(0, (fit_value, bins))
    else:
        fit_value, bins = lax.fori_loop(
            0, peers // block, lambda at, carry: collect(at * block, carry), (fit_value, bins)
        )
    count = bins[COUNT_ROW : COUNT_ROW + 1]
    for out, fit, base in (("fit_res", "fit_disp", 0), ("fit_tan", "fit_dir", 8)):
        ref[out][...] = 2.0 * (count * ref[fit][...] - bins[base : base + 6])

    pulled = 2.0 * (ties[...] - fit_value)
    node_row = lax.shift_right_logical(node, cols.bit_length() - 1)
    node_col = jnp.bitwise_and(node, cols - 1)
    hot_col = one_hot(node_col, cols)
    sides = split(pulled, 2)
    lhs = []
    for row in range(row_total):
        hit = (node_row == row).astype(F32).astype(BF16)
        lhs.append(jnp.concatenate([side * hit for side in sides], axis=1))
    tie_forces = dot(
        jnp.concatenate(lhs, axis=0), jnp.concatenate([hot_col] * 2, axis=1), ((1,), (1,))
    )

    for row in range(row_total):
        total = forces_in[row * COMPS : (row + 1) * COMPS, :] + tie_forces[row * COMPS : (row + 1) * COMPS]
        total = total + jnp.where(lane == 0, col_first[:, row : row + 1], 0.0)
        total = total + jnp.where(lane == cols - 1, col_last[:, row : row + 1], 0.0)
        if row == 0:
            total = total + row_first
        if row == row_total - 2:
            total = total + row_inner
        if row == row_total - 1:
            total = total + row_last
        scratch[row * COMPS : (row + 1) * COMPS, :] = total
    for comp in range(6):
        rows = slice(comp * row_total, (comp + 1) * row_total)
        ref["res"][rows, :] = scratch[pl.ds(comp, row_total, stride=COMPS), :] - load[rows, :]
        ref["tan"][rows, :] = scratch[pl.ds(8 + comp, row_total, stride=COMPS), :]


def per_device(
    displacement,
    direction,
    load,
    w_in,
    b_in,
    w_mid,
    b_mid,
    w_out,
    fitting_disp,
    fitting_dir,
    tie_node,
    tie_owner,
    tie_slot,
):
    tx_count = lax.axis_size("tx")
    ty_count = lax.axis_size("ty")
    pb_count = lax.axis_size("pb")
    peers = tx_count * ty_count
    axes = (tx_count, ty_count, pb_count)
    _, row_total, cols = displacement.shape
    slots = fitting_disp.shape[1]
    tie_total = tie_node.shape[0]
    hid = w_mid.shape[0]
    flat = (6 * row_total, cols)
    disp2 = displacement.reshape(flat)
    dir2 = direction.reshape(flat)
    load2 = load.reshape(flat)
    node2 = tie_node.reshape(tie_total // 128, 128)
    slot2 = tie_slot.reshape(tie_total // 128, 128)
    owner2 = tie_owner.reshape(1, tie_total)

    def shape(*dims, dtype=F32):
        return jax.ShapeDtypeStruct(dims, dtype)

    inputs = (disp2, dir2, fitting_disp, fitting_dir, node2, owner2, slot2)
    fields, ties, cols_out, pay = pl.pallas_call(
        lambda *refs: prepare(axes, *refs),
        out_shape=[
            shape(row_total * COMPS, cols),
            shape(COMPS, tie_total),
            shape(2 * COMPS, cols),
            shape(peers * pb_count, 2 * COMPS, slots),
        ],
        in_specs=local(len(inputs)),
        out_specs=local(4),
        name="prepare",
    )(*inputs)
    got = lax.all_to_all(pay, ("tx", "ty", "pb"), split_axis=0, concat_axis=0, tiled=True)

    inputs = (fields, w_in.T, b_in.reshape(1, hid), w_mid, b_mid.reshape(1, hid), w_out)
    forces, w_first, w_last, b_cols = pl.pallas_call(
        interior,
        out_shape=[
            shape(row_total * COMPS, cols),
            shape(8 * hid, 4 * COMPS, dtype=BF16),
            shape(128, hid, dtype=BF16),
            shape(hid, 128),
        ],
        in_specs=local(len(inputs)),
        out_specs=local(4),
        name="interior",
    )(*inputs)

    named = dict(
        got=got,
        fields=fields,
        ties=ties,
        forces=forces,
        load=load2,
        cols=cols_out,
        w_first=w_first,
        w_mid=w_mid,
        b_mid=b_cols,
        w_last=w_last,
        node=node2,
        slot=slot2,
        owner=owner2,
        fit_disp=fitting_disp,
        fit_dir=fitting_dir,
    )
    names = list(named)
    res, tan, fit_res, fit_tan = pl.pallas_call(
        lambda *refs: finish(names + ["res", "tan", "fit_res", "fit_tan", "scratch"], axes, *refs),
        out_shape=[shape(*flat), shape(*flat), shape(6, slots), shape(6, slots)],
        in_specs=local(len(names)),
        out_specs=local(4),
        scratch_shapes=[pltpu.VMEM((row_total * COMPS, cols), F32)],
        name="finish",
    )(*named.values())
    cube = displacement.shape
    return (res.reshape(cube), tan.reshape(cube), fit_res, fit_tan)


def solution(mesh):
    in_specs = (
        P(None, ("tx", "pb"), "ty"),
        P(None, ("tx", "pb"), "ty"),
        P(None, ("tx", "pb"), "ty"),
        P(),
        P(),
        P(),
        P(),
        P(),
        P(None, ("groups", "tx", "ty", "pb")),
        P(None, ("groups", "tx", "ty", "pb")),
        P(("groups", "tx", "ty", "pb")),
        P(("groups", "tx", "ty", "pb"), None),
        P(("groups", "tx", "ty", "pb")),
    )
    out_specs = (
        P(None, ("groups", "tx", "pb"), "ty"),
        P(None, ("groups", "tx", "pb"), "ty"),
        P(None, ("groups", "tx", "ty", "pb")),
        P(None, ("groups", "tx", "ty", "pb")),
    )
    return jax.shard_map(
        per_device, mesh=mesh, in_specs=in_specs, out_specs=out_specs, check_vma=False
    )
```

```python
import math

import jax
import jax.numpy as jnp
from jax import lax
from jax.experimental import pallas as pl
from jax.experimental.pallas import tpu as pltpu
from jax.sharding import PartitionSpec as P

F32 = jnp.float32
BF16 = jnp.bfloat16
GAUSS = (0.5 - 0.5 / math.sqrt(3.0), 0.5 + 0.5 / math.sqrt(3.0))
COMPS = 16
COUNT_ROW = 6
SPARE_ROWS = (6, 7, 14)
GROUP = 5
SMALL = 1 << 18


def local(count):
    return [pl.BlockSpec(memory_space=pltpu.VMEM)] * count


def on_chip(value):
    return pltpu.with_memory_space_constraint(value, pltpu.VMEM)


def dot(a, b, dims=((1,), (0,))):
    return lax.dot_general(a, b, (dims, ((), ())), preferred_element_type=F32)


def split(value, terms):
    parts = []
    for _ in range(terms):
        part = value.astype(BF16)
        parts.append(part)
        value = value - part.astype(F32)
    return parts


def rows_of(value):
    return lax.broadcasted_iota(jnp.int32, value, 0)


def lanes_of(value):
    return lax.broadcasted_iota(jnp.int32, value, 1)


def one_hot(index, size):
    shape = (size, index.shape[1])
    return (rows_of(shape) == index).astype(F32).astype(BF16)


def as_line(ref):
    return jnp.concatenate([ref[row : row + 1, :] for row in range(ref.shape[0])], axis=1)


def paired(top, bottom):
    spare = jnp.zeros((2, top.shape[1]), F32)
    return jnp.concatenate([top, spare, bottom, spare], axis=0)


def strain_tile(f00, f10, f01, f11):
    along_low = f10 - f00
    along_high = f11 - f01
    across_low = f01 - f00
    across_high = f11 - f10
    shape = f00.shape
    row = rows_of(shape)
    ones = ((row == 6) | (row == 7) | (row == 14)).astype(F32)
    groups = []
    for frac in GAUSS:
        groups.append((((1.0 - frac) * along_low + frac * along_high) + ones).astype(BF16))
    for frac in GAUSS:
        groups.append(((1.0 - frac) * across_low + frac * across_high).astype(BF16))
    return jnp.concatenate(groups, axis=0)


def stress_sums(strains, w_first, w_mid, b_mid, w_last):
    hid = w_mid.shape[0]
    tasks = [(tile, point) for tile in range(len(strains)) for point in range(4)]
    totals = [[None, None] for _ in strains]

    def layer_one(task):
        tile, point = task
        start = point * 2 * hid
        return (
            dot(w_first[start : start + hid, :], strains[tile]),
            dot(w_first[start + hid : start + 2 * hid, :], strains[tile]),
        )

    def activate(value, slope):
        act = jnp.tanh(value)
        return (act.astype(BF16), ((1.0 - act * act) * slope).astype(BF16))

    def layer_two(hidden):
        bias = b_mid[...]
        value = dot(w_mid[...], hidden[0])
        slope = dot(w_mid[...], hidden[1])
        bias = jnp.concatenate([bias] * (value.shape[1] // bias.shape[1]), axis=1)
        return (value + bias, slope)

    def layer_three(task, hidden):
        tile, point = task
        last = w_last[point * 32 : (point + 1) * 32, :]
        for side in range(2):
            part = dot(last, hidden[side])
            old = totals[tile][side]
            totals[tile][side] = part if old is None else old + part

    ones = {0: layer_one(tasks[0])}
    twos = {}
    for at in range(len(tasks) + 1):
        if at + 1 < len(tasks):
            ones[at + 1] = layer_one(tasks[at + 1])
        if at < len(tasks):
            hidden = activate(*ones.pop(at))
            twos[at] = layer_two(hidden)
        if at >= 1:
            layer_three(tasks[at - 1], activate(*twos.pop(at - 1)))
    return totals


def corner_forces(primal, tangent):
    def both(group):
        return jnp.concatenate([primal[group * 8 : group * 8 + 8], tangent[group * 8 : group * 8 + 8]], axis=0)

    along = (both(0), both(1))
    across = (both(2), both(3))

    def mix(pair, weights):
        return (0.25 * weights[0]) * pair[0] + (0.25 * weights[1]) * pair[1]

    rest = (1.0 - GAUSS[0], 1.0 - GAUSS[1])
    along_rest = mix(along, rest)
    along_frac = mix(along, GAUSS)
    across_rest = mix(across, rest)
    across_frac = mix(across, GAUSS)
    return (
        -along_rest - across_rest,
        along_rest - across_frac,
        across_rest - along_frac,
        along_frac + across_frac,
    )


def block_of(row_place, across, ty_count, pb_count):
    return (row_place // pb_count * ty_count + across) * pb_count + row_place % pb_count


def prepare(axes, *refs):
    (disp, dirn, fit_disp, fit_dir, node_ref, owner_ref, slot_ref) = refs[:7]
    (fields, ties, col_out, pay) = refs[7:]
    tx_count, ty_count, pb_count = axes
    row_total = fields.shape[0] // COMPS
    cols = fields.shape[1]
    slots = fit_disp.shape[1]
    tie_total = ties.shape[1]
    core = lax.axis_index("pb")
    across = lax.axis_index("ty")
    place = lax.axis_index("tx") * pb_count + core

    fields[...] = jnp.zeros(fields.shape, F32)
    for comp in range(6):
        fields[pl.ds(comp, row_total, stride=COMPS), :] = disp[comp * row_total : (comp + 1) * row_total, :]
        fields[pl.ds(8 + comp, row_total, stride=COMPS), :] = dirn[comp * row_total : (comp + 1) * row_total, :]

    lane = lanes_of((COMPS, cols))
    for side, column in enumerate((0, cols - 1)):
        gathered = jnp.zeros((COMPS, cols), F32)
        for row in range(row_total):
            value = fields[row * COMPS : (row + 1) * COMPS, column : column + 1]
            gathered = jnp.where(lane == row, value, gathered)
        col_out[side * COMPS : (side + 1) * COMPS, :] = gathered

    node = as_line(node_ref)
    slot = as_line(slot_ref)
    owner = owner_ref[...]
    node_row = lax.shift_right_logical(node, cols.bit_length() - 1)
    node_col = jnp.bitwise_and(node, cols - 1)
    hot_col = one_hot(node_col, cols)
    wide = dot(
        jnp.concatenate(split(fields[...], 2), axis=1), jnp.concatenate([hot_col] * 2, axis=0)
    )
    value = jnp.zeros((COMPS, tie_total), F32)
    for row in range(row_total):
        value = jnp.where(node_row == row, wide[row * COMPS : (row + 1) * COMPS], value)
    value = jnp.where(rows_of(value.shape) == COUNT_ROW, 1.0, value)
    ties[...] = value
    stack = jnp.concatenate(split(value, 2), axis=0)
    hot_slot = one_hot(slot, slots)
    fitting = paired(fit_disp[...], fit_dir[...])

    def bins(first, count):
        lhs = [
            stack * (owner == first + at).astype(F32).astype(BF16) for at in range(count)
        ]
        return dot(jnp.concatenate(lhs, axis=0), hot_slot, ((1,), (1,)))

    def folded(wide_bins, at):
        part = wide_bins[at * 2 * COMPS : (at + 1) * 2 * COMPS]
        return part[0:COMPS] + part[COMPS : 2 * COMPS]

    peers = tx_count * ty_count
    block = math.gcd(peers, 8)

    def fill(first):
        wide_bins = bins(first, block)
        for peer in range(block):
            at = (first + peer) * pb_count + core
            pay[at, 0:COMPS, :] = fitting
            pay[at, COMPS : 2 * COMPS, :] = folded(wide_bins, peer)

    if block == peers:
        fill(0)
    else:
        lax.fori_loop(0, peers // block, lambda at, carry: (fill(at * block), carry)[1], 0)

    for step, edge in ((-1, fields[0:COMPS, :]), (1, fields[(row_total - 1) * COMPS :, :])):
        for side in (-1, 0, 1):
            there, over = place + step, across + side
            valid = (there >= 0) & (there < tx_count * pb_count) & (over >= 0) & (over < ty_count)

            @pl.when(valid)
            def _():
                pay[block_of(there, over, ty_count, pb_count), 0:COMPS, :] = edge

    for side, edge in ((-1, 0), (1, 1)):
        over = across + side
        packed = pack_column(col_out[edge * COMPS : (edge + 1) * COMPS, :], row_total)

        @pl.when((over >= 0) & (over < ty_count))
        def _():
            at = block_of(place, over, ty_count, pb_count)
            for line, row in zip(packed, SPARE_ROWS):
                pay[at, row : row + 1, :] = line


def pack_column(column, width):
    each = column.shape[1] // width
    lines = []
    for first in range(0, 12, each):
        line = None
        for at in range(first, min(first + each, 12)):
            row = at % 6 + at // 6 * 8
            part = column[row : row + 1]
            if at > first:
                part = pltpu.roll(part, (at - first) * width, 1)
            line = part if line is None else line + part
        lines.append(line)
    assert len(lines) <= len(SPARE_ROWS)
    return lines


def unpack_column(block, width):
    shape = (COMPS, block.shape[1])
    each = shape[1] // width
    row = rows_of(shape)
    column = jnp.zeros(shape, F32)
    for at in range(12):
        spare = SPARE_ROWS[at // each]
        line = block[spare : spare + 1]
        if at % each:
            line = pltpu.roll(line, shape[1] - at % each * width, 1)
        column = jnp.where(row == at % 6 + at // 6 * 8, line, column)
    return jnp.where(lanes_of(shape) < width, column, 0.0)


def build_weights(w_in, b_in, b_mid, w_out, w_first, w_last, b_cols):
    hid = w_in.shape[1]
    bias_rows = split(b_in[...], 3)
    row = rows_of((8, hid))
    stacked = jnp.zeros((8, hid), F32)
    mid_stacked = jnp.zeros((8, hid), F32)
    for at, (one, two) in enumerate(zip(bias_rows, split(b_mid[...], 3))):
        stacked = jnp.where(row == at, one.astype(F32), stacked)
        mid_stacked = jnp.where(row == at, two.astype(F32), mid_stacked)
    lhs = jnp.concatenate([w_in[...].astype(F32), jnp.zeros((4, hid), F32), stacked], axis=0).astype(BF16)
    sel_shape = (24, 4 * COMPS)
    source = rows_of(sel_shape)
    target = lanes_of(sel_shape)
    for point in range(4):
        a_base = (point // 2) * COMPS
        c_base = (2 + point % 2) * COMPS
        for side in range(2):
            hit = (source < 6) & (target == a_base + 8 * side + source)
            hit = hit | ((source >= 6) & (source < 12) & (target == c_base + 8 * side + source - 6))
            if side == 0:
                for at, spot in enumerate((6, 7, 14)):
                    hit = hit | ((source == 16 + at) & (target == a_base + spot))
            block = dot(lhs, hit.astype(F32).astype(BF16), ((0,), (0,)))
            start = (2 * point + side) * hid
            w_first[start : start + hid, :] = block.astype(BF16)
    ones = (rows_of((8, 128)) < 3).astype(F32).astype(BF16)
    b_cols[...] = dot(mid_stacked.astype(BF16), ones, ((0,), (0,)))
    last_shape = (128, 12)
    target = rows_of(last_shape)
    source = lanes_of(last_shape)
    hit = target < 0
    for point in range(4):
        a_base = point * 32 + (point // 2) * 8
        c_base = point * 32 + 16 + (point % 2) * 8
        hit = hit | ((source < 6) & (target == a_base + source))
        hit = hit | ((source >= 6) & (target == c_base + source - 6))
    w_last[...] = dot(hit.astype(F32).astype(BF16), w_out[...]).astype(BF16)


def interior(fields, w_in, b_in, w_mid, b_mid, w_out, forces, w_first, w_last, b_cols):
    row_total, cols = fields.shape[0] // COMPS, fields.shape[1]
    pairs = (row_total - 1) // 2
    group = next(size for size in (GROUP, 3, 2, 1) if pairs % size == 0)
    keep = lanes_of((COMPS, cols)) < cols - 1
    build_weights(w_in, b_in, b_mid, w_out, w_first, w_last, b_cols)
    forces[...] = jnp.zeros(forces.shape, F32)

    def row_of(row):
        base = fields[pl.ds(pl.multiple_of(row * COMPS, COMPS), COMPS), :]
        return base, pltpu.roll(base, cols - 1, 1)

    def step(pair, carry):
        start = pair * group
        lines = [row_of(2 * start + at) for at in range(2 * group + 1)]
        tiles = [
            strain_tile(lines[at][0], lines[at + 1][0], lines[at][1], lines[at + 1][1])
            for at in range(2 * group)
        ]
        tiles = [jnp.concatenate(tiles[at : at + 2], axis=1) for at in range(0, 2 * group, 2)]
        sums = stress_sums(tiles, w_first, w_mid, b_cols, w_last)
        for tile, (primal, tangent) in enumerate(sums):
            for half in range(2):
                lanes = slice(half * cols, (half + 1) * cols)
                parts = corner_forces(primal[:, lanes], tangent[:, lanes])
                base, right, upper, corner = (jnp.where(keep, part, 0.0) for part in parts)
                at = pl.multiple_of((2 * (start + tile) + half) * COMPS, COMPS)
                forces[pl.ds(at, COMPS), :] += base + pltpu.roll(upper, 1, 1)
                forces[pl.ds(at + COMPS, COMPS), :] += right + pltpu.roll(corner, 1, 1)
        return carry

    lax.fori_loop(0, pairs // group, step, 0)


def finish(names, axes, *refs):
    ref = dict(zip(names, refs))
    tx_count, ty_count, pb_count = axes
    fields, ties, forces_in, load = ref["fields"], ref["ties"], ref["forces"], ref["load"]
    scratch, got = ref["scratch"], ref["got"]
    row_total, cols = fields.shape[0] // COMPS, fields.shape[1]
    slots = got.shape[2]
    tie_total = ties.shape[1]
    lane = lanes_of((COMPS, cols))
    core = lax.axis_index("pb")
    across = lax.axis_index("ty")
    place = lax.axis_index("tx") * pb_count + core

    def around(step, side):
        there, over = place + step, across + side
        valid = (there >= 0) & (there < tx_count * pb_count) & (over >= 0) & (over < ty_count)
        at = jnp.where(valid, block_of(there, over, ty_count, pb_count), 0)
        value = got[at, 0:COMPS, :]
        if step == 0:
            value = unpack_column(value, row_total)
        return jnp.where(valid, value, 0.0)

    prev_row = around(-1, 0)
    next_row = around(1, 0)
    next_col = around(0, 1)
    prev_col = around(0, -1)
    next_corner = (around(-1, 1)[:, 0:1], around(1, 1)[:, 0:1])
    prev_corner = (around(-1, -1)[:, cols - 1 : cols], around(1, -1)[:, cols - 1 : cols])

    def column(inner, before, after):
        line = pltpu.roll(inner, 1, 1)
        line = jnp.where(lane == 0, before, line)
        return jnp.where(lane == row_total + 1, after, line)

    own_cols = ref["cols"]
    line_prev = column(prev_col, prev_corner[0], prev_corner[1])
    line_next = column(next_col, next_corner[0], next_corner[1])
    line_first = column(own_cols[0:COMPS, :], prev_row[:, 0:1], next_row[:, 0:1])
    line_final = column(
        own_cols[COMPS : 2 * COMPS, :], prev_row[:, cols - 1 : cols], next_row[:, cols - 1 : cols]
    )

    def shifted(row_value, beyond):
        return jnp.where(lane == cols - 1, beyond, pltpu.roll(row_value, cols - 1, 1))

    first_row = fields[0:COMPS, :]
    last_row = fields[(row_total - 1) * COMPS :, :]
    inner_row = fields[(row_total - 2) * COMPS : (row_total - 1) * COMPS, :]

    tile_inner = strain_tile(
        inner_row, last_row, pltpu.roll(inner_row, cols - 1, 1), pltpu.roll(last_row, cols - 1, 1)
    )
    tile_before = strain_tile(
        prev_row,
        first_row,
        shifted(prev_row, next_corner[0]),
        shifted(first_row, next_col[:, 0:1]),
    )
    tile_after = strain_tile(
        last_row,
        next_row,
        shifted(last_row, next_col[:, row_total - 1 : row_total]),
        shifted(next_row, next_corner[1]),
    )
    half = cols // 2
    low = lane < half
    back = cols - 1

    def two(left, right_line):
        return jnp.where(low, left, pltpu.roll(right_line, half + back, 1))

    left_base = two(line_prev, line_final)
    left_upper = two(line_first, line_next)
    right_base = two(pltpu.roll(line_prev, back, 1), pltpu.roll(line_final, back, 1))
    right_upper = two(pltpu.roll(line_first, back, 1), pltpu.roll(line_next, back, 1))
    tile_side = strain_tile(left_base, right_base, left_upper, right_upper)

    parts = []
    edge_tiles = [jnp.concatenate(pair, axis=1) for pair in ((tile_inner, tile_before), (tile_after, tile_side))]
    edge_sums = stress_sums(edge_tiles, ref["w_first"], ref["w_mid"], ref["b_mid"], ref["w_last"])
    for primal, tangent in edge_sums:
        for at in range(2):
            lanes = slice(at * cols, (at + 1) * cols)
            parts.append(corner_forces(primal[:, lanes], tangent[:, lanes]))
    part_inner, part_before, part_after, part_side = parts

    def mask(value, keep):
        return jnp.where(keep, value, 0.0)

    def moved(value, keep):
        return pltpu.roll(mask(value, keep), 1, 1)

    inside = lane < cols - 1
    i_base, i_right, i_upper, i_corner = part_inner
    _, b_right, _, b_corner = part_before
    a_base, _, a_upper, _ = part_after
    s_base, s_right, s_upper, s_corner = part_side
    has_row = place > 0
    has_col = across > 0
    row_first = mask(mask(b_right, lane < cols) + moved(b_corner, inside), has_row)
    row_inner = mask(i_base, inside) + moved(i_upper, inside)
    row_last = mask(i_right, inside) + moved(i_corner, inside) + a_base + moved(a_upper, inside)
    first_lane = jnp.where(has_row, 0, 1)
    s_corner = mask(s_corner, (lane >= first_lane) & (lane < row_total))
    s_upper = mask(s_upper, (lane >= 1) & (lane <= row_total))
    col_first = mask(pltpu.roll(s_upper, back, 1) + s_corner, has_col)
    s_base = mask(s_base, (lane >= half) & (lane < half + row_total - 1))
    s_right = mask(s_right, (lane >= half) & (lane < half + row_total - 1))
    col_last = pltpu.roll(s_base + pltpu.roll(s_right, 1, 1), cols - half, 1)

    node = as_line(ref["node"])
    slot = as_line(ref["slot"])
    owner = ref["owner"][...]
    hot_slot = one_hot(slot, slots)
    hot_two = jnp.concatenate([hot_slot] * 2, axis=0)
    fit_value = jnp.zeros((COMPS, tie_total), F32)
    bins = jnp.zeros((COMPS, slots), F32)
    peers = tx_count * ty_count
    block = math.gcd(peers, 8)

    def collect(first, carry):
        fit_value, bins = carry
        parts = [got[(first + peer) * pb_count + core] for peer in range(block)]
        fit_all = jnp.concatenate([part[0:COMPS] for part in parts], axis=0)
        wide = dot(jnp.concatenate(split(fit_all, 2), axis=1), hot_two)
        for peer, part in enumerate(parts):
            fit_value = jnp.where(owner == first + peer, wide[peer * COMPS : (peer + 1) * COMPS], fit_value)
            bins = bins + part[COMPS : 2 * COMPS]
        return fit_value, bins

    if block == peers:
        fit_value, bins = collect(0, (fit_value, bins))
    else:
        fit_value, bins = lax.fori_loop(
            0, peers // block, lambda at, carry: collect(at * block, carry), (fit_value, bins)
        )
    count = bins[COUNT_ROW : COUNT_ROW + 1]
    for out, fit, base in (("fit_res", "fit_disp", 0), ("fit_tan", "fit_dir", 8)):
        ref[out][...] = 2.0 * (count * ref[fit][...] - bins[base : base + 6])

    pulled = 2.0 * (ties[...] - fit_value)
    node_row = lax.shift_right_logical(node, cols.bit_length() - 1)
    node_col = jnp.bitwise_and(node, cols - 1)
    hot_col = one_hot(node_col, cols)
    sides = split(pulled, 2)
    lhs = []
    for row in range(row_total):
        hit = (node_row == row).astype(F32).astype(BF16)
        lhs.append(jnp.concatenate([side * hit for side in sides], axis=1))
    tie_forces = dot(
        jnp.concatenate(lhs, axis=0), jnp.concatenate([hot_col] * 2, axis=1), ((1,), (1,))
    )

    for row in range(row_total):
        total = forces_in[row * COMPS : (row + 1) * COMPS, :] + tie_forces[row * COMPS : (row + 1) * COMPS]
        total = total + jnp.where(lane == 0, col_first[:, row : row + 1], 0.0)
        total = total + jnp.where(lane == cols - 1, col_last[:, row : row + 1], 0.0)
        if row == 0:
            total = total + row_first
        if row == row_total - 2:
            total = total + row_inner
        if row == row_total - 1:
            total = total + row_last
        scratch[row * COMPS : (row + 1) * COMPS, :] = total
    for comp in range(6):
        rows = slice(comp * row_total, (comp + 1) * row_total)
        ref["res"][rows, :] = scratch[pl.ds(comp, row_total, stride=COMPS), :] - load[rows, :]
        ref["tan"][rows, :] = scratch[pl.ds(8 + comp, row_total, stride=COMPS), :]


def per_device(
    displacement,
    direction,
    load,
    w_in,
    b_in,
    w_mid,
    b_mid,
    w_out,
    fitting_disp,
    fitting_dir,
    tie_node,
    tie_owner,
    tie_slot,
):
    tx_count = lax.axis_size("tx")
    ty_count = lax.axis_size("ty")
    pb_count = lax.axis_size("pb")
    peers = tx_count * ty_count
    axes = (tx_count, ty_count, pb_count)
    _, row_total, cols = displacement.shape
    slots = fitting_disp.shape[1]
    tie_total = tie_node.shape[0]
    hid = w_mid.shape[0]
    flat = (6 * row_total, cols)
    disp2 = displacement.reshape(flat)
    dir2 = direction.reshape(flat)
    load2 = load.reshape(flat)
    node2 = tie_node.reshape(tie_total // 128, 128)
    slot2 = tie_slot.reshape(tie_total // 128, 128)
    owner2 = tie_owner.reshape(1, tie_total)

    def shape(*dims, dtype=F32):
        return jax.ShapeDtypeStruct(dims, dtype)

    inputs = (disp2, dir2, fitting_disp, fitting_dir, node2, owner2, slot2)
    fields, ties, cols_out, pay = pl.pallas_call(
        lambda *refs: prepare(axes, *refs),
        out_shape=[
            pltpu.VMEM((row_total * COMPS, cols), F32),
            pltpu.VMEM((COMPS, tie_total), F32),
            pltpu.VMEM((2 * COMPS, cols), F32),
            shape(peers * pb_count, 2 * COMPS, slots),
        ],
        in_specs=local(len(inputs)),
        out_specs=local(4),
        name="prepare",
    )(*inputs)
    got = lax.all_to_all(pay, ("tx", "ty", "pb"), split_axis=0, concat_axis=0, tiled=True)

    inputs = (on_chip(fields), w_in.T, b_in.reshape(1, hid), w_mid, b_mid.reshape(1, hid), w_out)
    forces, w_first, w_last, b_cols = pl.pallas_call(
        interior,
        out_shape=[
            pltpu.VMEM((row_total * COMPS, cols), F32),
            pltpu.VMEM((8 * hid, 4 * COMPS), BF16),
            pltpu.VMEM((128, hid), BF16),
            pltpu.VMEM((hid, 128), F32),
        ],
        in_specs=local(len(inputs)),
        out_specs=local(4),
        name="interior",
    )(*inputs)

    named = dict(
        got=on_chip(got) if got.size <= SMALL else got,
        fields=on_chip(fields),
        ties=on_chip(ties),
        forces=on_chip(forces),
        load=load2,
        cols=on_chip(cols_out),
        w_first=on_chip(w_first),
        w_mid=w_mid,
        b_mid=on_chip(b_cols),
        w_last=on_chip(w_last),
        node=node2,
        slot=slot2,
        owner=owner2,
        fit_disp=fitting_disp,
        fit_dir=fitting_dir,
    )
    names = list(named)
    res, tan, fit_res, fit_tan = pl.pallas_call(
        lambda *refs: finish(names + ["res", "tan", "fit_res", "fit_tan", "scratch"], axes, *refs),
        out_shape=[shape(*flat), shape(*flat), shape(6, slots), shape(6, slots)],
        in_specs=local(len(names)),
        out_specs=local(4),
        scratch_shapes=[pltpu.VMEM((row_total * COMPS, cols), F32)],
        name="finish",
    )(*named.values())
    cube = displacement.shape
    return (res.reshape(cube), tan.reshape(cube), fit_res, fit_tan)


def solution(mesh):
    in_specs = (
        P(None, ("tx", "pb"), "ty"),
        P(None, ("tx", "pb"), "ty"),
        P(None, ("tx", "pb"), "ty"),
        P(),
        P(),
        P(),
        P(),
        P(),
        P(None, ("groups", "tx", "ty", "pb")),
        P(None, ("groups", "tx", "ty", "pb")),
        P(("groups", "tx", "ty", "pb")),
        P(("groups", "tx", "ty", "pb"), None),
        P(("groups", "tx", "ty", "pb")),
    )
    out_specs = (
        P(None, ("groups", "tx", "pb"), "ty"),
        P(None, ("groups", "tx", "pb"), "ty"),
        P(None, ("groups", "tx", "ty", "pb")),
        P(None, ("groups", "tx", "ty", "pb")),
    )
    return jax.shard_map(
        per_device, mesh=mesh, in_specs=in_specs, out_specs=out_specs, check_vma=False
    )
```

```python
import math

import jax
import jax.numpy as jnp
from jax import lax
from jax.experimental import pallas as pl
from jax.experimental.pallas import tpu as pltpu
from jax.sharding import PartitionSpec as P

F32 = jnp.float32
BF16 = jnp.bfloat16
GAUSS = (0.5 - 0.5 / math.sqrt(3.0), 0.5 + 0.5 / math.sqrt(3.0))
COMPS = 16
COUNT_ROW = 6
SPARE_ROWS = (6, 7, 14)
GROUP = 15
SMALL = 1 << 18


def local(count):
    return [pl.BlockSpec(memory_space=pltpu.VMEM)] * count


def on_chip(value):
    return pltpu.with_memory_space_constraint(value, pltpu.VMEM)


def dot(a, b, dims=((1,), (0,))):
    return lax.dot_general(a, b, (dims, ((), ())), preferred_element_type=F32)


def split(value, terms):
    parts = []
    for _ in range(terms):
        part = value.astype(BF16)
        parts.append(part)
        value = value - part.astype(F32)
    return parts


def rows_of(value):
    return lax.broadcasted_iota(jnp.int32, value, 0)


def lanes_of(value):
    return lax.broadcasted_iota(jnp.int32, value, 1)


def one_hot(index, size):
    shape = (size, index.shape[1])
    return (rows_of(shape) == index).astype(F32).astype(BF16)


def as_line(ref):
    return jnp.concatenate([ref[row : row + 1, :] for row in range(ref.shape[0])], axis=1)


def paired(top, bottom):
    spare = jnp.zeros((2, top.shape[1]), F32)
    return jnp.concatenate([top, spare, bottom, spare], axis=0)


def strain_tile(f00, f10, f01, f11):
    along_low = f10 - f00
    along_high = f11 - f01
    across_low = f01 - f00
    across_high = f11 - f10
    shape = f00.shape
    row = rows_of(shape)
    ones = ((row == 6) | (row == 7) | (row == 14)).astype(F32)
    groups = []
    for frac in GAUSS:
        groups.append((((1.0 - frac) * along_low + frac * along_high) + ones).astype(BF16))
    for frac in GAUSS:
        groups.append(((1.0 - frac) * across_low + frac * across_high).astype(BF16))
    return jnp.concatenate(groups, axis=0)


def stress_sums(strains, w_first, w_mid, b_mid, w_last):
    hid = w_mid.shape[0]
    tasks = [(tile, point) for tile in range(len(strains)) for point in range(4)]
    totals = [[None, None] for _ in strains]

    def layer_one(task):
        tile, point = task
        start = point * 2 * hid
        return (
            dot(w_first[start : start + hid, :], strains[tile]),
            dot(w_first[start + hid : start + 2 * hid, :], strains[tile]),
        )

    def activate(value, slope):
        act = jnp.tanh(value)
        return (act.astype(BF16), ((1.0 - act * act) * slope).astype(BF16))

    def layer_two(hidden):
        bias = b_mid[...]
        value = dot(w_mid[...], hidden[0])
        slope = dot(w_mid[...], hidden[1])
        bias = jnp.concatenate([bias] * (value.shape[1] // bias.shape[1]), axis=1)
        return (value + bias, slope)

    def layer_three(task, hidden):
        tile, point = task
        last = w_last[point * 32 : (point + 1) * 32, :]
        for side in range(2):
            part = dot(last, hidden[side])
            old = totals[tile][side]
            totals[tile][side] = part if old is None else old + part

    ones = {0: layer_one(tasks[0])}
    twos = {}
    for at in range(len(tasks) + 1):
        if at + 1 < len(tasks):
            ones[at + 1] = layer_one(tasks[at + 1])
        if at < len(tasks):
            hidden = activate(*ones.pop(at))
            twos[at] = layer_two(hidden)
        if at >= 1:
            layer_three(tasks[at - 1], activate(*twos.pop(at - 1)))
    return totals


def corner_forces(primal, tangent):
    def both(group):
        return jnp.concatenate([primal[group * 8 : group * 8 + 8], tangent[group * 8 : group * 8 + 8]], axis=0)

    along = (both(0), both(1))
    across = (both(2), both(3))

    def mix(pair, weights):
        return (0.25 * weights[0]) * pair[0] + (0.25 * weights[1]) * pair[1]

    rest = (1.0 - GAUSS[0], 1.0 - GAUSS[1])
    along_rest = mix(along, rest)
    along_frac = mix(along, GAUSS)
    across_rest = mix(across, rest)
    across_frac = mix(across, GAUSS)
    return (
        -along_rest - across_rest,
        along_rest - across_frac,
        across_rest - along_frac,
        along_frac + across_frac,
    )


def block_of(row_place, across, ty_count, pb_count):
    return (row_place // pb_count * ty_count + across) * pb_count + row_place % pb_count


def prepare(axes, *refs):
    (disp, dirn, fit_disp, fit_dir, node_ref, owner_ref, slot_ref) = refs[:7]
    (fields, ties, col_out, pay) = refs[7:]
    tx_count, ty_count, pb_count = axes
    row_total = fields.shape[0] // COMPS
    cols = fields.shape[1]
    slots = fit_disp.shape[1]
    tie_total = ties.shape[1]
    core = lax.axis_index("pb")
    across = lax.axis_index("ty")
    place = lax.axis_index("tx") * pb_count + core

    fields[...] = jnp.zeros(fields.shape, F32)
    for comp in range(6):
        fields[pl.ds(comp, row_total, stride=COMPS), :] = disp[comp * row_total : (comp + 1) * row_total, :]
        fields[pl.ds(8 + comp, row_total, stride=COMPS), :] = dirn[comp * row_total : (comp + 1) * row_total, :]

    lane = lanes_of((COMPS, cols))
    for side, column in enumerate((0, cols - 1)):
        gathered = jnp.zeros((COMPS, cols), F32)
        for row in range(row_total):
            value = fields[row * COMPS : (row + 1) * COMPS, column : column + 1]
            gathered = jnp.where(lane == row, value, gathered)
        col_out[side * COMPS : (side + 1) * COMPS, :] = gathered

    node = as_line(node_ref)
    slot = as_line(slot_ref)
    owner = owner_ref[...]
    node_row = lax.shift_right_logical(node, cols.bit_length() - 1)
    node_col = jnp.bitwise_and(node, cols - 1)
    hot_col = one_hot(node_col, cols)
    wide = dot(
        jnp.concatenate(split(fields[...], 2), axis=1), jnp.concatenate([hot_col] * 2, axis=0)
    )
    value = jnp.zeros((COMPS, tie_total), F32)
    for row in range(row_total):
        value = jnp.where(node_row == row, wide[row * COMPS : (row + 1) * COMPS], value)
    value = jnp.where(rows_of(value.shape) == COUNT_ROW, 1.0, value)
    ties[...] = value
    stack = jnp.concatenate(split(value, 2), axis=0)
    hot_slot = one_hot(slot, slots)
    fitting = paired(fit_disp[...], fit_dir[...])

    def bins(first, count):
        lhs = [
            stack * (owner == first + at).astype(F32).astype(BF16) for at in range(count)
        ]
        return dot(jnp.concatenate(lhs, axis=0), hot_slot, ((1,), (1,)))

    def folded(wide_bins, at):
        part = wide_bins[at * 2 * COMPS : (at + 1) * 2 * COMPS]
        return part[0:COMPS] + part[COMPS : 2 * COMPS]

    peers = tx_count * ty_count
    block = math.gcd(peers, 8)

    def fill(first):
        wide_bins = bins(first, block)
        for peer in range(block):
            at = (first + peer) * pb_count + core
            pay[at, 0:COMPS, :] = fitting
            pay[at, COMPS : 2 * COMPS, :] = folded(wide_bins, peer)

    if block == peers:
        fill(0)
    else:
        lax.fori_loop(0, peers // block, lambda at, carry: (fill(at * block), carry)[1], 0)

    for step, edge in ((-1, fields[0:COMPS, :]), (1, fields[(row_total - 1) * COMPS :, :])):
        for side in (-1, 0, 1):
            there, over = place + step, across + side
            valid = (there >= 0) & (there < tx_count * pb_count) & (over >= 0) & (over < ty_count)

            @pl.when(valid)
            def _():
                pay[block_of(there, over, ty_count, pb_count), 0:COMPS, :] = edge

    for side, edge in ((-1, 0), (1, 1)):
        over = across + side
        packed = pack_column(col_out[edge * COMPS : (edge + 1) * COMPS, :], row_total)

        @pl.when((over >= 0) & (over < ty_count))
        def _():
            at = block_of(place, over, ty_count, pb_count)
            for line, row in zip(packed, SPARE_ROWS):
                pay[at, row : row + 1, :] = line


def pack_column(column, width):
    each = column.shape[1] // width
    lines = []
    for first in range(0, 12, each):
        line = None
        for at in range(first, min(first + each, 12)):
            row = at % 6 + at // 6 * 8
            part = column[row : row + 1]
            if at > first:
                part = pltpu.roll(part, (at - first) * width, 1)
            line = part if line is None else line + part
        lines.append(line)
    assert len(lines) <= len(SPARE_ROWS)
    return lines


def unpack_column(block, width):
    shape = (COMPS, block.shape[1])
    each = shape[1] // width
    row = rows_of(shape)
    column = jnp.zeros(shape, F32)
    for at in range(12):
        spare = SPARE_ROWS[at // each]
        line = block[spare : spare + 1]
        if at % each:
            line = pltpu.roll(line, shape[1] - at % each * width, 1)
        column = jnp.where(row == at % 6 + at // 6 * 8, line, column)
    return jnp.where(lanes_of(shape) < width, column, 0.0)


def build_weights(w_in, b_in, b_mid, w_out, w_first, w_last, b_cols):
    hid = w_in.shape[1]
    bias_rows = split(b_in[...], 3)
    row = rows_of((8, hid))
    stacked = jnp.zeros((8, hid), F32)
    mid_stacked = jnp.zeros((8, hid), F32)
    for at, (one, two) in enumerate(zip(bias_rows, split(b_mid[...], 3))):
        stacked = jnp.where(row == at, one.astype(F32), stacked)
        mid_stacked = jnp.where(row == at, two.astype(F32), mid_stacked)
    lhs = jnp.concatenate([w_in[...].astype(F32), jnp.zeros((4, hid), F32), stacked], axis=0).astype(BF16)
    sel_shape = (24, 4 * COMPS)
    source = rows_of(sel_shape)
    target = lanes_of(sel_shape)
    for point in range(4):
        a_base = (point // 2) * COMPS
        c_base = (2 + point % 2) * COMPS
        for side in range(2):
            hit = (source < 6) & (target == a_base + 8 * side + source)
            hit = hit | ((source >= 6) & (source < 12) & (target == c_base + 8 * side + source - 6))
            if side == 0:
                for at, spot in enumerate((6, 7, 14)):
                    hit = hit | ((source == 16 + at) & (target == a_base + spot))
            block = dot(lhs, hit.astype(F32).astype(BF16), ((0,), (0,)))
            start = (2 * point + side) * hid
            w_first[start : start + hid, :] = block.astype(BF16)
    ones = (rows_of((8, 128)) < 3).astype(F32).astype(BF16)
    b_cols[...] = dot(mid_stacked.astype(BF16), ones, ((0,), (0,)))
    last_shape = (128, 12)
    target = rows_of(last_shape)
    source = lanes_of(last_shape)
    hit = target < 0
    for point in range(4):
        a_base = point * 32 + (point // 2) * 8
        c_base = point * 32 + 16 + (point % 2) * 8
        hit = hit | ((source < 6) & (target == a_base + source))
        hit = hit | ((source >= 6) & (target == c_base + source - 6))
    w_last[...] = dot(hit.astype(F32).astype(BF16), w_out[...]).astype(BF16)


def interior(fields, w_in, b_in, w_mid, b_mid, w_out, forces, w_first, w_last, b_cols):
    row_total, cols = fields.shape[0] // COMPS, fields.shape[1]
    pairs = (row_total - 1) // 2
    group = next(size for size in (GROUP, 3, 2, 1) if pairs % size == 0)
    keep = lanes_of((COMPS, cols)) < cols - 1
    build_weights(w_in, b_in, b_mid, w_out, w_first, w_last, b_cols)
    forces[...] = jnp.zeros(forces.shape, F32)

    def row_of(row):
        base = fields[pl.ds(pl.multiple_of(row * COMPS, COMPS), COMPS), :]
        return base, pltpu.roll(base, cols - 1, 1)

    def step(pair, carry):
        start = pair * group
        lines = [row_of(2 * start + at) for at in range(2 * group + 1)]
        tiles = [
            strain_tile(lines[at][0], lines[at + 1][0], lines[at][1], lines[at + 1][1])
            for at in range(2 * group)
        ]
        tiles = [jnp.concatenate(tiles[at : at + 2], axis=1) for at in range(0, 2 * group, 2)]
        sums = stress_sums(tiles, w_first, w_mid, b_cols, w_last)
        for tile, (primal, tangent) in enumerate(sums):
            for half in range(2):
                lanes = slice(half * cols, (half + 1) * cols)
                parts = corner_forces(primal[:, lanes], tangent[:, lanes])
                base, right, upper, corner = (jnp.where(keep, part, 0.0) for part in parts)
                at = pl.multiple_of((2 * (start + tile) + half) * COMPS, COMPS)
                forces[pl.ds(at, COMPS), :] += base + pltpu.roll(upper, 1, 1)
                forces[pl.ds(at + COMPS, COMPS), :] += right + pltpu.roll(corner, 1, 1)
        return carry

    if group == pairs:
        step(0, 0)
    else:
        lax.fori_loop(0, pairs // group, step, 0)


def finish(names, axes, *refs):
    ref = dict(zip(names, refs))
    tx_count, ty_count, pb_count = axes
    fields, ties, forces_in, load = ref["fields"], ref["ties"], ref["forces"], ref["load"]
    scratch, got = ref["scratch"], ref["got"]
    row_total, cols = fields.shape[0] // COMPS, fields.shape[1]
    slots = got.shape[2]
    tie_total = ties.shape[1]
    lane = lanes_of((COMPS, cols))
    core = lax.axis_index("pb")
    across = lax.axis_index("ty")
    place = lax.axis_index("tx") * pb_count + core

    def around(step, side):
        there, over = place + step, across + side
        valid = (there >= 0) & (there < tx_count * pb_count) & (over >= 0) & (over < ty_count)
        at = jnp.where(valid, block_of(there, over, ty_count, pb_count), 0)
        value = got[at, 0:COMPS, :]
        if step == 0:
            value = unpack_column(value, row_total)
        return jnp.where(valid, value, 0.0)

    prev_row = around(-1, 0)
    next_row = around(1, 0)
    next_col = around(0, 1)
    prev_col = around(0, -1)
    next_corner = (around(-1, 1)[:, 0:1], around(1, 1)[:, 0:1])
    prev_corner = (around(-1, -1)[:, cols - 1 : cols], around(1, -1)[:, cols - 1 : cols])

    def column(inner, before, after):
        line = pltpu.roll(inner, 1, 1)
        line = jnp.where(lane == 0, before, line)
        return jnp.where(lane == row_total + 1, after, line)

    own_cols = ref["cols"]
    line_prev = column(prev_col, prev_corner[0], prev_corner[1])
    line_next = column(next_col, next_corner[0], next_corner[1])
    line_first = column(own_cols[0:COMPS, :], prev_row[:, 0:1], next_row[:, 0:1])
    line_final = column(
        own_cols[COMPS : 2 * COMPS, :], prev_row[:, cols - 1 : cols], next_row[:, cols - 1 : cols]
    )

    def shifted(row_value, beyond):
        return jnp.where(lane == cols - 1, beyond, pltpu.roll(row_value, cols - 1, 1))

    first_row = fields[0:COMPS, :]
    last_row = fields[(row_total - 1) * COMPS :, :]
    inner_row = fields[(row_total - 2) * COMPS : (row_total - 1) * COMPS, :]

    tile_inner = strain_tile(
        inner_row, last_row, pltpu.roll(inner_row, cols - 1, 1), pltpu.roll(last_row, cols - 1, 1)
    )
    tile_before = strain_tile(
        prev_row,
        first_row,
        shifted(prev_row, next_corner[0]),
        shifted(first_row, next_col[:, 0:1]),
    )
    tile_after = strain_tile(
        last_row,
        next_row,
        shifted(last_row, next_col[:, row_total - 1 : row_total]),
        shifted(next_row, next_corner[1]),
    )
    half = cols // 2
    low = lane < half
    back = cols - 1

    def two(left, right_line):
        return jnp.where(low, left, pltpu.roll(right_line, half + back, 1))

    left_base = two(line_prev, line_final)
    left_upper = two(line_first, line_next)
    right_base = two(pltpu.roll(line_prev, back, 1), pltpu.roll(line_final, back, 1))
    right_upper = two(pltpu.roll(line_first, back, 1), pltpu.roll(line_next, back, 1))
    tile_side = strain_tile(left_base, right_base, left_upper, right_upper)

    parts = []
    edge_tiles = [jnp.concatenate(pair, axis=1) for pair in ((tile_inner, tile_before), (tile_after, tile_side))]
    edge_sums = stress_sums(edge_tiles, ref["w_first"], ref["w_mid"], ref["b_mid"], ref["w_last"])
    for primal, tangent in edge_sums:
        for at in range(2):
            lanes = slice(at * cols, (at + 1) * cols)
            parts.append(corner_forces(primal[:, lanes], tangent[:, lanes]))
    part_inner, part_before, part_after, part_side = parts

    def mask(value, keep):
        return jnp.where(keep, value, 0.0)

    def moved(value, keep):
        return pltpu.roll(mask(value, keep), 1, 1)

    inside = lane < cols - 1
    i_base, i_right, i_upper, i_corner = part_inner
    _, b_right, _, b_corner = part_before
    a_base, _, a_upper, _ = part_after
    s_base, s_right, s_upper, s_corner = part_side
    has_row = place > 0
    has_col = across > 0
    row_first = mask(mask(b_right, lane < cols) + moved(b_corner, inside), has_row)
    row_inner = mask(i_base, inside) + moved(i_upper, inside)
    row_last = mask(i_right, inside) + moved(i_corner, inside) + a_base + moved(a_upper, inside)
    first_lane = jnp.where(has_row, 0, 1)
    s_corner = mask(s_corner, (lane >= first_lane) & (lane < row_total))
    s_upper = mask(s_upper, (lane >= 1) & (lane <= row_total))
    col_first = mask(pltpu.roll(s_upper, back, 1) + s_corner, has_col)
    s_base = mask(s_base, (lane >= half) & (lane < half + row_total - 1))
    s_right = mask(s_right, (lane >= half) & (lane < half + row_total - 1))
    col_last = pltpu.roll(s_base + pltpu.roll(s_right, 1, 1), cols - half, 1)

    node = as_line(ref["node"])
    slot = as_line(ref["slot"])
    owner = ref["owner"][...]
    hot_slot = one_hot(slot, slots)
    hot_two = jnp.concatenate([hot_slot] * 2, axis=0)
    fit_value = jnp.zeros((COMPS, tie_total), F32)
    bins = jnp.zeros((COMPS, slots), F32)
    peers = tx_count * ty_count
    block = math.gcd(peers, 8)

    def collect(first, carry):
        fit_value, bins = carry
        parts = [got[(first + peer) * pb_count + core] for peer in range(block)]
        fit_all = jnp.concatenate([part[0:COMPS] for part in parts], axis=0)
        wide = dot(jnp.concatenate(split(fit_all, 2), axis=1), hot_two)
        for peer, part in enumerate(parts):
            fit_value = jnp.where(owner == first + peer, wide[peer * COMPS : (peer + 1) * COMPS], fit_value)
            bins = bins + part[COMPS : 2 * COMPS]
        return fit_value, bins

    if block == peers:
        fit_value, bins = collect(0, (fit_value, bins))
    else:
        fit_value, bins = lax.fori_loop(
            0, peers // block, lambda at, carry: collect(at * block, carry), (fit_value, bins)
        )
    count = bins[COUNT_ROW : COUNT_ROW + 1]
    for out, fit, base in (("fit_res", "fit_disp", 0), ("fit_tan", "fit_dir", 8)):
        ref[out][...] = 2.0 * (count * ref[fit][...] - bins[base : base + 6])

    pulled = 2.0 * (ties[...] - fit_value)
    node_row = lax.shift_right_logical(node, cols.bit_length() - 1)
    node_col = jnp.bitwise_and(node, cols - 1)
    hot_col = one_hot(node_col, cols)
    sides = split(pulled, 2)
    lhs = []
    for row in range(row_total):
        hit = (node_row == row).astype(F32).astype(BF16)
        lhs.append(jnp.concatenate([side * hit for side in sides], axis=1))
    tie_forces = dot(
        jnp.concatenate(lhs, axis=0), jnp.concatenate([hot_col] * 2, axis=1), ((1,), (1,))
    )

    for row in range(row_total):
        total = forces_in[row * COMPS : (row + 1) * COMPS, :] + tie_forces[row * COMPS : (row + 1) * COMPS]
        total = total + jnp.where(lane == 0, col_first[:, row : row + 1], 0.0)
        total = total + jnp.where(lane == cols - 1, col_last[:, row : row + 1], 0.0)
        if row == 0:
            total = total + row_first
        if row == row_total - 2:
            total = total + row_inner
        if row == row_total - 1:
            total = total + row_last
        scratch[row * COMPS : (row + 1) * COMPS, :] = total
    for comp in range(6):
        rows = slice(comp * row_total, (comp + 1) * row_total)
        ref["res"][rows, :] = scratch[pl.ds(comp, row_total, stride=COMPS), :] - load[rows, :]
        ref["tan"][rows, :] = scratch[pl.ds(8 + comp, row_total, stride=COMPS), :]


def per_device(
    displacement,
    direction,
    load,
    w_in,
    b_in,
    w_mid,
    b_mid,
    w_out,
    fitting_disp,
    fitting_dir,
    tie_node,
    tie_owner,
    tie_slot,
):
    tx_count = lax.axis_size("tx")
    ty_count = lax.axis_size("ty")
    pb_count = lax.axis_size("pb")
    peers = tx_count * ty_count
    axes = (tx_count, ty_count, pb_count)
    _, row_total, cols = displacement.shape
    slots = fitting_disp.shape[1]
    tie_total = tie_node.shape[0]
    hid = w_mid.shape[0]
    flat = (6 * row_total, cols)
    disp2 = displacement.reshape(flat)
    dir2 = direction.reshape(flat)
    load2 = load.reshape(flat)
    node2 = tie_node.reshape(tie_total // 128, 128)
    slot2 = tie_slot.reshape(tie_total // 128, 128)
    owner2 = tie_owner.reshape(1, tie_total)

    def shape(*dims, dtype=F32):
        return jax.ShapeDtypeStruct(dims, dtype)

    inputs = (disp2, dir2, fitting_disp, fitting_dir, node2, owner2, slot2)
    fields, ties, cols_out, pay = pl.pallas_call(
        lambda *refs: prepare(axes, *refs),
        out_shape=[
            pltpu.VMEM((row_total * COMPS, cols), F32),
            pltpu.VMEM((COMPS, tie_total), F32),
            pltpu.VMEM((2 * COMPS, cols), F32),
            shape(peers * pb_count, 2 * COMPS, slots),
        ],
        in_specs=local(len(inputs)),
        out_specs=local(4),
        name="prepare",
    )(*inputs)
    got = lax.all_to_all(pay, ("tx", "ty", "pb"), split_axis=0, concat_axis=0, tiled=True)

    inputs = (fields, w_in.T, b_in.reshape(1, hid), w_mid, b_mid.reshape(1, hid), w_out)
    inputs = tuple(on_chip(value) for value in inputs)
    forces, w_first, w_last, b_cols = pl.pallas_call(
        interior,
        out_shape=[
            pltpu.VMEM((row_total * COMPS, cols), F32),
            pltpu.VMEM((8 * hid, 4 * COMPS), BF16),
            pltpu.VMEM((128, hid), BF16),
            pltpu.VMEM((hid, 128), F32),
        ],
        in_specs=local(len(inputs)),
        out_specs=local(4),
        name="interior",
    )(*inputs)

    named = dict(
        got=got,
        fields=fields,
        ties=ties,
        forces=forces,
        load=load2,
        cols=cols_out,
        w_first=w_first,
        w_mid=w_mid,
        b_mid=b_cols,
        w_last=w_last,
        node=node2,
        slot=slot2,
        owner=owner2,
        fit_disp=fitting_disp,
        fit_dir=fitting_dir,
    )
    named = {name: on_chip(value) if value.size <= SMALL else value for name, value in named.items()}
    names = list(named)
    res, tan, fit_res, fit_tan = pl.pallas_call(
        lambda *refs: finish(names + ["res", "tan", "fit_res", "fit_tan", "scratch"], axes, *refs),
        out_shape=[shape(*flat), shape(*flat), shape(6, slots), shape(6, slots)],
        in_specs=local(len(names)),
        out_specs=local(4),
        scratch_shapes=[pltpu.VMEM((row_total * COMPS, cols), F32)],
        name="finish",
    )(*named.values())
    cube = displacement.shape
    return (res.reshape(cube), tan.reshape(cube), fit_res, fit_tan)


def solution(mesh):
    in_specs = (
        P(None, ("tx", "pb"), "ty"),
        P(None, ("tx", "pb"), "ty"),
        P(None, ("tx", "pb"), "ty"),
        P(),
        P(),
        P(),
        P(),
        P(),
        P(None, ("groups", "tx", "ty", "pb")),
        P(None, ("groups", "tx", "ty", "pb")),
        P(("groups", "tx", "ty", "pb")),
        P(("groups", "tx", "ty", "pb"), None),
        P(("groups", "tx", "ty", "pb")),
    )
    out_specs = (
        P(None, ("groups", "tx", "pb"), "ty"),
        P(None, ("groups", "tx", "pb"), "ty"),
        P(None, ("groups", "tx", "ty", "pb")),
        P(None, ("groups", "tx", "ty", "pb")),
    )
    return jax.shard_map(
        per_device, mesh=mesh, in_specs=in_specs, out_specs=out_specs, check_vma=False
    )
```

```python
import math

import jax
import jax.numpy as jnp
from jax import lax
from jax.experimental import pallas as pl
from jax.experimental.pallas import tpu as pltpu
from jax.sharding import PartitionSpec as P

F32 = jnp.float32
BF16 = jnp.bfloat16
GAUSS = (0.5 - 0.5 / math.sqrt(3.0), 0.5 + 0.5 / math.sqrt(3.0))
COMPS = 16
COUNT_ROW = 6
SPARE_ROWS = (6, 7, 14)
SMALL = 1 << 18


def local(count):
    return [pl.BlockSpec(memory_space=pltpu.VMEM)] * count


def on_chip(value):
    return pltpu.with_memory_space_constraint(value, pltpu.VMEM)


def dot(a, b, dims=((1,), (0,))):
    return lax.dot_general(a, b, (dims, ((), ())), preferred_element_type=F32)


def split(value, terms):
    parts = []
    for _ in range(terms):
        part = value.astype(BF16)
        parts.append(part)
        value = value - part.astype(F32)
    return parts


def rows_of(value):
    return lax.broadcasted_iota(jnp.int32, value, 0)


def lanes_of(value):
    return lax.broadcasted_iota(jnp.int32, value, 1)


def one_hot(index, size):
    shape = (size, index.shape[1])
    return (rows_of(shape) == index).astype(F32).astype(BF16)


def as_line(ref):
    return jnp.concatenate([ref[row : row + 1, :] for row in range(ref.shape[0])], axis=1)


def paired(top, bottom):
    spare = jnp.zeros((2, top.shape[1]), F32)
    return jnp.concatenate([top, spare, bottom, spare], axis=0)


def strain_tile(f00, f10, f01, f11):
    along_low = f10 - f00
    along_high = f11 - f01
    across_low = f01 - f00
    across_high = f11 - f10
    shape = f00.shape
    row = rows_of(shape)
    ones = ((row == 6) | (row == 7) | (row == 14)).astype(F32)
    groups = []
    for frac in GAUSS:
        groups.append((((1.0 - frac) * along_low + frac * along_high) + ones).astype(BF16))
    for frac in GAUSS:
        groups.append(((1.0 - frac) * across_low + frac * across_high).astype(BF16))
    return jnp.concatenate(groups, axis=0)


def stress_sums(strains, w_first, w_mid, b_mid, w_last):
    hid = w_mid.shape[0]
    tasks = [(tile, point) for tile in range(len(strains)) for point in range(4)]
    totals = [[None, None] for _ in strains]

    def layer_one(task):
        tile, point = task
        start = point * 2 * hid
        return (
            dot(w_first[start : start + hid, :], strains[tile]),
            dot(w_first[start + hid : start + 2 * hid, :], strains[tile]),
        )

    def activate(value, slope):
        act = jnp.tanh(value)
        return (act.astype(BF16), ((1.0 - act * act) * slope).astype(BF16))

    def layer_two(hidden):
        bias = b_mid[...]
        value = dot(w_mid[...], hidden[0])
        slope = dot(w_mid[...], hidden[1])
        bias = jnp.concatenate([bias] * (value.shape[1] // bias.shape[1]), axis=1)
        return (value + bias, slope)

    def layer_three(task, hidden):
        tile, point = task
        last = w_last[point * 32 : (point + 1) * 32, :]
        for side in range(2):
            part = dot(last, hidden[side])
            old = totals[tile][side]
            totals[tile][side] = part if old is None else old + part

    ones = {0: layer_one(tasks[0])}
    twos = {}
    for at in range(len(tasks) + 1):
        if at + 1 < len(tasks):
            ones[at + 1] = layer_one(tasks[at + 1])
        if at < len(tasks):
            hidden = activate(*ones.pop(at))
            twos[at] = layer_two(hidden)
        if at >= 1:
            layer_three(tasks[at - 1], activate(*twos.pop(at - 1)))
    return totals


def corner_forces(primal, tangent):
    def both(group):
        return jnp.concatenate([primal[group * 8 : group * 8 + 8], tangent[group * 8 : group * 8 + 8]], axis=0)

    along = (both(0), both(1))
    across = (both(2), both(3))

    def mix(pair, weights):
        return (0.25 * weights[0]) * pair[0] + (0.25 * weights[1]) * pair[1]

    rest = (1.0 - GAUSS[0], 1.0 - GAUSS[1])
    along_rest = mix(along, rest)
    along_frac = mix(along, GAUSS)
    across_rest = mix(across, rest)
    across_frac = mix(across, GAUSS)
    return (
        -along_rest - across_rest,
        along_rest - across_frac,
        across_rest - along_frac,
        along_frac + across_frac,
    )


def block_of(row_place, across, ty_count, pb_count):
    return (row_place // pb_count * ty_count + across) * pb_count + row_place % pb_count


def prepare(axes, *refs):
    (disp, dirn, fit_disp, fit_dir, node_ref, owner_ref, slot_ref, b_in, b_mid) = refs[:9]
    (fields, ties, col_out, pay) = refs[9:13]
    for source, target in zip(refs[2:9], refs[13:]):
        target[...] = source[...]
    tx_count, ty_count, pb_count = axes
    row_total = fields.shape[0] // COMPS
    cols = fields.shape[1]
    slots = fit_disp.shape[1]
    tie_total = ties.shape[1]
    core = lax.axis_index("pb")
    across = lax.axis_index("ty")
    place = lax.axis_index("tx") * pb_count + core

    fields[...] = jnp.zeros(fields.shape, F32)
    for comp in range(6):
        fields[pl.ds(comp, row_total, stride=COMPS), :] = disp[comp * row_total : (comp + 1) * row_total, :]
        fields[pl.ds(8 + comp, row_total, stride=COMPS), :] = dirn[comp * row_total : (comp + 1) * row_total, :]

    lane = lanes_of((COMPS, cols))
    for side, column in enumerate((0, cols - 1)):
        gathered = jnp.zeros((COMPS, cols), F32)
        for row in range(row_total):
            value = fields[row * COMPS : (row + 1) * COMPS, column : column + 1]
            gathered = jnp.where(lane == row, value, gathered)
        col_out[side * COMPS : (side + 1) * COMPS, :] = gathered

    node = as_line(node_ref)
    slot = as_line(slot_ref)
    owner = owner_ref[...]
    node_row = lax.shift_right_logical(node, cols.bit_length() - 1)
    node_col = jnp.bitwise_and(node, cols - 1)
    hot_col = one_hot(node_col, cols)
    wide = dot(
        jnp.concatenate(split(fields[...], 2), axis=1), jnp.concatenate([hot_col] * 2, axis=0)
    )
    value = jnp.zeros((COMPS, tie_total), F32)
    for row in range(row_total):
        value = jnp.where(node_row == row, wide[row * COMPS : (row + 1) * COMPS], value)
    value = jnp.where(rows_of(value.shape) == COUNT_ROW, 1.0, value)
    ties[...] = value
    stack = jnp.concatenate(split(value, 2), axis=0)
    hot_slot = one_hot(slot, slots)
    fitting = paired(fit_disp[...], fit_dir[...])

    def bins(first, count):
        lhs = [
            stack * (owner == first + at).astype(F32).astype(BF16) for at in range(count)
        ]
        return dot(jnp.concatenate(lhs, axis=0), hot_slot, ((1,), (1,)))

    def folded(wide_bins, at):
        part = wide_bins[at * 2 * COMPS : (at + 1) * 2 * COMPS]
        return part[0:COMPS] + part[COMPS : 2 * COMPS]

    peers = tx_count * ty_count
    block = math.gcd(peers, 8)

    def fill(first):
        wide_bins = bins(first, block)
        for peer in range(block):
            at = (first + peer) * pb_count + core
            pay[at, 0:COMPS, :] = fitting
            pay[at, COMPS : 2 * COMPS, :] = folded(wide_bins, peer)

    if block == peers:
        fill(0)
    else:
        lax.fori_loop(0, peers // block, lambda at, carry: (fill(at * block), carry)[1], 0)

    for step, edge in ((-1, fields[0:COMPS, :]), (1, fields[(row_total - 1) * COMPS :, :])):
        for side in (-1, 0, 1):
            there, over = place + step, across + side
            valid = (there >= 0) & (there < tx_count * pb_count) & (over >= 0) & (over < ty_count)

            @pl.when(valid)
            def _():
                pay[block_of(there, over, ty_count, pb_count), 0:COMPS, :] = edge

    for side, edge in ((-1, 0), (1, 1)):
        over = across + side
        packed = pack_column(col_out[edge * COMPS : (edge + 1) * COMPS, :], row_total)

        @pl.when((over >= 0) & (over < ty_count))
        def _():
            at = block_of(place, over, ty_count, pb_count)
            for line, row in zip(packed, SPARE_ROWS):
                pay[at, row : row + 1, :] = line


def pack_column(column, width):
    each = column.shape[1] // width
    lines = []
    for first in range(0, 12, each):
        line = None
        for at in range(first, min(first + each, 12)):
            row = at % 6 + at // 6 * 8
            part = column[row : row + 1]
            if at > first:
                part = pltpu.roll(part, (at - first) * width, 1)
            line = part if line is None else line + part
        lines.append(line)
    assert len(lines) <= len(SPARE_ROWS)
    return lines


def unpack_column(block, width):
    shape = (COMPS, block.shape[1])
    each = shape[1] // width
    row = rows_of(shape)
    column = jnp.zeros(shape, F32)
    for at in range(12):
        spare = SPARE_ROWS[at // each]
        line = block[spare : spare + 1]
        if at % each:
            line = pltpu.roll(line, shape[1] - at % each * width, 1)
        column = jnp.where(row == at % 6 + at // 6 * 8, line, column)
    return jnp.where(lanes_of(shape) < width, column, 0.0)


def build_weights(w_in, b_in, b_mid, w_out, w_first, w_last, b_cols):
    hid = w_in.shape[1]
    bias_rows = split(b_in[...], 3)
    row = rows_of((8, hid))
    stacked = jnp.zeros((8, hid), F32)
    mid_stacked = jnp.zeros((8, hid), F32)
    for at, (one, two) in enumerate(zip(bias_rows, split(b_mid[...], 3))):
        stacked = jnp.where(row == at, one.astype(F32), stacked)
        mid_stacked = jnp.where(row == at, two.astype(F32), mid_stacked)
    lhs = jnp.concatenate([w_in[...].astype(F32), jnp.zeros((4, hid), F32), stacked], axis=0).astype(BF16)
    sel_shape = (24, 4 * COMPS)
    source = rows_of(sel_shape)
    target = lanes_of(sel_shape)
    for point in range(4):
        a_base = (point // 2) * COMPS
        c_base = (2 + point % 2) * COMPS
        for side in range(2):
            hit = (source < 6) & (target == a_base + 8 * side + source)
            hit = hit | ((source >= 6) & (source < 12) & (target == c_base + 8 * side + source - 6))
            if side == 0:
                for at, spot in enumerate((6, 7, 14)):
                    hit = hit | ((source == 16 + at) & (target == a_base + spot))
            block = dot(lhs, hit.astype(F32).astype(BF16), ((0,), (0,)))
            start = (2 * point + side) * hid
            w_first[start : start + hid, :] = block.astype(BF16)
    ones = (rows_of((8, 128)) < 3).astype(F32).astype(BF16)
    b_cols[...] = dot(mid_stacked.astype(BF16), ones, ((0,), (0,)))
    last_shape = (128, 12)
    target = rows_of(last_shape)
    source = lanes_of(last_shape)
    hit = target < 0
    for point in range(4):
        a_base = point * 32 + (point // 2) * 8
        c_base = point * 32 + 16 + (point % 2) * 8
        hit = hit | ((source < 6) & (target == a_base + source))
        hit = hit | ((source >= 6) & (target == c_base + source - 6))
    w_last[...] = dot(hit.astype(F32).astype(BF16), w_out[...]).astype(BF16)


def interior(pick, fields, w_in, b_in, w_mid, b_mid, w_out, forces, w_first, w_last, b_cols):
    row_total, cols = fields.shape[0] // COMPS, fields.shape[1]
    half = row_total // 2
    which = lax.axis_index("groups") if pick is None else pick
    first = which * (row_total - 1 - half)
    keep = lanes_of((COMPS, cols)) < cols - 1
    build_weights(w_in, b_in, b_mid, w_out, w_first, w_last, b_cols)
    forces[...] = jnp.zeros(forces.shape, F32)
    lines = []
    for at in range(half + 1):
        base = fields[pl.ds(pl.multiple_of((first + at) * COMPS, COMPS), COMPS), :]
        lines.append((base, pltpu.roll(base, cols - 1, 1)))
    tiles = [
        strain_tile(lines[at][0], lines[at + 1][0], lines[at][1], lines[at + 1][1]) for at in range(half)
    ]
    tiles = [jnp.concatenate(tiles[at : at + 2], axis=1) for at in range(0, half, 2)]
    sums = stress_sums(tiles, w_first, w_mid, b_cols, w_last)
    for tile, (primal, tangent) in enumerate(sums):
        for side in range(2):
            lanes = slice(side * cols, (side + 1) * cols)
            parts = corner_forces(primal[:, lanes], tangent[:, lanes])
            mask = keep if tile + side > 0 else keep & (which == 0)
            base, right, upper, corner = (jnp.where(mask, part, 0.0) for part in parts)
            at = (2 * tile + side) * COMPS
            forces[at : at + COMPS, :] += base + pltpu.roll(upper, 1, 1)
            forces[at + COMPS : at + 2 * COMPS, :] += right + pltpu.roll(corner, 1, 1)


def edges(names, axes, *refs):
    ref = dict(zip(names, refs))
    tx_count, ty_count, pb_count = axes
    fields, ties, partial, got = ref["fields"], ref["ties"], ref["partial"], ref["got"]
    row_total, cols = fields.shape[0] // COMPS, fields.shape[1]
    slots = got.shape[2]
    tie_total = ties.shape[1]
    lane = lanes_of((COMPS, cols))
    core = lax.axis_index("pb")
    across = lax.axis_index("ty")
    place = lax.axis_index("tx") * pb_count + core

    def around(step, side):
        there, over = place + step, across + side
        valid = (there >= 0) & (there < tx_count * pb_count) & (over >= 0) & (over < ty_count)
        at = jnp.where(valid, block_of(there, over, ty_count, pb_count), 0)
        value = got[at, 0:COMPS, :]
        if step == 0:
            value = unpack_column(value, row_total)
        return jnp.where(valid, value, 0.0)

    prev_row = around(-1, 0)
    next_row = around(1, 0)
    next_col = around(0, 1)
    prev_col = around(0, -1)
    next_corner = (around(-1, 1)[:, 0:1], around(1, 1)[:, 0:1])
    prev_corner = (around(-1, -1)[:, cols - 1 : cols], around(1, -1)[:, cols - 1 : cols])

    def column(inner, before, after):
        line = pltpu.roll(inner, 1, 1)
        line = jnp.where(lane == 0, before, line)
        return jnp.where(lane == row_total + 1, after, line)

    own_cols = ref["cols"]
    line_prev = column(prev_col, prev_corner[0], prev_corner[1])
    line_next = column(next_col, next_corner[0], next_corner[1])
    line_first = column(own_cols[0:COMPS, :], prev_row[:, 0:1], next_row[:, 0:1])
    line_final = column(
        own_cols[COMPS : 2 * COMPS, :], prev_row[:, cols - 1 : cols], next_row[:, cols - 1 : cols]
    )

    def shifted(row_value, beyond):
        return jnp.where(lane == cols - 1, beyond, pltpu.roll(row_value, cols - 1, 1))

    first_row = fields[0:COMPS, :]
    last_row = fields[(row_total - 1) * COMPS :, :]
    tile_before = strain_tile(
        prev_row,
        first_row,
        shifted(prev_row, next_corner[0]),
        shifted(first_row, next_col[:, 0:1]),
    )
    tile_after = strain_tile(
        last_row,
        next_row,
        shifted(last_row, next_col[:, row_total - 1 : row_total]),
        shifted(next_row, next_corner[1]),
    )
    half = cols // 2
    low = lane < half
    back = cols - 1

    def two(left, right_line):
        return jnp.where(low, left, pltpu.roll(right_line, half + back, 1))

    left_base = two(line_prev, line_final)
    left_upper = two(line_first, line_next)
    right_base = two(pltpu.roll(line_prev, back, 1), pltpu.roll(line_final, back, 1))
    right_upper = two(pltpu.roll(line_first, back, 1), pltpu.roll(line_next, back, 1))
    tile_side = strain_tile(left_base, right_base, left_upper, right_upper)

    parts = []
    edge_tiles = [jnp.concatenate((tile_before, tile_after), axis=1), tile_side]
    edge_sums = stress_sums(edge_tiles, ref["w_first"], ref["w_mid"], ref["b_mid"], ref["w_last"])
    for primal, tangent in edge_sums:
        for start in range(0, primal.shape[1], cols):
            lanes = slice(start, start + cols)
            parts.append(corner_forces(primal[:, lanes], tangent[:, lanes]))
    part_before, part_after, part_side = parts

    def mask(value, keep):
        return jnp.where(keep, value, 0.0)

    def moved(value, keep):
        return pltpu.roll(mask(value, keep), 1, 1)

    inside = lane < cols - 1
    _, b_right, _, b_corner = part_before
    a_base, _, a_upper, _ = part_after
    s_base, s_right, s_upper, s_corner = part_side
    has_row = place > 0
    has_col = across > 0
    row_first = mask(mask(b_right, lane < cols) + moved(b_corner, inside), has_row)
    row_last = a_base + moved(a_upper, inside)
    first_lane = jnp.where(has_row, 0, 1)
    s_corner = mask(s_corner, (lane >= first_lane) & (lane < row_total))
    s_upper = mask(s_upper, (lane >= 1) & (lane <= row_total))
    col_first = mask(pltpu.roll(s_upper, back, 1) + s_corner, has_col)
    s_base = mask(s_base, (lane >= half) & (lane < half + row_total - 1))
    s_right = mask(s_right, (lane >= half) & (lane < half + row_total - 1))
    col_last = pltpu.roll(s_base + pltpu.roll(s_right, 1, 1), cols - half, 1)

    node = as_line(ref["node"])
    slot = as_line(ref["slot"])
    owner = ref["owner"][...]
    hot_slot = one_hot(slot, slots)
    hot_two = jnp.concatenate([hot_slot] * 2, axis=0)
    fit_value = jnp.zeros((COMPS, tie_total), F32)
    bins = jnp.zeros((COMPS, slots), F32)
    peers = tx_count * ty_count
    block = math.gcd(peers, 8)

    def collect(first, carry):
        fit_value, bins = carry
        parts = [got[(first + peer) * pb_count + core] for peer in range(block)]
        fit_all = jnp.concatenate([part[0:COMPS] for part in parts], axis=0)
        wide = dot(jnp.concatenate(split(fit_all, 2), axis=1), hot_two)
        for peer, part in enumerate(parts):
            fit_value = jnp.where(owner == first + peer, wide[peer * COMPS : (peer + 1) * COMPS], fit_value)
            bins = bins + part[COMPS : 2 * COMPS]
        return fit_value, bins

    if block == peers:
        fit_value, bins = collect(0, (fit_value, bins))
    else:
        fit_value, bins = lax.fori_loop(
            0, peers // block, lambda at, carry: collect(at * block, carry), (fit_value, bins)
        )
    count = bins[COUNT_ROW : COUNT_ROW + 1]
    for out, fit, base in (("fit_res", "fit_disp", 0), ("fit_tan", "fit_dir", 8)):
        ref[out][...] = 2.0 * (count * ref[fit][...] - bins[base : base + 6])

    pulled = 2.0 * (ties[...] - fit_value)
    node_row = lax.shift_right_logical(node, cols.bit_length() - 1)
    node_col = jnp.bitwise_and(node, cols - 1)
    hot_col = one_hot(node_col, cols)
    sides = split(pulled, 2)
    lhs = []
    for row in range(row_total):
        hit = (node_row == row).astype(F32).astype(BF16)
        lhs.append(jnp.concatenate([side * hit for side in sides], axis=1))
    tie_forces = dot(
        jnp.concatenate(lhs, axis=0), jnp.concatenate([hot_col] * 2, axis=1), ((1,), (1,))
    )

    for row in range(row_total):
        total = tie_forces[row * COMPS : (row + 1) * COMPS]
        total = total + jnp.where(lane == 0, col_first[:, row : row + 1], 0.0)
        total = total + jnp.where(lane == cols - 1, col_last[:, row : row + 1], 0.0)
        if row == 0:
            total = total + row_first
        if row == row_total - 1:
            total = total + row_last
        partial[row * COMPS : (row + 1) * COMPS, :] = total


def combine(swapped, partial, own, other, load, res, tan, scratch):
    row_total = partial.shape[0] // COMPS
    held = own.shape[0]
    skip = partial.shape[0] - held
    first, second = own[...], other[...]
    if swapped:
        here = lax.axis_index("groups") == 0
        first, second = jnp.where(here, first, second), jnp.where(here, second, first)
    scratch[...] = partial[...]
    scratch[0:held, :] += first
    scratch[skip : skip + held, :] += second
    for comp in range(6):
        rows = slice(comp * row_total, (comp + 1) * row_total)
        res[rows, :] = scratch[pl.ds(comp, row_total, stride=COMPS), :] - load[rows, :]
        tan[rows, :] = scratch[pl.ds(8 + comp, row_total, stride=COMPS), :]


def per_device(
    displacement,
    direction,
    load,
    w_in,
    b_in,
    w_mid,
    b_mid,
    w_out,
    fitting_disp,
    fitting_dir,
    tie_node,
    tie_owner,
    tie_slot,
):
    tx_count = lax.axis_size("tx")
    ty_count = lax.axis_size("ty")
    pb_count = lax.axis_size("pb")
    peers = tx_count * ty_count
    axes = (tx_count, ty_count, pb_count)
    _, row_total, cols = displacement.shape
    slots = fitting_disp.shape[1]
    tie_total = tie_node.shape[0]
    hid = w_mid.shape[0]
    flat = (6 * row_total, cols)
    disp2 = displacement.reshape(flat)
    dir2 = direction.reshape(flat)
    load2 = load.reshape(flat)
    node2 = tie_node.reshape(tie_total // 128, 128)
    slot2 = tie_slot.reshape(tie_total // 128, 128)
    owner2 = tie_owner.reshape(1, tie_total)

    def shape(*dims, dtype=F32):
        return jax.ShapeDtypeStruct(dims, dtype)

    inputs = (
        disp2,
        dir2,
        fitting_disp,
        fitting_dir,
        node2,
        owner2,
        slot2,
        b_in.reshape(1, hid),
        b_mid.reshape(1, hid),
    )
    outs = pl.pallas_call(
        lambda *refs: prepare(axes, *refs),
        out_shape=[
            pltpu.VMEM((row_total * COMPS, cols), F32),
            pltpu.VMEM((COMPS, tie_total), F32),
            pltpu.VMEM((2 * COMPS, cols), F32),
            shape(peers * pb_count, 2 * COMPS, slots),
        ]
        + [pltpu.VMEM(value.shape, value.dtype) for value in inputs[2:]],
        in_specs=local(len(inputs)),
        out_specs=local(4 + len(inputs[2:])),
        name="prepare",
    )(*inputs)
    fields, ties, cols_out, pay, fit_disp, fit_dir, node, owner, slot, b_first, b_second = outs
    got = lax.all_to_all(pay, ("tx", "ty", "pb"), split_axis=0, concat_axis=0, tiled=True)

    inputs = tuple(on_chip(value) for value in (fields, w_in.T, b_first, w_mid, b_second, w_out))
    groups = lax.axis_size("groups")
    halves = []
    for pick in (None,) if groups == 2 else (0, 1):
        half, w_first, w_last, b_cols = pl.pallas_call(
            lambda *refs: interior(pick, *refs),
            out_shape=[
                pltpu.VMEM(((row_total // 2 + 1) * COMPS, cols), F32),
                pltpu.VMEM((8 * hid, 4 * COMPS), BF16),
                pltpu.VMEM((128, hid), BF16),
                pltpu.VMEM((hid, 128), F32),
            ],
            in_specs=local(len(inputs)),
            out_specs=local(4),
            name="interior",
        )(*inputs)
        halves.append(half)
    if groups == 2:
        halves.append(lax.ppermute(halves[0], "groups", [(0, 1), (1, 0)]))

    named = dict(
        got=got,
        fields=fields,
        ties=ties,
        cols=cols_out,
        w_first=w_first,
        w_mid=w_mid,
        b_mid=b_cols,
        w_last=w_last,
        node=node,
        slot=slot,
        owner=owner,
        fit_disp=fit_disp,
        fit_dir=fit_dir,
    )
    named = {name: on_chip(value) if value.size <= SMALL else value for name, value in named.items()}
    names = list(named)
    partial, fit_res, fit_tan = pl.pallas_call(
        lambda *refs: edges(names + ["partial", "fit_res", "fit_tan"], axes, *refs),
        out_shape=[pltpu.VMEM((row_total * COMPS, cols), F32), shape(6, slots), shape(6, slots)],
        in_specs=local(len(names)),
        out_specs=local(3),
        name="edges",
    )(*named.values())

    inputs = tuple(on_chip(value) for value in (partial, halves[0], halves[1], load2))
    res, tan = pl.pallas_call(
        lambda *refs: combine(groups == 2, *refs),
        out_shape=[shape(*flat), shape(*flat)],
        in_specs=local(len(inputs)),
        out_specs=local(2),
        scratch_shapes=[pltpu.VMEM((row_total * COMPS, cols), F32)],
        name="combine",
    )(*inputs)
    cube = displacement.shape
    return (res.reshape(cube), tan.reshape(cube), fit_res, fit_tan)


def solution(mesh):
    in_specs = (
        P(None, ("tx", "pb"), "ty"),
        P(None, ("tx", "pb"), "ty"),
        P(None, ("tx", "pb"), "ty"),
        P(),
        P(),
        P(),
        P(),
        P(),
        P(None, ("groups", "tx", "ty", "pb")),
        P(None, ("groups", "tx", "ty", "pb")),
        P(("groups", "tx", "ty", "pb")),
        P(("groups", "tx", "ty", "pb"), None),
        P(("groups", "tx", "ty", "pb")),
    )
    out_specs = (
        P(None, ("groups", "tx", "pb"), "ty"),
        P(None, ("groups", "tx", "pb"), "ty"),
        P(None, ("groups", "tx", "ty", "pb")),
        P(None, ("groups", "tx", "ty", "pb")),
    )
    return jax.shard_map(
        per_device, mesh=mesh, in_specs=in_specs, out_specs=out_specs, check_vma=False
    )
```

```python
import math

import jax
import jax.numpy as jnp
from jax import lax
from jax.experimental import pallas as pl
from jax.experimental.pallas import tpu as pltpu
from jax.sharding import PartitionSpec as P

F32 = jnp.float32
BF16 = jnp.bfloat16
GAUSS = (0.5 - 0.5 / math.sqrt(3.0), 0.5 + 0.5 / math.sqrt(3.0))
COMPS = 16
COUNT_ROW = 6
SPARE_ROWS = (6, 7, 14)
SMALL = 1 << 18


def local(count):
    return [pl.BlockSpec(memory_space=pltpu.VMEM)] * count


def on_chip(value):
    return pltpu.with_memory_space_constraint(value, pltpu.VMEM)


def dot(a, b, dims=((1,), (0,))):
    return lax.dot_general(a, b, (dims, ((), ())), preferred_element_type=F32)


def split(value, terms):
    parts = []
    for _ in range(terms):
        part = value.astype(BF16)
        parts.append(part)
        value = value - part.astype(F32)
    return parts


def rows_of(value):
    return lax.broadcasted_iota(jnp.int32, value, 0)


def lanes_of(value):
    return lax.broadcasted_iota(jnp.int32, value, 1)


def one_hot(index, size):
    shape = (size, index.shape[1])
    return (rows_of(shape) == index).astype(F32).astype(BF16)


def as_line(ref):
    return jnp.concatenate([ref[row : row + 1, :] for row in range(ref.shape[0])], axis=1)


def paired(top, bottom):
    spare = jnp.zeros((2, top.shape[1]), F32)
    return jnp.concatenate([top, spare, bottom, spare], axis=0)


def strain_tile(f00, f10, f01, f11):
    along_low = f10 - f00
    along_high = f11 - f01
    across_low = f01 - f00
    across_high = f11 - f10
    shape = f00.shape
    row = rows_of(shape)
    ones = ((row == 6) | (row == 7) | (row == 14)).astype(F32)
    groups = []
    for frac in GAUSS:
        groups.append((((1.0 - frac) * along_low + frac * along_high) + ones).astype(BF16))
    for frac in GAUSS:
        groups.append(((1.0 - frac) * across_low + frac * across_high).astype(BF16))
    return jnp.concatenate(groups, axis=0)


def stress_sums(strains, w_first, w_mid, b_mid, w_last):
    hid = w_mid.shape[0]
    tasks = [(tile, point) for tile in range(len(strains)) for point in range(4)]
    totals = [[None, None] for _ in strains]

    def layer_one(task):
        tile, point = task
        start = point * 2 * hid
        return (
            dot(w_first[start : start + hid, :], strains[tile]),
            dot(w_first[start + hid : start + 2 * hid, :], strains[tile]),
        )

    def activate(value, slope):
        act = jnp.tanh(value)
        return (act.astype(BF16), ((1.0 - act * act) * slope).astype(BF16))

    def layer_two(hidden):
        bias = b_mid[...]
        value = dot(w_mid[...], hidden[0])
        slope = dot(w_mid[...], hidden[1])
        bias = jnp.concatenate([bias] * (value.shape[1] // bias.shape[1]), axis=1)
        return (value + bias, slope)

    def layer_three(task, hidden):
        tile, point = task
        last = w_last[point * 32 : (point + 1) * 32, :]
        for side in range(2):
            part = dot(last, hidden[side])
            old = totals[tile][side]
            totals[tile][side] = part if old is None else old + part

    ones = {0: layer_one(tasks[0])}
    twos = {}
    for at in range(len(tasks) + 1):
        if at + 1 < len(tasks):
            ones[at + 1] = layer_one(tasks[at + 1])
        if at < len(tasks):
            hidden = activate(*ones.pop(at))
            twos[at] = layer_two(hidden)
        if at >= 1:
            layer_three(tasks[at - 1], activate(*twos.pop(at - 1)))
    return totals


def corner_forces(primal, tangent):
    def both(group):
        return jnp.concatenate([primal[group * 8 : group * 8 + 8], tangent[group * 8 : group * 8 + 8]], axis=0)

    along = (both(0), both(1))
    across = (both(2), both(3))

    def mix(pair, weights):
        return (0.25 * weights[0]) * pair[0] + (0.25 * weights[1]) * pair[1]

    rest = (1.0 - GAUSS[0], 1.0 - GAUSS[1])
    along_rest = mix(along, rest)
    along_frac = mix(along, GAUSS)
    across_rest = mix(across, rest)
    across_frac = mix(across, GAUSS)
    return (
        -along_rest - across_rest,
        along_rest - across_frac,
        across_rest - along_frac,
        along_frac + across_frac,
    )


def gather_nodes(count, disp, dirn, *refs):
    fields, rows = refs[count : count + 2]
    for source, target in zip(refs[:count], refs[count + 2 :]):
        target[...] = source[...]
    row_total = fields.shape[0] // COMPS
    fields[...] = jnp.zeros(fields.shape, F32)
    for comp in range(6):
        part = slice(comp * row_total, (comp + 1) * row_total)
        fields[pl.ds(comp, row_total, stride=COMPS), :] = disp[part, :]
        fields[pl.ds(8 + comp, row_total, stride=COMPS), :] = dirn[part, :]
    rows[0:COMPS, :] = fields[0:COMPS, :]
    rows[COMPS : 2 * COMPS, :] = fields[(row_total - 1) * COMPS :, :]


def sum_ties(peers, *refs):
    (fields, fit_disp, fit_dir, node_ref, owner_ref, slot_ref, ties, col_out, pay) = refs
    row_total = fields.shape[0] // COMPS
    cols = fields.shape[1]
    slots = fit_disp.shape[1]
    tie_total = ties.shape[1]

    lane = lanes_of((COMPS, cols))
    for side, column in enumerate((0, cols - 1)):
        gathered = jnp.zeros((COMPS, cols), F32)
        for row in range(row_total):
            value = fields[row * COMPS : (row + 1) * COMPS, column : column + 1]
            gathered = jnp.where(lane == row, value, gathered)
        col_out[side * COMPS : (side + 1) * COMPS, :] = gathered

    node = as_line(node_ref)
    slot = as_line(slot_ref)
    owner = owner_ref[...]
    node_row = lax.shift_right_logical(node, cols.bit_length() - 1)
    node_col = jnp.bitwise_and(node, cols - 1)
    hot_col = one_hot(node_col, cols)
    wide = dot(
        jnp.concatenate(split(fields[...], 2), axis=1), jnp.concatenate([hot_col] * 2, axis=0)
    )
    value = jnp.zeros((COMPS, tie_total), F32)
    for row in range(row_total):
        value = jnp.where(node_row == row, wide[row * COMPS : (row + 1) * COMPS], value)
    value = jnp.where(rows_of(value.shape) == COUNT_ROW, 1.0, value)
    ties[...] = value
    stack = jnp.concatenate(split(value, 2), axis=0)
    hot_slot = one_hot(slot, slots)
    fitting = paired(fit_disp[...], fit_dir[...])

    def bins(first, count):
        lhs = [
            stack * (owner == first + at).astype(F32).astype(BF16) for at in range(count)
        ]
        return dot(jnp.concatenate(lhs, axis=0), hot_slot, ((1,), (1,)))

    def folded(wide_bins, at):
        part = wide_bins[at * 2 * COMPS : (at + 1) * 2 * COMPS]
        return part[0:COMPS] + part[COMPS : 2 * COMPS]

    block = math.gcd(peers, 8)

    def fill(first):
        wide_bins = bins(first, block)
        for peer in range(block):
            pay[first + peer, 0:COMPS, :] = fitting
            pay[first + peer, COMPS : 2 * COMPS, :] = folded(wide_bins, peer)

    if block == peers:
        fill(0)
    else:
        lax.fori_loop(0, peers // block, lambda at, carry: (fill(at * block), carry)[1], 0)


def mate_rows(mate):
    upper = lax.axis_index("pb") == 0
    first, last = mate[0:COMPS, :], mate[COMPS : 2 * COMPS, :]
    return jnp.where(upper, first, last), jnp.where(upper, last, first)


def fill_blocks(axes, row_total, sums, columns, mate, pay):
    tx_count, ty_count = axes
    along, across = lax.axis_index("tx"), lax.axis_index("ty")
    near, far = mate_rows(mate)
    pay[:, 0 : 2 * COMPS, :] = sums[...]
    ahead = along + 1 - 2 * lax.axis_index("pb")
    for side in (-1, 0, 1):
        over = across + side
        inside = (over >= 0) & (over < ty_count)

        @pl.when(inside & (ahead >= 0) & (ahead < tx_count))
        def _():
            pay[ahead * ty_count + over, 2 * COMPS : 3 * COMPS, :] = far

        if side == 0:
            continue
        edge = 0 if side < 0 else 1
        packed = pack_column(columns[edge * COMPS : (edge + 1) * COMPS, :], row_total)

        @pl.when(inside)
        def _():
            at = along * ty_count + over
            pay[at, 2 * COMPS : 3 * COMPS, :] = near
            for line, row in zip(packed, SPARE_ROWS):
                pay[at, row : row + 1, :] = line


def pack_column(column, width):
    each = column.shape[1] // width
    lines = []
    for first in range(0, 12, each):
        line = None
        for at in range(first, min(first + each, 12)):
            row = at % 6 + at // 6 * 8
            part = column[row : row + 1]
            if at > first:
                part = pltpu.roll(part, (at - first) * width, 1)
            line = part if line is None else line + part
        lines.append(line)
    assert len(lines) <= len(SPARE_ROWS)
    return lines


def unpack_column(block, width):
    shape = (COMPS, block.shape[1])
    each = shape[1] // width
    row = rows_of(shape)
    column = jnp.zeros(shape, F32)
    for at in range(12):
        spare = SPARE_ROWS[at // each]
        line = block[spare : spare + 1]
        if at % each:
            line = pltpu.roll(line, shape[1] - at % each * width, 1)
        column = jnp.where(row == at % 6 + at // 6 * 8, line, column)
    return jnp.where(lanes_of(shape) < width, column, 0.0)


def build_weights(w_in, b_in, b_mid, w_out, w_first, w_last, b_cols):
    hid = w_in.shape[1]
    bias_rows = split(b_in[...], 3)
    row = rows_of((8, hid))
    stacked = jnp.zeros((8, hid), F32)
    mid_stacked = jnp.zeros((8, hid), F32)
    for at, (one, two) in enumerate(zip(bias_rows, split(b_mid[...], 3))):
        stacked = jnp.where(row == at, one.astype(F32), stacked)
        mid_stacked = jnp.where(row == at, two.astype(F32), mid_stacked)
    lhs = jnp.concatenate([w_in[...].astype(F32), jnp.zeros((4, hid), F32), stacked], axis=0).astype(BF16)
    sel_shape = (24, 4 * COMPS)
    source = rows_of(sel_shape)
    target = lanes_of(sel_shape)
    for point in range(4):
        a_base = (point // 2) * COMPS
        c_base = (2 + point % 2) * COMPS
        for side in range(2):
            hit = (source < 6) & (target == a_base + 8 * side + source)
            hit = hit | ((source >= 6) & (source < 12) & (target == c_base + 8 * side + source - 6))
            if side == 0:
                for at, spot in enumerate((6, 7, 14)):
                    hit = hit | ((source == 16 + at) & (target == a_base + spot))
            block = dot(lhs, hit.astype(F32).astype(BF16), ((0,), (0,)))
            start = (2 * point + side) * hid
            w_first[start : start + hid, :] = block.astype(BF16)
    ones = (rows_of((8, 128)) < 3).astype(F32).astype(BF16)
    b_cols[...] = dot(mid_stacked.astype(BF16), ones, ((0,), (0,)))
    last_shape = (128, 12)
    target = rows_of(last_shape)
    source = lanes_of(last_shape)
    hit = target < 0
    for point in range(4):
        a_base = point * 32 + (point // 2) * 8
        c_base = point * 32 + 16 + (point % 2) * 8
        hit = hit | ((source < 6) & (target == a_base + source))
        hit = hit | ((source >= 6) & (target == c_base + source - 6))
    w_last[...] = dot(hit.astype(F32).astype(BF16), w_out[...]).astype(BF16)


def interior(pick, fields, w_in, b_in, w_mid, b_mid, w_out, sent, w_first, w_last, b_cols, forces):
    row_total, cols = fields.shape[0] // COMPS, fields.shape[1]
    half = row_total // 2
    which = lax.axis_index("groups") if pick is None else pick
    first = which * (row_total - 1 - half)
    keep = lanes_of((COMPS, cols)) < cols - 1
    build_weights(w_in, b_in, b_mid, w_out, w_first, w_last, b_cols)
    forces[...] = jnp.zeros(forces.shape, F32)
    lines = []
    for at in range(half + 1):
        base = fields[pl.ds(pl.multiple_of((first + at) * COMPS, COMPS), COMPS), :]
        lines.append((base, pltpu.roll(base, cols - 1, 1)))
    tiles = [
        strain_tile(lines[at][0], lines[at + 1][0], lines[at][1], lines[at + 1][1]) for at in range(half)
    ]
    tiles = [jnp.concatenate(tiles[at : at + 2], axis=1) for at in range(0, half, 2)]
    sums = stress_sums(tiles, w_first, w_mid, b_cols, w_last)
    for tile, (primal, tangent) in enumerate(sums):
        for side in range(2):
            lanes = slice(side * cols, (side + 1) * cols)
            parts = corner_forces(primal[:, lanes], tangent[:, lanes])
            mask = keep if tile + side > 0 else keep & (which == 0)
            base, right, upper, corner = (jnp.where(mask, part, 0.0) for part in parts)
            at = (2 * tile + side) * COMPS
            forces[at : at + COMPS, :] += base + pltpu.roll(upper, 1, 1)
            forces[at + COMPS : at + 2 * COMPS, :] += right + pltpu.roll(corner, 1, 1)
    held = half + 1
    for comp in range(12):
        sent[comp * held : (comp + 1) * held, :] = forces[pl.ds(comp % 6 + comp // 6 * 8, held, stride=COMPS), :]


def edges(names, axes, *refs):
    ref = dict(zip(names, refs))
    tx_count, ty_count, pb_count = axes
    fields, ties, partial, got = ref["fields"], ref["ties"], ref["partial"], ref["got"]
    row_total, cols = fields.shape[0] // COMPS, fields.shape[1]
    slots = got.shape[2]
    tie_total = ties.shape[1]
    lane = lanes_of((COMPS, cols))
    core = lax.axis_index("pb")
    across = lax.axis_index("ty")
    along = lax.axis_index("tx")
    place = along * pb_count + core

    def around(step, side, packed=False):
        there, over = along + step, across + side
        valid = (there >= 0) & (there < tx_count) & (over >= 0) & (over < ty_count)
        block = got.at[jnp.where(valid, there * ty_count + over, 0)]
        if packed:
            value = unpack_column(block[0:COMPS, :], row_total)
        else:
            value = block[2 * COMPS : 3 * COMPS, :]
        return jnp.where(valid, value, 0.0)

    upper = core == 0
    behind = 2 * core - 1
    near, _ = mate_rows(ref["mate"])
    rows_near = (around(0, -1), near, around(0, 1))
    rows_far = tuple(around(behind, side) for side in (-1, 0, 1))
    next_rows = [jnp.where(upper, one, two) for one, two in zip(rows_near, rows_far)]
    prev_rows = [jnp.where(upper, two, one) for one, two in zip(rows_near, rows_far)]
    prev_row, next_row = prev_rows[1], next_rows[1]
    next_col = around(0, 1, True)
    prev_col = around(0, -1, True)
    next_corner = (prev_rows[2][:, 0:1], next_rows[2][:, 0:1])
    prev_corner = (prev_rows[0][:, cols - 1 : cols], next_rows[0][:, cols - 1 : cols])

    def column(inner, before, after):
        line = pltpu.roll(inner, 1, 1)
        line = jnp.where(lane == 0, before, line)
        return jnp.where(lane == row_total + 1, after, line)

    own_cols = ref["cols"]
    line_prev = column(prev_col, prev_corner[0], prev_corner[1])
    line_next = column(next_col, next_corner[0], next_corner[1])
    line_first = column(own_cols[0:COMPS, :], prev_row[:, 0:1], next_row[:, 0:1])
    line_final = column(
        own_cols[COMPS : 2 * COMPS, :], prev_row[:, cols - 1 : cols], next_row[:, cols - 1 : cols]
    )

    def shifted(row_value, beyond):
        return jnp.where(lane == cols - 1, beyond, pltpu.roll(row_value, cols - 1, 1))

    first_row = fields[0:COMPS, :]
    last_row = fields[(row_total - 1) * COMPS :, :]
    tile_before = strain_tile(
        prev_row,
        first_row,
        shifted(prev_row, next_corner[0]),
        shifted(first_row, next_col[:, 0:1]),
    )
    tile_after = strain_tile(
        last_row,
        next_row,
        shifted(last_row, next_col[:, row_total - 1 : row_total]),
        shifted(next_row, next_corner[1]),
    )
    half = cols // 2
    low = lane < half
    back = cols - 1

    def two(left, right_line):
        return jnp.where(low, left, pltpu.roll(right_line, half + back, 1))

    left_base = two(line_prev, line_final)
    left_upper = two(line_first, line_next)
    right_base = two(pltpu.roll(line_prev, back, 1), pltpu.roll(line_final, back, 1))
    right_upper = two(pltpu.roll(line_first, back, 1), pltpu.roll(line_next, back, 1))
    tile_side = strain_tile(left_base, right_base, left_upper, right_upper)

    parts = []
    edge_tiles = [jnp.concatenate((tile_before, tile_after), axis=1), tile_side]
    edge_sums = stress_sums(edge_tiles, ref["w_first"], ref["w_mid"], ref["b_mid"], ref["w_last"])
    for primal, tangent in edge_sums:
        for start in range(0, primal.shape[1], cols):
            lanes = slice(start, start + cols)
            parts.append(corner_forces(primal[:, lanes], tangent[:, lanes]))
    part_before, part_after, part_side = parts

    def mask(value, keep):
        return jnp.where(keep, value, 0.0)

    def moved(value, keep):
        return pltpu.roll(mask(value, keep), 1, 1)

    inside = lane < cols - 1
    _, b_right, _, b_corner = part_before
    a_base, _, a_upper, _ = part_after
    s_base, s_right, s_upper, s_corner = part_side
    has_row = place > 0
    has_col = across > 0
    row_first = mask(mask(b_right, lane < cols) + moved(b_corner, inside), has_row)
    row_last = a_base + moved(a_upper, inside)
    first_lane = jnp.where(has_row, 0, 1)
    s_corner = mask(s_corner, (lane >= first_lane) & (lane < row_total))
    s_upper = mask(s_upper, (lane >= 1) & (lane <= row_total))
    col_first = mask(pltpu.roll(s_upper, back, 1) + s_corner, has_col)
    s_base = mask(s_base, (lane >= half) & (lane < half + row_total - 1))
    s_right = mask(s_right, (lane >= half) & (lane < half + row_total - 1))
    col_last = pltpu.roll(s_base + pltpu.roll(s_right, 1, 1), cols - half, 1)

    node = as_line(ref["node"])
    slot = as_line(ref["slot"])
    owner = ref["owner"][...]
    hot_slot = one_hot(slot, slots)
    hot_two = jnp.concatenate([hot_slot] * 2, axis=0)
    fit_value = jnp.zeros((COMPS, tie_total), F32)
    bins = jnp.zeros((COMPS, slots), F32)
    peers = tx_count * ty_count
    block = math.gcd(peers, 8)

    def collect(first, carry):
        fit_value, bins = carry
        parts = [got[first + peer] for peer in range(block)]
        fit_all = jnp.concatenate([part[0:COMPS] for part in parts], axis=0)
        wide = dot(jnp.concatenate(split(fit_all, 2), axis=1), hot_two)
        for peer, part in enumerate(parts):
            fit_value = jnp.where(owner == first + peer, wide[peer * COMPS : (peer + 1) * COMPS], fit_value)
            bins = bins + part[COMPS : 2 * COMPS]
        return fit_value, bins

    if block == peers:
        fit_value, bins = collect(0, (fit_value, bins))
    else:
        fit_value, bins = lax.fori_loop(
            0, peers // block, lambda at, carry: collect(at * block, carry), (fit_value, bins)
        )
    count = bins[COUNT_ROW : COUNT_ROW + 1]
    for out, fit, base in (("fit_res", "fit_disp", 0), ("fit_tan", "fit_dir", 8)):
        ref[out][...] = 2.0 * (count * ref[fit][...] - bins[base : base + 6])

    pulled = 2.0 * (ties[...] - fit_value)
    node_row = lax.shift_right_logical(node, cols.bit_length() - 1)
    node_col = jnp.bitwise_and(node, cols - 1)
    hot_col = one_hot(node_col, cols)
    sides = split(pulled, 2)
    lhs = []
    for row in range(row_total):
        hit = (node_row == row).astype(F32).astype(BF16)
        lhs.append(jnp.concatenate([side * hit for side in sides], axis=1))
    tie_forces = dot(
        jnp.concatenate(lhs, axis=0), jnp.concatenate([hot_col] * 2, axis=1), ((1,), (1,))
    )

    for row in range(row_total):
        total = tie_forces[row * COMPS : (row + 1) * COMPS]
        total = total + jnp.where(lane == 0, col_first[:, row : row + 1], 0.0)
        total = total + jnp.where(lane == cols - 1, col_last[:, row : row + 1], 0.0)
        if row == 0:
            total = total + row_first
        if row == row_total - 1:
            total = total + row_last
        partial[row * COMPS : (row + 1) * COMPS, :] = total


def combine(swapped, partial, own, other, load, res, tan):
    row_total = partial.shape[0] // COMPS
    held = own.shape[0] // 12
    skip = row_total - held
    first, second = own[...], other[...]
    if swapped:
        here = lax.axis_index("groups") == 0
        first, second = jnp.where(here, first, second), jnp.where(here, second, first)
    for comp in range(12):
        target = res if comp < 6 else tan
        start = comp % 6 * row_total
        value = partial[pl.ds(comp % 6 + comp // 6 * 8, row_total, stride=COMPS), :]
        if comp < 6:
            value = value - load[start : start + row_total, :]
        rows = slice(comp * held, (comp + 1) * held)
        target[start : start + row_total, :] = value
        target[start : start + held, :] += first[rows]
        target[start + skip : start + row_total, :] += second[rows]


def per_device(
    displacement,
    direction,
    load,
    w_in,
    b_in,
    w_mid,
    b_mid,
    w_out,
    fitting_disp,
    fitting_dir,
    tie_node,
    tie_owner,
    tie_slot,
):
    tx_count = lax.axis_size("tx")
    ty_count = lax.axis_size("ty")
    pb_count = lax.axis_size("pb")
    peers = tx_count * ty_count
    axes = (tx_count, ty_count, pb_count)
    _, row_total, cols = displacement.shape
    slots = fitting_disp.shape[1]
    tie_total = tie_node.shape[0]
    hid = w_mid.shape[0]
    flat = (6 * row_total, cols)
    disp2 = displacement.reshape(flat)
    dir2 = direction.reshape(flat)
    load2 = load.reshape(flat)
    node2 = tie_node.reshape(tie_total // 128, 128)
    slot2 = tie_slot.reshape(tie_total // 128, 128)
    owner2 = tie_owner.reshape(1, tie_total)

    def shape(*dims, dtype=F32):
        return jax.ShapeDtypeStruct(dims, dtype)

    assert pb_count == 2 and slots == cols
    smalls = (
        fitting_disp,
        fitting_dir,
        node2,
        owner2,
        slot2,
        b_in.reshape(1, hid),
        b_mid.reshape(1, hid),
    )
    outs = pl.pallas_call(
        lambda *refs: gather_nodes(len(smalls), *refs),
        out_shape=[pltpu.VMEM((row_total * COMPS, cols), F32), pltpu.VMEM((2 * COMPS, cols), F32)]
        + [pltpu.VMEM(value.shape, value.dtype) for value in smalls],
        in_specs=local(2 + len(smalls)),
        out_specs=local(2 + len(smalls)),
        name="gather_nodes",
    )(disp2, dir2, *smalls)
    fields, rows, fit_disp, fit_dir, node, owner, slot, b_first, b_second = outs
    mate = lax.ppermute(rows, "pb", [(0, 1), (1, 0)])

    inputs = tuple(on_chip(value) for value in (fields, fit_disp, fit_dir, node, owner, slot))
    small = peers * 2 * COMPS * slots <= SMALL
    ties, cols_out, sums = pl.pallas_call(
        lambda *refs: sum_ties(peers, *refs),
        out_shape=[
            pltpu.VMEM((COMPS, tie_total), F32),
            pltpu.VMEM((2 * COMPS, cols), F32),
            (pltpu.VMEM if small else jax.ShapeDtypeStruct)((peers, 2 * COMPS, slots), F32),
        ],
        in_specs=local(len(inputs)),
        out_specs=local(3),
        name="sum_ties",
    )(*inputs)
    inputs = [on_chip(value) if value.size <= SMALL else value for value in (sums, cols_out, mate)]
    pay = pl.pallas_call(
        lambda *refs: fill_blocks((tx_count, ty_count), row_total, *refs),
        out_shape=shape(peers, 3 * COMPS, slots),
        in_specs=local(len(inputs)),
        out_specs=local(1)[0],
        name="fill_blocks",
    )(*inputs)
    got = lax.all_to_all(pay, ("tx", "ty"), split_axis=0, concat_axis=0, tiled=True)

    inputs = tuple(on_chip(value) for value in (fields, w_in.T, b_first, w_mid, b_second, w_out))
    groups = lax.axis_size("groups")
    halves = []
    for pick in (None,) if groups == 2 else (0, 1):
        half, w_first, w_last, b_cols = pl.pallas_call(
            lambda *refs: interior(pick, *refs),
            out_shape=[
                pltpu.VMEM(((row_total // 2 + 1) * 12, cols), F32),
                pltpu.VMEM((8 * hid, 4 * COMPS), BF16),
                pltpu.VMEM((128, hid), BF16),
                pltpu.VMEM((hid, 128), F32),
            ],
            in_specs=local(len(inputs)),
            out_specs=local(4),
            scratch_shapes=[pltpu.VMEM(((row_total // 2 + 1) * COMPS, cols), F32)],
            name="interior",
        )(*inputs)
        halves.append(half)
    if groups == 2:
        halves.append(lax.ppermute(halves[0], "groups", [(0, 1), (1, 0)]))

    named = dict(
        got=got,
        mate=mate,
        fields=fields,
        ties=ties,
        cols=cols_out,
        w_first=w_first,
        w_mid=w_mid,
        b_mid=b_cols,
        w_last=w_last,
        node=node,
        slot=slot,
        owner=owner,
        fit_disp=fit_disp,
        fit_dir=fit_dir,
    )
    named = {name: on_chip(value) if value.size <= SMALL else value for name, value in named.items()}
    names = list(named)
    partial, fit_res, fit_tan = pl.pallas_call(
        lambda *refs: edges(names + ["partial", "fit_res", "fit_tan"], axes, *refs),
        out_shape=[pltpu.VMEM((row_total * COMPS, cols), F32), shape(6, slots), shape(6, slots)],
        in_specs=local(len(names)),
        out_specs=local(3),
        name="edges",
    )(*named.values())

    inputs = tuple(on_chip(value) for value in (partial, halves[0], halves[1], load2))
    res, tan = pl.pallas_call(
        lambda *refs: combine(groups == 2, *refs),
        out_shape=[shape(*flat), shape(*flat)],
        in_specs=local(len(inputs)),
        out_specs=local(2),
        name="combine",
    )(*inputs)
    cube = displacement.shape
    return (res.reshape(cube), tan.reshape(cube), fit_res, fit_tan)


def solution(mesh):
    in_specs = (
        P(None, ("tx", "pb"), "ty"),
        P(None, ("tx", "pb"), "ty"),
        P(None, ("tx", "pb"), "ty"),
        P(),
        P(),
        P(),
        P(),
        P(),
        P(None, ("groups", "tx", "ty", "pb")),
        P(None, ("groups", "tx", "ty", "pb")),
        P(("groups", "tx", "ty", "pb")),
        P(("groups", "tx", "ty", "pb"), None),
        P(("groups", "tx", "ty", "pb")),
    )
    out_specs = (
        P(None, ("groups", "tx", "pb"), "ty"),
        P(None, ("groups", "tx", "pb"), "ty"),
        P(None, ("groups", "tx", "ty", "pb")),
        P(None, ("groups", "tx", "ty", "pb")),
    )
    return jax.shard_map(
        per_device, mesh=mesh, in_specs=in_specs, out_specs=out_specs, check_vma=False
    )
```

```python
import math

import jax
import jax.numpy as jnp
from jax import lax
from jax.experimental import pallas as pl
from jax.experimental.pallas import tpu as pltpu
from jax.sharding import PartitionSpec as P

F32 = jnp.float32
BF16 = jnp.bfloat16
GAUSS = (0.5 - 0.5 / math.sqrt(3.0), 0.5 + 0.5 / math.sqrt(3.0))
COMPS = 16
COUNT_ROW = 6
SPARE_ROWS = (6, 7, 14)
SMALL = 1 << 18


def local(count):
    return [pl.BlockSpec(memory_space=pltpu.VMEM)] * count


def on_chip(value):
    return pltpu.with_memory_space_constraint(value, pltpu.VMEM)


def dot(a, b, dims=((1,), (0,))):
    return lax.dot_general(a, b, (dims, ((), ())), preferred_element_type=F32)


def split(value, terms):
    parts = []
    for _ in range(terms):
        part = value.astype(BF16)
        parts.append(part)
        value = value - part.astype(F32)
    return parts


def rows_of(value):
    return lax.broadcasted_iota(jnp.int32, value, 0)


def lanes_of(value):
    return lax.broadcasted_iota(jnp.int32, value, 1)


def one_hot(index, size):
    shape = (size, index.shape[1])
    return (rows_of(shape) == index).astype(F32).astype(BF16)


def as_line(ref):
    return jnp.concatenate([ref[row : row + 1, :] for row in range(ref.shape[0])], axis=1)


def paired(top, bottom):
    spare = jnp.zeros((2, top.shape[1]), F32)
    return jnp.concatenate([top, spare, bottom, spare], axis=0)


def strain_tile(f00, f10, f01, f11):
    along_low = f10 - f00
    along_high = f11 - f01
    across_low = f01 - f00
    across_high = f11 - f10
    shape = f00.shape
    row = rows_of(shape)
    ones = ((row == 6) | (row == 7) | (row == 14)).astype(F32)
    groups = []
    for frac in GAUSS:
        groups.append((((1.0 - frac) * along_low + frac * along_high) + ones).astype(BF16))
    for frac in GAUSS:
        groups.append(((1.0 - frac) * across_low + frac * across_high).astype(BF16))
    return jnp.concatenate(groups, axis=0)


def stress_sums(strains, w_first, w_mid, b_mid, w_last):
    hid = w_mid.shape[0]
    tasks = [(tile, point) for tile in range(len(strains)) for point in range(4)]
    totals = [[None, None] for _ in strains]

    def layer_one(task):
        tile, point = task
        start = point * 2 * hid
        return (
            dot(w_first[start : start + hid, :], strains[tile]),
            dot(w_first[start + hid : start + 2 * hid, :], strains[tile]),
        )

    def activate(value, slope):
        act = jnp.tanh(value)
        return (act.astype(BF16), ((1.0 - act * act) * slope).astype(BF16))

    def layer_two(hidden):
        bias = b_mid[...]
        value = dot(w_mid[...], hidden[0])
        slope = dot(w_mid[...], hidden[1])
        bias = jnp.concatenate([bias] * (value.shape[1] // bias.shape[1]), axis=1)
        return (value + bias, slope)

    def layer_three(task, hidden):
        tile, point = task
        last = w_last[point * 32 : (point + 1) * 32, :]
        for side in range(2):
            part = dot(last, hidden[side])
            old = totals[tile][side]
            totals[tile][side] = part if old is None else old + part

    ones = {0: layer_one(tasks[0])}
    twos = {}
    for at in range(len(tasks) + 1):
        if at + 1 < len(tasks):
            ones[at + 1] = layer_one(tasks[at + 1])
        if at < len(tasks):
            hidden = activate(*ones.pop(at))
            twos[at] = layer_two(hidden)
        if at >= 1:
            layer_three(tasks[at - 1], activate(*twos.pop(at - 1)))
    return totals


def corner_forces(primal, tangent):
    def both(group):
        return jnp.concatenate([primal[group * 8 : group * 8 + 8], tangent[group * 8 : group * 8 + 8]], axis=0)

    along = (both(0), both(1))
    across = (both(2), both(3))

    def mix(pair, weights):
        return (0.25 * weights[0]) * pair[0] + (0.25 * weights[1]) * pair[1]

    rest = (1.0 - GAUSS[0], 1.0 - GAUSS[1])
    along_rest = mix(along, rest)
    along_frac = mix(along, GAUSS)
    across_rest = mix(across, rest)
    across_frac = mix(across, GAUSS)
    return (
        -along_rest - across_rest,
        along_rest - across_frac,
        across_rest - along_frac,
        along_frac + across_frac,
    )


def gather_nodes(count, disp, dirn, *refs):
    fields, rows = refs[count : count + 2]
    for source, target in zip(refs[:count], refs[count + 2 :]):
        target[...] = source[...]
    row_total = fields.shape[0] // COMPS
    fields[...] = jnp.zeros(fields.shape, F32)
    for comp in range(6):
        part = slice(comp * row_total, (comp + 1) * row_total)
        fields[pl.ds(comp, row_total, stride=COMPS), :] = disp[part, :]
        fields[pl.ds(8 + comp, row_total, stride=COMPS), :] = dirn[part, :]
    rows[0:COMPS, :] = fields[0:COMPS, :]
    rows[COMPS : 2 * COMPS, :] = fields[(row_total - 1) * COMPS :, :]


def sum_ties(peers, *refs):
    (fields, fit_disp, fit_dir, node_ref, owner_ref, slot_ref, ties, col_out, pay) = refs
    row_total = fields.shape[0] // COMPS
    cols = fields.shape[1]
    slots = fit_disp.shape[1]
    tie_total = ties.shape[1]

    lane = lanes_of((COMPS, cols))
    for side, column in enumerate((0, cols - 1)):
        gathered = jnp.zeros((COMPS, cols), F32)
        for row in range(row_total):
            value = fields[row * COMPS : (row + 1) * COMPS, column : column + 1]
            gathered = jnp.where(lane == row, value, gathered)
        col_out[side * COMPS : (side + 1) * COMPS, :] = gathered

    node = as_line(node_ref)
    slot = as_line(slot_ref)
    owner = owner_ref[...]
    node_row = lax.shift_right_logical(node, cols.bit_length() - 1)
    node_col = jnp.bitwise_and(node, cols - 1)
    hot_col = one_hot(node_col, cols)
    wide = dot(
        jnp.concatenate(split(fields[...], 2), axis=1), jnp.concatenate([hot_col] * 2, axis=0)
    )
    value = jnp.zeros((COMPS, tie_total), F32)
    for row in range(row_total):
        value = jnp.where(node_row == row, wide[row * COMPS : (row + 1) * COMPS], value)
    value = jnp.where(rows_of(value.shape) == COUNT_ROW, 1.0, value)
    ties[...] = value
    stack = jnp.concatenate(split(value, 2), axis=0)
    hot_slot = one_hot(slot, slots)
    fitting = paired(fit_disp[...], fit_dir[...])

    def bins(first, count):
        lhs = [
            stack * (owner == first + at).astype(F32).astype(BF16) for at in range(count)
        ]
        return dot(jnp.concatenate(lhs, axis=0), hot_slot, ((1,), (1,)))

    def folded(wide_bins, at):
        part = wide_bins[at * 2 * COMPS : (at + 1) * 2 * COMPS]
        return part[0:COMPS] + part[COMPS : 2 * COMPS]

    block = math.gcd(peers, 8)

    def fill(first):
        wide_bins = bins(first, block)
        for peer in range(block):
            pay[first + peer, 0:COMPS, :] = fitting
            pay[first + peer, COMPS : 2 * COMPS, :] = folded(wide_bins, peer)

    if block == peers:
        fill(0)
    else:
        lax.fori_loop(0, peers // block, lambda at, carry: (fill(at * block), carry)[1], 0)


def mate_rows(mate):
    upper = lax.axis_index("pb") == 0
    first, last = mate[0:COMPS, :], mate[COMPS : 2 * COMPS, :]
    return jnp.where(upper, first, last), jnp.where(upper, last, first)


def fill_blocks(axes, row_total, sums, columns, mate, w_in, b_in, b_mid, w_out, out, w_first, w_last, b_cols, pay, done):
    tx_count, ty_count = axes
    along, across = lax.axis_index("tx"), lax.axis_index("ty")
    near, far = mate_rows(mate)
    pay[:, 0 : 2 * COMPS, :] = sums[...]
    ahead = along + 1 - 2 * lax.axis_index("pb")
    for side in (-1, 0, 1):
        over = across + side
        inside = (over >= 0) & (over < ty_count)

        @pl.when(inside & (ahead >= 0) & (ahead < tx_count))
        def _():
            pay[ahead * ty_count + over, 2 * COMPS : 3 * COMPS, :] = far

        if side == 0:
            continue
        edge = 0 if side < 0 else 1
        packed = pack_column(columns[edge * COMPS : (edge + 1) * COMPS, :], row_total)

        @pl.when(inside)
        def _():
            at = along * ty_count + over
            pay[at, 2 * COMPS : 3 * COMPS, :] = near
            for line, row in zip(packed, SPARE_ROWS):
                pay[at, row : row + 1, :] = line

    copy = pltpu.make_async_copy(pay, out, done)
    copy.start()
    build_weights(w_in, b_in, b_mid, w_out, w_first, w_last, b_cols)
    copy.wait()


def pack_column(column, width):
    each = column.shape[1] // width
    lines = []
    for first in range(0, 12, each):
        line = None
        for at in range(first, min(first + each, 12)):
            row = at % 6 + at // 6 * 8
            part = column[row : row + 1]
            if at > first:
                part = pltpu.roll(part, (at - first) * width, 1)
            line = part if line is None else line + part
        lines.append(line)
    assert len(lines) <= len(SPARE_ROWS)
    return lines


def unpack_column(block, width):
    shape = (COMPS, block.shape[1])
    each = shape[1] // width
    row = rows_of(shape)
    column = jnp.zeros(shape, F32)
    for at in range(12):
        spare = SPARE_ROWS[at // each]
        line = block[spare : spare + 1]
        if at % each:
            line = pltpu.roll(line, shape[1] - at % each * width, 1)
        column = jnp.where(row == at % 6 + at // 6 * 8, line, column)
    return jnp.where(lanes_of(shape) < width, column, 0.0)


def build_weights(w_in, b_in, b_mid, w_out, w_first, w_last, b_cols):
    hid = w_in.shape[1]
    bias_rows = split(b_in[...], 3)
    row = rows_of((8, hid))
    stacked = jnp.zeros((8, hid), F32)
    mid_stacked = jnp.zeros((8, hid), F32)
    for at, (one, two) in enumerate(zip(bias_rows, split(b_mid[...], 3))):
        stacked = jnp.where(row == at, one.astype(F32), stacked)
        mid_stacked = jnp.where(row == at, two.astype(F32), mid_stacked)
    lhs = jnp.concatenate([w_in[...].astype(F32), jnp.zeros((4, hid), F32), stacked], axis=0).astype(BF16)
    sel_shape = (24, 4 * COMPS)
    source = rows_of(sel_shape)
    target = lanes_of(sel_shape)
    for point in range(4):
        a_base = (point // 2) * COMPS
        c_base = (2 + point % 2) * COMPS
        for side in range(2):
            hit = (source < 6) & (target == a_base + 8 * side + source)
            hit = hit | ((source >= 6) & (source < 12) & (target == c_base + 8 * side + source - 6))
            if side == 0:
                for at, spot in enumerate((6, 7, 14)):
                    hit = hit | ((source == 16 + at) & (target == a_base + spot))
            block = dot(lhs, hit.astype(F32).astype(BF16), ((0,), (0,)))
            start = (2 * point + side) * hid
            w_first[start : start + hid, :] = block.astype(BF16)
    ones = (rows_of((8, 128)) < 3).astype(F32).astype(BF16)
    b_cols[...] = dot(mid_stacked.astype(BF16), ones, ((0,), (0,)))
    last_shape = (128, 12)
    target = rows_of(last_shape)
    source = lanes_of(last_shape)
    hit = target < 0
    for point in range(4):
        a_base = point * 32 + (point // 2) * 8
        c_base = point * 32 + 16 + (point % 2) * 8
        hit = hit | ((source < 6) & (target == a_base + source))
        hit = hit | ((source >= 6) & (target == c_base + source - 6))
    w_last[...] = dot(hit.astype(F32).astype(BF16), w_out[...]).astype(BF16)


def interior(pick, fields, mate, w_first, w_mid, b_cols, w_last, sent, forces):
    row_total, cols = fields.shape[0] // COMPS, fields.shape[1]
    half = row_total // 2
    held = half + 1
    group = lax.axis_index("groups") if pick is None else pick
    core = lax.axis_index("pb")
    first = group * half - core
    near, _ = mate_rows(mate)
    lines = []
    for at in range(half + 1):
        row = first + at
        if at == 0:
            row = jnp.maximum(row, 0)
        if at == half:
            row = jnp.minimum(row, row_total - 1)
        base = fields[pl.ds(pl.multiple_of(row * COMPS, COMPS), COMPS), :]
        if at == 0:
            base = jnp.where((core == 1) & (group == 0), near, base)
        if at == half:
            base = jnp.where((core == 0) & (group == 1), near, base)
        lines.append((base, pltpu.roll(base, cols - 1, 1)))
    tiles = [
        strain_tile(lines[at][0], lines[at + 1][0], lines[at][1], lines[at + 1][1]) for at in range(half)
    ]
    tiles = [jnp.concatenate(tiles[at : at + 2], axis=1) for at in range(0, half, 2)]
    sums = stress_sums(tiles, w_first, w_mid, b_cols, w_last)
    keep = lanes_of((COMPS, cols)) < cols - 1
    forces[...] = jnp.zeros(forces.shape, F32)
    for tile, (primal, tangent) in enumerate(sums):
        for side in range(2):
            lanes = slice(side * cols, (side + 1) * cols)
            parts = corner_forces(primal[:, lanes], tangent[:, lanes])
            base, right, upper, corner = (jnp.where(keep, part, 0.0) for part in parts)
            at = (2 * tile + side + 1) * COMPS
            forces[at : at + COMPS, :] += base + pltpu.roll(upper, 1, 1)
            forces[at + COMPS : at + 2 * COMPS, :] += right + pltpu.roll(corner, 1, 1)
    start = 1 + group * (row_total - held) - first
    for comp in range(12):
        rows = pl.ds(start * COMPS + comp % 6 + comp // 6 * 8, held, stride=COMPS)
        sent[comp * held : (comp + 1) * held, :] = forces[rows, :]


def edges(names, axes, *refs):
    ref = dict(zip(names, refs))
    tx_count, ty_count, pb_count = axes
    fields, ties, partial, got = ref["fields"], ref["ties"], ref["partial"], ref["got"]
    row_total, cols = fields.shape[0] // COMPS, fields.shape[1]
    slots = got.shape[2]
    tie_total = ties.shape[1]
    lane = lanes_of((COMPS, cols))
    core = lax.axis_index("pb")
    across = lax.axis_index("ty")
    along = lax.axis_index("tx")
    place = along * pb_count + core

    def around(step, side, packed=False):
        there, over = along + step, across + side
        valid = (there >= 0) & (there < tx_count) & (over >= 0) & (over < ty_count)
        block = got.at[jnp.where(valid, there * ty_count + over, 0)]
        if packed:
            value = unpack_column(block[0:COMPS, :], row_total)
        else:
            value = block[2 * COMPS : 3 * COMPS, :]
        return jnp.where(valid, value, 0.0)

    upper = core == 0
    behind = 2 * core - 1
    near, _ = mate_rows(ref["mate"])
    rows_near = (around(0, -1), near, around(0, 1))
    rows_far = tuple(around(behind, side) for side in (-1, 0, 1))
    next_rows = [jnp.where(upper, one, two) for one, two in zip(rows_near, rows_far)]
    prev_rows = [jnp.where(upper, two, one) for one, two in zip(rows_near, rows_far)]
    prev_row, next_row = prev_rows[1], next_rows[1]
    next_col = around(0, 1, True)
    prev_col = around(0, -1, True)
    next_corner = (prev_rows[2][:, 0:1], next_rows[2][:, 0:1])
    prev_corner = (prev_rows[0][:, cols - 1 : cols], next_rows[0][:, cols - 1 : cols])

    def column(inner, before, after):
        line = pltpu.roll(inner, 1, 1)
        line = jnp.where(lane == 0, before, line)
        return jnp.where(lane == row_total + 1, after, line)

    own_cols = ref["cols"]
    line_prev = column(prev_col, prev_corner[0], prev_corner[1])
    line_next = column(next_col, next_corner[0], next_corner[1])
    line_first = column(own_cols[0:COMPS, :], prev_row[:, 0:1], next_row[:, 0:1])
    line_final = column(
        own_cols[COMPS : 2 * COMPS, :], prev_row[:, cols - 1 : cols], next_row[:, cols - 1 : cols]
    )

    def shifted(row_value, beyond):
        return jnp.where(lane == cols - 1, beyond, pltpu.roll(row_value, cols - 1, 1))

    first_row = fields[0:COMPS, :]
    last_row = fields[(row_total - 1) * COMPS :, :]
    far_row = rows_far[1]
    lower_row = jnp.where(upper, far_row, last_row)
    upper_row = jnp.where(upper, first_row, far_row)
    own_beyond = jnp.where(upper, next_col[:, 0:1], next_col[:, row_total - 1 : row_total])
    far_beyond = rows_far[2][:, 0:1]
    tile_far = strain_tile(
        lower_row,
        upper_row,
        shifted(lower_row, jnp.where(upper, far_beyond, own_beyond)),
        shifted(upper_row, jnp.where(upper, own_beyond, far_beyond)),
    )
    half = cols // 2
    low = lane < half
    back = cols - 1

    def two(left, right_line):
        return jnp.where(low, left, pltpu.roll(right_line, half, 1))

    left_base = two(line_prev, line_final)
    left_upper = two(line_first, line_next)
    right_base = two(pltpu.roll(line_prev, back, 1), pltpu.roll(line_final, back, 1))
    right_upper = two(pltpu.roll(line_first, back, 1), pltpu.roll(line_next, back, 1))
    tile_side = strain_tile(left_base, right_base, left_upper, right_upper)

    edge_tile = jnp.concatenate((tile_far, tile_side), axis=1)
    primal, tangent = stress_sums([edge_tile], ref["w_first"], ref["w_mid"], ref["b_mid"], ref["w_last"])[0]
    f_base, f_right, f_upper, f_corner = corner_forces(primal[:, :cols], tangent[:, :cols])
    s_base, s_right, s_upper, s_corner = corner_forces(primal[:, cols:], tangent[:, cols:])

    def mask(value, keep):
        return jnp.where(keep, value, 0.0)

    def moved(value):
        return pltpu.roll(mask(value, lane < cols - 1), 1, 1)

    has_row = place > 0
    has_col = across > 0
    row_first = mask(f_right + moved(f_corner), upper & has_row)
    row_last = mask(f_base + moved(f_upper), core == 1)
    first_lane = jnp.where(has_row, 0, 1)
    s_corner = mask(s_corner, (lane >= first_lane) & (lane < row_total))
    s_upper = mask(s_upper, (lane >= 1) & (lane <= row_total))
    col_first = mask(pltpu.roll(s_upper, back, 1) + s_corner, has_col)
    valid = (lane >= half + 1 - core) & (lane <= half + row_total - core)
    s_base = mask(s_base, valid)
    s_right = mask(s_right, valid)
    col_last = pltpu.roll(pltpu.roll(s_base, back, 1) + s_right, cols - half, 1)

    node = as_line(ref["node"])
    slot = as_line(ref["slot"])
    owner = ref["owner"][...]
    hot_slot = one_hot(slot, slots)
    hot_two = jnp.concatenate([hot_slot] * 2, axis=0)
    fit_value = jnp.zeros((COMPS, tie_total), F32)
    bins = jnp.zeros((COMPS, slots), F32)
    peers = tx_count * ty_count
    block = math.gcd(peers, 8)

    def collect(first, carry):
        fit_value, bins = carry
        parts = [got[first + peer] for peer in range(block)]
        fit_all = jnp.concatenate([part[0:COMPS] for part in parts], axis=0)
        wide = dot(jnp.concatenate(split(fit_all, 2), axis=1), hot_two)
        for peer, part in enumerate(parts):
            fit_value = jnp.where(owner == first + peer, wide[peer * COMPS : (peer + 1) * COMPS], fit_value)
            bins = bins + part[COMPS : 2 * COMPS]
        return fit_value, bins

    if block == peers:
        fit_value, bins = collect(0, (fit_value, bins))
    else:
        fit_value, bins = lax.fori_loop(
            0, peers // block, lambda at, carry: collect(at * block, carry), (fit_value, bins)
        )
    count = bins[COUNT_ROW : COUNT_ROW + 1]
    for out, fit, base in (("fit_res", "fit_disp", 0), ("fit_tan", "fit_dir", 8)):
        ref[out][...] = 2.0 * (count * ref[fit][...] - bins[base : base + 6])

    pulled = 2.0 * (ties[...] - fit_value)
    node_row = lax.shift_right_logical(node, cols.bit_length() - 1)
    node_col = jnp.bitwise_and(node, cols - 1)
    hot_col = one_hot(node_col, cols)
    sides = split(pulled, 2)
    lhs = []
    for row in range(row_total):
        hit = (node_row == row).astype(F32).astype(BF16)
        lhs.append(jnp.concatenate([side * hit for side in sides], axis=1))
    tie_forces = dot(
        jnp.concatenate(lhs, axis=0), jnp.concatenate([hot_col] * 2, axis=1), ((1,), (1,))
    )

    for row in range(row_total):
        total = tie_forces[row * COMPS : (row + 1) * COMPS]
        total = total + jnp.where(lane == 0, col_first[:, row : row + 1], 0.0)
        total = total + jnp.where(lane == cols - 1, col_last[:, row : row + 1], 0.0)
        if row == 0:
            total = total + row_first
        if row == row_total - 1:
            total = total + row_last
        partial[row * COMPS : (row + 1) * COMPS, :] = total


def combine(swapped, partial, own, other, load, res, tan):
    row_total = partial.shape[0] // COMPS
    held = own.shape[0] // 12
    skip = row_total - held
    first, second = own[...], other[...]
    if swapped:
        here = lax.axis_index("groups") == 0
        first, second = jnp.where(here, first, second), jnp.where(here, second, first)
    for comp in range(12):
        target = res if comp < 6 else tan
        start = comp % 6 * row_total
        value = partial[pl.ds(comp % 6 + comp // 6 * 8, row_total, stride=COMPS), :]
        if comp < 6:
            value = value - load[start : start + row_total, :]
        rows = slice(comp * held, (comp + 1) * held)
        target[start : start + row_total, :] = value
        target[start : start + held, :] += first[rows]
        target[start + skip : start + row_total, :] += second[rows]


def per_device(
    displacement,
    direction,
    load,
    w_in,
    b_in,
    w_mid,
    b_mid,
    w_out,
    fitting_disp,
    fitting_dir,
    tie_node,
    tie_owner,
    tie_slot,
):
    tx_count = lax.axis_size("tx")
    ty_count = lax.axis_size("ty")
    pb_count = lax.axis_size("pb")
    peers = tx_count * ty_count
    axes = (tx_count, ty_count, pb_count)
    _, row_total, cols = displacement.shape
    slots = fitting_disp.shape[1]
    tie_total = tie_node.shape[0]
    hid = w_mid.shape[0]
    flat = (6 * row_total, cols)
    disp2 = displacement.reshape(flat)
    dir2 = direction.reshape(flat)
    load2 = load.reshape(flat)
    node2 = tie_node.reshape(tie_total // 128, 128)
    slot2 = tie_slot.reshape(tie_total // 128, 128)
    owner2 = tie_owner.reshape(1, tie_total)

    def shape(*dims, dtype=F32):
        return jax.ShapeDtypeStruct(dims, dtype)

    assert pb_count == 2 and slots == cols
    smalls = (
        fitting_disp,
        fitting_dir,
        node2,
        owner2,
        slot2,
        b_in.reshape(1, hid),
        b_mid.reshape(1, hid),
        w_in.T,
        w_out,
    )
    outs = pl.pallas_call(
        lambda *refs: gather_nodes(len(smalls), *refs),
        out_shape=[pltpu.VMEM((row_total * COMPS, cols), F32), pltpu.VMEM((2 * COMPS, cols), F32)]
        + [pltpu.VMEM(value.shape, value.dtype) for value in smalls],
        in_specs=local(2 + len(smalls)),
        out_specs=local(2 + len(smalls)),
        name="gather_nodes",
    )(disp2, dir2, *smalls)
    fields, rows, fit_disp, fit_dir, node, owner, slot, b_first, b_second, w_first_in, w_final = outs
    mate = lax.ppermute(rows, "pb", [(0, 1), (1, 0)])

    inputs = tuple(on_chip(value) for value in (fields, fit_disp, fit_dir, node, owner, slot))
    small = peers * 2 * COMPS * slots <= SMALL
    ties, cols_out, sums = pl.pallas_call(
        lambda *refs: sum_ties(peers, *refs),
        out_shape=[
            pltpu.VMEM((COMPS, tie_total), F32),
            pltpu.VMEM((2 * COMPS, cols), F32),
            (pltpu.VMEM if small else jax.ShapeDtypeStruct)((peers, 2 * COMPS, slots), F32),
        ],
        in_specs=local(len(inputs)),
        out_specs=local(3),
        name="sum_ties",
    )(*inputs)
    inputs = (sums, cols_out, mate, w_first_in, b_first, b_second, w_final)
    inputs = [on_chip(value) if value.size <= SMALL else value for value in inputs]
    pay, w_first, w_last, b_cols = pl.pallas_call(
        lambda *refs: fill_blocks((tx_count, ty_count), row_total, *refs),
        out_shape=[
            shape(peers, 3 * COMPS, slots),
            pltpu.VMEM((8 * hid, 4 * COMPS), BF16),
            pltpu.VMEM((128, hid), BF16),
            pltpu.VMEM((hid, 128), F32),
        ],
        in_specs=local(len(inputs)),
        out_specs=[pl.BlockSpec(memory_space=pl.ANY)] + local(3),
        scratch_shapes=[pltpu.VMEM((peers, 3 * COMPS, slots), F32), pltpu.SemaphoreType.DMA(())],
        name="fill_blocks",
    )(*inputs)
    got = lax.all_to_all(pay, ("tx", "ty"), split_axis=0, concat_axis=0, tiled=True)

    inputs = tuple(on_chip(value) for value in (fields, mate, w_first, w_mid, b_cols, w_last))
    groups = lax.axis_size("groups")
    halves = []
    for pick in (None,) if groups == 2 else (0, 1):
        half = pl.pallas_call(
            lambda *refs: interior(pick, *refs),
            out_shape=pltpu.VMEM(((row_total // 2 + 1) * 12, cols), F32),
            in_specs=local(len(inputs)),
            out_specs=local(1)[0],
            scratch_shapes=[pltpu.VMEM(((row_total // 2 + 3) * COMPS, cols), F32)],
            name="interior",
        )(*inputs)
        halves.append(half)
    if groups == 2:
        halves.append(lax.ppermute(halves[0], "groups", [(0, 1), (1, 0)]))

    named = dict(
        got=got,
        mate=mate,
        fields=fields,
        ties=ties,
        cols=cols_out,
        w_first=w_first,
        w_mid=w_mid,
        b_mid=b_cols,
        w_last=w_last,
        node=node,
        slot=slot,
        owner=owner,
        fit_disp=fit_disp,
        fit_dir=fit_dir,
    )
    named = {name: on_chip(value) if value.size <= SMALL else value for name, value in named.items()}
    names = list(named)
    partial, fit_res, fit_tan = pl.pallas_call(
        lambda *refs: edges(names + ["partial", "fit_res", "fit_tan"], axes, *refs),
        out_shape=[pltpu.VMEM((row_total * COMPS, cols), F32), shape(6, slots), shape(6, slots)],
        in_specs=local(len(names)),
        out_specs=local(3),
        name="edges",
    )(*named.values())

    inputs = tuple(on_chip(value) for value in (partial, halves[0], halves[1], load2))
    res, tan = pl.pallas_call(
        lambda *refs: combine(groups == 2, *refs),
        out_shape=[shape(*flat), shape(*flat)],
        in_specs=local(len(inputs)),
        out_specs=local(2),
        name="combine",
    )(*inputs)
    cube = displacement.shape
    return (res.reshape(cube), tan.reshape(cube), fit_res, fit_tan)


def solution(mesh):
    in_specs = (
        P(None, ("tx", "pb"), "ty"),
        P(None, ("tx", "pb"), "ty"),
        P(None, ("tx", "pb"), "ty"),
        P(),
        P(),
        P(),
        P(),
        P(),
        P(None, ("groups", "tx", "ty", "pb")),
        P(None, ("groups", "tx", "ty", "pb")),
        P(("groups", "tx", "ty", "pb")),
        P(("groups", "tx", "ty", "pb"), None),
        P(("groups", "tx", "ty", "pb")),
    )
    out_specs = (
        P(None, ("groups", "tx", "pb"), "ty"),
        P(None, ("groups", "tx", "pb"), "ty"),
        P(None, ("groups", "tx", "ty", "pb")),
        P(None, ("groups", "tx", "ty", "pb")),
    )
    return jax.shard_map(
        per_device, mesh=mesh, in_specs=in_specs, out_specs=out_specs, check_vma=False
    )
```

```python
import math

import jax
import jax.numpy as jnp
from jax import lax
from jax.experimental import pallas as pl
from jax.experimental.pallas import tpu as pltpu
from jax.sharding import PartitionSpec as P

F32 = jnp.float32
BF16 = jnp.bfloat16
GAUSS = (0.5 - 0.5 / math.sqrt(3.0), 0.5 + 0.5 / math.sqrt(3.0))
COMPS = 16
COUNT_ROW = 6
SPARE_ROWS = (6, 7, 14)
SMALL = 1 << 18


def local(count):
    return [pl.BlockSpec(memory_space=pltpu.VMEM)] * count


def on_chip(value):
    return pltpu.with_memory_space_constraint(value, pltpu.VMEM)


def dot(a, b, dims=((1,), (0,))):
    return lax.dot_general(a, b, (dims, ((), ())), preferred_element_type=F32)


def split(value, terms):
    parts = []
    for _ in range(terms):
        part = value.astype(BF16)
        parts.append(part)
        value = value - part.astype(F32)
    return parts


def rows_of(value):
    return lax.broadcasted_iota(jnp.int32, value, 0)


def lanes_of(value):
    return lax.broadcasted_iota(jnp.int32, value, 1)


def one_hot(index, size):
    shape = (size, index.shape[1])
    return (rows_of(shape) == index).astype(F32).astype(BF16)


def as_line(ref):
    return jnp.concatenate([ref[row : row + 1, :] for row in range(ref.shape[0])], axis=1)


def paired(top, bottom):
    spare = jnp.zeros((2, top.shape[1]), F32)
    return jnp.concatenate([top, spare, bottom, spare], axis=0)


def strain_tile(f00, f10, f01, f11):
    along_low = f10 - f00
    along_high = f11 - f01
    across_low = f01 - f00
    across_high = f11 - f10
    shape = f00.shape
    row = rows_of(shape)
    ones = ((row == 6) | (row == 7) | (row == 14)).astype(F32)
    groups = []
    for frac in GAUSS:
        groups.append((((1.0 - frac) * along_low + frac * along_high) + ones).astype(BF16))
    for frac in GAUSS:
        groups.append(((1.0 - frac) * across_low + frac * across_high).astype(BF16))
    return jnp.concatenate(groups, axis=0)


def stress_sums(strains, w_first, w_mid, b_mid, w_last):
    hid = w_mid.shape[0]
    tasks = [(tile, point) for tile in range(len(strains)) for point in range(4)]
    totals = [[None, None] for _ in strains]

    def layer_one(task):
        tile, point = task
        start = point * 2 * hid
        return (
            dot(w_first[start : start + hid, :], strains[tile]),
            dot(w_first[start + hid : start + 2 * hid, :], strains[tile]),
        )

    def activate(value, slope):
        act = jnp.tanh(value)
        return (act.astype(BF16), ((1.0 - act * act) * slope).astype(BF16))

    def layer_two(hidden):
        bias = b_mid[...]
        value = dot(w_mid[...], hidden[0])
        slope = dot(w_mid[...], hidden[1])
        bias = jnp.concatenate([bias] * (value.shape[1] // bias.shape[1]), axis=1)
        return (value + bias, slope)

    def layer_three(task, hidden):
        tile, point = task
        last = w_last[point * 32 : (point + 1) * 32, :]
        for side in range(2):
            part = dot(last, hidden[side])
            old = totals[tile][side]
            totals[tile][side] = part if old is None else old + part

    ones = {0: layer_one(tasks[0])}
    twos = {}
    for at in range(len(tasks) + 1):
        if at + 1 < len(tasks):
            ones[at + 1] = layer_one(tasks[at + 1])
        if at < len(tasks):
            hidden = activate(*ones.pop(at))
            twos[at] = layer_two(hidden)
        if at >= 1:
            layer_three(tasks[at - 1], activate(*twos.pop(at - 1)))
    return totals


def corner_forces(primal, tangent):
    def both(group):
        return jnp.concatenate([primal[group * 8 : group * 8 + 8], tangent[group * 8 : group * 8 + 8]], axis=0)

    along = (both(0), both(1))
    across = (both(2), both(3))

    def mix(pair, weights):
        return (0.25 * weights[0]) * pair[0] + (0.25 * weights[1]) * pair[1]

    rest = (1.0 - GAUSS[0], 1.0 - GAUSS[1])
    along_rest = mix(along, rest)
    along_frac = mix(along, GAUSS)
    across_rest = mix(across, rest)
    across_frac = mix(across, GAUSS)
    return (
        -along_rest - across_rest,
        along_rest - across_frac,
        across_rest - along_frac,
        along_frac + across_frac,
    )


def gather_nodes(count, disp, dirn, *refs):
    fields, rows = refs[count : count + 2]
    for source, target in zip(refs[:count], refs[count + 2 :]):
        target[...] = source[...]
    row_total = fields.shape[0] // COMPS
    fields[...] = jnp.zeros(fields.shape, F32)
    for comp in range(6):
        part = slice(comp * row_total, (comp + 1) * row_total)
        fields[pl.ds(comp, row_total, stride=COMPS), :] = disp[part, :]
        fields[pl.ds(8 + comp, row_total, stride=COMPS), :] = dirn[part, :]
    rows[0:COMPS, :] = fields[0:COMPS, :]
    rows[COMPS : 2 * COMPS, :] = fields[(row_total - 1) * COMPS :, :]


def sum_ties(axes, *refs):
    (fields, fit_disp, fit_dir, node_ref, owner_ref, slot_ref) = refs[:6]
    (ties, col_out, hot_col_out, hot_slot_out, hot_row_out, out, pay, done) = refs[6:]
    tx_count, ty_count = axes
    peers = tx_count * ty_count
    row_total = fields.shape[0] // COMPS
    cols = fields.shape[1]
    slots = fit_disp.shape[1]
    tie_total = ties.shape[1]

    lane = lanes_of((COMPS, cols))
    for side, column in enumerate((0, cols - 1)):
        gathered = jnp.zeros((COMPS, cols), F32)
        for row in range(row_total):
            value = fields[row * COMPS : (row + 1) * COMPS, column : column + 1]
            gathered = jnp.where(lane == row, value, gathered)
        col_out[side * COMPS : (side + 1) * COMPS, :] = gathered

    node = as_line(node_ref)
    slot = as_line(slot_ref)
    owner = owner_ref[...]
    node_row = lax.shift_right_logical(node, cols.bit_length() - 1)
    node_col = jnp.bitwise_and(node, cols - 1)
    hot_col = one_hot(node_col, cols)
    hot_col_out[...] = hot_col
    hot_row_out[...] = one_hot(node_row, row_total)
    wide = dot(
        jnp.concatenate(split(fields[...], 2), axis=1), jnp.concatenate([hot_col] * 2, axis=0)
    )
    value = jnp.zeros((COMPS, tie_total), F32)
    for row in range(row_total):
        value = jnp.where(node_row == row, wide[row * COMPS : (row + 1) * COMPS], value)
    value = jnp.where(rows_of(value.shape) == COUNT_ROW, 1.0, value)
    ties[...] = value
    stack = jnp.concatenate(split(value, 2), axis=0)
    hot_slot = one_hot(slot, slots)
    hot_slot_out[...] = hot_slot
    fitting = paired(fit_disp[...], fit_dir[...])

    def bins(first, count):
        lhs = [
            stack * (owner == first + at).astype(F32).astype(BF16) for at in range(count)
        ]
        return dot(jnp.concatenate(lhs, axis=0), hot_slot, ((1,), (1,)))

    def folded(wide_bins, at):
        part = wide_bins[at * 2 * COMPS : (at + 1) * 2 * COMPS]
        return part[0:COMPS] + part[COMPS : 2 * COMPS]

    block = math.gcd(peers, 8)

    def fill(first):
        wide_bins = bins(first, block)
        for peer in range(block):
            pay[first + peer, 0:COMPS, :] = fitting
            pay[first + peer, COMPS : 2 * COMPS, :] = folded(wide_bins, peer)

    if block == peers:
        fill(0)
    else:
        lax.fori_loop(0, peers // block, lambda at, carry: (fill(at * block), carry)[1], 0)

    along, across = lax.axis_index("tx"), lax.axis_index("ty")
    for side, edge in ((-1, 0), (1, 1)):
        over = across + side
        packed = pack_column(col_out[edge * COMPS : (edge + 1) * COMPS, :], row_total)

        @pl.when((over >= 0) & (over < ty_count))
        def _():
            for line, row in zip(packed, SPARE_ROWS):
                pay[along * ty_count + over, row : row + 1, :] = line

    copy = pltpu.make_async_copy(pay, out.at[:, 0 : 2 * COMPS, :], done)
    copy.start()
    copy.wait()


def mate_rows(mate):
    upper = lax.axis_index("pb") == 0
    first, last = mate[0:COMPS, :], mate[COMPS : 2 * COMPS, :]
    return jnp.where(upper, first, last), jnp.where(upper, last, first)


def fill_rows(axes, mate, w_in, b_in, b_mid, w_out, _, w_first, w_last, b_cols, out, rows, done):
    tx_count, ty_count = axes
    along, across = lax.axis_index("tx"), lax.axis_index("ty")
    near, far = mate_rows(mate)
    ahead = along + 1 - 2 * lax.axis_index("pb")
    rows[...] = jnp.zeros(rows.shape, F32)
    for side in (-1, 0, 1):
        over = across + side
        inside = (over >= 0) & (over < ty_count)

        @pl.when(inside & (ahead >= 0) & (ahead < tx_count))
        def _():
            rows[ahead * ty_count + over] = far

        if side == 0:
            continue

        @pl.when(inside)
        def _():
            rows[along * ty_count + over] = near

    copy = pltpu.make_async_copy(rows, out.at[:, 2 * COMPS : 3 * COMPS, :], done)
    copy.start()
    build_weights(w_in, b_in, b_mid, w_out, w_first, w_last, b_cols)
    copy.wait()


def pack_column(column, width):
    each = column.shape[1] // width
    lines = []
    for first in range(0, 12, each):
        line = None
        for at in range(first, min(first + each, 12)):
            row = at % 6 + at // 6 * 8
            part = column[row : row + 1]
            if at > first:
                part = pltpu.roll(part, (at - first) * width, 1)
            line = part if line is None else line + part
        lines.append(line)
    assert len(lines) <= len(SPARE_ROWS)
    return lines


def unpack_column(block, width):
    shape = (COMPS, block.shape[1])
    each = shape[1] // width
    row = rows_of(shape)
    column = jnp.zeros(shape, F32)
    for at in range(12):
        spare = SPARE_ROWS[at // each]
        line = block[spare : spare + 1]
        if at % each:
            line = pltpu.roll(line, shape[1] - at % each * width, 1)
        column = jnp.where(row == at % 6 + at // 6 * 8, line, column)
    return jnp.where(lanes_of(shape) < width, column, 0.0)


def build_weights(w_in, b_in, b_mid, w_out, w_first, w_last, b_cols):
    hid = w_in.shape[1]
    bias_rows = split(b_in[...], 3)
    row = rows_of((8, hid))
    stacked = jnp.zeros((8, hid), F32)
    mid_stacked = jnp.zeros((8, hid), F32)
    for at, (one, two) in enumerate(zip(bias_rows, split(b_mid[...], 3))):
        stacked = jnp.where(row == at, one.astype(F32), stacked)
        mid_stacked = jnp.where(row == at, two.astype(F32), mid_stacked)
    lhs = jnp.concatenate([w_in[...].astype(F32), jnp.zeros((4, hid), F32), stacked], axis=0).astype(BF16)
    sel_shape = (24, 4 * COMPS)
    source = rows_of(sel_shape)
    target = lanes_of(sel_shape)
    for point in range(4):
        a_base = (point // 2) * COMPS
        c_base = (2 + point % 2) * COMPS
        for side in range(2):
            hit = (source < 6) & (target == a_base + 8 * side + source)
            hit = hit | ((source >= 6) & (source < 12) & (target == c_base + 8 * side + source - 6))
            if side == 0:
                for at, spot in enumerate((6, 7, 14)):
                    hit = hit | ((source == 16 + at) & (target == a_base + spot))
            block = dot(lhs, hit.astype(F32).astype(BF16), ((0,), (0,)))
            start = (2 * point + side) * hid
            w_first[start : start + hid, :] = block.astype(BF16)
    ones = (rows_of((8, 128)) < 3).astype(F32).astype(BF16)
    b_cols[...] = dot(mid_stacked.astype(BF16), ones, ((0,), (0,)))
    last_shape = (128, 12)
    target = rows_of(last_shape)
    source = lanes_of(last_shape)
    hit = target < 0
    for point in range(4):
        a_base = point * 32 + (point // 2) * 8
        c_base = point * 32 + 16 + (point % 2) * 8
        hit = hit | ((source < 6) & (target == a_base + source))
        hit = hit | ((source >= 6) & (target == c_base + source - 6))
    w_last[...] = dot(hit.astype(F32).astype(BF16), w_out[...]).astype(BF16)


def interior(pick, begin, end, low, high, *refs):
    fields, mate, w_first, w_mid, b_cols, w_last = refs[:6]
    before = refs[6] if begin else None
    sent, forces = refs[-2:]
    row_total, cols = fields.shape[0] // COMPS, fields.shape[1]
    half = row_total // 2
    group = lax.axis_index("groups") if pick is None else pick
    core = lax.axis_index("pb")
    first = group * half - core
    near, _ = mate_rows(mate)
    lines = []
    for at in range(begin, end + 1):
        row = first + at
        if at == 0:
            row = jnp.maximum(row, 0)
        if at == half:
            row = jnp.minimum(row, row_total - 1)
        base = fields[pl.ds(pl.multiple_of(row * COMPS, COMPS), COMPS), :]
        if at == 0:
            base = jnp.where((core == 1) & (group == 0), near, base)
        if at == half:
            base = jnp.where((core == 0) & (group == 1), near, base)
        lines.append((base, pltpu.roll(base, cols - 1, 1)))
    tiles = [
        strain_tile(one[0], two[0], one[1], two[1]) for one, two in zip(lines[:-1], lines[1:])
    ]
    tiles = [jnp.concatenate(tiles[at : at + 2], axis=1) for at in range(0, end - begin, 2)]
    sums = stress_sums(tiles, w_first, w_mid, b_cols, w_last)
    keep = lanes_of((COMPS, cols)) < cols - 1
    forces[...] = jnp.zeros(forces.shape, F32) if before is None else before[...]
    for tile, (primal, tangent) in enumerate(sums):
        for side in range(2):
            lanes = slice(side * cols, (side + 1) * cols)
            parts = corner_forces(primal[:, lanes], tangent[:, lanes])
            base, right, upper, corner = (jnp.where(keep, part, 0.0) for part in parts)
            at = (begin + 2 * tile + side + 1) * COMPS
            forces[at : at + COMPS, :] += base + pltpu.roll(upper, 1, 1)
            forces[at + COMPS : at + 2 * COMPS, :] += right + pltpu.roll(corner, 1, 1)
    start = 1 + group * (row_total - half - 1) - first + low
    count = high - low
    for comp in range(12):
        rows = pl.ds(start * COMPS + comp % 6 + comp // 6 * 8, count, stride=COMPS)
        sent[comp * count : (comp + 1) * count, :] = forces[rows, :]


def finish(names, axes, pieces, swapped, *refs):
    ref = dict(zip(names, refs))
    tx_count, ty_count, pb_count = axes
    fields, ties, got, load = ref["fields"], ref["ties"], ref["got"], ref["load"]
    row_total, cols = fields.shape[0] // COMPS, fields.shape[1]
    slots = got.shape[2]
    tie_total = ties.shape[1]
    lane = lanes_of((COMPS, cols))
    core = lax.axis_index("pb")
    across = lax.axis_index("ty")
    along = lax.axis_index("tx")
    place = along * pb_count + core

    def around(step, side, packed=False):
        there, over = along + step, across + side
        valid = (there >= 0) & (there < tx_count) & (over >= 0) & (over < ty_count)
        block = got.at[jnp.where(valid, there * ty_count + over, 0)]
        if packed:
            value = unpack_column(block[0:COMPS, :], row_total)
        else:
            value = block[2 * COMPS : 3 * COMPS, :]
        return jnp.where(valid, value, 0.0)

    upper = core == 0
    behind = 2 * core - 1
    near, _ = mate_rows(ref["mate"])
    rows_near = (around(0, -1), near, around(0, 1))
    rows_far = tuple(around(behind, side) for side in (-1, 0, 1))
    next_rows = [jnp.where(upper, one, two) for one, two in zip(rows_near, rows_far)]
    prev_rows = [jnp.where(upper, two, one) for one, two in zip(rows_near, rows_far)]
    prev_row, next_row = prev_rows[1], next_rows[1]
    next_col = around(0, 1, True)
    prev_col = around(0, -1, True)
    next_corner = (prev_rows[2][:, 0:1], next_rows[2][:, 0:1])
    prev_corner = (prev_rows[0][:, cols - 1 : cols], next_rows[0][:, cols - 1 : cols])

    def column(inner, before, after):
        line = pltpu.roll(inner, 1, 1)
        line = jnp.where(lane == 0, before, line)
        return jnp.where(lane == row_total + 1, after, line)

    own_cols = ref["cols"]
    line_prev = column(prev_col, prev_corner[0], prev_corner[1])
    line_next = column(next_col, next_corner[0], next_corner[1])
    line_first = column(own_cols[0:COMPS, :], prev_row[:, 0:1], next_row[:, 0:1])
    line_final = column(
        own_cols[COMPS : 2 * COMPS, :], prev_row[:, cols - 1 : cols], next_row[:, cols - 1 : cols]
    )

    def shifted(row_value, beyond):
        return jnp.where(lane == cols - 1, beyond, pltpu.roll(row_value, cols - 1, 1))

    first_row = fields[0:COMPS, :]
    last_row = fields[(row_total - 1) * COMPS :, :]
    far_row = rows_far[1]
    lower_row = jnp.where(upper, far_row, last_row)
    upper_row = jnp.where(upper, first_row, far_row)
    own_beyond = jnp.where(upper, next_col[:, 0:1], next_col[:, row_total - 1 : row_total])
    far_beyond = rows_far[2][:, 0:1]
    tile_far = strain_tile(
        lower_row,
        upper_row,
        shifted(lower_row, jnp.where(upper, far_beyond, own_beyond)),
        shifted(upper_row, jnp.where(upper, own_beyond, far_beyond)),
    )
    half = cols // 2
    low = lane < half
    back = cols - 1

    def two(left, right_line):
        return jnp.where(low, left, pltpu.roll(right_line, half, 1))

    left_base = two(line_prev, line_final)
    left_upper = two(line_first, line_next)
    right_base = two(pltpu.roll(line_prev, back, 1), pltpu.roll(line_final, back, 1))
    right_upper = two(pltpu.roll(line_first, back, 1), pltpu.roll(line_next, back, 1))
    tile_side = strain_tile(left_base, right_base, left_upper, right_upper)

    edge_tile = jnp.concatenate((tile_far, tile_side), axis=1)
    primal, tangent = stress_sums([edge_tile], ref["w_first"], ref["w_mid"], ref["b_mid"], ref["w_last"])[0]
    f_base, f_right, f_upper, f_corner = corner_forces(primal[:, :cols], tangent[:, :cols])
    s_base, s_right, s_upper, s_corner = corner_forces(primal[:, cols:], tangent[:, cols:])

    def mask(value, keep):
        return jnp.where(keep, value, 0.0)

    def moved(value):
        return pltpu.roll(mask(value, lane < cols - 1), 1, 1)

    has_row = place > 0
    has_col = across > 0
    row_first = mask(f_right + moved(f_corner), upper & has_row)
    row_last = mask(f_base + moved(f_upper), core == 1)
    first_lane = jnp.where(has_row, 0, 1)
    s_corner = mask(s_corner, (lane >= first_lane) & (lane < row_total))
    s_upper = mask(s_upper, (lane >= 1) & (lane <= row_total))
    col_first = mask(pltpu.roll(s_upper, back, 1) + s_corner, has_col)
    valid = (lane >= half + 1 - core) & (lane <= half + row_total - core)
    s_base = mask(s_base, valid)
    s_right = mask(s_right, valid)
    col_last = pltpu.roll(pltpu.roll(s_base, back, 1) + s_right, cols - half, 1)

    owner = ref["owner"][...]
    hot_slot = ref["hot_slot"][...]
    hot_two = jnp.concatenate([hot_slot] * 2, axis=0)
    fit_value = jnp.zeros((COMPS, tie_total), F32)
    bins = jnp.zeros((COMPS, slots), F32)
    peers = tx_count * ty_count
    block = math.gcd(peers, 8)

    def collect(first, carry):
        fit_value, bins = carry
        parts = [got[first + peer] for peer in range(block)]
        fit_all = jnp.concatenate([part[0:COMPS] for part in parts], axis=0)
        wide = dot(jnp.concatenate(split(fit_all, 2), axis=1), hot_two)
        for peer, part in enumerate(parts):
            fit_value = jnp.where(owner == first + peer, wide[peer * COMPS : (peer + 1) * COMPS], fit_value)
            bins = bins + part[COMPS : 2 * COMPS]
        return fit_value, bins

    if block == peers:
        fit_value, bins = collect(0, (fit_value, bins))
    else:
        fit_value, bins = lax.fori_loop(
            0, peers // block, lambda at, carry: collect(at * block, carry), (fit_value, bins)
        )
    count = bins[COUNT_ROW : COUNT_ROW + 1]
    for out, fit, base in (("fit_res", "fit_disp", 0), ("fit_tan", "fit_dir", 8)):
        ref[out][...] = 2.0 * (count * ref[fit][...] - bins[base : base + 6])

    pulled = split(2.0 * (ties[...] - fit_value), 2)
    hot_row = ref["hot_row"][...]
    places = [comp % 6 + comp // 6 * 8 for comp in range(12)]
    lhs = [
        jnp.concatenate([hot_row * part[place_of : place_of + 1] for part in pulled], axis=1)
        for place_of in places
    ]
    hot_col = ref["hot_col"][...]
    tie_forces = dot(jnp.concatenate(lhs, axis=0), jnp.concatenate([hot_col] * 2, axis=1), ((1,), (1,)))

    assert 4 * row_total <= cols
    line = jnp.zeros((COMPS, cols), F32)
    for at, part in enumerate(split(col_first, 2) + split(col_last, 2)):
        part = part.astype(F32)
        part = pltpu.roll(part, at * row_total, 1) if at else part
        line = jnp.where((lane >= at * row_total) & (lane < (at + 1) * row_total), part, line)
    shape = (row_total, cols)
    eye = jnp.bitwise_and(lanes_of(shape), row_total - 1) == rows_of(shape)
    lhs = [jnp.where(eye, line[place_of : place_of + 1], 0.0).astype(BF16) for place_of in places]
    shape = (cols, cols)
    in_first = (rows_of(shape) == 0) & (lanes_of(shape) < 2 * row_total)
    in_last = (rows_of(shape) == cols - 1) & (lanes_of(shape) >= 2 * row_total)
    ends = (in_first | (in_last & (lanes_of(shape) < 4 * row_total))).astype(F32).astype(BF16)
    col_forces = dot(jnp.concatenate(lhs, axis=0), ends, ((1,), (1,)))

    row = rows_of((row_total, cols))
    here = lax.axis_index("groups") == 0
    for comp, place_of in enumerate(places):
        rows = slice(comp * row_total, (comp + 1) * row_total)
        value = tie_forces[rows] + col_forces[rows]
        value = value + jnp.where(row == 0, row_first[place_of : place_of + 1], 0.0)
        value = value + jnp.where(row == row_total - 1, row_last[place_of : place_of + 1], 0.0)
        if comp < 6:
            value = value - load[rows, :]
        target = ref["res"] if comp < 6 else ref["tan"]
        start = comp % 6 * row_total
        target[start : start + row_total, :] = value
        for piece, (low, high) in enumerate(pieces):
            count = high - low
            part = slice(comp * count, (comp + 1) * count)
            first, second = ref[f"own{piece}"][part, :], ref[f"other{piece}"][part, :]
            if swapped:
                first, second = jnp.where(here, first, second), jnp.where(here, second, first)
            target[start + low : start + high, :] += first
            shift = start + row_total // 2 - 1
            target[shift + low : shift + high, :] += second


def per_device(
    displacement,
    direction,
    load,
    w_in,
    b_in,
    w_mid,
    b_mid,
    w_out,
    fitting_disp,
    fitting_dir,
    tie_node,
    tie_owner,
    tie_slot,
):
    tx_count = lax.axis_size("tx")
    ty_count = lax.axis_size("ty")
    pb_count = lax.axis_size("pb")
    peers = tx_count * ty_count
    axes = (tx_count, ty_count, pb_count)
    _, row_total, cols = displacement.shape
    slots = fitting_disp.shape[1]
    tie_total = tie_node.shape[0]
    hid = w_mid.shape[0]
    flat = (6 * row_total, cols)
    disp2 = displacement.reshape(flat)
    dir2 = direction.reshape(flat)
    load2 = load.reshape(flat)
    node2 = tie_node.reshape(tie_total // 128, 128)
    slot2 = tie_slot.reshape(tie_total // 128, 128)
    owner2 = tie_owner.reshape(1, tie_total)

    def shape(*dims, dtype=F32):
        return jax.ShapeDtypeStruct(dims, dtype)

    assert pb_count == 2 and slots == cols
    smalls = (
        fitting_disp,
        fitting_dir,
        node2,
        owner2,
        slot2,
        b_in.reshape(1, hid),
        b_mid.reshape(1, hid),
        w_in.T,
        w_out,
    )
    outs = pl.pallas_call(
        lambda *refs: gather_nodes(len(smalls), *refs),
        out_shape=[pltpu.VMEM((row_total * COMPS, cols), F32), pltpu.VMEM((2 * COMPS, cols), F32)]
        + [pltpu.VMEM(value.shape, value.dtype) for value in smalls],
        in_specs=local(2 + len(smalls)),
        out_specs=local(2 + len(smalls)),
        name="gather_nodes",
    )(disp2, dir2, *smalls)
    fields, rows, fit_disp, fit_dir, node, owner, slot, b_first, b_second, w_first_in, w_final = outs
    mate = lax.ppermute(rows, "pb", [(0, 1), (1, 0)])

    inputs = tuple(on_chip(value) for value in (fields, fit_disp, fit_dir, node, owner, slot))
    blocks = shape(peers, 3 * COMPS, slots)
    hbm = pl.BlockSpec(memory_space=pl.ANY)
    ties, cols_out, hot_col, hot_slot, hot_row, pay = pl.pallas_call(
        lambda *refs: sum_ties((tx_count, ty_count), *refs),
        out_shape=[
            pltpu.VMEM((COMPS, tie_total), F32),
            pltpu.VMEM((2 * COMPS, cols), F32),
            pltpu.VMEM((cols, tie_total), BF16),
            pltpu.VMEM((slots, tie_total), BF16),
            pltpu.VMEM((row_total, tie_total), BF16),
            blocks,
        ],
        in_specs=local(len(inputs)),
        out_specs=local(5) + [hbm],
        scratch_shapes=[pltpu.VMEM((peers, 2 * COMPS, slots), F32), pltpu.SemaphoreType.DMA(())],
        name="sum_ties",
    )(*inputs)
    inputs = [on_chip(value) for value in (mate, w_first_in, b_first, b_second, w_final)] + [pay]
    w_first, w_last, b_cols, pay = pl.pallas_call(
        lambda *refs: fill_rows((tx_count, ty_count), *refs),
        out_shape=[
            pltpu.VMEM((8 * hid, 4 * COMPS), BF16),
            pltpu.VMEM((128, hid), BF16),
            pltpu.VMEM((hid, 128), F32),
            blocks,
        ],
        in_specs=local(5) + [hbm],
        out_specs=local(3) + [hbm],
        scratch_shapes=[pltpu.VMEM((peers, COMPS, slots), F32), pltpu.SemaphoreType.DMA(())],
        input_output_aliases={5: 3},
        name="fill_rows",
    )(*inputs)
    got = lax.all_to_all(pay, ("tx", "ty"), split_axis=0, concat_axis=0, tiled=True)

    groups = lax.axis_size("groups")
    half = row_total // 2
    cut = half * 3 // 4 // 2 * 2
    chunks = [(0, cut), (cut, half)]
    pieces = [(0, cut - 1), (cut - 1, half + 1)]
    halves = {}
    for name, pick in (("own", None),) if groups == 2 else (("own", 0), ("other", 1)):
        before = ()
        for piece, (begin, end) in enumerate(chunks):
            inputs = (fields, mate, w_first, w_mid, b_cols, w_last, *before)
            low, high = pieces[piece]
            results = [((high - low) * 12, cols), ((half + 3) * COMPS, cols)]
            kept = 2 if end < half else 1
            sent, *before = pl.pallas_call(
                lambda *refs: interior(pick, begin, end, low, high, *refs),
                out_shape=[pltpu.VMEM(size, F32) for size in results[:kept]],
                in_specs=local(len(inputs)),
                out_specs=local(kept),
                scratch_shapes=[pltpu.VMEM(size, F32) for size in results[kept:]],
                name="interior",
            )(*(on_chip(value) for value in inputs))
            halves[name + str(piece)] = sent
            if groups == 2:
                halves["other" + str(piece)] = lax.ppermute(sent, "groups", [(0, 1), (1, 0)])

    named = dict(
        got=got,
        mate=mate,
        fields=fields,
        ties=ties,
        cols=cols_out,
        load=load2,
        w_first=w_first,
        w_mid=w_mid,
        b_mid=b_cols,
        w_last=w_last,
        hot_col=hot_col,
        hot_slot=hot_slot,
        hot_row=hot_row,
        owner=owner,
        fit_disp=fit_disp,
        fit_dir=fit_dir,
        **halves,
    )
    named = {name: on_chip(value) if value.size <= SMALL else value for name, value in named.items()}
    names = list(named) + ["res", "tan", "fit_res", "fit_tan"]
    res, tan, fit_res, fit_tan = pl.pallas_call(
        lambda *refs: finish(names, axes, pieces, groups == 2, *refs),
        out_shape=[shape(*flat), shape(*flat), shape(6, slots), shape(6, slots)],
        in_specs=local(len(named)),
        out_specs=local(4),
        name="finish",
    )(*named.values())
    cube = displacement.shape
    return (res.reshape(cube), tan.reshape(cube), fit_res, fit_tan)


def solution(mesh):
    in_specs = (
        P(None, ("tx", "pb"), "ty"),
        P(None, ("tx", "pb"), "ty"),
        P(None, ("tx", "pb"), "ty"),
        P(),
        P(),
        P(),
        P(),
        P(),
        P(None, ("groups", "tx", "ty", "pb")),
        P(None, ("groups", "tx", "ty", "pb")),
        P(("groups", "tx", "ty", "pb")),
        P(("groups", "tx", "ty", "pb"), None),
        P(("groups", "tx", "ty", "pb")),
    )
    out_specs = (
        P(None, ("groups", "tx", "pb"), "ty"),
        P(None, ("groups", "tx", "pb"), "ty"),
        P(None, ("groups", "tx", "ty", "pb")),
        P(None, ("groups", "tx", "ty", "pb")),
    )
    return jax.shard_map(
        per_device, mesh=mesh, in_specs=in_specs, out_specs=out_specs, check_vma=False
    )
```

```python
import math

import jax
import jax.numpy as jnp
from jax import lax
from jax.experimental import pallas as pl
from jax.experimental.pallas import tpu as pltpu
from jax.sharding import PartitionSpec as P

F32 = jnp.float32
BF16 = jnp.bfloat16
GAUSS = (0.5 - 0.5 / math.sqrt(3.0), 0.5 + 0.5 / math.sqrt(3.0))
COMPS = 16
COUNT_ROW = 6
SPARE_ROWS = (6, 7, 14)
SMALL = 1 << 18


def local(count):
    return [pl.BlockSpec(memory_space=pltpu.VMEM)] * count


def on_chip(value):
    return pltpu.with_memory_space_constraint(value, pltpu.VMEM)


def dot(a, b, dims=((1,), (0,))):
    return lax.dot_general(a, b, (dims, ((), ())), preferred_element_type=F32)


def split(value, terms):
    parts = []
    for _ in range(terms):
        part = value.astype(BF16)
        parts.append(part)
        value = value - part.astype(F32)
    return parts


def rows_of(value):
    return lax.broadcasted_iota(jnp.int32, value, 0)


def lanes_of(value):
    return lax.broadcasted_iota(jnp.int32, value, 1)


def one_hot(index, size):
    shape = (size, index.shape[1])
    return (rows_of(shape) == index).astype(F32).astype(BF16)


def as_line(ref):
    return jnp.concatenate([ref[row : row + 1, :] for row in range(ref.shape[0])], axis=1)


def paired(top, bottom):
    spare = jnp.zeros((2, top.shape[1]), F32)
    return jnp.concatenate([top, spare, bottom, spare], axis=0)


def strain_tile(f00, f10, f01, f11):
    along_low = f10 - f00
    along_high = f11 - f01
    across_low = f01 - f00
    across_high = f11 - f10
    shape = f00.shape
    row = rows_of(shape)
    ones = ((row == 6) | (row == 7) | (row == 14)).astype(F32)
    groups = []
    for frac in GAUSS:
        groups.append((((1.0 - frac) * along_low + frac * along_high) + ones).astype(BF16))
    for frac in GAUSS:
        groups.append(((1.0 - frac) * across_low + frac * across_high).astype(BF16))
    return jnp.concatenate(groups, axis=0)


def stress_sums(strains, w_first, w_mid, b_mid, w_last):
    hid = w_mid.shape[0]
    tasks = [(tile, point) for tile in range(len(strains)) for point in range(4)]
    totals = [[None, None] for _ in strains]

    def layer_one(task):
        tile, point = task
        start = point * 2 * hid
        return (
            dot(w_first[start : start + hid, :], strains[tile]),
            dot(w_first[start + hid : start + 2 * hid, :], strains[tile]),
        )

    def activate(value, slope):
        act = jnp.tanh(value)
        return (act.astype(BF16), ((1.0 - act * act) * slope).astype(BF16))

    def layer_two(hidden):
        bias = b_mid[...]
        value = dot(w_mid[...], hidden[0])
        slope = dot(w_mid[...], hidden[1])
        bias = jnp.concatenate([bias] * (value.shape[1] // bias.shape[1]), axis=1)
        return (value + bias, slope)

    def layer_three(task, hidden):
        tile, point = task
        last = w_last[point * 32 : (point + 1) * 32, :]
        for side in range(2):
            part = dot(last, hidden[side])
            old = totals[tile][side]
            totals[tile][side] = part if old is None else old + part

    ones = {0: layer_one(tasks[0])}
    twos = {}
    for at in range(len(tasks) + 1):
        if at + 1 < len(tasks):
            ones[at + 1] = layer_one(tasks[at + 1])
        if at < len(tasks):
            hidden = activate(*ones.pop(at))
            twos[at] = layer_two(hidden)
        if at >= 1:
            layer_three(tasks[at - 1], activate(*twos.pop(at - 1)))
    return totals


def corner_forces(primal, tangent):
    def both(group):
        return jnp.concatenate([primal[group * 8 : group * 8 + 8], tangent[group * 8 : group * 8 + 8]], axis=0)

    along = (both(0), both(1))
    across = (both(2), both(3))

    def mix(pair, weights):
        return (0.25 * weights[0]) * pair[0] + (0.25 * weights[1]) * pair[1]

    rest = (1.0 - GAUSS[0], 1.0 - GAUSS[1])
    along_rest = mix(along, rest)
    along_frac = mix(along, GAUSS)
    across_rest = mix(across, rest)
    across_frac = mix(across, GAUSS)
    return (
        -along_rest - across_rest,
        along_rest - across_frac,
        across_rest - along_frac,
        along_frac + across_frac,
    )


def gather_nodes(count, disp, dirn, *refs):
    fields, rows = refs[count : count + 2]
    for source, target in zip(refs[:count], refs[count + 2 :]):
        target[...] = source[...]
    row_total = fields.shape[0] // COMPS
    fields[...] = jnp.zeros(fields.shape, F32)
    for comp in range(6):
        part = slice(comp * row_total, (comp + 1) * row_total)
        fields[pl.ds(comp, row_total, stride=COMPS), :] = disp[part, :]
        fields[pl.ds(8 + comp, row_total, stride=COMPS), :] = dirn[part, :]
    rows[0:COMPS, :] = fields[0:COMPS, :]
    rows[COMPS : 2 * COMPS, :] = fields[(row_total - 1) * COMPS :, :]


def sum_ties(peers, *refs):
    (fields, fit_disp, fit_dir, node_ref, owner_ref, slot_ref) = refs[:6]
    (ties, col_out, hot_col_out, hot_slot_out, hot_row_out, pay) = refs[6:]
    row_total = fields.shape[0] // COMPS
    cols = fields.shape[1]
    slots = fit_disp.shape[1]
    tie_total = ties.shape[1]

    lane = lanes_of((COMPS, cols))
    for side, column in enumerate((0, cols - 1)):
        gathered = jnp.zeros((COMPS, cols), F32)
        for row in range(row_total):
            value = fields[row * COMPS : (row + 1) * COMPS, column : column + 1]
            gathered = jnp.where(lane == row, value, gathered)
        col_out[side * COMPS : (side + 1) * COMPS, :] = gathered

    node = as_line(node_ref)
    slot = as_line(slot_ref)
    owner = owner_ref[...]
    node_row = lax.shift_right_logical(node, cols.bit_length() - 1)
    node_col = jnp.bitwise_and(node, cols - 1)
    hot_col = one_hot(node_col, cols)
    hot_col_out[...] = hot_col
    hot_row_out[...] = one_hot(node_row, row_total)
    wide = dot(
        jnp.concatenate(split(fields[...], 2), axis=1), jnp.concatenate([hot_col] * 2, axis=0)
    )
    value = jnp.zeros((COMPS, tie_total), F32)
    for row in range(row_total):
        value = jnp.where(node_row == row, wide[row * COMPS : (row + 1) * COMPS], value)
    value = jnp.where(rows_of(value.shape) == COUNT_ROW, 1.0, value)
    ties[...] = value
    stack = jnp.concatenate(split(value, 2), axis=0)
    hot_slot = one_hot(slot, slots)
    hot_slot_out[...] = hot_slot
    fitting = paired(fit_disp[...], fit_dir[...])

    def bins(first, count):
        lhs = [
            stack * (owner == first + at).astype(F32).astype(BF16) for at in range(count)
        ]
        return dot(jnp.concatenate(lhs, axis=0), hot_slot, ((1,), (1,)))

    def folded(wide_bins, at):
        part = wide_bins[at * 2 * COMPS : (at + 1) * 2 * COMPS]
        return part[0:COMPS] + part[COMPS : 2 * COMPS]

    block = math.gcd(peers, 8)

    def fill(first):
        wide_bins = bins(first, block)
        for peer in range(block):
            pay[first + peer, 0:COMPS, :] = fitting
            pay[first + peer, COMPS : 2 * COMPS, :] = folded(wide_bins, peer)

    if block == peers:
        fill(0)
    else:
        lax.fori_loop(0, peers // block, lambda at, carry: (fill(at * block), carry)[1], 0)


def mate_rows(mate):
    upper = lax.axis_index("pb") == 0
    first, last = mate[0:COMPS, :], mate[COMPS : 2 * COMPS, :]
    return jnp.where(upper, first, last), jnp.where(upper, last, first)


def fill_blocks(axes, row_total, sums, columns, mate, w_in, b_in, b_mid, w_out, out, w_first, w_last, b_cols, pay, done):
    tx_count, ty_count = axes
    along, across = lax.axis_index("tx"), lax.axis_index("ty")
    near, far = mate_rows(mate)
    pay[:, 0 : 2 * COMPS, :] = sums[...]
    ahead = along + 1 - 2 * lax.axis_index("pb")
    for side in (-1, 0, 1):
        over = across + side
        inside = (over >= 0) & (over < ty_count)

        @pl.when(inside & (ahead >= 0) & (ahead < tx_count))
        def _():
            pay[ahead * ty_count + over, 2 * COMPS : 3 * COMPS, :] = far

        if side == 0:
            continue
        edge = 0 if side < 0 else 1
        packed = pack_column(columns[edge * COMPS : (edge + 1) * COMPS, :], row_total)

        @pl.when(inside)
        def _():
            at = along * ty_count + over
            pay[at, 2 * COMPS : 3 * COMPS, :] = near
            for line, row in zip(packed, SPARE_ROWS):
                pay[at, row : row + 1, :] = line

    copy = pltpu.make_async_copy(pay, out, done)
    copy.start()
    build_weights(w_in, b_in, b_mid, w_out, w_first, w_last, b_cols)
    copy.wait()


def pack_column(column, width):
    each = column.shape[1] // width
    lines = []
    for first in range(0, 12, each):
        line = None
        for at in range(first, min(first + each, 12)):
            row = at % 6 + at // 6 * 8
            part = column[row : row + 1]
            if at > first:
                part = pltpu.roll(part, (at - first) * width, 1)
            line = part if line is None else line + part
        lines.append(line)
    assert len(lines) <= len(SPARE_ROWS)
    return lines


def unpack_column(block, width):
    shape = (COMPS, block.shape[1])
    each = shape[1] // width
    row = rows_of(shape)
    column = jnp.zeros(shape, F32)
    for at in range(12):
        spare = SPARE_ROWS[at // each]
        line = block[spare : spare + 1]
        if at % each:
            line = pltpu.roll(line, shape[1] - at % each * width, 1)
        column = jnp.where(row == at % 6 + at // 6 * 8, line, column)
    return jnp.where(lanes_of(shape) < width, column, 0.0)


def build_weights(w_in, b_in, b_mid, w_out, w_first, w_last, b_cols):
    hid = w_in.shape[1]
    bias_rows = split(b_in[...], 3)
    row = rows_of((8, hid))
    stacked = jnp.zeros((8, hid), F32)
    mid_stacked = jnp.zeros((8, hid), F32)
    for at, (one, two) in enumerate(zip(bias_rows, split(b_mid[...], 3))):
        stacked = jnp.where(row == at, one.astype(F32), stacked)
        mid_stacked = jnp.where(row == at, two.astype(F32), mid_stacked)
    lhs = jnp.concatenate([w_in[...].astype(F32), jnp.zeros((4, hid), F32), stacked], axis=0).astype(BF16)
    sel_shape = (24, 4 * COMPS)
    source = rows_of(sel_shape)
    target = lanes_of(sel_shape)
    for point in range(4):
        a_base = (point // 2) * COMPS
        c_base = (2 + point % 2) * COMPS
        for side in range(2):
            hit = (source < 6) & (target == a_base + 8 * side + source)
            hit = hit | ((source >= 6) & (source < 12) & (target == c_base + 8 * side + source - 6))
            if side == 0:
                for at, spot in enumerate((6, 7, 14)):
                    hit = hit | ((source == 16 + at) & (target == a_base + spot))
            block = dot(lhs, hit.astype(F32).astype(BF16), ((0,), (0,)))
            start = (2 * point + side) * hid
            w_first[start : start + hid, :] = block.astype(BF16)
    ones = (rows_of((8, 128)) < 3).astype(F32).astype(BF16)
    b_cols[...] = dot(mid_stacked.astype(BF16), ones, ((0,), (0,)))
    last_shape = (128, 12)
    target = rows_of(last_shape)
    source = lanes_of(last_shape)
    hit = target < 0
    for point in range(4):
        a_base = point * 32 + (point // 2) * 8
        c_base = point * 32 + 16 + (point % 2) * 8
        hit = hit | ((source < 6) & (target == a_base + source))
        hit = hit | ((source >= 6) & (target == c_base + source - 6))
    w_last[...] = dot(hit.astype(F32).astype(BF16), w_out[...]).astype(BF16)


def interior(pick, fields, mate, w_first, w_mid, b_cols, w_last, sent, forces):
    row_total, cols = fields.shape[0] // COMPS, fields.shape[1]
    half = row_total // 2
    held = half + 1
    group = lax.axis_index("groups") if pick is None else pick
    core = lax.axis_index("pb")
    first = group * half - core
    near, _ = mate_rows(mate)
    lines = []
    for at in range(half + 1):
        row = first + at
        if at == 0:
            row = jnp.maximum(row, 0)
        if at == half:
            row = jnp.minimum(row, row_total - 1)
        base = fields[pl.ds(pl.multiple_of(row * COMPS, COMPS), COMPS), :]
        if at == 0:
            base = jnp.where((core == 1) & (group == 0), near, base)
        if at == half:
            base = jnp.where((core == 0) & (group == 1), near, base)
        lines.append((base, pltpu.roll(base, cols - 1, 1)))
    tiles = [
        strain_tile(lines[at][0], lines[at + 1][0], lines[at][1], lines[at + 1][1]) for at in range(half)
    ]
    tiles = [jnp.concatenate(tiles[at : at + 2], axis=1) for at in range(0, half, 2)]
    sums = stress_sums(tiles, w_first, w_mid, b_cols, w_last)
    keep = lanes_of((COMPS, cols)) < cols - 1
    forces[...] = jnp.zeros(forces.shape, F32)
    for tile, (primal, tangent) in enumerate(sums):
        for side in range(2):
            lanes = slice(side * cols, (side + 1) * cols)
            parts = corner_forces(primal[:, lanes], tangent[:, lanes])
            base, right, upper, corner = (jnp.where(keep, part, 0.0) for part in parts)
            at = (2 * tile + side + 1) * COMPS
            forces[at : at + COMPS, :] += base + pltpu.roll(upper, 1, 1)
            forces[at + COMPS : at + 2 * COMPS, :] += right + pltpu.roll(corner, 1, 1)
    start = 1 + group * (row_total - held) - first
    for comp in range(12):
        rows = pl.ds(start * COMPS + comp % 6 + comp // 6 * 8, held, stride=COMPS)
        sent[comp * held : (comp + 1) * held, :] = forces[rows, :]


def edges(names, axes, *refs):
    ref = dict(zip(names, refs))
    tx_count, ty_count, pb_count = axes
    fields, ties, partial, got = ref["fields"], ref["ties"], ref["partial"], ref["got"]
    row_total, cols = fields.shape[0] // COMPS, fields.shape[1]
    slots = got.shape[2]
    tie_total = ties.shape[1]
    lane = lanes_of((COMPS, cols))
    core = lax.axis_index("pb")
    across = lax.axis_index("ty")
    along = lax.axis_index("tx")
    place = along * pb_count + core

    def around(step, side, packed=False):
        there, over = along + step, across + side
        valid = (there >= 0) & (there < tx_count) & (over >= 0) & (over < ty_count)
        block = got.at[jnp.where(valid, there * ty_count + over, 0)]
        if packed:
            value = unpack_column(block[0:COMPS, :], row_total)
        else:
            value = block[2 * COMPS : 3 * COMPS, :]
        return jnp.where(valid, value, 0.0)

    upper = core == 0
    behind = 2 * core - 1
    near, _ = mate_rows(ref["mate"])
    rows_near = (around(0, -1), near, around(0, 1))
    rows_far = tuple(around(behind, side) for side in (-1, 0, 1))
    next_rows = [jnp.where(upper, one, two) for one, two in zip(rows_near, rows_far)]
    prev_rows = [jnp.where(upper, two, one) for one, two in zip(rows_near, rows_far)]
    prev_row, next_row = prev_rows[1], next_rows[1]
    next_col = around(0, 1, True)
    prev_col = around(0, -1, True)
    next_corner = (prev_rows[2][:, 0:1], next_rows[2][:, 0:1])
    prev_corner = (prev_rows[0][:, cols - 1 : cols], next_rows[0][:, cols - 1 : cols])

    def column(inner, before, after):
        line = pltpu.roll(inner, 1, 1)
        line = jnp.where(lane == 0, before, line)
        return jnp.where(lane == row_total + 1, after, line)

    own_cols = ref["cols"]
    line_prev = column(prev_col, prev_corner[0], prev_corner[1])
    line_next = column(next_col, next_corner[0], next_corner[1])
    line_first = column(own_cols[0:COMPS, :], prev_row[:, 0:1], next_row[:, 0:1])
    line_final = column(
        own_cols[COMPS : 2 * COMPS, :], prev_row[:, cols - 1 : cols], next_row[:, cols - 1 : cols]
    )

    def shifted(row_value, beyond):
        return jnp.where(lane == cols - 1, beyond, pltpu.roll(row_value, cols - 1, 1))

    first_row = fields[0:COMPS, :]
    last_row = fields[(row_total - 1) * COMPS :, :]
    far_row = rows_far[1]
    lower_row = jnp.where(upper, far_row, last_row)
    upper_row = jnp.where(upper, first_row, far_row)
    own_beyond = jnp.where(upper, next_col[:, 0:1], next_col[:, row_total - 1 : row_total])
    far_beyond = rows_far[2][:, 0:1]
    tile_far = strain_tile(
        lower_row,
        upper_row,
        shifted(lower_row, jnp.where(upper, far_beyond, own_beyond)),
        shifted(upper_row, jnp.where(upper, own_beyond, far_beyond)),
    )
    half = cols // 2
    low = lane < half
    back = cols - 1

    def two(left, right_line):
        return jnp.where(low, left, pltpu.roll(right_line, half, 1))

    left_base = two(line_prev, line_final)
    left_upper = two(line_first, line_next)
    right_base = two(pltpu.roll(line_prev, back, 1), pltpu.roll(line_final, back, 1))
    right_upper = two(pltpu.roll(line_first, back, 1), pltpu.roll(line_next, back, 1))
    tile_side = strain_tile(left_base, right_base, left_upper, right_upper)

    edge_tile = jnp.concatenate((tile_far, tile_side), axis=1)
    primal, tangent = stress_sums([edge_tile], ref["w_first"], ref["w_mid"], ref["b_mid"], ref["w_last"])[0]
    f_base, f_right, f_upper, f_corner = corner_forces(primal[:, :cols], tangent[:, :cols])
    s_base, s_right, s_upper, s_corner = corner_forces(primal[:, cols:], tangent[:, cols:])

    def mask(value, keep):
        return jnp.where(keep, value, 0.0)

    def moved(value):
        return pltpu.roll(mask(value, lane < cols - 1), 1, 1)

    has_row = place > 0
    has_col = across > 0
    row_first = mask(f_right + moved(f_corner), upper & has_row)
    row_last = mask(f_base + moved(f_upper), core == 1)
    first_lane = jnp.where(has_row, 0, 1)
    s_corner = mask(s_corner, (lane >= first_lane) & (lane < row_total))
    s_upper = mask(s_upper, (lane >= 1) & (lane <= row_total))
    col_first = mask(pltpu.roll(s_upper, back, 1) + s_corner, has_col)
    valid = (lane >= half + 1 - core) & (lane <= half + row_total - core)
    s_base = mask(s_base, valid)
    s_right = mask(s_right, valid)
    col_last = pltpu.roll(pltpu.roll(s_base, back, 1) + s_right, cols - half, 1)

    owner = ref["owner"][...]
    hot_slot = ref["hot_slot"][...]
    hot_two = jnp.concatenate([hot_slot] * 2, axis=0)
    fit_value = jnp.zeros((COMPS, tie_total), F32)
    bins = jnp.zeros((COMPS, slots), F32)
    peers = tx_count * ty_count
    block = math.gcd(peers, 8)

    def collect(first, carry):
        fit_value, bins = carry
        parts = [got[first + peer] for peer in range(block)]
        fit_all = jnp.concatenate([part[0:COMPS] for part in parts], axis=0)
        wide = dot(jnp.concatenate(split(fit_all, 2), axis=1), hot_two)
        for peer, part in enumerate(parts):
            fit_value = jnp.where(owner == first + peer, wide[peer * COMPS : (peer + 1) * COMPS], fit_value)
            bins = bins + part[COMPS : 2 * COMPS]
        return fit_value, bins

    if block == peers:
        fit_value, bins = collect(0, (fit_value, bins))
    else:
        fit_value, bins = lax.fori_loop(
            0, peers // block, lambda at, carry: collect(at * block, carry), (fit_value, bins)
        )
    count = bins[COUNT_ROW : COUNT_ROW + 1]
    for out, fit, base in (("fit_res", "fit_disp", 0), ("fit_tan", "fit_dir", 8)):
        ref[out][...] = 2.0 * (count * ref[fit][...] - bins[base : base + 6])

    pulled = split(2.0 * (ties[...] - fit_value), 2)
    hot_row = ref["hot_row"][...]
    places = [comp % 6 + comp // 6 * 8 for comp in range(12)]
    lhs = [
        jnp.concatenate([hot_row * part[place_of : place_of + 1] for part in pulled], axis=1)
        for place_of in places
    ]
    hot_col = ref["hot_col"][...]
    tie_forces = dot(jnp.concatenate(lhs, axis=0), jnp.concatenate([hot_col] * 2, axis=1), ((1,), (1,)))

    assert 4 * row_total <= cols
    line = jnp.zeros((COMPS, cols), F32)
    for at, part in enumerate(split(col_first, 2) + split(col_last, 2)):
        part = part.astype(F32)
        part = pltpu.roll(part, at * row_total, 1) if at else part
        line = jnp.where((lane >= at * row_total) & (lane < (at + 1) * row_total), part, line)
    shape = (row_total, cols)
    eye = jnp.bitwise_and(lanes_of(shape), row_total - 1) == rows_of(shape)
    lhs = [jnp.where(eye, line[place_of : place_of + 1], 0.0).astype(BF16) for place_of in places]
    shape = (cols, cols)
    in_first = (rows_of(shape) == 0) & (lanes_of(shape) < 2 * row_total)
    in_last = (rows_of(shape) == cols - 1) & (lanes_of(shape) >= 2 * row_total)
    ends = (in_first | (in_last & (lanes_of(shape) < 4 * row_total))).astype(F32).astype(BF16)
    col_forces = dot(jnp.concatenate(lhs, axis=0), ends, ((1,), (1,)))

    row = rows_of((row_total, cols))
    for comp, place_of in enumerate(places):
        rows = slice(comp * row_total, (comp + 1) * row_total)
        value = tie_forces[rows] + col_forces[rows]
        value = value + jnp.where(row == 0, row_first[place_of : place_of + 1], 0.0)
        value = value + jnp.where(row == row_total - 1, row_last[place_of : place_of + 1], 0.0)
        partial[rows, :] = value - ref["load"][rows, :] if comp < 6 else value


def combine(swapped, partial, own, other, res, tan):
    row_total = partial.shape[0] // 12
    held = own.shape[0] // 12
    skip = row_total - held
    here = lax.axis_index("groups") == 0
    for comp in range(12):
        target = res if comp < 6 else tan
        start = comp % 6 * row_total
        rows = slice(comp * held, (comp + 1) * held)
        first, second = own[rows, :], other[rows, :]
        if swapped:
            first, second = jnp.where(here, first, second), jnp.where(here, second, first)
        target[start : start + row_total, :] = partial[comp * row_total : (comp + 1) * row_total, :]
        target[start : start + held, :] += first
        target[start + skip : start + row_total, :] += second


def per_device(
    displacement,
    direction,
    load,
    w_in,
    b_in,
    w_mid,
    b_mid,
    w_out,
    fitting_disp,
    fitting_dir,
    tie_node,
    tie_owner,
    tie_slot,
):
    tx_count = lax.axis_size("tx")
    ty_count = lax.axis_size("ty")
    pb_count = lax.axis_size("pb")
    peers = tx_count * ty_count
    axes = (tx_count, ty_count, pb_count)
    _, row_total, cols = displacement.shape
    slots = fitting_disp.shape[1]
    tie_total = tie_node.shape[0]
    hid = w_mid.shape[0]
    flat = (6 * row_total, cols)
    disp2 = displacement.reshape(flat)
    dir2 = direction.reshape(flat)
    load2 = load.reshape(flat)
    node2 = tie_node.reshape(tie_total // 128, 128)
    slot2 = tie_slot.reshape(tie_total // 128, 128)
    owner2 = tie_owner.reshape(1, tie_total)

    def shape(*dims, dtype=F32):
        return jax.ShapeDtypeStruct(dims, dtype)

    assert pb_count == 2 and slots == cols
    smalls = (
        fitting_disp,
        fitting_dir,
        node2,
        owner2,
        slot2,
        b_in.reshape(1, hid),
        b_mid.reshape(1, hid),
        w_in.T,
        w_out,
    )
    outs = pl.pallas_call(
        lambda *refs: gather_nodes(len(smalls), *refs),
        out_shape=[pltpu.VMEM((row_total * COMPS, cols), F32), pltpu.VMEM((2 * COMPS, cols), F32)]
        + [pltpu.VMEM(value.shape, value.dtype) for value in smalls],
        in_specs=local(2 + len(smalls)),
        out_specs=local(2 + len(smalls)),
        name="gather_nodes",
    )(disp2, dir2, *smalls)
    fields, rows, fit_disp, fit_dir, node, owner, slot, b_first, b_second, w_first_in, w_final = outs
    mate = lax.ppermute(rows, "pb", [(0, 1), (1, 0)])

    inputs = tuple(on_chip(value) for value in (fields, fit_disp, fit_dir, node, owner, slot))
    small = peers * 2 * COMPS * slots <= SMALL
    ties, cols_out, hot_col, hot_slot, hot_row, sums = pl.pallas_call(
        lambda *refs: sum_ties(peers, *refs),
        out_shape=[
            pltpu.VMEM((COMPS, tie_total), F32),
            pltpu.VMEM((2 * COMPS, cols), F32),
            pltpu.VMEM((cols, tie_total), BF16),
            pltpu.VMEM((slots, tie_total), BF16),
            pltpu.VMEM((row_total, tie_total), BF16),
            (pltpu.VMEM if small else jax.ShapeDtypeStruct)((peers, 2 * COMPS, slots), F32),
        ],
        in_specs=local(len(inputs)),
        out_specs=local(6),
        name="sum_ties",
    )(*inputs)
    inputs = (sums, cols_out, mate, w_first_in, b_first, b_second, w_final)
    inputs = [on_chip(value) if value.size <= SMALL else value for value in inputs]
    pay, w_first, w_last, b_cols = pl.pallas_call(
        lambda *refs: fill_blocks((tx_count, ty_count), row_total, *refs),
        out_shape=[
            shape(peers, 3 * COMPS, slots),
            pltpu.VMEM((8 * hid, 4 * COMPS), BF16),
            pltpu.VMEM((128, hid), BF16),
            pltpu.VMEM((hid, 128), F32),
        ],
        in_specs=local(len(inputs)),
        out_specs=[pl.BlockSpec(memory_space=pl.ANY)] + local(3),
        scratch_shapes=[pltpu.VMEM((peers, 3 * COMPS, slots), F32), pltpu.SemaphoreType.DMA(())],
        name="fill_blocks",
    )(*inputs)
    got = lax.all_to_all(pay, ("tx", "ty"), split_axis=0, concat_axis=0, tiled=True)

    inputs = tuple(on_chip(value) for value in (fields, mate, w_first, w_mid, b_cols, w_last))
    groups = lax.axis_size("groups")
    halves = []
    for pick in (None,) if groups == 2 else (0, 1):
        half = pl.pallas_call(
            lambda *refs: interior(pick, *refs),
            out_shape=pltpu.VMEM(((row_total // 2 + 1) * 12, cols), F32),
            in_specs=local(len(inputs)),
            out_specs=local(1)[0],
            scratch_shapes=[pltpu.VMEM(((row_total // 2 + 3) * COMPS, cols), F32)],
            name="interior",
        )(*inputs)
        halves.append(half)
    if groups == 2:
        halves.append(lax.ppermute(halves[0], "groups", [(0, 1), (1, 0)]))

    named = dict(
        got=got,
        mate=mate,
        fields=fields,
        ties=ties,
        cols=cols_out,
        w_first=w_first,
        w_mid=w_mid,
        b_mid=b_cols,
        w_last=w_last,
        hot_col=hot_col,
        hot_slot=hot_slot,
        hot_row=hot_row,
        load=load2,
        owner=owner,
        fit_disp=fit_disp,
        fit_dir=fit_dir,
    )
    named = {name: on_chip(value) if value.size <= SMALL else value for name, value in named.items()}
    names = list(named)
    partial, fit_res, fit_tan = pl.pallas_call(
        lambda *refs: edges(names + ["partial", "fit_res", "fit_tan"], axes, *refs),
        out_shape=[pltpu.VMEM((12 * row_total, cols), F32), shape(6, slots), shape(6, slots)],
        in_specs=local(len(names)),
        out_specs=local(3),
        name="edges",
    )(*named.values())

    inputs = tuple(on_chip(value) for value in (partial, halves[0], halves[1]))
    res, tan = pl.pallas_call(
        lambda *refs: combine(groups == 2, *refs),
        out_shape=[shape(*flat), shape(*flat)],
        in_specs=local(len(inputs)),
        out_specs=local(2),
        name="combine",
    )(*inputs)
    cube = displacement.shape
    return (res.reshape(cube), tan.reshape(cube), fit_res, fit_tan)


def solution(mesh):
    in_specs = (
        P(None, ("tx", "pb"), "ty"),
        P(None, ("tx", "pb"), "ty"),
        P(None, ("tx", "pb"), "ty"),
        P(),
        P(),
        P(),
        P(),
        P(),
        P(None, ("groups", "tx", "ty", "pb")),
        P(None, ("groups", "tx", "ty", "pb")),
        P(("groups", "tx", "ty", "pb")),
        P(("groups", "tx", "ty", "pb"), None),
        P(("groups", "tx", "ty", "pb")),
    )
    out_specs = (
        P(None, ("groups", "tx", "pb"), "ty"),
        P(None, ("groups", "tx", "pb"), "ty"),
        P(None, ("groups", "tx", "ty", "pb")),
        P(None, ("groups", "tx", "ty", "pb")),
    )
    return jax.shard_map(
        per_device, mesh=mesh, in_specs=in_specs, out_specs=out_specs, check_vma=False
    )
```

```python
import math

import jax
import jax.numpy as jnp
from jax import lax
from jax.experimental import pallas as pl
from jax.experimental.pallas import tpu as pltpu
from jax.sharding import PartitionSpec as P

F32 = jnp.float32
BF16 = jnp.bfloat16
GAUSS = (0.5 - 0.5 / math.sqrt(3.0), 0.5 + 0.5 / math.sqrt(3.0))
COMPS = 16
COUNT_ROW = 6
SPARE_ROWS = (6, 7, 14)
SMALL = 1 << 18


def local(count):
    return [pl.BlockSpec(memory_space=pltpu.VMEM)] * count


def on_chip(value):
    return pltpu.with_memory_space_constraint(value, pltpu.VMEM)


def dot(a, b, dims=((1,), (0,))):
    return lax.dot_general(a, b, (dims, ((), ())), preferred_element_type=F32)


def split(value, terms):
    parts = []
    for _ in range(terms):
        part = value.astype(BF16)
        parts.append(part)
        value = value - part.astype(F32)
    return parts


def rows_of(value):
    return lax.broadcasted_iota(jnp.int32, value, 0)


def lanes_of(value):
    return lax.broadcasted_iota(jnp.int32, value, 1)


def one_hot(index, size):
    shape = (size, index.shape[1])
    return (rows_of(shape) == index).astype(F32).astype(BF16)


def as_line(ref):
    return jnp.concatenate([ref[row : row + 1, :] for row in range(ref.shape[0])], axis=1)


def paired(top, bottom):
    spare = jnp.zeros((2, top.shape[1]), F32)
    return jnp.concatenate([top, spare, bottom, spare], axis=0)


def strain_tile(f00, f10, f01, f11):
    along_low = f10 - f00
    along_high = f11 - f01
    across_low = f01 - f00
    across_high = f11 - f10
    shape = f00.shape
    row = rows_of(shape)
    ones = ((row == 6) | (row == 7) | (row == 14)).astype(F32)
    groups = []
    for frac in GAUSS:
        groups.append((((1.0 - frac) * along_low + frac * along_high) + ones).astype(BF16))
    for frac in GAUSS:
        groups.append(((1.0 - frac) * across_low + frac * across_high).astype(BF16))
    return jnp.concatenate(groups, axis=0)


def stress_sums(strains, w_first, w_mid, b_mid, w_last):
    hid = w_mid.shape[0]
    tasks = [(tile, point) for tile in range(len(strains)) for point in range(4)]
    totals = [[None, None] for _ in strains]

    def layer_one(task):
        tile, point = task
        start = point * 2 * hid
        return (
            dot(w_first[start : start + hid, :], strains[tile]),
            dot(w_first[start + hid : start + 2 * hid, :], strains[tile]),
        )

    def activate(value, slope):
        act = jnp.tanh(value)
        return (act.astype(BF16), ((1.0 - act * act) * slope).astype(BF16))

    def layer_two(hidden):
        bias = b_mid[...]
        value = dot(w_mid[...], hidden[0])
        slope = dot(w_mid[...], hidden[1])
        bias = jnp.concatenate([bias] * (value.shape[1] // bias.shape[1]), axis=1)
        return (value + bias, slope)

    def layer_three(task, hidden):
        tile, point = task
        last = w_last[point * 32 : (point + 1) * 32, :]
        for side in range(2):
            part = dot(last, hidden[side])
            old = totals[tile][side]
            totals[tile][side] = part if old is None else old + part

    ones = {0: layer_one(tasks[0])}
    twos = {}
    for at in range(len(tasks) + 1):
        if at + 1 < len(tasks):
            ones[at + 1] = layer_one(tasks[at + 1])
        if at < len(tasks):
            hidden = activate(*ones.pop(at))
            twos[at] = layer_two(hidden)
        if at >= 1:
            layer_three(tasks[at - 1], activate(*twos.pop(at - 1)))
    return totals


def corner_forces(primal, tangent):
    def both(group):
        return jnp.concatenate([primal[group * 8 : group * 8 + 8], tangent[group * 8 : group * 8 + 8]], axis=0)

    along = (both(0), both(1))
    across = (both(2), both(3))

    def mix(pair, weights):
        return (0.25 * weights[0]) * pair[0] + (0.25 * weights[1]) * pair[1]

    rest = (1.0 - GAUSS[0], 1.0 - GAUSS[1])
    along_rest = mix(along, rest)
    along_frac = mix(along, GAUSS)
    across_rest = mix(across, rest)
    across_frac = mix(across, GAUSS)
    return (
        -along_rest - across_rest,
        along_rest - across_frac,
        across_rest - along_frac,
        along_frac + across_frac,
    )


def gather_nodes(count, disp, dirn, *refs):
    fields, rows = refs[count : count + 2]
    for source, target in zip(refs[:count], refs[count + 2 :]):
        target[...] = source[...]
    row_total = fields.shape[0] // COMPS
    fields[...] = jnp.zeros(fields.shape, F32)
    for comp in range(6):
        part = slice(comp * row_total, (comp + 1) * row_total)
        fields[pl.ds(comp, row_total, stride=COMPS), :] = disp[part, :]
        fields[pl.ds(8 + comp, row_total, stride=COMPS), :] = dirn[part, :]
    rows[0:COMPS, :] = fields[0:COMPS, :]
    rows[COMPS : 2 * COMPS, :] = fields[(row_total - 1) * COMPS :, :]


def sum_ties(peers, *refs):
    (fields, fit_disp, fit_dir, node_ref, owner_ref, slot_ref) = refs[:6]
    (ties, col_out, hot_col_out, hot_slot_out, hot_row_out, pay) = refs[6:]
    row_total = fields.shape[0] // COMPS
    cols = fields.shape[1]
    slots = fit_disp.shape[1]
    tie_total = ties.shape[1]

    lane = lanes_of((COMPS, cols))
    for side, column in enumerate((0, cols - 1)):
        gathered = jnp.zeros((COMPS, cols), F32)
        for row in range(row_total):
            value = fields[row * COMPS : (row + 1) * COMPS, column : column + 1]
            gathered = jnp.where(lane == row, value, gathered)
        col_out[side * COMPS : (side + 1) * COMPS, :] = gathered

    node = as_line(node_ref)
    slot = as_line(slot_ref)
    owner = owner_ref[...]
    node_row = lax.shift_right_logical(node, cols.bit_length() - 1)
    node_col = jnp.bitwise_and(node, cols - 1)
    hot_col = one_hot(node_col, cols)
    hot_col_out[...] = hot_col
    hot_row_out[...] = one_hot(node_row, row_total)
    wide = dot(
        jnp.concatenate(split(fields[...], 2), axis=1), jnp.concatenate([hot_col] * 2, axis=0)
    )
    value = jnp.zeros((COMPS, tie_total), F32)
    for row in range(row_total):
        value = jnp.where(node_row == row, wide[row * COMPS : (row + 1) * COMPS], value)
    value = jnp.where(rows_of(value.shape) == COUNT_ROW, 1.0, value)
    ties[...] = value
    stack = jnp.concatenate(split(value, 2), axis=0)
    hot_slot = one_hot(slot, slots)
    hot_slot_out[...] = hot_slot
    fitting = paired(fit_disp[...], fit_dir[...])

    def bins(first, count):
        lhs = [
            stack * (owner == first + at).astype(F32).astype(BF16) for at in range(count)
        ]
        return dot(jnp.concatenate(lhs, axis=0), hot_slot, ((1,), (1,)))

    def folded(wide_bins, at):
        part = wide_bins[at * 2 * COMPS : (at + 1) * 2 * COMPS]
        return part[0:COMPS] + part[COMPS : 2 * COMPS]

    block = math.gcd(peers, 8)

    def fill(first):
        wide_bins = bins(first, block)
        for peer in range(block):
            pay[first + peer, 0:COMPS, :] = fitting
            pay[first + peer, COMPS : 2 * COMPS, :] = folded(wide_bins, peer)

    if block == peers:
        fill(0)
    else:
        lax.fori_loop(0, peers // block, lambda at, carry: (fill(at * block), carry)[1], 0)


def mate_rows(mate):
    upper = lax.axis_index("pb") == 0
    first, last = mate[0:COMPS, :], mate[COMPS : 2 * COMPS, :]
    return jnp.where(upper, first, last), jnp.where(upper, last, first)


def fill_blocks(axes, row_total, sums, columns, mate, w_in, b_in, b_mid, w_out, out, w_first, w_last, b_cols, pay, done):
    tx_count, ty_count = axes
    along, across = lax.axis_index("tx"), lax.axis_index("ty")
    near, far = mate_rows(mate)
    pay[:, 0 : 2 * COMPS, :] = sums[...]
    ahead = along + 1 - 2 * lax.axis_index("pb")
    for side in (-1, 0, 1):
        over = across + side
        inside = (over >= 0) & (over < ty_count)

        @pl.when(inside & (ahead >= 0) & (ahead < tx_count))
        def _():
            pay[ahead * ty_count + over, 2 * COMPS : 3 * COMPS, :] = far

        if side == 0:
            continue
        edge = 0 if side < 0 else 1
        packed = pack_column(columns[edge * COMPS : (edge + 1) * COMPS, :], row_total)

        @pl.when(inside)
        def _():
            at = along * ty_count + over
            pay[at, 2 * COMPS : 3 * COMPS, :] = near
            for line, row in zip(packed, SPARE_ROWS):
                pay[at, row : row + 1, :] = line

    copy = pltpu.make_async_copy(pay, out, done)
    copy.start()
    build_weights(w_in, b_in, b_mid, w_out, w_first, w_last, b_cols)
    copy.wait()


def pack_column(column, width):
    each = column.shape[1] // width
    lines = []
    for first in range(0, 12, each):
        line = None
        for at in range(first, min(first + each, 12)):
            row = at % 6 + at // 6 * 8
            part = column[row : row + 1]
            if at > first:
                part = pltpu.roll(part, (at - first) * width, 1)
            line = part if line is None else line + part
        lines.append(line)
    assert len(lines) <= len(SPARE_ROWS)
    return lines


def unpack_column(block, width):
    shape = (COMPS, block.shape[1])
    each = shape[1] // width
    row = rows_of(shape)
    column = jnp.zeros(shape, F32)
    for at in range(12):
        spare = SPARE_ROWS[at // each]
        line = block[spare : spare + 1]
        if at % each:
            line = pltpu.roll(line, shape[1] - at % each * width, 1)
        column = jnp.where(row == at % 6 + at // 6 * 8, line, column)
    return jnp.where(lanes_of(shape) < width, column, 0.0)


def build_weights(w_in, b_in, b_mid, w_out, w_first, w_last, b_cols):
    hid = w_in.shape[1]
    bias_rows = split(b_in[...], 3)
    row = rows_of((8, hid))
    stacked = jnp.zeros((8, hid), F32)
    mid_stacked = jnp.zeros((8, hid), F32)
    for at, (one, two) in enumerate(zip(bias_rows, split(b_mid[...], 3))):
        stacked = jnp.where(row == at, one.astype(F32), stacked)
        mid_stacked = jnp.where(row == at, two.astype(F32), mid_stacked)
    lhs = jnp.concatenate([w_in[...].astype(F32), jnp.zeros((4, hid), F32), stacked], axis=0).astype(BF16)
    sel_shape = (24, 4 * COMPS)
    source = rows_of(sel_shape)
    target = lanes_of(sel_shape)
    for point in range(4):
        a_base = (point // 2) * COMPS
        c_base = (2 + point % 2) * COMPS
        for side in range(2):
            hit = (source < 6) & (target == a_base + 8 * side + source)
            hit = hit | ((source >= 6) & (source < 12) & (target == c_base + 8 * side + source - 6))
            if side == 0:
                for at, spot in enumerate((6, 7, 14)):
                    hit = hit | ((source == 16 + at) & (target == a_base + spot))
            block = dot(lhs, hit.astype(F32).astype(BF16), ((0,), (0,)))
            start = (2 * point + side) * hid
            w_first[start : start + hid, :] = block.astype(BF16)
    ones = (rows_of((8, 128)) < 3).astype(F32).astype(BF16)
    b_cols[...] = dot(mid_stacked.astype(BF16), ones, ((0,), (0,)))
    last_shape = (128, 12)
    target = rows_of(last_shape)
    source = lanes_of(last_shape)
    hit = target < 0
    for point in range(4):
        a_base = point * 32 + (point // 2) * 8
        c_base = point * 32 + 16 + (point % 2) * 8
        hit = hit | ((source < 6) & (target == a_base + source))
        hit = hit | ((source >= 6) & (target == c_base + source - 6))
    w_last[...] = dot(hit.astype(F32).astype(BF16), w_out[...]).astype(BF16)


def interior(pick, fields, mate, w_first, w_mid, b_cols, w_last, sent, forces):
    row_total, cols = fields.shape[0] // COMPS, fields.shape[1]
    half = row_total // 2
    held = half + 1
    group = lax.axis_index("groups") if pick is None else pick
    core = lax.axis_index("pb")
    first = group * half - core
    near, _ = mate_rows(mate)
    lines = []
    for at in range(half + 1):
        row = first + at
        if at == 0:
            row = jnp.maximum(row, 0)
        if at == half:
            row = jnp.minimum(row, row_total - 1)
        base = fields[pl.ds(pl.multiple_of(row * COMPS, COMPS), COMPS), :]
        if at == 0:
            base = jnp.where((core == 1) & (group == 0), near, base)
        if at == half:
            base = jnp.where((core == 0) & (group == 1), near, base)
        lines.append((base, pltpu.roll(base, cols - 1, 1)))
    tiles = [
        strain_tile(lines[at][0], lines[at + 1][0], lines[at][1], lines[at + 1][1]) for at in range(half)
    ]
    tiles = [jnp.concatenate(tiles[at : at + 2], axis=1) for at in range(0, half, 2)]
    sums = stress_sums(tiles, w_first, w_mid, b_cols, w_last)
    keep = lanes_of((COMPS, cols)) < cols - 1
    forces[...] = jnp.zeros(forces.shape, F32)
    for tile, (primal, tangent) in enumerate(sums):
        for side in range(2):
            lanes = slice(side * cols, (side + 1) * cols)
            parts = corner_forces(primal[:, lanes], tangent[:, lanes])
            base, right, upper, corner = (jnp.where(keep, part, 0.0) for part in parts)
            at = (2 * tile + side + 1) * COMPS
            forces[at : at + COMPS, :] += base + pltpu.roll(upper, 1, 1)
            forces[at + COMPS : at + 2 * COMPS, :] += right + pltpu.roll(corner, 1, 1)
    start = 1 + group * (row_total - held) - first
    for comp in range(12):
        rows = pl.ds(start * COMPS + comp % 6 + comp // 6 * 8, held, stride=COMPS)
        sent[comp * held : (comp + 1) * held, :] = forces[rows, :]


def edges(names, axes, *refs):
    ref = dict(zip(names, refs))
    tx_count, ty_count, pb_count = axes
    fields, ties, partial, got = ref["fields"], ref["ties"], ref["partial"], ref["got"]
    row_total, cols = fields.shape[0] // COMPS, fields.shape[1]
    slots = got.shape[2]
    tie_total = ties.shape[1]
    lane = lanes_of((COMPS, cols))
    core = lax.axis_index("pb")
    across = lax.axis_index("ty")
    along = lax.axis_index("tx")
    place = along * pb_count + core

    def around(step, side, packed=False):
        there, over = along + step, across + side
        valid = (there >= 0) & (there < tx_count) & (over >= 0) & (over < ty_count)
        block = got.at[jnp.where(valid, there * ty_count + over, 0)]
        if packed:
            value = unpack_column(block[0:COMPS, :], row_total)
        else:
            value = block[2 * COMPS : 3 * COMPS, :]
        return jnp.where(valid, value, 0.0)

    upper = core == 0
    behind = 2 * core - 1
    near, _ = mate_rows(ref["mate"])
    rows_near = (around(0, -1), near, around(0, 1))
    rows_far = tuple(around(behind, side) for side in (-1, 0, 1))
    next_rows = [jnp.where(upper, one, two) for one, two in zip(rows_near, rows_far)]
    prev_rows = [jnp.where(upper, two, one) for one, two in zip(rows_near, rows_far)]
    prev_row, next_row = prev_rows[1], next_rows[1]
    next_col = around(0, 1, True)
    prev_col = around(0, -1, True)
    next_corner = (prev_rows[2][:, 0:1], next_rows[2][:, 0:1])
    prev_corner = (prev_rows[0][:, cols - 1 : cols], next_rows[0][:, cols - 1 : cols])

    def column(inner, before, after):
        line = pltpu.roll(inner, 1, 1)
        line = jnp.where(lane == 0, before, line)
        return jnp.where(lane == row_total + 1, after, line)

    own_cols = ref["cols"]
    line_prev = column(prev_col, prev_corner[0], prev_corner[1])
    line_next = column(next_col, next_corner[0], next_corner[1])
    line_first = column(own_cols[0:COMPS, :], prev_row[:, 0:1], next_row[:, 0:1])
    line_final = column(
        own_cols[COMPS : 2 * COMPS, :], prev_row[:, cols - 1 : cols], next_row[:, cols - 1 : cols]
    )

    def shifted(row_value, beyond):
        return jnp.where(lane == cols - 1, beyond, pltpu.roll(row_value, cols - 1, 1))

    first_row = fields[0:COMPS, :]
    last_row = fields[(row_total - 1) * COMPS :, :]
    far_row = rows_far[1]
    lower_row = jnp.where(upper, far_row, last_row)
    upper_row = jnp.where(upper, first_row, far_row)
    own_beyond = jnp.where(upper, next_col[:, 0:1], next_col[:, row_total - 1 : row_total])
    far_beyond = rows_far[2][:, 0:1]
    tile_far = strain_tile(
        lower_row,
        upper_row,
        shifted(lower_row, jnp.where(upper, far_beyond, own_beyond)),
        shifted(upper_row, jnp.where(upper, own_beyond, far_beyond)),
    )
    half = cols // 2
    low = lane < half
    back = cols - 1

    def two(left, right_line):
        return jnp.where(low, left, pltpu.roll(right_line, half, 1))

    left_base = two(line_prev, line_final)
    left_upper = two(line_first, line_next)
    right_base = two(pltpu.roll(line_prev, back, 1), pltpu.roll(line_final, back, 1))
    right_upper = two(pltpu.roll(line_first, back, 1), pltpu.roll(line_next, back, 1))
    tile_side = strain_tile(left_base, right_base, left_upper, right_upper)

    edge_tile = jnp.concatenate((tile_far, tile_side), axis=1)
    primal, tangent = stress_sums([edge_tile], ref["w_first"], ref["w_mid"], ref["b_mid"], ref["w_last"])[0]
    f_base, f_right, f_upper, f_corner = corner_forces(primal[:, :cols], tangent[:, :cols])
    s_base, s_right, s_upper, s_corner = corner_forces(primal[:, cols:], tangent[:, cols:])

    def mask(value, keep):
        return jnp.where(keep, value, 0.0)

    def moved(value):
        return pltpu.roll(mask(value, lane < cols - 1), 1, 1)

    has_row = place > 0
    has_col = across > 0
    row_first = mask(f_right + moved(f_corner), upper & has_row)
    row_last = mask(f_base + moved(f_upper), core == 1)
    first_lane = jnp.where(has_row, 0, 1)
    s_corner = mask(s_corner, (lane >= first_lane) & (lane < row_total))
    s_upper = mask(s_upper, (lane >= 1) & (lane <= row_total))
    col_first = mask(pltpu.roll(s_upper, back, 1) + s_corner, has_col)
    valid = (lane >= half + 1 - core) & (lane <= half + row_total - core)
    s_base = mask(s_base, valid)
    s_right = mask(s_right, valid)
    col_last = pltpu.roll(pltpu.roll(s_base, back, 1) + s_right, cols - half, 1)

    owner = ref["owner"][...]
    hot_slot = ref["hot_slot"][...]
    hot_two = jnp.concatenate([hot_slot] * 2, axis=0)
    fit_value = jnp.zeros((COMPS, tie_total), F32)
    bins = jnp.zeros((COMPS, slots), F32)
    peers = tx_count * ty_count
    block = math.gcd(peers, 8)

    def collect(first, carry):
        fit_value, bins = carry
        parts = [got[first + peer] for peer in range(block)]
        fit_all = jnp.concatenate([part[0:COMPS] for part in parts], axis=0)
        wide = dot(jnp.concatenate(split(fit_all, 2), axis=1), hot_two)
        for peer, part in enumerate(parts):
            fit_value = jnp.where(owner == first + peer, wide[peer * COMPS : (peer + 1) * COMPS], fit_value)
            bins = bins + part[COMPS : 2 * COMPS]
        return fit_value, bins

    if block == peers:
        fit_value, bins = collect(0, (fit_value, bins))
    else:
        fit_value, bins = lax.fori_loop(
            0, peers // block, lambda at, carry: collect(at * block, carry), (fit_value, bins)
        )
    count = bins[COUNT_ROW : COUNT_ROW + 1]
    for out, fit, base in (("fit_res", "fit_disp", 0), ("fit_tan", "fit_dir", 8)):
        ref[out][...] = 2.0 * (count * ref[fit][...] - bins[base : base + 6])

    pulled = split(2.0 * (ties[...] - fit_value), 2)
    hot_row = ref["hot_row"][...]
    places = [comp % 6 + comp // 6 * 8 for comp in range(12)]
    lhs = [
        jnp.concatenate([hot_row * part[place_of : place_of + 1] for part in pulled], axis=1)
        for place_of in places
    ]
    hot_col = ref["hot_col"][...]
    tie_forces = dot(jnp.concatenate(lhs, axis=0), jnp.concatenate([hot_col] * 2, axis=1), ((1,), (1,)))

    assert 4 * row_total <= cols
    line = jnp.zeros((COMPS, cols), F32)
    for at, part in enumerate(split(col_first, 2) + split(col_last, 2)):
        part = part.astype(F32)
        part = pltpu.roll(part, at * row_total, 1) if at else part
        line = jnp.where((lane >= at * row_total) & (lane < (at + 1) * row_total), part, line)
    shape = (row_total, cols)
    eye = jnp.bitwise_and(lanes_of(shape), row_total - 1) == rows_of(shape)
    lhs = [jnp.where(eye, line[place_of : place_of + 1], 0.0).astype(BF16) for place_of in places]
    shape = (cols, cols)
    in_first = (rows_of(shape) == 0) & (lanes_of(shape) < 2 * row_total)
    in_last = (rows_of(shape) == cols - 1) & (lanes_of(shape) >= 2 * row_total)
    ends = (in_first | (in_last & (lanes_of(shape) < 4 * row_total))).astype(F32).astype(BF16)
    col_forces = dot(jnp.concatenate(lhs, axis=0), ends, ((1,), (1,)))

    row = rows_of((row_total, cols))
    for comp, place_of in enumerate(places):
        rows = slice(comp * row_total, (comp + 1) * row_total)
        value = tie_forces[rows] + col_forces[rows]
        value = value + jnp.where(row == 0, row_first[place_of : place_of + 1], 0.0)
        value = value + jnp.where(row == row_total - 1, row_last[place_of : place_of + 1], 0.0)
        partial[rows, :] = value - ref["load"][rows, :] if comp < 6 else value


def combine(swapped, partial, own, other, fit_one, fit_two, res, tan, fit_res, fit_tan):
    fit_res[...] = fit_one[...]
    fit_tan[...] = fit_two[...]
    row_total = partial.shape[0] // 12
    held = own.shape[0] // 12
    skip = row_total - held
    here = lax.axis_index("groups") == 0
    for comp in range(12):
        target = res if comp < 6 else tan
        start = comp % 6 * row_total
        rows = slice(comp * held, (comp + 1) * held)
        first, second = own[rows, :], other[rows, :]
        if swapped:
            first, second = jnp.where(here, first, second), jnp.where(here, second, first)
        target[start : start + row_total, :] = partial[comp * row_total : (comp + 1) * row_total, :]
        target[start : start + held, :] += first
        target[start + skip : start + row_total, :] += second


def per_device(
    displacement,
    direction,
    load,
    w_in,
    b_in,
    w_mid,
    b_mid,
    w_out,
    fitting_disp,
    fitting_dir,
    tie_node,
    tie_owner,
    tie_slot,
):
    tx_count = lax.axis_size("tx")
    ty_count = lax.axis_size("ty")
    pb_count = lax.axis_size("pb")
    peers = tx_count * ty_count
    axes = (tx_count, ty_count, pb_count)
    _, row_total, cols = displacement.shape
    slots = fitting_disp.shape[1]
    tie_total = tie_node.shape[0]
    hid = w_mid.shape[0]
    flat = (6 * row_total, cols)
    disp2 = displacement.reshape(flat)
    dir2 = direction.reshape(flat)
    load2 = load.reshape(flat)
    node2 = tie_node.reshape(tie_total // 128, 128)
    slot2 = tie_slot.reshape(tie_total // 128, 128)
    owner2 = tie_owner.reshape(1, tie_total)

    def shape(*dims, dtype=F32):
        return jax.ShapeDtypeStruct(dims, dtype)

    assert pb_count == 2 and slots == cols
    smalls = (
        fitting_disp,
        fitting_dir,
        node2,
        owner2,
        slot2,
        b_in.reshape(1, hid),
        b_mid.reshape(1, hid),
        w_in.T,
        w_out,
    )
    outs = pl.pallas_call(
        lambda *refs: gather_nodes(len(smalls), *refs),
        out_shape=[pltpu.VMEM((row_total * COMPS, cols), F32), pltpu.VMEM((2 * COMPS, cols), F32)]
        + [pltpu.VMEM(value.shape, value.dtype) for value in smalls],
        in_specs=local(2 + len(smalls)),
        out_specs=local(2 + len(smalls)),
        name="gather_nodes",
    )(disp2, dir2, *smalls)
    fields, rows, fit_disp, fit_dir, node, owner, slot, b_first, b_second, w_first_in, w_final = outs
    mate = lax.ppermute(rows, "pb", [(0, 1), (1, 0)])

    inputs = tuple(on_chip(value) for value in (fields, fit_disp, fit_dir, node, owner, slot))
    small = peers * 2 * COMPS * slots <= SMALL
    ties, cols_out, hot_col, hot_slot, hot_row, sums = pl.pallas_call(
        lambda *refs: sum_ties(peers, *refs),
        out_shape=[
            pltpu.VMEM((COMPS, tie_total), F32),
            pltpu.VMEM((2 * COMPS, cols), F32),
            pltpu.VMEM((cols, tie_total), BF16),
            pltpu.VMEM((slots, tie_total), BF16),
            pltpu.VMEM((row_total, tie_total), BF16),
            (pltpu.VMEM if small else jax.ShapeDtypeStruct)((peers, 2 * COMPS, slots), F32),
        ],
        in_specs=local(len(inputs)),
        out_specs=local(6),
        name="sum_ties",
    )(*inputs)
    inputs = (sums, cols_out, mate, w_first_in, b_first, b_second, w_final)
    inputs = [on_chip(value) if value.size <= SMALL else value for value in inputs]
    pay, w_first, w_last, b_cols = pl.pallas_call(
        lambda *refs: fill_blocks((tx_count, ty_count), row_total, *refs),
        out_shape=[
            shape(peers, 3 * COMPS, slots),
            pltpu.VMEM((8 * hid, 4 * COMPS), BF16),
            pltpu.VMEM((128, hid), BF16),
            pltpu.VMEM((hid, 128), F32),
        ],
        in_specs=local(len(inputs)),
        out_specs=[pl.BlockSpec(memory_space=pl.ANY)] + local(3),
        scratch_shapes=[pltpu.VMEM((peers, 3 * COMPS, slots), F32), pltpu.SemaphoreType.DMA(())],
        name="fill_blocks",
    )(*inputs)
    got = lax.all_to_all(pay, ("tx", "ty"), split_axis=0, concat_axis=0, tiled=True)

    inputs = tuple(on_chip(value) for value in (fields, mate, w_first, w_mid, b_cols, w_last))
    groups = lax.axis_size("groups")
    halves = []
    for pick in (None,) if groups == 2 else (0, 1):
        half = pl.pallas_call(
            lambda *refs: interior(pick, *refs),
            out_shape=pltpu.VMEM(((row_total // 2 + 1) * 12, cols), F32),
            in_specs=local(len(inputs)),
            out_specs=local(1)[0],
            scratch_shapes=[pltpu.VMEM(((row_total // 2 + 3) * COMPS, cols), F32)],
            name="interior",
        )(*inputs)
        halves.append(half)
    if groups == 2:
        halves.append(lax.ppermute(halves[0], "groups", [(0, 1), (1, 0)]))

    named = dict(
        got=got,
        mate=mate,
        fields=fields,
        ties=ties,
        cols=cols_out,
        w_first=w_first,
        w_mid=w_mid,
        b_mid=b_cols,
        w_last=w_last,
        hot_col=hot_col,
        hot_slot=hot_slot,
        hot_row=hot_row,
        load=load2,
        owner=owner,
        fit_disp=fit_disp,
        fit_dir=fit_dir,
    )
    named = {name: on_chip(value) if value.size <= SMALL else value for name, value in named.items()}
    names = list(named)
    partial, fit_one, fit_two = pl.pallas_call(
        lambda *refs: edges(names + ["partial", "fit_res", "fit_tan"], axes, *refs),
        out_shape=[pltpu.VMEM(size, F32) for size in ((12 * row_total, cols), (6, slots), (6, slots))],
        in_specs=local(len(names)),
        out_specs=local(3),
        name="edges",
    )(*named.values())

    inputs = tuple(on_chip(value) for value in (partial, halves[0], halves[1], fit_one, fit_two))
    res, tan, fit_res, fit_tan = pl.pallas_call(
        lambda *refs: combine(groups == 2, *refs),
        out_shape=[shape(*flat), shape(*flat), shape(6, slots), shape(6, slots)],
        in_specs=local(len(inputs)),
        out_specs=local(4),
        name="combine",
    )(*inputs)
    cube = displacement.shape
    return (res.reshape(cube), tan.reshape(cube), fit_res, fit_tan)


def solution(mesh):
    in_specs = (
        P(None, ("tx", "pb"), "ty"),
        P(None, ("tx", "pb"), "ty"),
        P(None, ("tx", "pb"), "ty"),
        P(),
        P(),
        P(),
        P(),
        P(),
        P(None, ("groups", "tx", "ty", "pb")),
        P(None, ("groups", "tx", "ty", "pb")),
        P(("groups", "tx", "ty", "pb")),
        P(("groups", "tx", "ty", "pb"), None),
        P(("groups", "tx", "ty", "pb")),
    )
    out_specs = (
        P(None, ("groups", "tx", "pb"), "ty"),
        P(None, ("groups", "tx", "pb"), "ty"),
        P(None, ("groups", "tx", "ty", "pb")),
        P(None, ("groups", "tx", "ty", "pb")),
    )
    return jax.shard_map(
        per_device, mesh=mesh, in_specs=in_specs, out_specs=out_specs, check_vma=False
    )
```

```python
import math

import jax
import jax.numpy as jnp
from jax import lax
from jax.experimental import pallas as pl
from jax.experimental.pallas import tpu as pltpu
from jax.sharding import PartitionSpec as P

F32 = jnp.float32
BF16 = jnp.bfloat16
GAUSS = (0.5 - 0.5 / math.sqrt(3.0), 0.5 + 0.5 / math.sqrt(3.0))
COMPS = 16
COUNT_ROW = 6
SPARE_ROWS = (6, 7, 14)
SMALL = 1 << 18
SHARED_ROWS = 4


def local(count):
    return [pl.BlockSpec(memory_space=pltpu.VMEM)] * count


def on_chip(value):
    return pltpu.with_memory_space_constraint(value, pltpu.VMEM)


def dot(a, b, dims=((1,), (0,))):
    return lax.dot_general(a, b, (dims, ((), ())), preferred_element_type=F32)


def split(value, terms):
    parts = []
    for _ in range(terms):
        part = value.astype(BF16)
        parts.append(part)
        value = value - part.astype(F32)
    return parts


def rows_of(value):
    return lax.broadcasted_iota(jnp.int32, value, 0)


def lanes_of(value):
    return lax.broadcasted_iota(jnp.int32, value, 1)


def one_hot(index, size):
    shape = (size, index.shape[1])
    return (rows_of(shape) == index).astype(F32).astype(BF16)


def as_line(ref):
    return jnp.concatenate([ref[row : row + 1, :] for row in range(ref.shape[0])], axis=1)


def paired(top, bottom):
    spare = jnp.zeros((2, top.shape[1]), F32)
    return jnp.concatenate([top, spare, bottom, spare], axis=0)


def strain_tile(f00, f10, f01, f11):
    along_low = f10 - f00
    along_high = f11 - f01
    across_low = f01 - f00
    across_high = f11 - f10
    shape = f00.shape
    row = rows_of(shape)
    ones = ((row == 6) | (row == 7) | (row == 14)).astype(F32)
    groups = []
    for frac in GAUSS:
        groups.append((((1.0 - frac) * along_low + frac * along_high) + ones).astype(BF16))
    for frac in GAUSS:
        groups.append(((1.0 - frac) * across_low + frac * across_high).astype(BF16))
    return jnp.concatenate(groups, axis=0)


def stress_sums(strains, w_first, w_mid, b_mid, w_last):
    hid = w_mid.shape[0]
    tasks = [(tile, point) for tile in range(len(strains)) for point in range(4)]
    totals = [[None, None] for _ in strains]

    def layer_one(task):
        tile, point = task
        start = point * 2 * hid
        return (
            dot(w_first[start : start + hid, :], strains[tile]),
            dot(w_first[start + hid : start + 2 * hid, :], strains[tile]),
        )

    def activate(value, slope):
        act = jnp.tanh(value)
        return (act.astype(BF16), ((1.0 - act * act) * slope).astype(BF16))

    def layer_two(hidden):
        bias = b_mid[...]
        value = dot(w_mid[...], hidden[0])
        slope = dot(w_mid[...], hidden[1])
        bias = jnp.concatenate([bias] * (value.shape[1] // bias.shape[1]), axis=1)
        return (value + bias, slope)

    def layer_three(task, hidden):
        tile, point = task
        last = w_last[point * 32 : (point + 1) * 32, :]
        for side in range(2):
            part = dot(last, hidden[side])
            old = totals[tile][side]
            totals[tile][side] = part if old is None else old + part

    ones = {0: layer_one(tasks[0])}
    twos = {}
    for at in range(len(tasks) + 1):
        if at + 1 < len(tasks):
            ones[at + 1] = layer_one(tasks[at + 1])
        if at < len(tasks):
            hidden = activate(*ones.pop(at))
            twos[at] = layer_two(hidden)
        if at >= 1:
            layer_three(tasks[at - 1], activate(*twos.pop(at - 1)))
    return totals


def corner_forces(primal, tangent):
    def both(group):
        return jnp.concatenate([primal[group * 8 : group * 8 + 8], tangent[group * 8 : group * 8 + 8]], axis=0)

    along = (both(0), both(1))
    across = (both(2), both(3))

    def mix(pair, weights):
        return (0.25 * weights[0]) * pair[0] + (0.25 * weights[1]) * pair[1]

    rest = (1.0 - GAUSS[0], 1.0 - GAUSS[1])
    along_rest = mix(along, rest)
    along_frac = mix(along, GAUSS)
    across_rest = mix(across, rest)
    across_frac = mix(across, GAUSS)
    return (
        -along_rest - across_rest,
        along_rest - across_frac,
        across_rest - along_frac,
        along_frac + across_frac,
    )


def gather_nodes(count, disp, dirn, *refs):
    fields, rows = refs[count : count + 2]
    for source, target in zip(refs[:count], refs[count + 2 :]):
        target[...] = source[...]
    row_total = fields.shape[0] // COMPS
    fields[...] = jnp.zeros(fields.shape, F32)
    for comp in range(6):
        part = slice(comp * row_total, (comp + 1) * row_total)
        fields[pl.ds(comp, row_total, stride=COMPS), :] = disp[part, :]
        fields[pl.ds(8 + comp, row_total, stride=COMPS), :] = dirn[part, :]
    rows[0:COMPS, :] = fields[0:COMPS, :]
    rows[COMPS : 2 * COMPS, :] = fields[(row_total - 1) * COMPS :, :]


def sum_ties(peers, *refs):
    (fields, fit_disp, fit_dir, node_ref, owner_ref, slot_ref) = refs[:6]
    (ties, col_out, hot_col_out, hot_slot_out, hot_row_out, pay) = refs[10:16]
    build_weights(*refs[6:10], *refs[16:])
    row_total = fields.shape[0] // COMPS
    cols = fields.shape[1]
    slots = fit_disp.shape[1]
    tie_total = ties.shape[1]

    lane = lanes_of((COMPS, cols))
    for side, column in enumerate((0, cols - 1)):
        gathered = jnp.zeros((COMPS, cols), F32)
        for row in range(row_total):
            value = fields[row * COMPS : (row + 1) * COMPS, column : column + 1]
            gathered = jnp.where(lane == row, value, gathered)
        col_out[side * COMPS : (side + 1) * COMPS, :] = gathered

    node = as_line(node_ref)
    slot = as_line(slot_ref)
    owner = owner_ref[...]
    node_row = lax.shift_right_logical(node, cols.bit_length() - 1)
    node_col = jnp.bitwise_and(node, cols - 1)
    hot_col = one_hot(node_col, cols)
    hot_col_out[...] = hot_col
    hot_row_out[...] = one_hot(node_row, row_total)
    wide = dot(
        jnp.concatenate(split(fields[...], 2), axis=1), jnp.concatenate([hot_col] * 2, axis=0)
    )
    value = jnp.zeros((COMPS, tie_total), F32)
    for row in range(row_total):
        value = jnp.where(node_row == row, wide[row * COMPS : (row + 1) * COMPS], value)
    value = jnp.where(rows_of(value.shape) == COUNT_ROW, 1.0, value)
    ties[...] = value
    stack = jnp.concatenate(split(value, 2), axis=0)
    hot_slot = one_hot(slot, slots)
    hot_slot_out[...] = hot_slot
    fitting = paired(fit_disp[...], fit_dir[...])

    def bins(first, count):
        lhs = [
            stack * (owner == first + at).astype(F32).astype(BF16) for at in range(count)
        ]
        return dot(jnp.concatenate(lhs, axis=0), hot_slot, ((1,), (1,)))

    def folded(wide_bins, at):
        part = wide_bins[at * 2 * COMPS : (at + 1) * 2 * COMPS]
        return part[0:COMPS] + part[COMPS : 2 * COMPS]

    block = math.gcd(peers, 8)

    def fill(first):
        wide_bins = bins(first, block)
        for peer in range(block):
            pay[first + peer, 0:COMPS, :] = fitting
            pay[first + peer, COMPS : 2 * COMPS, :] = folded(wide_bins, peer)

    if block == peers:
        fill(0)
    else:
        lax.fori_loop(0, peers // block, lambda at, carry: (fill(at * block), carry)[1], 0)


def mate_rows(mate):
    upper = lax.axis_index("pb") == 0
    first, last = mate[0:COMPS, :], mate[COMPS : 2 * COMPS, :]
    return jnp.where(upper, first, last), jnp.where(upper, last, first)


def fill_blocks(axes, row_total, sums, columns, mate, pay):
    tx_count, ty_count = axes
    along, across = lax.axis_index("tx"), lax.axis_index("ty")
    near, far = mate_rows(mate)
    pay[:, 0 : 2 * COMPS, :] = sums[...]
    ahead = along + 1 - 2 * lax.axis_index("pb")
    for side in (-1, 0, 1):
        over = across + side
        inside = (over >= 0) & (over < ty_count)

        @pl.when(inside & (ahead >= 0) & (ahead < tx_count))
        def _():
            pay[ahead * ty_count + over, 2 * COMPS : 3 * COMPS, :] = far

        if side == 0:
            continue
        edge = 0 if side < 0 else 1
        packed = pack_column(columns[edge * COMPS : (edge + 1) * COMPS, :], row_total)

        @pl.when(inside)
        def _():
            at = along * ty_count + over
            pay[at, 2 * COMPS : 3 * COMPS, :] = near
            for line, row in zip(packed, SPARE_ROWS):
                pay[at, row : row + 1, :] = line


def pack_column(column, width):
    each = column.shape[1] // width
    lines = []
    for first in range(0, 12, each):
        line = None
        for at in range(first, min(first + each, 12)):
            row = at % 6 + at // 6 * 8
            part = column[row : row + 1]
            if at > first:
                part = pltpu.roll(part, (at - first) * width, 1)
            line = part if line is None else line + part
        lines.append(line)
    assert len(lines) <= len(SPARE_ROWS)
    return lines


def unpack_column(block, width):
    shape = (COMPS, block.shape[1])
    each = shape[1] // width
    row = rows_of(shape)
    column = jnp.zeros(shape, F32)
    for at in range(12):
        spare = SPARE_ROWS[at // each]
        line = block[spare : spare + 1]
        if at % each:
            line = pltpu.roll(line, shape[1] - at % each * width, 1)
        column = jnp.where(row == at % 6 + at // 6 * 8, line, column)
    return jnp.where(lanes_of(shape) < width, column, 0.0)


def build_weights(w_in, b_in, b_mid, w_out, w_first, w_last, b_cols):
    hid = w_in.shape[1]
    bias_rows = split(b_in[...], 3)
    row = rows_of((8, hid))
    stacked = jnp.zeros((8, hid), F32)
    mid_stacked = jnp.zeros((8, hid), F32)
    for at, (one, two) in enumerate(zip(bias_rows, split(b_mid[...], 3))):
        stacked = jnp.where(row == at, one.astype(F32), stacked)
        mid_stacked = jnp.where(row == at, two.astype(F32), mid_stacked)
    lhs = jnp.concatenate([w_in[...].astype(F32), jnp.zeros((4, hid), F32), stacked], axis=0).astype(BF16)
    sel_shape = (24, 4 * COMPS)
    source = rows_of(sel_shape)
    target = lanes_of(sel_shape)
    for point in range(4):
        a_base = (point // 2) * COMPS
        c_base = (2 + point % 2) * COMPS
        for side in range(2):
            hit = (source < 6) & (target == a_base + 8 * side + source)
            hit = hit | ((source >= 6) & (source < 12) & (target == c_base + 8 * side + source - 6))
            if side == 0:
                for at, spot in enumerate((6, 7, 14)):
                    hit = hit | ((source == 16 + at) & (target == a_base + spot))
            block = dot(lhs, hit.astype(F32).astype(BF16), ((0,), (0,)))
            start = (2 * point + side) * hid
            w_first[start : start + hid, :] = block.astype(BF16)
    ones = (rows_of((8, 128)) < 3).astype(F32).astype(BF16)
    b_cols[...] = dot(mid_stacked.astype(BF16), ones, ((0,), (0,)))
    last_shape = (128, 12)
    target = rows_of(last_shape)
    source = lanes_of(last_shape)
    hit = target < 0
    for point in range(4):
        a_base = point * 32 + (point // 2) * 8
        c_base = point * 32 + 16 + (point % 2) * 8
        hit = hit | ((source < 6) & (target == a_base + source))
        hit = hit | ((source >= 6) & (target == c_base + source - 6))
    w_last[...] = dot(hit.astype(F32).astype(BF16), w_out[...]).astype(BF16)


def row_forces(fields, lines, first, weights, forces):
    cols = fields.shape[1]
    lines = [(line, pltpu.roll(line, cols - 1, 1)) for line in lines]
    tiles = [
        strain_tile(one[0], two[0], one[1], two[1]) for one, two in zip(lines[:-1], lines[1:])
    ]
    tiles = [jnp.concatenate(tiles[at : at + 2], axis=1) for at in range(0, len(tiles), 2)]
    sums = stress_sums(tiles, *weights)
    keep = lanes_of((COMPS, cols)) < cols - 1
    forces[...] = jnp.zeros(forces.shape, F32)
    for tile, (primal, tangent) in enumerate(sums):
        for side in range(2):
            lanes = slice(side * cols, (side + 1) * cols)
            parts = corner_forces(primal[:, lanes], tangent[:, lanes])
            base, right, upper, corner = (jnp.where(keep, part, 0.0) for part in parts)
            at = (2 * tile + side + 1) * COMPS
            forces[at : at + COMPS, :] += base + pltpu.roll(upper, 1, 1)
            forces[at + COMPS : at + 2 * COMPS, :] += right + pltpu.roll(corner, 1, 1)


def component_rows(forces, start, sent):
    held = sent.shape[0] // 12
    for comp in range(12):
        rows = pl.ds(start * COMPS + comp % 6 + comp // 6 * 8, held, stride=COMPS)
        sent[comp * held : (comp + 1) * held, :] = forces[rows, :]


def node_row(fields, row):
    return fields[pl.ds(pl.multiple_of(row * COMPS, COMPS), COMPS), :]


def interior(pick, count, fields, mate, w_first, w_mid, b_cols, w_last, sent, forces):
    row_total = fields.shape[0] // COMPS
    group = lax.axis_index("groups") if pick is None else pick
    core = lax.axis_index("pb")
    first = group * (row_total - count) - core
    near, _ = mate_rows(mate)
    lines = [jnp.where((core == 1) & (group == 0), near, node_row(fields, jnp.maximum(first, 0)))]
    lines += [node_row(fields, first + at) for at in range(1, count)]
    last = node_row(fields, jnp.minimum(first + count, row_total - 1))
    lines.append(jnp.where((core == 0) & (group == 1), near, last))
    row_forces(fields, lines, first, (w_first, w_mid, b_cols, w_last), forces)
    component_rows(forces, 1 + group * (row_total - count - 1) - first, sent)


def middle(count, fields, w_first, w_mid, b_cols, w_last, kept, forces):
    row_total = fields.shape[0] // COMPS
    core = lax.axis_index("pb")
    first = count - core
    lines = [node_row(fields, first + at) for at in range(row_total - 2 * count + 1)]
    row_forces(fields, lines, first, (w_first, w_mid, b_cols, w_last), forces)
    component_rows(forces, core, kept)


def edges(names, axes, *refs):
    ref = dict(zip(names, refs))
    tx_count, ty_count, pb_count = axes
    fields, ties, partial, got = ref["fields"], ref["ties"], ref["partial"], ref["got"]
    row_total, cols = fields.shape[0] // COMPS, fields.shape[1]
    slots = got.shape[2]
    tie_total = ties.shape[1]
    lane = lanes_of((COMPS, cols))
    core = lax.axis_index("pb")
    across = lax.axis_index("ty")
    along = lax.axis_index("tx")
    place = along * pb_count + core

    def around(step, side, packed=False):
        there, over = along + step, across + side
        valid = (there >= 0) & (there < tx_count) & (over >= 0) & (over < ty_count)
        block = got.at[jnp.where(valid, there * ty_count + over, 0)]
        if packed:
            value = unpack_column(block[0:COMPS, :], row_total)
        else:
            value = block[2 * COMPS : 3 * COMPS, :]
        return jnp.where(valid, value, 0.0)

    upper = core == 0
    behind = 2 * core - 1
    near, _ = mate_rows(ref["mate"])
    rows_near = (around(0, -1), near, around(0, 1))
    rows_far = tuple(around(behind, side) for side in (-1, 0, 1))
    next_rows = [jnp.where(upper, one, two) for one, two in zip(rows_near, rows_far)]
    prev_rows = [jnp.where(upper, two, one) for one, two in zip(rows_near, rows_far)]
    prev_row, next_row = prev_rows[1], next_rows[1]
    next_col = around(0, 1, True)
    prev_col = around(0, -1, True)
    next_corner = (prev_rows[2][:, 0:1], next_rows[2][:, 0:1])
    prev_corner = (prev_rows[0][:, cols - 1 : cols], next_rows[0][:, cols - 1 : cols])

    def column(inner, before, after):
        line = pltpu.roll(inner, 1, 1)
        line = jnp.where(lane == 0, before, line)
        return jnp.where(lane == row_total + 1, after, line)

    own_cols = ref["cols"]
    line_prev = column(prev_col, prev_corner[0], prev_corner[1])
    line_next = column(next_col, next_corner[0], next_corner[1])
    line_first = column(own_cols[0:COMPS, :], prev_row[:, 0:1], next_row[:, 0:1])
    line_final = column(
        own_cols[COMPS : 2 * COMPS, :], prev_row[:, cols - 1 : cols], next_row[:, cols - 1 : cols]
    )

    def shifted(row_value, beyond):
        return jnp.where(lane == cols - 1, beyond, pltpu.roll(row_value, cols - 1, 1))

    first_row = fields[0:COMPS, :]
    last_row = fields[(row_total - 1) * COMPS :, :]
    far_row = rows_far[1]
    lower_row = jnp.where(upper, far_row, last_row)
    upper_row = jnp.where(upper, first_row, far_row)
    own_beyond = jnp.where(upper, next_col[:, 0:1], next_col[:, row_total - 1 : row_total])
    far_beyond = rows_far[2][:, 0:1]
    tile_far = strain_tile(
        lower_row,
        upper_row,
        shifted(lower_row, jnp.where(upper, far_beyond, own_beyond)),
        shifted(upper_row, jnp.where(upper, own_beyond, far_beyond)),
    )
    half = cols // 2
    low = lane < half
    back = cols - 1

    def two(left, right_line):
        return jnp.where(low, left, pltpu.roll(right_line, half, 1))

    left_base = two(line_prev, line_final)
    left_upper = two(line_first, line_next)
    right_base = two(pltpu.roll(line_prev, back, 1), pltpu.roll(line_final, back, 1))
    right_upper = two(pltpu.roll(line_first, back, 1), pltpu.roll(line_next, back, 1))
    tile_side = strain_tile(left_base, right_base, left_upper, right_upper)

    edge_tile = jnp.concatenate((tile_far, tile_side), axis=1)
    primal, tangent = stress_sums([edge_tile], ref["w_first"], ref["w_mid"], ref["b_mid"], ref["w_last"])[0]
    f_base, f_right, f_upper, f_corner = corner_forces(primal[:, :cols], tangent[:, :cols])
    s_base, s_right, s_upper, s_corner = corner_forces(primal[:, cols:], tangent[:, cols:])

    def mask(value, keep):
        return jnp.where(keep, value, 0.0)

    def moved(value):
        return pltpu.roll(mask(value, lane < cols - 1), 1, 1)

    has_row = place > 0
    has_col = across > 0
    row_first = mask(f_right + moved(f_corner), upper & has_row)
    row_last = mask(f_base + moved(f_upper), core == 1)
    first_lane = jnp.where(has_row, 0, 1)
    s_corner = mask(s_corner, (lane >= first_lane) & (lane < row_total))
    s_upper = mask(s_upper, (lane >= 1) & (lane <= row_total))
    col_first = mask(pltpu.roll(s_upper, back, 1) + s_corner, has_col)
    valid = (lane >= half + 1 - core) & (lane <= half + row_total - core)
    s_base = mask(s_base, valid)
    s_right = mask(s_right, valid)
    col_last = pltpu.roll(pltpu.roll(s_base, back, 1) + s_right, cols - half, 1)

    owner = ref["owner"][...]
    hot_slot = ref["hot_slot"][...]
    hot_two = jnp.concatenate([hot_slot] * 2, axis=0)
    fit_value = jnp.zeros((COMPS, tie_total), F32)
    bins = jnp.zeros((COMPS, slots), F32)
    peers = tx_count * ty_count
    block = math.gcd(peers, 8)

    def collect(first, carry):
        fit_value, bins = carry
        parts = [got[first + peer] for peer in range(block)]
        fit_all = jnp.concatenate([part[0:COMPS] for part in parts], axis=0)
        wide = dot(jnp.concatenate(split(fit_all, 2), axis=1), hot_two)
        for peer, part in enumerate(parts):
            fit_value = jnp.where(owner == first + peer, wide[peer * COMPS : (peer + 1) * COMPS], fit_value)
            bins = bins + part[COMPS : 2 * COMPS]
        return fit_value, bins

    if block == peers:
        fit_value, bins = collect(0, (fit_value, bins))
    else:
        fit_value, bins = lax.fori_loop(
            0, peers // block, lambda at, carry: collect(at * block, carry), (fit_value, bins)
        )
    count = bins[COUNT_ROW : COUNT_ROW + 1]
    for out, fit, base in (("fit_res", "fit_disp", 0), ("fit_tan", "fit_dir", 8)):
        ref[out][...] = 2.0 * (count * ref[fit][...] - bins[base : base + 6])

    pulled = split(2.0 * (ties[...] - fit_value), 2)
    hot_row = ref["hot_row"][...]
    places = [comp % 6 + comp // 6 * 8 for comp in range(12)]
    lhs = [
        jnp.concatenate([hot_row * part[place_of : place_of + 1] for part in pulled], axis=1)
        for place_of in places
    ]
    hot_col = ref["hot_col"][...]
    tie_forces = dot(jnp.concatenate(lhs, axis=0), jnp.concatenate([hot_col] * 2, axis=1), ((1,), (1,)))

    assert 4 * row_total <= cols
    line = jnp.zeros((COMPS, cols), F32)
    for at, part in enumerate(split(col_first, 2) + split(col_last, 2)):
        part = part.astype(F32)
        part = pltpu.roll(part, at * row_total, 1) if at else part
        line = jnp.where((lane >= at * row_total) & (lane < (at + 1) * row_total), part, line)
    shape = (row_total, cols)
    eye = jnp.bitwise_and(lanes_of(shape), row_total - 1) == rows_of(shape)
    lhs = [jnp.where(eye, line[place_of : place_of + 1], 0.0).astype(BF16) for place_of in places]
    shape = (cols, cols)
    in_first = (rows_of(shape) == 0) & (lanes_of(shape) < 2 * row_total)
    in_last = (rows_of(shape) == cols - 1) & (lanes_of(shape) >= 2 * row_total)
    ends = (in_first | (in_last & (lanes_of(shape) < 4 * row_total))).astype(F32).astype(BF16)
    col_forces = dot(jnp.concatenate(lhs, axis=0), ends, ((1,), (1,)))

    row = rows_of((row_total, cols))
    for comp, place_of in enumerate(places):
        rows = slice(comp * row_total, (comp + 1) * row_total)
        value = tie_forces[rows] + col_forces[rows]
        value = value + jnp.where(row == 0, row_first[place_of : place_of + 1], 0.0)
        value = value + jnp.where(row == row_total - 1, row_last[place_of : place_of + 1], 0.0)
        partial[rows, :] = value - ref["load"][rows, :] if comp < 6 else value


def combine(swapped, partial, own, other, between, fit_one, fit_two, res, tan, fit_res, fit_tan):
    fit_res[...] = fit_one[...]
    fit_tan[...] = fit_two[...]
    row_total = partial.shape[0] // 12
    held = own.shape[0] // 12
    skip = row_total - held
    here = lax.axis_index("groups") == 0
    for comp in range(12):
        target = res if comp < 6 else tan
        start = comp % 6 * row_total
        rows = slice(comp * held, (comp + 1) * held)
        first, second = own[rows, :], other[rows, :]
        if swapped:
            first, second = jnp.where(here, first, second), jnp.where(here, second, first)
        target[start : start + row_total, :] = partial[comp * row_total : (comp + 1) * row_total, :]
        target[start : start + held, :] += first
        target[start + skip : start + row_total, :] += second
        count = between.shape[0] // 12
        low = start + held - 2
        target[low : low + count, :] += between[comp * count : (comp + 1) * count, :]


def per_device(
    displacement,
    direction,
    load,
    w_in,
    b_in,
    w_mid,
    b_mid,
    w_out,
    fitting_disp,
    fitting_dir,
    tie_node,
    tie_owner,
    tie_slot,
):
    tx_count = lax.axis_size("tx")
    ty_count = lax.axis_size("ty")
    pb_count = lax.axis_size("pb")
    peers = tx_count * ty_count
    axes = (tx_count, ty_count, pb_count)
    _, row_total, cols = displacement.shape
    slots = fitting_disp.shape[1]
    tie_total = tie_node.shape[0]
    hid = w_mid.shape[0]
    flat = (6 * row_total, cols)
    disp2 = displacement.reshape(flat)
    dir2 = direction.reshape(flat)
    load2 = load.reshape(flat)
    node2 = tie_node.reshape(tie_total // 128, 128)
    slot2 = tie_slot.reshape(tie_total // 128, 128)
    owner2 = tie_owner.reshape(1, tie_total)

    def shape(*dims, dtype=F32):
        return jax.ShapeDtypeStruct(dims, dtype)

    assert pb_count == 2 and slots == cols
    smalls = (
        fitting_disp,
        fitting_dir,
        node2,
        owner2,
        slot2,
        b_in.reshape(1, hid),
        b_mid.reshape(1, hid),
        w_in.T,
        w_out,
    )
    outs = pl.pallas_call(
        lambda *refs: gather_nodes(len(smalls), *refs),
        out_shape=[pltpu.VMEM((row_total * COMPS, cols), F32), pltpu.VMEM((2 * COMPS, cols), F32)]
        + [pltpu.VMEM(value.shape, value.dtype) for value in smalls],
        in_specs=local(2 + len(smalls)),
        out_specs=local(2 + len(smalls)),
        name="gather_nodes",
    )(disp2, dir2, *smalls)
    fields, rows, fit_disp, fit_dir, node, owner, slot, b_first, b_second, w_first_in, w_final = outs
    mate = lax.ppermute(rows, "pb", [(0, 1), (1, 0)])

    inputs = (fields, fit_disp, fit_dir, node, owner, slot, w_first_in, b_first, b_second, w_final)
    inputs = tuple(on_chip(value) for value in inputs)
    small = peers * 2 * COMPS * slots <= SMALL
    ties, cols_out, hot_col, hot_slot, hot_row, sums, w_first, w_last, b_cols = pl.pallas_call(
        lambda *refs: sum_ties(peers, *refs),
        out_shape=[
            pltpu.VMEM((COMPS, tie_total), F32),
            pltpu.VMEM((2 * COMPS, cols), F32),
            pltpu.VMEM((cols, tie_total), BF16),
            pltpu.VMEM((slots, tie_total), BF16),
            pltpu.VMEM((row_total, tie_total), BF16),
            (pltpu.VMEM if small else jax.ShapeDtypeStruct)((peers, 2 * COMPS, slots), F32),
            pltpu.VMEM((8 * hid, 4 * COMPS), BF16),
            pltpu.VMEM((128, hid), BF16),
            pltpu.VMEM((hid, 128), F32),
        ],
        in_specs=local(len(inputs)),
        out_specs=local(9),
        name="sum_ties",
    )(*inputs)
    inputs = [on_chip(value) if value.size <= SMALL else value for value in (sums, cols_out, mate)]
    pay = pl.pallas_call(
        lambda *refs: fill_blocks((tx_count, ty_count), row_total, *refs),
        out_shape=shape(peers, 3 * COMPS, slots),
        in_specs=local(len(inputs)),
        out_specs=local(1)[0],
        name="fill_blocks",
    )(*inputs)
    got = lax.all_to_all(pay, ("tx", "ty"), split_axis=0, concat_axis=0, tiled=True)

    inputs = tuple(on_chip(value) for value in (fields, mate, w_first, w_mid, b_cols, w_last))
    groups = lax.axis_size("groups")
    count = (row_total - SHARED_ROWS) // 2
    halves = []
    for pick in (None,) if groups == 2 else (0, 1):
        half = pl.pallas_call(
            lambda *refs: interior(pick, count, *refs),
            out_shape=pltpu.VMEM(((count + 1) * 12, cols), F32),
            in_specs=local(len(inputs)),
            out_specs=local(1)[0],
            scratch_shapes=[pltpu.VMEM(((count + 3) * COMPS, cols), F32)],
            name="interior",
        )(*inputs)
        halves.append(half)
    if groups == 2:
        halves.append(lax.ppermute(halves[0], "groups", [(0, 1), (1, 0)]))
    fields_late, _ = lax.optimization_barrier((fields, halves[0]))
    inputs = tuple(on_chip(value) for value in (fields_late, w_first, w_mid, b_cols, w_last))
    between = pl.pallas_call(
        lambda *refs: middle(count, *refs),
        out_shape=pltpu.VMEM(((SHARED_ROWS + 2) * 12, cols), F32),
        in_specs=local(len(inputs)),
        out_specs=local(1)[0],
        scratch_shapes=[pltpu.VMEM(((SHARED_ROWS + 3) * COMPS, cols), F32)],
        name="middle",
    )(*inputs)

    named = dict(
        got=got,
        mate=mate,
        fields=fields,
        ties=ties,
        cols=cols_out,
        w_first=w_first,
        w_mid=w_mid,
        b_mid=b_cols,
        w_last=w_last,
        hot_col=hot_col,
        hot_slot=hot_slot,
        hot_row=hot_row,
        load=load2,
        owner=owner,
        fit_disp=fit_disp,
        fit_dir=fit_dir,
    )
    named = {name: on_chip(value) if value.size <= SMALL else value for name, value in named.items()}
    names = list(named)
    partial, fit_one, fit_two = pl.pallas_call(
        lambda *refs: edges(names + ["partial", "fit_res", "fit_tan"], axes, *refs),
        out_shape=[pltpu.VMEM(size, F32) for size in ((12 * row_total, cols), (6, slots), (6, slots))],
        in_specs=local(len(names)),
        out_specs=local(3),
        name="edges",
    )(*named.values())

    inputs = tuple(on_chip(value) for value in (partial, halves[0], halves[1], between, fit_one, fit_two))
    res, tan, fit_res, fit_tan = pl.pallas_call(
        lambda *refs: combine(groups == 2, *refs),
        out_shape=[shape(*flat), shape(*flat), shape(6, slots), shape(6, slots)],
        in_specs=local(len(inputs)),
        out_specs=local(4),
        name="combine",
    )(*inputs)
    cube = displacement.shape
    return (res.reshape(cube), tan.reshape(cube), fit_res, fit_tan)


def solution(mesh):
    in_specs = (
        P(None, ("tx", "pb"), "ty"),
        P(None, ("tx", "pb"), "ty"),
        P(None, ("tx", "pb"), "ty"),
        P(),
        P(),
        P(),
        P(),
        P(),
        P(None, ("groups", "tx", "ty", "pb")),
        P(None, ("groups", "tx", "ty", "pb")),
        P(("groups", "tx", "ty", "pb")),
        P(("groups", "tx", "ty", "pb"), None),
        P(("groups", "tx", "ty", "pb")),
    )
    out_specs = (
        P(None, ("groups", "tx", "pb"), "ty"),
        P(None, ("groups", "tx", "pb"), "ty"),
        P(None, ("groups", "tx", "ty", "pb")),
        P(None, ("groups", "tx", "ty", "pb")),
    )
    return jax.shard_map(
        per_device, mesh=mesh, in_specs=in_specs, out_specs=out_specs, check_vma=False
    )
```

```python
import math

import jax
import jax.numpy as jnp
from jax import lax
from jax.experimental import pallas as pl
from jax.experimental.pallas import tpu as pltpu
from jax.sharding import PartitionSpec as P

F32 = jnp.float32
BF16 = jnp.bfloat16
GAUSS = (0.5 - 0.5 / math.sqrt(3.0), 0.5 + 0.5 / math.sqrt(3.0))
COMPS = 16
COUNT_ROW = 6
SPARE_ROWS = (6, 7, 14)
SMALL = 1 << 18
SHARED_ROWS = 4


def local(count):
    return [pl.BlockSpec(memory_space=pltpu.VMEM)] * count


def on_chip(value):
    return pltpu.with_memory_space_constraint(value, pltpu.VMEM)


def dot(a, b, dims=((1,), (0,))):
    return lax.dot_general(a, b, (dims, ((), ())), preferred_element_type=F32)


def split(value, terms):
    parts = []
    for _ in range(terms):
        part = value.astype(BF16)
        parts.append(part)
        value = value - part.astype(F32)
    return parts


def rows_of(value):
    return lax.broadcasted_iota(jnp.int32, value, 0)


def lanes_of(value):
    return lax.broadcasted_iota(jnp.int32, value, 1)


def one_hot(index, size):
    shape = (size, index.shape[1])
    return (rows_of(shape) == index).astype(F32).astype(BF16)


def as_line(ref):
    return jnp.concatenate([ref[row : row + 1, :] for row in range(ref.shape[0])], axis=1)


def paired(top, bottom):
    spare = jnp.zeros((2, top.shape[1]), F32)
    return jnp.concatenate([top, spare, bottom, spare], axis=0)


def strain_tile(f00, f10, f01, f11):
    along_low = f10 - f00
    along_high = f11 - f01
    across_low = f01 - f00
    across_high = f11 - f10
    shape = f00.shape
    row = rows_of(shape)
    ones = ((row == 6) | (row == 7) | (row == 14)).astype(F32)
    groups = []
    for frac in GAUSS:
        groups.append((((1.0 - frac) * along_low + frac * along_high) + ones).astype(BF16))
    for frac in GAUSS:
        groups.append(((1.0 - frac) * across_low + frac * across_high).astype(BF16))
    return jnp.concatenate(groups, axis=0)


def stress_sums(strains, w_first, w_mid, b_mid, w_last):
    hid = w_mid.shape[0]
    tasks = [(tile, point) for tile in range(len(strains)) for point in range(4)]
    totals = [[None, None] for _ in strains]

    def layer_one(task):
        tile, point = task
        start = point * 2 * hid
        return (
            dot(w_first[start : start + hid, :], strains[tile]),
            dot(w_first[start + hid : start + 2 * hid, :], strains[tile]),
        )

    def activate(value, slope):
        act = jnp.tanh(value)
        return (act.astype(BF16), ((1.0 - act * act) * slope).astype(BF16))

    def layer_two(hidden):
        bias = b_mid[...]
        value = dot(w_mid[...], hidden[0])
        slope = dot(w_mid[...], hidden[1])
        bias = jnp.concatenate([bias] * (value.shape[1] // bias.shape[1]), axis=1)
        return (value + bias, slope)

    def layer_three(task, hidden):
        tile, point = task
        last = w_last[point * 32 : (point + 1) * 32, :]
        for side in range(2):
            part = dot(last, hidden[side])
            old = totals[tile][side]
            totals[tile][side] = part if old is None else old + part

    ones = {0: layer_one(tasks[0])}
    twos = {}
    for at in range(len(tasks) + 1):
        if at + 1 < len(tasks):
            ones[at + 1] = layer_one(tasks[at + 1])
        if at < len(tasks):
            hidden = activate(*ones.pop(at))
            twos[at] = layer_two(hidden)
        if at >= 1:
            layer_three(tasks[at - 1], activate(*twos.pop(at - 1)))
    return totals


def corner_forces(primal, tangent):
    def both(group):
        return jnp.concatenate([primal[group * 8 : group * 8 + 8], tangent[group * 8 : group * 8 + 8]], axis=0)

    along = (both(0), both(1))
    across = (both(2), both(3))

    def mix(pair, weights):
        return (0.25 * weights[0]) * pair[0] + (0.25 * weights[1]) * pair[1]

    rest = (1.0 - GAUSS[0], 1.0 - GAUSS[1])
    along_rest = mix(along, rest)
    along_frac = mix(along, GAUSS)
    across_rest = mix(across, rest)
    across_frac = mix(across, GAUSS)
    return (
        -along_rest - across_rest,
        along_rest - across_frac,
        across_rest - along_frac,
        along_frac + across_frac,
    )


def gather_nodes(count, disp, dirn, *refs):
    fields, rows = refs[count : count + 2]
    for source, target in zip(refs[:count], refs[count + 2 :]):
        target[...] = source[...]
    row_total = fields.shape[0] // COMPS
    fields[...] = jnp.zeros(fields.shape, F32)
    for comp in range(6):
        part = slice(comp * row_total, (comp + 1) * row_total)
        fields[pl.ds(comp, row_total, stride=COMPS), :] = disp[part, :]
        fields[pl.ds(8 + comp, row_total, stride=COMPS), :] = dirn[part, :]
    rows[0:COMPS, :] = fields[0:COMPS, :]
    rows[COMPS : 2 * COMPS, :] = fields[(row_total - 1) * COMPS :, :]


def sum_ties(peers, *refs):
    (fields, fit_disp, fit_dir, node_ref, owner_ref, slot_ref) = refs[:6]
    (ties, col_out, hot_col_out, hot_slot_out, hot_row_out, pay) = refs[10:16]
    build_weights(*refs[6:10], *refs[16:])
    row_total = fields.shape[0] // COMPS
    cols = fields.shape[1]
    slots = fit_disp.shape[1]
    tie_total = ties.shape[1]

    lane = lanes_of((COMPS, cols))
    for side, column in enumerate((0, cols - 1)):
        gathered = jnp.zeros((COMPS, cols), F32)
        for row in range(row_total):
            value = fields[row * COMPS : (row + 1) * COMPS, column : column + 1]
            gathered = jnp.where(lane == row, value, gathered)
        col_out[side * COMPS : (side + 1) * COMPS, :] = gathered

    node = as_line(node_ref)
    slot = as_line(slot_ref)
    owner = owner_ref[...]
    node_row = lax.shift_right_logical(node, cols.bit_length() - 1)
    node_col = jnp.bitwise_and(node, cols - 1)
    hot_col = one_hot(node_col, cols)
    hot_col_out[...] = hot_col
    hot_row_out[...] = one_hot(node_row, row_total)
    wide = dot(
        jnp.concatenate(split(fields[...], 2), axis=1), jnp.concatenate([hot_col] * 2, axis=0)
    )
    value = jnp.zeros((COMPS, tie_total), F32)
    for row in range(row_total):
        value = jnp.where(node_row == row, wide[row * COMPS : (row + 1) * COMPS], value)
    value = jnp.where(rows_of(value.shape) == COUNT_ROW, 1.0, value)
    ties[...] = value
    stack = jnp.concatenate(split(value, 2), axis=0)
    hot_slot = one_hot(slot, slots)
    hot_slot_out[...] = hot_slot
    fitting = paired(fit_disp[...], fit_dir[...])

    def bins(first, count):
        lhs = [
            stack * (owner == first + at).astype(F32).astype(BF16) for at in range(count)
        ]
        return dot(jnp.concatenate(lhs, axis=0), hot_slot, ((1,), (1,)))

    def folded(wide_bins, at):
        part = wide_bins[at * 2 * COMPS : (at + 1) * 2 * COMPS]
        return part[0:COMPS] + part[COMPS : 2 * COMPS]

    block = math.gcd(peers, 8)

    def fill(first):
        wide_bins = bins(first, block)
        for peer in range(block):
            pay[first + peer, 0:COMPS, :] = fitting
            pay[first + peer, COMPS : 2 * COMPS, :] = folded(wide_bins, peer)

    if block == peers:
        fill(0)
    else:
        lax.fori_loop(0, peers // block, lambda at, carry: (fill(at * block), carry)[1], 0)


def mate_rows(mate):
    upper = lax.axis_index("pb") == 0
    first, last = mate[0:COMPS, :], mate[COMPS : 2 * COMPS, :]
    return jnp.where(upper, first, last), jnp.where(upper, last, first)


def fill_blocks(axes, row_total, sums, columns, mate, pay):
    tx_count, ty_count = axes
    along, across = lax.axis_index("tx"), lax.axis_index("ty")
    near, far = mate_rows(mate)
    pay[:, 0 : 2 * COMPS, :] = sums[...]
    ahead = along + 1 - 2 * lax.axis_index("pb")
    for side in (-1, 0, 1):
        over = across + side
        inside = (over >= 0) & (over < ty_count)

        @pl.when(inside & (ahead >= 0) & (ahead < tx_count))
        def _():
            pay[ahead * ty_count + over, 2 * COMPS : 3 * COMPS, :] = far

        if side == 0:
            continue
        edge = 0 if side < 0 else 1
        packed = pack_column(columns[edge * COMPS : (edge + 1) * COMPS, :], row_total)

        @pl.when(inside)
        def _():
            at = along * ty_count + over
            pay[at, 2 * COMPS : 3 * COMPS, :] = near
            for line, row in zip(packed, SPARE_ROWS):
                pay[at, row : row + 1, :] = line


def pack_column(column, width):
    each = column.shape[1] // width
    lines = []
    for first in range(0, 12, each):
        line = None
        for at in range(first, min(first + each, 12)):
            row = at % 6 + at // 6 * 8
            part = column[row : row + 1]
            if at > first:
                part = pltpu.roll(part, (at - first) * width, 1)
            line = part if line is None else line + part
        lines.append(line)
    assert len(lines) <= len(SPARE_ROWS)
    return lines


def unpack_column(block, width):
    shape = (COMPS, block.shape[1])
    each = shape[1] // width
    row = rows_of(shape)
    column = jnp.zeros(shape, F32)
    for at in range(12):
        spare = SPARE_ROWS[at // each]
        line = block[spare : spare + 1]
        if at % each:
            line = pltpu.roll(line, shape[1] - at % each * width, 1)
        column = jnp.where(row == at % 6 + at // 6 * 8, line, column)
    return jnp.where(lanes_of(shape) < width, column, 0.0)


def build_weights(w_in, b_in, b_mid, w_out, w_first, w_last, b_cols):
    hid = w_in.shape[1]
    bias_rows = split(b_in[...], 3)
    row = rows_of((8, hid))
    stacked = jnp.zeros((8, hid), F32)
    mid_stacked = jnp.zeros((8, hid), F32)
    for at, (one, two) in enumerate(zip(bias_rows, split(b_mid[...], 3))):
        stacked = jnp.where(row == at, one.astype(F32), stacked)
        mid_stacked = jnp.where(row == at, two.astype(F32), mid_stacked)
    lhs = jnp.concatenate([w_in[...].astype(F32), jnp.zeros((4, hid), F32), stacked], axis=0).astype(BF16)
    sel_shape = (24, 4 * COMPS)
    source = rows_of(sel_shape)
    target = lanes_of(sel_shape)
    for point in range(4):
        a_base = (point // 2) * COMPS
        c_base = (2 + point % 2) * COMPS
        for side in range(2):
            hit = (source < 6) & (target == a_base + 8 * side + source)
            hit = hit | ((source >= 6) & (source < 12) & (target == c_base + 8 * side + source - 6))
            if side == 0:
                for at, spot in enumerate((6, 7, 14)):
                    hit = hit | ((source == 16 + at) & (target == a_base + spot))
            block = dot(lhs, hit.astype(F32).astype(BF16), ((0,), (0,)))
            start = (2 * point + side) * hid
            w_first[start : start + hid, :] = block.astype(BF16)
    ones = (rows_of((8, 128)) < 3).astype(F32).astype(BF16)
    b_cols[...] = dot(mid_stacked.astype(BF16), ones, ((0,), (0,)))
    last_shape = (128, 12)
    target = rows_of(last_shape)
    source = lanes_of(last_shape)
    hit = target < 0
    for point in range(4):
        a_base = point * 32 + (point // 2) * 8
        c_base = point * 32 + 16 + (point % 2) * 8
        hit = hit | ((source < 6) & (target == a_base + source))
        hit = hit | ((source >= 6) & (target == c_base + source - 6))
    w_last[...] = dot(hit.astype(F32).astype(BF16), w_out[...]).astype(BF16)


def row_forces(fields, lines, first, weights, forces):
    cols = fields.shape[1]
    lines = [(line, pltpu.roll(line, cols - 1, 1)) for line in lines]
    tiles = [
        strain_tile(one[0], two[0], one[1], two[1]) for one, two in zip(lines[:-1], lines[1:])
    ]
    tiles = [jnp.concatenate(tiles[at : at + 2], axis=1) for at in range(0, len(tiles), 2)]
    sums = stress_sums(tiles, *weights)
    keep = lanes_of((COMPS, cols)) < cols - 1
    forces[...] = jnp.zeros(forces.shape, F32)
    for tile, (primal, tangent) in enumerate(sums):
        for side in range(2):
            lanes = slice(side * cols, (side + 1) * cols)
            parts = corner_forces(primal[:, lanes], tangent[:, lanes])
            base, right, upper, corner = (jnp.where(keep, part, 0.0) for part in parts)
            at = (2 * tile + side + 1) * COMPS
            forces[at : at + COMPS, :] += base + pltpu.roll(upper, 1, 1)
            forces[at + COMPS : at + 2 * COMPS, :] += right + pltpu.roll(corner, 1, 1)


def component_rows(forces, start, sent):
    held = sent.shape[0] // 12
    for comp in range(12):
        rows = pl.ds(start * COMPS + comp % 6 + comp // 6 * 8, held, stride=COMPS)
        sent[comp * held : (comp + 1) * held, :] = forces[rows, :]


def node_row(fields, row):
    return fields[pl.ds(pl.multiple_of(row * COMPS, COMPS), COMPS), :]


def interior(pick, count, fields, mate, w_first, w_mid, b_cols, w_last, sent, forces):
    row_total = fields.shape[0] // COMPS
    group = lax.axis_index("groups") if pick is None else pick
    core = lax.axis_index("pb")
    first = group * (row_total - count) - core
    near, _ = mate_rows(mate)
    lines = [jnp.where((core == 1) & (group == 0), near, node_row(fields, jnp.maximum(first, 0)))]
    lines += [node_row(fields, first + at) for at in range(1, count)]
    last = node_row(fields, jnp.minimum(first + count, row_total - 1))
    lines.append(jnp.where((core == 0) & (group == 1), near, last))
    row_forces(fields, lines, first, (w_first, w_mid, b_cols, w_last), forces)
    component_rows(forces, 1 + group * (row_total - count - 1) - first, sent)


def middle(count, fields, w_first, w_mid, b_cols, w_last, kept, forces):
    row_total = fields.shape[0] // COMPS
    core = lax.axis_index("pb")
    first = count - core
    lines = [node_row(fields, first + at) for at in range(row_total - 2 * count + 1)]
    row_forces(fields, lines, first, (w_first, w_mid, b_cols, w_last), forces)
    component_rows(forces, core, kept)


def edges(names, axes, *refs):
    ref = dict(zip(names, refs))
    tx_count, ty_count, pb_count = axes
    fields, ties, partial, got = ref["fields"], ref["ties"], ref["partial"], ref["got"]
    row_total, cols = fields.shape[0] // COMPS, fields.shape[1]
    slots = got.shape[2]
    tie_total = ties.shape[1]
    lane = lanes_of((COMPS, cols))
    core = lax.axis_index("pb")
    across = lax.axis_index("ty")
    along = lax.axis_index("tx")
    place = along * pb_count + core

    owner = ref["owner"][...]
    hot_slot = ref["hot_slot"][...]
    hot_two = jnp.concatenate([hot_slot] * 2, axis=0)
    fit_value = jnp.zeros((COMPS, tie_total), F32)
    bins = jnp.zeros((COMPS, slots), F32)
    peers = tx_count * ty_count
    block = math.gcd(peers, 8)

    def collect(first, carry):
        fit_value, bins = carry
        parts = [got[first + peer] for peer in range(block)]
        fit_all = jnp.concatenate([part[0:COMPS] for part in parts], axis=0)
        wide = dot(jnp.concatenate(split(fit_all, 2), axis=1), hot_two)
        for peer, part in enumerate(parts):
            fit_value = jnp.where(owner == first + peer, wide[peer * COMPS : (peer + 1) * COMPS], fit_value)
            bins = bins + part[COMPS : 2 * COMPS]
        return fit_value, bins

    if block == peers:
        fit_value, bins = collect(0, (fit_value, bins))
    else:
        fit_value, bins = lax.fori_loop(
            0, peers // block, lambda at, carry: collect(at * block, carry), (fit_value, bins)
        )
    count = bins[COUNT_ROW : COUNT_ROW + 1]
    for out, fit, base in (("fit_res", "fit_disp", 0), ("fit_tan", "fit_dir", 8)):
        ref[out][...] = 2.0 * (count * ref[fit][...] - bins[base : base + 6])

    pulled = split(2.0 * (ties[...] - fit_value), 2)
    hot_row = ref["hot_row"][...]
    places = [comp % 6 + comp // 6 * 8 for comp in range(12)]
    lhs = [
        jnp.concatenate([hot_row * part[place_of : place_of + 1] for part in pulled], axis=1)
        for place_of in places
    ]
    hot_col = ref["hot_col"][...]
    tie_forces = dot(jnp.concatenate(lhs, axis=0), jnp.concatenate([hot_col] * 2, axis=1), ((1,), (1,)))

    def around(step, side, packed=False):
        there, over = along + step, across + side
        valid = (there >= 0) & (there < tx_count) & (over >= 0) & (over < ty_count)
        block = got.at[jnp.where(valid, there * ty_count + over, 0)]
        if packed:
            value = unpack_column(block[0:COMPS, :], row_total)
        else:
            value = block[2 * COMPS : 3 * COMPS, :]
        return jnp.where(valid, value, 0.0)

    upper = core == 0
    behind = 2 * core - 1
    near, _ = mate_rows(ref["mate"])
    rows_near = (around(0, -1), near, around(0, 1))
    rows_far = tuple(around(behind, side) for side in (-1, 0, 1))
    next_rows = [jnp.where(upper, one, two) for one, two in zip(rows_near, rows_far)]
    prev_rows = [jnp.where(upper, two, one) for one, two in zip(rows_near, rows_far)]
    prev_row, next_row = prev_rows[1], next_rows[1]
    next_col = around(0, 1, True)
    prev_col = around(0, -1, True)
    next_corner = (prev_rows[2][:, 0:1], next_rows[2][:, 0:1])
    prev_corner = (prev_rows[0][:, cols - 1 : cols], next_rows[0][:, cols - 1 : cols])

    def column(inner, before, after):
        line = pltpu.roll(inner, 1, 1)
        line = jnp.where(lane == 0, before, line)
        return jnp.where(lane == row_total + 1, after, line)

    own_cols = ref["cols"]
    line_prev = column(prev_col, prev_corner[0], prev_corner[1])
    line_next = column(next_col, next_corner[0], next_corner[1])
    line_first = column(own_cols[0:COMPS, :], prev_row[:, 0:1], next_row[:, 0:1])
    line_final = column(
        own_cols[COMPS : 2 * COMPS, :], prev_row[:, cols - 1 : cols], next_row[:, cols - 1 : cols]
    )

    def shifted(row_value, beyond):
        return jnp.where(lane == cols - 1, beyond, pltpu.roll(row_value, cols - 1, 1))

    first_row = fields[0:COMPS, :]
    last_row = fields[(row_total - 1) * COMPS :, :]
    far_row = rows_far[1]
    lower_row = jnp.where(upper, far_row, last_row)
    upper_row = jnp.where(upper, first_row, far_row)
    own_beyond = jnp.where(upper, next_col[:, 0:1], next_col[:, row_total - 1 : row_total])
    far_beyond = rows_far[2][:, 0:1]
    tile_far = strain_tile(
        lower_row,
        upper_row,
        shifted(lower_row, jnp.where(upper, far_beyond, own_beyond)),
        shifted(upper_row, jnp.where(upper, own_beyond, far_beyond)),
    )
    half = cols // 2
    low = lane < half
    back = cols - 1

    def two(left, right_line):
        return jnp.where(low, left, pltpu.roll(right_line, half, 1))

    left_base = two(line_prev, line_final)
    left_upper = two(line_first, line_next)
    right_base = two(pltpu.roll(line_prev, back, 1), pltpu.roll(line_final, back, 1))
    right_upper = two(pltpu.roll(line_first, back, 1), pltpu.roll(line_next, back, 1))
    tile_side = strain_tile(left_base, right_base, left_upper, right_upper)

    edge_tile = jnp.concatenate((tile_far, tile_side), axis=1)
    primal, tangent = stress_sums([edge_tile], ref["w_first"], ref["w_mid"], ref["b_mid"], ref["w_last"])[0]
    f_base, f_right, f_upper, f_corner = corner_forces(primal[:, :cols], tangent[:, :cols])
    s_base, s_right, s_upper, s_corner = corner_forces(primal[:, cols:], tangent[:, cols:])

    def mask(value, keep):
        return jnp.where(keep, value, 0.0)

    def moved(value):
        return pltpu.roll(mask(value, lane < cols - 1), 1, 1)

    has_row = place > 0
    has_col = across > 0
    row_first = mask(f_right + moved(f_corner), upper & has_row)
    row_last = mask(f_base + moved(f_upper), core == 1)
    first_lane = jnp.where(has_row, 0, 1)
    s_corner = mask(s_corner, (lane >= first_lane) & (lane < row_total))
    s_upper = mask(s_upper, (lane >= 1) & (lane <= row_total))
    col_first = mask(pltpu.roll(s_upper, back, 1) + s_corner, has_col)
    valid = (lane >= half + 1 - core) & (lane <= half + row_total - core)
    s_base = mask(s_base, valid)
    s_right = mask(s_right, valid)
    col_last = pltpu.roll(pltpu.roll(s_base, back, 1) + s_right, cols - half, 1)

    assert 4 * row_total <= cols
    line = jnp.zeros((COMPS, cols), F32)
    for at, part in enumerate(split(col_first, 2) + split(col_last, 2)):
        part = part.astype(F32)
        part = pltpu.roll(part, at * row_total, 1) if at else part
        line = jnp.where((lane >= at * row_total) & (lane < (at + 1) * row_total), part, line)
    shape = (row_total, cols)
    eye = jnp.bitwise_and(lanes_of(shape), row_total - 1) == rows_of(shape)
    lhs = [jnp.where(eye, line[place_of : place_of + 1], 0.0).astype(BF16) for place_of in places]
    shape = (cols, cols)
    in_first = (rows_of(shape) == 0) & (lanes_of(shape) < 2 * row_total)
    in_last = (rows_of(shape) == cols - 1) & (lanes_of(shape) >= 2 * row_total)
    ends = (in_first | (in_last & (lanes_of(shape) < 4 * row_total))).astype(F32).astype(BF16)
    col_forces = dot(jnp.concatenate(lhs, axis=0), ends, ((1,), (1,)))

    row = rows_of((row_total, cols))
    for comp, place_of in enumerate(places):
        rows = slice(comp * row_total, (comp + 1) * row_total)
        value = tie_forces[rows] + col_forces[rows]
        value = value + jnp.where(row == 0, row_first[place_of : place_of + 1], 0.0)
        value = value + jnp.where(row == row_total - 1, row_last[place_of : place_of + 1], 0.0)
        partial[rows, :] = value - ref["load"][rows, :] if comp < 6 else value


def combine(swapped, partial, own, other, between, fit_one, fit_two, res, tan, fit_res, fit_tan):
    fit_res[...] = fit_one[...]
    fit_tan[...] = fit_two[...]
    row_total = partial.shape[0] // 12
    held = own.shape[0] // 12
    skip = row_total - held
    here = lax.axis_index("groups") == 0
    for comp in range(12):
        target = res if comp < 6 else tan
        start = comp % 6 * row_total
        rows = slice(comp * held, (comp + 1) * held)
        first, second = own[rows, :], other[rows, :]
        if swapped:
            first, second = jnp.where(here, first, second), jnp.where(here, second, first)
        target[start : start + row_total, :] = partial[comp * row_total : (comp + 1) * row_total, :]
        target[start : start + held, :] += first
        target[start + skip : start + row_total, :] += second
        count = between.shape[0] // 12
        low = start + held - 2
        target[low : low + count, :] += between[comp * count : (comp + 1) * count, :]


def per_device(
    displacement,
    direction,
    load,
    w_in,
    b_in,
    w_mid,
    b_mid,
    w_out,
    fitting_disp,
    fitting_dir,
    tie_node,
    tie_owner,
    tie_slot,
):
    tx_count = lax.axis_size("tx")
    ty_count = lax.axis_size("ty")
    pb_count = lax.axis_size("pb")
    peers = tx_count * ty_count
    axes = (tx_count, ty_count, pb_count)
    _, row_total, cols = displacement.shape
    slots = fitting_disp.shape[1]
    tie_total = tie_node.shape[0]
    hid = w_mid.shape[0]
    flat = (6 * row_total, cols)
    disp2 = displacement.reshape(flat)
    dir2 = direction.reshape(flat)
    load2 = load.reshape(flat)
    node2 = tie_node.reshape(tie_total // 128, 128)
    slot2 = tie_slot.reshape(tie_total // 128, 128)
    owner2 = tie_owner.reshape(1, tie_total)

    def shape(*dims, dtype=F32):
        return jax.ShapeDtypeStruct(dims, dtype)

    assert pb_count == 2 and slots == cols
    smalls = (
        fitting_disp,
        fitting_dir,
        node2,
        owner2,
        slot2,
        b_in.reshape(1, hid),
        b_mid.reshape(1, hid),
        w_in.T,
        w_out,
    )
    outs = pl.pallas_call(
        lambda *refs: gather_nodes(len(smalls), *refs),
        out_shape=[pltpu.VMEM((row_total * COMPS, cols), F32), pltpu.VMEM((2 * COMPS, cols), F32)]
        + [pltpu.VMEM(value.shape, value.dtype) for value in smalls],
        in_specs=local(2 + len(smalls)),
        out_specs=local(2 + len(smalls)),
        name="gather_nodes",
    )(disp2, dir2, *smalls)
    fields, rows, fit_disp, fit_dir, node, owner, slot, b_first, b_second, w_first_in, w_final = outs
    mate = lax.ppermute(rows, "pb", [(0, 1), (1, 0)])

    inputs = (fields, fit_disp, fit_dir, node, owner, slot, w_first_in, b_first, b_second, w_final)
    inputs = tuple(on_chip(value) for value in inputs)
    small = peers * 2 * COMPS * slots <= SMALL
    ties, cols_out, hot_col, hot_slot, hot_row, sums, w_first, w_last, b_cols = pl.pallas_call(
        lambda *refs: sum_ties(peers, *refs),
        out_shape=[
            pltpu.VMEM((COMPS, tie_total), F32),
            pltpu.VMEM((2 * COMPS, cols), F32),
            pltpu.VMEM((cols, tie_total), BF16),
            pltpu.VMEM((slots, tie_total), BF16),
            pltpu.VMEM((row_total, tie_total), BF16),
            (pltpu.VMEM if small else jax.ShapeDtypeStruct)((peers, 2 * COMPS, slots), F32),
            pltpu.VMEM((8 * hid, 4 * COMPS), BF16),
            pltpu.VMEM((128, hid), BF16),
            pltpu.VMEM((hid, 128), F32),
        ],
        in_specs=local(len(inputs)),
        out_specs=local(9),
        name="sum_ties",
    )(*inputs)
    inputs = [on_chip(value) if value.size <= SMALL else value for value in (sums, cols_out, mate)]
    pay = pl.pallas_call(
        lambda *refs: fill_blocks((tx_count, ty_count), row_total, *refs),
        out_shape=shape(peers, 3 * COMPS, slots),
        in_specs=local(len(inputs)),
        out_specs=local(1)[0],
        name="fill_blocks",
    )(*inputs)
    got = lax.all_to_all(pay, ("tx", "ty"), split_axis=0, concat_axis=0, tiled=True)

    inputs = tuple(on_chip(value) for value in (fields, mate, w_first, w_mid, b_cols, w_last))
    groups = lax.axis_size("groups")
    count = (row_total - SHARED_ROWS) // 2
    halves = []
    for pick in (None,) if groups == 2 else (0, 1):
        half = pl.pallas_call(
            lambda *refs: interior(pick, count, *refs),
            out_shape=pltpu.VMEM(((count + 1) * 12, cols), F32),
            in_specs=local(len(inputs)),
            out_specs=local(1)[0],
            scratch_shapes=[pltpu.VMEM(((count + 3) * COMPS, cols), F32)],
            name="interior",
        )(*inputs)
        halves.append(half)
    if groups == 2:
        halves.append(lax.ppermute(halves[0], "groups", [(0, 1), (1, 0)]))
    fields_late, _ = lax.optimization_barrier((fields, halves[0]))
    inputs = tuple(on_chip(value) for value in (fields_late, w_first, w_mid, b_cols, w_last))
    between = pl.pallas_call(
        lambda *refs: middle(count, *refs),
        out_shape=pltpu.VMEM(((SHARED_ROWS + 2) * 12, cols), F32),
        in_specs=local(len(inputs)),
        out_specs=local(1)[0],
        scratch_shapes=[pltpu.VMEM(((SHARED_ROWS + 3) * COMPS, cols), F32)],
        name="middle",
    )(*inputs)

    named = dict(
        got=got,
        mate=mate,
        fields=fields,
        ties=ties,
        cols=cols_out,
        w_first=w_first,
        w_mid=w_mid,
        b_mid=b_cols,
        w_last=w_last,
        hot_col=hot_col,
        hot_slot=hot_slot,
        hot_row=hot_row,
        load=load2,
        owner=owner,
        fit_disp=fit_disp,
        fit_dir=fit_dir,
    )
    named = {name: on_chip(value) if value.size <= SMALL else value for name, value in named.items()}
    names = list(named)
    partial, fit_one, fit_two = pl.pallas_call(
        lambda *refs: edges(names + ["partial", "fit_res", "fit_tan"], axes, *refs),
        out_shape=[pltpu.VMEM(size, F32) for size in ((12 * row_total, cols), (6, slots), (6, slots))],
        in_specs=local(len(names)),
        out_specs=local(3),
        name="edges",
    )(*named.values())

    inputs = tuple(on_chip(value) for value in (partial, halves[0], halves[1], between, fit_one, fit_two))
    res, tan, fit_res, fit_tan = pl.pallas_call(
        lambda *refs: combine(groups == 2, *refs),
        out_shape=[shape(*flat), shape(*flat), shape(6, slots), shape(6, slots)],
        in_specs=local(len(inputs)),
        out_specs=local(4),
        name="combine",
    )(*inputs)
    cube = displacement.shape
    return (res.reshape(cube), tan.reshape(cube), fit_res, fit_tan)


def solution(mesh):
    in_specs = (
        P(None, ("tx", "pb"), "ty"),
        P(None, ("tx", "pb"), "ty"),
        P(None, ("tx", "pb"), "ty"),
        P(),
        P(),
        P(),
        P(),
        P(),
        P(None, ("groups", "tx", "ty", "pb")),
        P(None, ("groups", "tx", "ty", "pb")),
        P(("groups", "tx", "ty", "pb")),
        P(("groups", "tx", "ty", "pb"), None),
        P(("groups", "tx", "ty", "pb")),
    )
    out_specs = (
        P(None, ("groups", "tx", "pb"), "ty"),
        P(None, ("groups", "tx", "pb"), "ty"),
        P(None, ("groups", "tx", "ty", "pb")),
        P(None, ("groups", "tx", "ty", "pb")),
    )
    return jax.shard_map(
        per_device, mesh=mesh, in_specs=in_specs, out_specs=out_specs, check_vma=False
    )
```

```python
import math

import jax
import jax.numpy as jnp
from jax import lax
from jax.experimental import pallas as pl
from jax.experimental.pallas import tpu as pltpu
from jax.sharding import PartitionSpec as P

F32 = jnp.float32
BF16 = jnp.bfloat16
GAUSS = (0.5 - 0.5 / math.sqrt(3.0), 0.5 + 0.5 / math.sqrt(3.0))
COMPS = 16
COUNT_ROW = 6
SPARE_ROWS = (6, 7, 14)
SMALL = 1 << 18
SHARED_ROWS = 4
PAD = 8


def local(count):
    return [pl.BlockSpec(memory_space=pltpu.VMEM)] * count


def on_chip(value):
    return pltpu.with_memory_space_constraint(value, pltpu.VMEM)


def dot(a, b, dims=((1,), (0,))):
    return lax.dot_general(a, b, (dims, ((), ())), preferred_element_type=F32)


def split(value, terms):
    parts = []
    for _ in range(terms):
        part = value.astype(BF16)
        parts.append(part)
        value = value - part.astype(F32)
    return parts


def rows_of(value):
    return lax.broadcasted_iota(jnp.int32, value, 0)


def lanes_of(value):
    return lax.broadcasted_iota(jnp.int32, value, 1)


def one_hot(index, size):
    shape = (size, index.shape[1])
    return (rows_of(shape) == index).astype(F32).astype(BF16)


def as_line(ref):
    value = ref[...]
    return jnp.concatenate([value[row : row + 1] for row in range(value.shape[0])], axis=1)


def paired(top, bottom):
    spare = jnp.zeros((2, top.shape[1]), F32)
    return jnp.concatenate([top, spare, bottom, spare], axis=0)


def strain_tile(f00, f10, f01, f11):
    along_low = f10 - f00
    along_high = f11 - f01
    across_low = f01 - f00
    across_high = f11 - f10
    shape = f00.shape
    row = rows_of(shape)
    ones = ((row == 6) | (row == 7) | (row == 14)).astype(F32)
    groups = []
    for frac in GAUSS:
        groups.append((((1.0 - frac) * along_low + frac * along_high) + ones).astype(BF16))
    for frac in GAUSS:
        groups.append(((1.0 - frac) * across_low + frac * across_high).astype(BF16))
    return jnp.concatenate(groups, axis=0)


def stress_sums(strains, w_first, w_mid, b_mid, w_last):
    hid = w_mid.shape[0]
    tasks = [(tile, point) for tile in range(len(strains)) for point in range(4)]
    totals = [[None, None] for _ in strains]

    def layer_one(task):
        tile, point = task
        start = point * 2 * hid
        return (
            dot(w_first[start : start + hid, :], strains[tile]),
            dot(w_first[start + hid : start + 2 * hid, :], strains[tile]),
        )

    def activate(value, slope):
        act = jnp.tanh(value)
        return (act.astype(BF16), ((1.0 - act * act) * slope).astype(BF16))

    def layer_two(hidden):
        bias = b_mid[...]
        value = dot(w_mid[...], hidden[0])
        slope = dot(w_mid[...], hidden[1])
        bias = jnp.concatenate([bias] * (value.shape[1] // bias.shape[1]), axis=1)
        return (value + bias, slope)

    def layer_three(task, hidden):
        tile, point = task
        last = w_last[point * 32 : (point + 1) * 32, :]
        for side in range(2):
            part = dot(last, hidden[side])
            old = totals[tile][side]
            totals[tile][side] = part if old is None else old + part

    ones = {0: layer_one(tasks[0])}
    twos = {}
    for at in range(len(tasks) + 1):
        if at + 1 < len(tasks):
            ones[at + 1] = layer_one(tasks[at + 1])
        if at < len(tasks):
            hidden = activate(*ones.pop(at))
            twos[at] = layer_two(hidden)
        if at >= 1:
            layer_three(tasks[at - 1], activate(*twos.pop(at - 1)))
    return totals


def corner_forces(primal, tangent):
    def both(group):
        return jnp.concatenate([primal[group * 8 : group * 8 + 8], tangent[group * 8 : group * 8 + 8]], axis=0)

    along = (both(0), both(1))
    across = (both(2), both(3))

    def mix(pair, weights):
        return (0.25 * weights[0]) * pair[0] + (0.25 * weights[1]) * pair[1]

    rest = (1.0 - GAUSS[0], 1.0 - GAUSS[1])
    along_rest = mix(along, rest)
    along_frac = mix(along, GAUSS)
    across_rest = mix(across, rest)
    across_frac = mix(across, GAUSS)
    return (
        -along_rest - across_rest,
        along_rest - across_frac,
        across_rest - along_frac,
        along_frac + across_frac,
    )


def gather_nodes(count, disp, dirn, *refs):
    fields, rows = refs[count : count + 2]
    for source, target in zip(refs[:count], refs[count + 2 :]):
        target[...] = source[...]
    row_total = fields.shape[0] // COMPS
    fields[...] = jnp.zeros(fields.shape, F32)
    for comp in range(6):
        part = slice(comp * row_total, (comp + 1) * row_total)
        fields[pl.ds(comp, row_total, stride=COMPS), :] = disp[part, :]
        fields[pl.ds(8 + comp, row_total, stride=COMPS), :] = dirn[part, :]
    rows[0:COMPS, :] = fields[0:COMPS, :]
    rows[COMPS : 2 * COMPS, :] = fields[(row_total - 1) * COMPS :, :]


def sum_ties(peers, *refs):
    (fields, fit_disp, fit_dir, node_ref, owner_ref, slot_ref) = refs[:6]
    (ties, col_out, hot_col_out, hot_slot_out, hot_row_out, pay) = refs[10:16]
    build_weights(*refs[6:10], *refs[16:])
    row_total = fields.shape[0] // COMPS
    cols = fields.shape[1]
    slots = fit_disp.shape[1]
    tie_total = ties.shape[1]

    lane = lanes_of((COMPS, cols))
    for side, column in enumerate((0, cols - 1)):
        gathered = jnp.zeros((COMPS, cols), F32)
        for row in range(row_total):
            value = fields[row * COMPS : (row + 1) * COMPS, column : column + 1]
            gathered = jnp.where(lane == row, value, gathered)
        col_out[side * COMPS : (side + 1) * COMPS, :] = gathered

    node = as_line(node_ref)
    slot = as_line(slot_ref)
    owner = owner_ref[...]
    node_row = lax.shift_right_logical(node, cols.bit_length() - 1)
    node_col = jnp.bitwise_and(node, cols - 1)
    hot_col = one_hot(node_col, cols)
    hot_col_out[...] = hot_col
    hot_row_out[...] = one_hot(node_row, row_total)
    wide = dot(
        jnp.concatenate(split(fields[...], 2), axis=1), jnp.concatenate([hot_col] * 2, axis=0)
    )
    value = jnp.zeros((COMPS, tie_total), F32)
    for row in range(row_total):
        value = jnp.where(node_row == row, wide[row * COMPS : (row + 1) * COMPS], value)
    value = jnp.where(rows_of(value.shape) == COUNT_ROW, 1.0, value)
    ties[...] = value
    stack = jnp.concatenate(split(value, 2), axis=0)
    hot_slot = one_hot(slot, slots)
    hot_slot_out[...] = hot_slot
    fitting = paired(fit_disp[...], fit_dir[...])

    def bins(first, count):
        lhs = [
            stack * (owner == first + at).astype(F32).astype(BF16) for at in range(count)
        ]
        return dot(jnp.concatenate(lhs, axis=0), hot_slot, ((1,), (1,)))

    def folded(wide_bins, at):
        part = wide_bins[at * 2 * COMPS : (at + 1) * 2 * COMPS]
        return part[0:COMPS] + part[COMPS : 2 * COMPS]

    block = math.gcd(peers, 8)

    def fill(first):
        wide_bins = bins(first, block)
        for peer in range(block):
            pay[first + peer, 0:COMPS, :] = fitting
            pay[first + peer, COMPS : 2 * COMPS, :] = folded(wide_bins, peer)

    if block == peers:
        fill(0)
    else:
        lax.fori_loop(0, peers // block, lambda at, carry: (fill(at * block), carry)[1], 0)


def mate_rows(mate):
    upper = lax.axis_index("pb") == 0
    first, last = mate[0:COMPS, :], mate[COMPS : 2 * COMPS, :]
    return jnp.where(upper, first, last), jnp.where(upper, last, first)


def fill_blocks(axes, row_total, sums, columns, mate, pay):
    tx_count, ty_count = axes
    along, across = lax.axis_index("tx"), lax.axis_index("ty")
    near, far = mate_rows(mate)
    pay[:, 0 : 2 * COMPS, :] = sums[...]
    ahead = along + 1 - 2 * lax.axis_index("pb")
    for side in (-1, 0, 1):
        over = across + side
        inside = (over >= 0) & (over < ty_count)

        @pl.when(inside & (ahead >= 0) & (ahead < tx_count))
        def _():
            pay[ahead * ty_count + over, 2 * COMPS : 3 * COMPS, :] = far

        if side == 0:
            continue
        edge = 0 if side < 0 else 1
        packed = pack_column(columns[edge * COMPS : (edge + 1) * COMPS, :], row_total)

        @pl.when(inside)
        def _():
            at = along * ty_count + over
            pay[at, 2 * COMPS : 3 * COMPS, :] = near
            for line, row in zip(packed, SPARE_ROWS):
                pay[at, row : row + 1, :] = line


def pack_column(column, width):
    each = column.shape[1] // width
    lines = []
    for first in range(0, 12, each):
        line = None
        for at in range(first, min(first + each, 12)):
            row = at % 6 + at // 6 * 8
            part = column[row : row + 1]
            if at > first:
                part = pltpu.roll(part, (at - first) * width, 1)
            line = part if line is None else line + part
        lines.append(line)
    assert len(lines) <= len(SPARE_ROWS)
    return lines


def unpack_column(block, width):
    shape = (COMPS, block.shape[1])
    each = shape[1] // width
    row = rows_of(shape)
    column = jnp.zeros(shape, F32)
    for at in range(12):
        spare = SPARE_ROWS[at // each]
        line = block[spare : spare + 1]
        if at % each:
            line = pltpu.roll(line, shape[1] - at % each * width, 1)
        column = jnp.where(row == at % 6 + at // 6 * 8, line, column)
    return jnp.where(lanes_of(shape) < width, column, 0.0)


def build_weights(w_in, b_in, b_mid, w_out, w_first, w_last, b_cols):
    hid = w_in.shape[1]
    bias_rows = split(b_in[...], 3)
    row = rows_of((8, hid))
    stacked = jnp.zeros((8, hid), F32)
    mid_stacked = jnp.zeros((8, hid), F32)
    for at, (one, two) in enumerate(zip(bias_rows, split(b_mid[...], 3))):
        stacked = jnp.where(row == at, one.astype(F32), stacked)
        mid_stacked = jnp.where(row == at, two.astype(F32), mid_stacked)
    lhs = jnp.concatenate([w_in[...].astype(F32), jnp.zeros((4, hid), F32), stacked], axis=0).astype(BF16)
    sel_shape = (24, 4 * COMPS)
    source = rows_of(sel_shape)
    target = lanes_of(sel_shape)
    for point in range(4):
        a_base = (point // 2) * COMPS
        c_base = (2 + point % 2) * COMPS
        for side in range(2):
            hit = (source < 6) & (target == a_base + 8 * side + source)
            hit = hit | ((source >= 6) & (source < 12) & (target == c_base + 8 * side + source - 6))
            if side == 0:
                for at, spot in enumerate((6, 7, 14)):
                    hit = hit | ((source == 16 + at) & (target == a_base + spot))
            block = dot(lhs, hit.astype(F32).astype(BF16), ((0,), (0,)))
            start = (2 * point + side) * hid
            w_first[start : start + hid, :] = block.astype(BF16)
    ones = (rows_of((8, 128)) < 3).astype(F32).astype(BF16)
    b_cols[...] = dot(mid_stacked.astype(BF16), ones, ((0,), (0,)))
    last_shape = (128, 12)
    target = rows_of(last_shape)
    source = lanes_of(last_shape)
    hit = target < 0
    for point in range(4):
        a_base = point * 32 + (point // 2) * 8
        c_base = point * 32 + 16 + (point % 2) * 8
        hit = hit | ((source < 6) & (target == a_base + source))
        hit = hit | ((source >= 6) & (target == c_base + source - 6))
    w_last[...] = dot(hit.astype(F32).astype(BF16), w_out[...]).astype(BF16)


def row_forces(fields, lines, first, weights, forces):
    cols = fields.shape[1]
    lines = [(line, pltpu.roll(line, cols - 1, 1)) for line in lines]
    tiles = [
        strain_tile(one[0], two[0], one[1], two[1]) for one, two in zip(lines[:-1], lines[1:])
    ]
    tiles = [jnp.concatenate(tiles[at : at + 2], axis=1) for at in range(0, len(tiles), 2)]
    sums = stress_sums(tiles, *weights)
    keep = lanes_of((COMPS, cols)) < cols - 1
    forces[...] = jnp.zeros(forces.shape, F32)
    for tile, (primal, tangent) in enumerate(sums):
        for side in range(2):
            lanes = slice(side * cols, (side + 1) * cols)
            parts = corner_forces(primal[:, lanes], tangent[:, lanes])
            base, right, upper, corner = (jnp.where(keep, part, 0.0) for part in parts)
            at = (2 * tile + side + 1) * COMPS
            forces[at : at + COMPS, :] += base + pltpu.roll(upper, 1, 1)
            forces[at + COMPS : at + 2 * COMPS, :] += right + pltpu.roll(corner, 1, 1)


def component_rows(forces, start, sent):
    held = (sent.shape[0] - PAD) // 12
    for comp in range(12):
        rows = pl.ds(start * COMPS + comp % 6 + comp // 6 * 8, held, stride=COMPS)
        sent[comp * held : (comp + 1) * held, :] = forces[rows, :]


def node_row(fields, row):
    return fields[pl.ds(pl.multiple_of(row * COMPS, COMPS), COMPS), :]


def interior(pick, count, fields, mate, w_first, w_mid, b_cols, w_last, sent, forces):
    row_total = fields.shape[0] // COMPS
    group = lax.axis_index("groups") if pick is None else pick
    core = lax.axis_index("pb")
    first = group * (row_total - count) - core
    near, _ = mate_rows(mate)
    lines = [jnp.where((core == 1) & (group == 0), near, node_row(fields, jnp.maximum(first, 0)))]
    lines += [node_row(fields, first + at) for at in range(1, count)]
    last = node_row(fields, jnp.minimum(first + count, row_total - 1))
    lines.append(jnp.where((core == 0) & (group == 1), near, last))
    row_forces(fields, lines, first, (w_first, w_mid, b_cols, w_last), forces)
    component_rows(forces, 1 + group * (row_total - count - 1) - first, sent)


def middle(count, fields, w_first, w_mid, b_cols, w_last, kept, forces):
    row_total = fields.shape[0] // COMPS
    core = lax.axis_index("pb")
    first = count - core
    lines = [node_row(fields, first + at) for at in range(row_total - 2 * count + 1)]
    row_forces(fields, lines, first, (w_first, w_mid, b_cols, w_last), forces)
    component_rows(forces, core, kept)


def edges(names, axes, *refs):
    ref = dict(zip(names, refs))
    tx_count, ty_count, pb_count = axes
    fields, ties, partial, got = ref["fields"], ref["ties"], ref["partial"], ref["got"]
    row_total, cols = fields.shape[0] // COMPS, fields.shape[1]
    slots = got.shape[2]
    tie_total = ties.shape[1]
    lane = lanes_of((COMPS, cols))
    core = lax.axis_index("pb")
    across = lax.axis_index("ty")
    along = lax.axis_index("tx")
    place = along * pb_count + core

    owner = ref["owner"][...]
    hot_slot = ref["hot_slot"][...]
    hot_two = jnp.concatenate([hot_slot] * 2, axis=0)
    fit_value = jnp.zeros((COMPS, tie_total), F32)
    bins = jnp.zeros((COMPS, slots), F32)
    peers = tx_count * ty_count
    block = math.gcd(peers, 8)

    def collect(first, carry):
        fit_value, bins = carry
        parts = [got[first + peer] for peer in range(block)]
        fit_all = jnp.concatenate([part[0:COMPS] for part in parts], axis=0)
        wide = dot(jnp.concatenate(split(fit_all, 2), axis=1), hot_two)
        for peer, part in enumerate(parts):
            fit_value = jnp.where(owner == first + peer, wide[peer * COMPS : (peer + 1) * COMPS], fit_value)
            bins = bins + part[COMPS : 2 * COMPS]
        return fit_value, bins

    if block == peers:
        fit_value, bins = collect(0, (fit_value, bins))
    else:
        fit_value, bins = lax.fori_loop(
            0, peers // block, lambda at, carry: collect(at * block, carry), (fit_value, bins)
        )
    count = bins[COUNT_ROW : COUNT_ROW + 1]
    for out, fit, base in (("fit_res", "fit_disp", 0), ("fit_tan", "fit_dir", 8)):
        ref[out][...] = 2.0 * (count * ref[fit][...] - bins[base : base + 6])

    pulled = split(2.0 * (ties[...] - fit_value), 2)
    hot_row = ref["hot_row"][...]
    places = [comp % 6 + comp // 6 * 8 for comp in range(12)]
    lhs = [
        jnp.concatenate([hot_row * part[place_of : place_of + 1] for part in pulled], axis=1)
        for place_of in places
    ]
    hot_col = ref["hot_col"][...]
    tie_forces = dot(jnp.concatenate(lhs, axis=0), jnp.concatenate([hot_col] * 2, axis=1), ((1,), (1,)))

    def around(step, side, packed=False):
        there, over = along + step, across + side
        valid = (there >= 0) & (there < tx_count) & (over >= 0) & (over < ty_count)
        block = got.at[jnp.where(valid, there * ty_count + over, 0)]
        if packed:
            value = unpack_column(block[0:COMPS, :], row_total)
        else:
            value = block[2 * COMPS : 3 * COMPS, :]
        return jnp.where(valid, value, 0.0)

    upper = core == 0
    behind = 2 * core - 1
    near, _ = mate_rows(ref["mate"])
    rows_near = (around(0, -1), near, around(0, 1))
    rows_far = tuple(around(behind, side) for side in (-1, 0, 1))
    next_rows = [jnp.where(upper, one, two) for one, two in zip(rows_near, rows_far)]
    prev_rows = [jnp.where(upper, two, one) for one, two in zip(rows_near, rows_far)]
    prev_row, next_row = prev_rows[1], next_rows[1]
    next_col = around(0, 1, True)
    prev_col = around(0, -1, True)
    next_corner = (prev_rows[2][:, 0:1], next_rows[2][:, 0:1])
    prev_corner = (prev_rows[0][:, cols - 1 : cols], next_rows[0][:, cols - 1 : cols])

    def column(inner, before, after):
        line = pltpu.roll(inner, 1, 1)
        line = jnp.where(lane == 0, before, line)
        return jnp.where(lane == row_total + 1, after, line)

    own_cols = ref["cols"]
    line_prev = column(prev_col, prev_corner[0], prev_corner[1])
    line_next = column(next_col, next_corner[0], next_corner[1])
    line_first = column(own_cols[0:COMPS, :], prev_row[:, 0:1], next_row[:, 0:1])
    line_final = column(
        own_cols[COMPS : 2 * COMPS, :], prev_row[:, cols - 1 : cols], next_row[:, cols - 1 : cols]
    )

    def shifted(row_value, beyond):
        return jnp.where(lane == cols - 1, beyond, pltpu.roll(row_value, cols - 1, 1))

    first_row = fields[0:COMPS, :]
    last_row = fields[(row_total - 1) * COMPS :, :]
    far_row = rows_far[1]
    lower_row = jnp.where(upper, far_row, last_row)
    upper_row = jnp.where(upper, first_row, far_row)
    own_beyond = jnp.where(upper, next_col[:, 0:1], next_col[:, row_total - 1 : row_total])
    far_beyond = rows_far[2][:, 0:1]
    tile_far = strain_tile(
        lower_row,
        upper_row,
        shifted(lower_row, jnp.where(upper, far_beyond, own_beyond)),
        shifted(upper_row, jnp.where(upper, own_beyond, far_beyond)),
    )
    half = cols // 2
    low = lane < half
    back = cols - 1

    def two(left, right_line):
        return jnp.where(low, left, pltpu.roll(right_line, half, 1))

    left_base = two(line_prev, line_final)
    left_upper = two(line_first, line_next)
    right_base = two(pltpu.roll(line_prev, back, 1), pltpu.roll(line_final, back, 1))
    right_upper = two(pltpu.roll(line_first, back, 1), pltpu.roll(line_next, back, 1))
    tile_side = strain_tile(left_base, right_base, left_upper, right_upper)

    edge_tile = jnp.concatenate((tile_far, tile_side), axis=1)
    primal, tangent = stress_sums([edge_tile], ref["w_first"], ref["w_mid"], ref["b_mid"], ref["w_last"])[0]
    f_base, f_right, f_upper, f_corner = corner_forces(primal[:, :cols], tangent[:, :cols])
    s_base, s_right, s_upper, s_corner = corner_forces(primal[:, cols:], tangent[:, cols:])

    def mask(value, keep):
        return jnp.where(keep, value, 0.0)

    def moved(value):
        return pltpu.roll(mask(value, lane < cols - 1), 1, 1)

    has_row = place > 0
    has_col = across > 0
    row_first = mask(f_right + moved(f_corner), upper & has_row)
    row_last = mask(f_base + moved(f_upper), core == 1)
    first_lane = jnp.where(has_row, 0, 1)
    s_corner = mask(s_corner, (lane >= first_lane) & (lane < row_total))
    s_upper = mask(s_upper, (lane >= 1) & (lane <= row_total))
    col_first = mask(pltpu.roll(s_upper, back, 1) + s_corner, has_col)
    valid = (lane >= half + 1 - core) & (lane <= half + row_total - core)
    s_base = mask(s_base, valid)
    s_right = mask(s_right, valid)
    col_last = pltpu.roll(pltpu.roll(s_base, back, 1) + s_right, cols - half, 1)

    assert 4 * row_total <= cols
    line = jnp.zeros((COMPS, cols), F32)
    for at, part in enumerate(split(col_first, 2) + split(col_last, 2)):
        part = part.astype(F32)
        part = pltpu.roll(part, at * row_total, 1) if at else part
        line = jnp.where((lane >= at * row_total) & (lane < (at + 1) * row_total), part, line)
    shape = (row_total, cols)
    eye = jnp.bitwise_and(lanes_of(shape), row_total - 1) == rows_of(shape)
    lhs = [jnp.where(eye, line[place_of : place_of + 1], 0.0).astype(BF16) for place_of in places]
    shape = (cols, cols)
    in_first = (rows_of(shape) == 0) & (lanes_of(shape) < 2 * row_total)
    in_last = (rows_of(shape) == cols - 1) & (lanes_of(shape) >= 2 * row_total)
    ends = (in_first | (in_last & (lanes_of(shape) < 4 * row_total))).astype(F32).astype(BF16)
    col_forces = dot(jnp.concatenate(lhs, axis=0), ends, ((1,), (1,)))

    row = rows_of((row_total, cols))
    for comp, place_of in enumerate(places):
        rows = slice(comp * row_total, (comp + 1) * row_total)
        value = tie_forces[rows] + col_forces[rows]
        value = value + jnp.where(row == 0, row_first[place_of : place_of + 1], 0.0)
        value = value + jnp.where(row == row_total - 1, row_last[place_of : place_of + 1], 0.0)
        partial[rows, :] = value - ref["load"][rows, :] if comp < 6 else value


def combine(swapped, partial, own, other, between, fit_one, fit_two, res, tan, fit_res, fit_tan, total):
    fit_res[...] = fit_one[...]
    fit_tan[...] = fit_two[...]
    row_total = partial.shape[0] // 12
    held = (own.shape[0] - PAD) // 12
    count = (between.shape[0] - PAD) // 12
    here = lax.axis_index("groups") == 0
    for comp in range(12):
        start = comp * row_total
        rows = slice(comp * held, (comp + 1) * held)
        first, second = own[rows, :], other[rows, :]
        if swapped:
            first, second = jnp.where(here, first, second), jnp.where(here, second, first)
        total[start : start + row_total, :] = partial[start : start + row_total, :]
        total[start : start + held, :] += first
        total[start + row_total - held : start + row_total, :] += second
        low = start + held - 2
        total[low : low + count, :] += between[comp * count : (comp + 1) * count, :]
    res[...] = total[0 : 6 * row_total, :]
    tan[...] = total[6 * row_total : 12 * row_total, :]


def per_device(
    displacement,
    direction,
    load,
    w_in,
    b_in,
    w_mid,
    b_mid,
    w_out,
    fitting_disp,
    fitting_dir,
    tie_node,
    tie_owner,
    tie_slot,
):
    tx_count = lax.axis_size("tx")
    ty_count = lax.axis_size("ty")
    pb_count = lax.axis_size("pb")
    peers = tx_count * ty_count
    axes = (tx_count, ty_count, pb_count)
    _, row_total, cols = displacement.shape
    slots = fitting_disp.shape[1]
    tie_total = tie_node.shape[0]
    hid = w_mid.shape[0]
    flat = (6 * row_total, cols)
    disp2 = displacement.reshape(flat)
    dir2 = direction.reshape(flat)
    load2 = load.reshape(flat)
    node2 = tie_node.reshape(tie_total // 128, 128)
    slot2 = tie_slot.reshape(tie_total // 128, 128)
    owner2 = tie_owner.reshape(1, tie_total)

    def shape(*dims, dtype=F32):
        return jax.ShapeDtypeStruct(dims, dtype)

    assert pb_count == 2 and slots == cols
    smalls = (
        fitting_disp,
        fitting_dir,
        node2,
        owner2,
        slot2,
        b_in.reshape(1, hid),
        b_mid.reshape(1, hid),
        w_in.T,
        w_out,
    )
    outs = pl.pallas_call(
        lambda *refs: gather_nodes(len(smalls), *refs),
        out_shape=[pltpu.VMEM((row_total * COMPS, cols), F32), pltpu.VMEM((2 * COMPS, cols), F32)]
        + [pltpu.VMEM(value.shape, value.dtype) for value in smalls],
        in_specs=local(2 + len(smalls)),
        out_specs=local(2 + len(smalls)),
        name="gather_nodes",
    )(disp2, dir2, *smalls)
    fields, rows, fit_disp, fit_dir, node, owner, slot, b_first, b_second, w_first_in, w_final = outs
    mate = lax.ppermute(rows, "pb", [(0, 1), (1, 0)])

    inputs = (fields, fit_disp, fit_dir, node, owner, slot, w_first_in, b_first, b_second, w_final)
    inputs = tuple(on_chip(value) for value in inputs)
    small = peers * 2 * COMPS * slots <= SMALL
    ties, cols_out, hot_col, hot_slot, hot_row, sums, w_first, w_last, b_cols = pl.pallas_call(
        lambda *refs: sum_ties(peers, *refs),
        out_shape=[
            pltpu.VMEM((COMPS, tie_total), F32),
            pltpu.VMEM((2 * COMPS, cols), F32),
            pltpu.VMEM((cols, tie_total), BF16),
            pltpu.VMEM((slots, tie_total), BF16),
            pltpu.VMEM((row_total, tie_total), BF16),
            (pltpu.VMEM if small else jax.ShapeDtypeStruct)((peers, 2 * COMPS, slots), F32),
            pltpu.VMEM((8 * hid, 4 * COMPS), BF16),
            pltpu.VMEM((128, hid), BF16),
            pltpu.VMEM((hid, 128), F32),
        ],
        in_specs=local(len(inputs)),
        out_specs=local(9),
        name="sum_ties",
    )(*inputs)
    inputs = [on_chip(value) if value.size <= SMALL else value for value in (sums, cols_out, mate)]
    pay = pl.pallas_call(
        lambda *refs: fill_blocks((tx_count, ty_count), row_total, *refs),
        out_shape=shape(peers, 3 * COMPS, slots),
        in_specs=local(len(inputs)),
        out_specs=local(1)[0],
        name="fill_blocks",
    )(*inputs)
    got = lax.all_to_all(pay, ("tx", "ty"), split_axis=0, concat_axis=0, tiled=True)

    inputs = tuple(on_chip(value) for value in (fields, mate, w_first, w_mid, b_cols, w_last))
    groups = lax.axis_size("groups")
    count = (row_total - SHARED_ROWS) // 2
    halves = []
    for pick in (None,) if groups == 2 else (0, 1):
        half = pl.pallas_call(
            lambda *refs: interior(pick, count, *refs),
            out_shape=pltpu.VMEM(((count + 1) * 12 + PAD, cols), F32),
            in_specs=local(len(inputs)),
            out_specs=local(1)[0],
            scratch_shapes=[pltpu.VMEM(((count + 3 + PAD) * COMPS, cols), F32)],
            name="interior",
        )(*inputs)
        halves.append(half)
    if groups == 2:
        halves.append(lax.ppermute(halves[0], "groups", [(0, 1), (1, 0)]))
    fields_late, _ = lax.optimization_barrier((fields, halves[0]))
    inputs = tuple(on_chip(value) for value in (fields_late, w_first, w_mid, b_cols, w_last))
    between = pl.pallas_call(
        lambda *refs: middle(count, *refs),
        out_shape=pltpu.VMEM(((SHARED_ROWS + 2) * 12 + PAD, cols), F32),
        in_specs=local(len(inputs)),
        out_specs=local(1)[0],
        scratch_shapes=[pltpu.VMEM(((SHARED_ROWS + 3 + PAD) * COMPS, cols), F32)],
        name="middle",
    )(*inputs)

    named = dict(
        got=got,
        mate=mate,
        fields=fields,
        ties=ties,
        cols=cols_out,
        w_first=w_first,
        w_mid=w_mid,
        b_mid=b_cols,
        w_last=w_last,
        hot_col=hot_col,
        hot_slot=hot_slot,
        hot_row=hot_row,
        load=load2,
        owner=owner,
        fit_disp=fit_disp,
        fit_dir=fit_dir,
    )
    named = {name: on_chip(value) if value.size <= SMALL else value for name, value in named.items()}
    names = list(named)
    partial, fit_one, fit_two = pl.pallas_call(
        lambda *refs: edges(names + ["partial", "fit_res", "fit_tan"], axes, *refs),
        out_shape=[pltpu.VMEM(size, F32) for size in ((12 * row_total, cols), (6, slots), (6, slots))],
        in_specs=local(len(names)),
        out_specs=local(3),
        name="edges",
    )(*named.values())

    inputs = tuple(on_chip(value) for value in (partial, halves[0], halves[1], between, fit_one, fit_two))
    res, tan, fit_res, fit_tan = pl.pallas_call(
        lambda *refs: combine(groups == 2, *refs),
        out_shape=[shape(*flat), shape(*flat), shape(6, slots), shape(6, slots)],
        in_specs=local(len(inputs)),
        out_specs=local(4),
        scratch_shapes=[pltpu.VMEM((12 * row_total + PAD, cols), F32)],
        name="combine",
    )(*inputs)
    cube = displacement.shape
    return (res.reshape(cube), tan.reshape(cube), fit_res, fit_tan)


def solution(mesh):
    in_specs = (
        P(None, ("tx", "pb"), "ty"),
        P(None, ("tx", "pb"), "ty"),
        P(None, ("tx", "pb"), "ty"),
        P(),
        P(),
        P(),
        P(),
        P(),
        P(None, ("groups", "tx", "ty", "pb")),
        P(None, ("groups", "tx", "ty", "pb")),
        P(("groups", "tx", "ty", "pb")),
        P(("groups", "tx", "ty", "pb"), None),
        P(("groups", "tx", "ty", "pb")),
    )
    out_specs = (
        P(None, ("groups", "tx", "pb"), "ty"),
        P(None, ("groups", "tx", "pb"), "ty"),
        P(None, ("groups", "tx", "ty", "pb")),
        P(None, ("groups", "tx", "ty", "pb")),
    )
    return jax.shard_map(
        per_device, mesh=mesh, in_specs=in_specs, out_specs=out_specs, check_vma=False
    )
```
